32 devices in a mesh: dp: 16 (over z, y, x), band: 2 (over core).
Axes of the slice: x: 2, y: 2, z: 4, core: 2. Of those that a mesh axis runs over, the one named last changes fastest.
Arguments:
- inputs: float32 [16, 2048, 768], P('dp', 'band'), may hold values from -6 to 6
- segment_ids: int32 [16, 2048], P('dp', 'band'), may hold values from 0 to 15, as said below
- cotangent: float32 [16, 2048, 768], P('dp', 'band'), may hold values from -6 to 6
- first_gain: float32 [768], replicated, may hold values from 0.5 to 1.5
- first_bias: float32 [768], replicated, may hold values from -4 to 4
- w_qkv: bfloat16 [768, 2304], replicated, may hold values from -0.21875 to 0.21875
- query_bias: float32 [768], replicated, may hold values from -4 to 4
- value_bias: float32 [768], replicated, may hold values from -4 to 4
- w_proj: bfloat16 [768, 768], replicated, may hold values from -0.875 to 0.875
- proj_bias: float32 [768], replicated, may hold values from -4 to 4
- second_gain: float32 [768], replicated, may hold values from 0.5 to 1.5
- second_bias: float32 [768], replicated, may hold values from -4 to 4
- w_up: bfloat16 [768, 3072], replicated, may hold values from -0.21875 to 0.21875
- up_bias: float32 [3072], replicated, may hold values from -4 to 4
- w_down: bfloat16 [3072, 768], replicated, may hold values from -0.109375 to 0.109375
- down_bias: float32 [768], replicated, may hold values from -4 to 4
Outputs:
- output: float32 [16, 2048, 768], P('dp', 'band')
- input_grad: float32 [16, 2048, 768], P('dp', 'band')
- first_gain_grad: float32 [768], P('dp')
- first_bias_grad: float32 [768], P('dp')
- qkv_grad: float32 [768, 2304], P('dp', 'band')
- query_bias_grad: float32 [768], P('dp')
- value_bias_grad: float32 [768], P('dp')
- proj_grad: float32 [768, 768], P('dp', 'band')
- proj_bias_grad: float32 [768], P('dp')
- second_gain_grad: float32 [768], P('dp')
- second_bias_grad: float32 [768], P('dp')
- up_grad: float32 [768, 3072], P('dp', 'band')
- up_bias_grad: float32 [3072], P('dp')
- down_grad: float32 [3072, 768], P('dp', 'band')
- down_bias_grad: float32 [768], P('dp')
The draws below stay inside these ranges and needn't reach their ends.
Inputs may be any that keep to these rules, and one draw needn't show every extreme that they name: `segment_ids`: in every sequence the ids start at 0, never fall, and rise by one where a new tile begins; every sequence has the same number of tiles; positions 512 to 1535 of every sequence lie in one tile.
All inputs are finite; a program needn't handle non-finite values.
Results may differ from the reference program's by a relative error of at most 0.012.
Values may be sent and summed in bfloat16 or wider, within the bound.
A program may use at most 384 MiB of HBM per device.

```python
import jax
import jax.numpy as jnp
from jax import lax

D = 768
HEADS = 12
HEAD_DIM = 64
FF = 3072
SEQ = 2048
SEQS = 16


def draw_segment_ids(key, part):
    period = max(SEQ // 64, 2)
    quarter_steps = SEQ // 4 // period
    groups = SEQ // period // 2
    picks = jax.random.randint(key, (SEQS, groups), 0, 2).astype(jnp.int32)
    place = jnp.arange(SEQ, dtype=jnp.int32)
    step_index = place // period
    group_index = step_index // 2
    on_grid = place % period == 0
    in_first = (group_index >= 1) & (group_index < quarter_steps // 2)
    in_last = group_index >= 3 * quarter_steps // 2
    usable = on_grid & (in_first | in_last)
    chosen = jnp.take_along_axis(picks, jnp.broadcast_to(group_index[None, :], (SEQS, SEQ)), axis=1)
    starts = (usable[None, :] & ((step_index % 2)[None, :] == chosen)).astype(jnp.int32)
    return jnp.cumsum(starts, axis=1).astype(jnp.int32)


def strengthened(values, own_key, source, target, blocks, factor):
    def block_of(position):
        return (jnp.arange(values.shape[position]) // (values.shape[position] // blocks)).reshape((-1,) + (1,) * (values.ndim - 1 - position))

    one_side = jax.random.permutation(own_key, blocks)[block_of(target)]
    second = (block_of(target) + blocks // 2) % blocks
    return jnp.where((block_of(source) == one_side) | (block_of(source) == second), factor * values, values)


def steps_of(stream_key, dims, cuts, low, high):
    def one(axis_at, blocks):
        draws = jax.random.uniform(jax.random.fold_in(jax.random.fold_in(stream_key, 6), axis_at), (blocks,), jnp.float32, low / len(cuts), high / len(cuts))
        return jnp.repeat(jnp.exp(draws), dims[axis_at] // blocks).reshape((-1,) + (1,) * (len(dims) - axis_at - 1))

    level = one(*cuts[0])
    for cut in cuts[1:]:
        level = level * one(*cut)
    return level


def scatter_about(own_key, dims, width, bound, cuts=(), held_as=jnp.bfloat16):
    drawn = jax.random.normal(own_key, dims, jnp.float32) * width
    if len(cuts) > 0:
        drawn = steps_of(own_key, dims, cuts, -0.22, 0.18) * drawn
    return jnp.clip(drawn, min=-bound, max=bound).astype(held_as)


def bell_draw_with(own_key, extent, deviation, most, shards, heavy, kind=jnp.bfloat16):
    values = deviation * jax.random.normal(own_key, extent, jnp.float32)
    if shards:
        values = values * steps_of(own_key, extent, shards, -0.22, 0.18)
    return jnp.clip(strengthened(values, jax.random.fold_in(own_key, 3), *heavy), -most, most).astype(kind)


def setup_inputs(seed: int = 0) -> dict:
    streams_of = jax.random.split(jax.random.key(seed), 17)
    inputs = scatter_about(streams_of[0], (SEQS, SEQ, D), 1.0, 6.0, ((0, 16), (1, 2)), jnp.float32)
    segment_ids = draw_segment_ids(jax.random.fold_in(streams_of[16], 71), 0)
    cotangent = bell_draw_with(streams_of[2], (SEQS, SEQ, D), 1.0, 6.0, ((0, 16), (1, 2)), (0, 2, 16, 2.0), jnp.float32)
    first_gain = jnp.clip(1.0 + 0.1 * jax.random.normal(streams_of[3], (D,), jnp.float32), 0.5, 1.5)
    first_bias = scatter_about(streams_of[4], (D,), 0.3, 4.0, (), jnp.float32)
    w_qkv = scatter_about(streams_of[5], (D, 3 * D), D ** -0.5, 0.21875)
    query_bias = scatter_about(streams_of[6], (D,), 0.3, 4.0, (), jnp.float32)
    value_bias = scatter_about(streams_of[7], (D,), 0.3, 4.0, (), jnp.float32)
    w_proj = scatter_about(streams_of[8], (D, D), (D // 16) ** -0.5, 0.875)
    proj_bias = scatter_about(streams_of[9], (D,), 0.3, 4.0, (), jnp.float32)
    second_gain = jnp.clip(1.0 + 0.1 * jax.random.normal(streams_of[10], (D,), jnp.float32), 0.5, 1.5)
    second_bias = scatter_about(streams_of[11], (D,), 0.3, 4.0, (), jnp.float32)
    w_up = scatter_about(streams_of[12], (D, FF), D ** -0.5, 0.21875)
    up_bias = scatter_about(streams_of[13], (FF,), 0.3, 4.0, (), jnp.float32)
    w_down = scatter_about(streams_of[14], (FF, D), FF ** -0.5, 0.109375)
    down_bias = scatter_about(streams_of[15], (D,), 0.3, 4.0, (), jnp.float32)
    return dict(inputs=inputs, segment_ids=segment_ids, cotangent=cotangent, first_gain=first_gain, first_bias=first_bias, w_qkv=w_qkv, query_bias=query_bias, value_bias=value_bias, w_proj=w_proj, proj_bias=proj_bias, second_gain=second_gain, second_bias=second_bias, w_up=w_up, up_bias=up_bias, w_down=w_down, down_bias=down_bias)


@jax.custom_vjp
def low(v):
    return lax.optimization_barrier(v.astype(jnp.bfloat16)).astype(jnp.float32)

@jax.custom_vjp
def low_back(v):
    return v

def low_keep(v):
    return (low(v), None)

def low_pass(kept, grad):
    return (grad,)

def back_keep(v):
    return (v, None)

def back_low(kept, grad):
    return (low(grad),)
low.defvjp(low_keep, low_pass)
low_back.defvjp(back_keep, back_low)
EPS = 1e-05
NEG_LARGE = -1e+30
PRECISE = lax.Precision.HIGHEST

def layer_norm(values, gain, shift):
    average = lax.optimization_barrier(jnp.mean(values, axis=-1, keepdims=True))
    centred = values - average
    spread = lax.optimization_barrier(jnp.mean(centred * centred, axis=-1, keepdims=True))
    return centred * lax.rsqrt(spread + EPS) * gain + shift

def sequence_forward(tokens, segments, params):
    first_gain, first_bias, w_qkv, query_bias, value_bias, w_proj, proj_bias, second_gain, second_bias, w_up, up_bias, w_down, down_bias = params
    softmax_scale = HEAD_DIM ** (-0.5)
    normed_one = layer_norm(tokens, first_gain, first_bias)
    packed = jnp.dot(low(normed_one), w_qkv, precision=PRECISE)
    queries = low(low_back(packed[:, :D] + query_bias)).reshape(SEQ, HEADS, HEAD_DIM)
    key_rows = low(low_back(packed[:, D:2 * D])).reshape(SEQ, HEADS, HEAD_DIM)
    value_rows = low(low_back(packed[:, 2 * D:] + value_bias)).reshape(SEQ, HEADS, HEAD_DIM)
    raw_scores = low_back(jnp.einsum('qhd,khd->hqk', queries, key_rows, precision=PRECISE) * softmax_scale)
    allowed = segments[:, None] == segments[None, :]
    scores = jnp.where(allowed[None], raw_scores, NEG_LARGE)
    row_max = lax.optimization_barrier(jnp.max(scores, axis=-1, keepdims=True))
    lifted = jnp.exp(scores - row_max)
    probs = lifted / lax.optimization_barrier(jnp.sum(lifted, axis=-1, keepdims=True))
    mixed = jnp.einsum('hqk,khd->qhd', low(probs), value_rows, precision=PRECISE).reshape(SEQ, D)
    attended = low(low_back(mixed))
    residual = tokens + low_back(jnp.dot(attended, w_proj, precision=PRECISE) + proj_bias)
    normed_two = layer_norm(residual, second_gain, second_bias)
    upper = low_back(jnp.dot(low(normed_two), w_up, precision=PRECISE) + up_bias)
    hidden = low(jax.nn.gelu(upper, approximate=False))
    return residual + low_back(jnp.dot(hidden, w_down, precision=PRECISE) + down_bias)

def reference(inputs, segment_ids, cotangent, first_gain, first_bias, w_qkv, query_bias, value_bias, w_proj, proj_bias, second_gain, second_bias, w_up, up_bias, w_down, down_bias):
    params = tuple((weight.astype(jnp.float32) for weight in (first_gain, first_bias, w_qkv, query_bias, value_bias, w_proj, proj_bias, second_gain, second_bias, w_up, up_bias, w_down, down_bias)))

    def one_sequence(totals, pieces):
        tokens, segments, upstream = pieces

        def forward(values, weights):
            return sequence_forward(values, segments, weights)
        result, pull = jax.vjp(forward, tokens, params)
        token_grad, weight_grads = pull(upstream)
        totals = jax.tree.map(jnp.add, totals, weight_grads)
        return (totals, (result, token_grad))
    initial = tuple((jnp.zeros(weight.shape, jnp.float32) for weight in params))
    totals, (output, input_grad) = lax.scan(one_sequence, initial, (inputs, segment_ids, cotangent))
    return (output, input_grad, totals[0], totals[1], totals[2], totals[3], totals[4], totals[5], totals[6], totals[7], totals[8], totals[9], totals[10], totals[11], totals[12])
```

```python
import functools

import jax
import jax.numpy as jnp
from jax import lax
from jax.experimental import pallas as pl
from jax.experimental.pallas import tpu as pltpu
from jax.sharding import PartitionSpec as P

EPS = 1e-05
HEADS = 12
HEAD_DIM = 64
NEG_LARGE = -1e30
PAIRS = HEADS // 2
CHUNK = 256
MIB = 1 << 20
f32, bf16 = jnp.float32, jnp.bfloat16
NN = (((1,), (0,)), ((), ()))
NT = (((1,), (1,)), ((), ()))


def mm(a, b, dims=NN):
    return lax.dot_general(a, b, dims, preferred_element_type=f32)


def low_lanes(rows):
    return lax.broadcasted_iota(jnp.int32, (rows, 128), 1) < HEAD_DIM


def side_lanes(rows):
    return lax.broadcasted_iota(jnp.int32, (rows, 128), 1) & (HEAD_DIM - 1)


def split3(x):
    high = x.astype(bf16).astype(f32)
    middle = (x - high).astype(bf16).astype(f32)
    return high, middle, x - high - middle


def place(side, parts, base):
    for t, part in enumerate(parts):
        base = jnp.where(side == 16 + t, part, base)
    return base


def fill_pairs(src, dst, rows, low, extra):
    for p in range(PAIRS):
        pair = src[:, p * 128 : (p + 1) * 128]
        dst[2 * p, rows, :] = jnp.where(low, pair, extra)
        dst[2 * p + 1, rows, :] = jnp.where(low, extra, pair)


def fill_keys(band, i, k_own, k_far, v_own, v_far, seg_own, seg_far, kaug, vaug, value_extra):
    local = kaug.shape[1] // 2
    low, side = low_lanes(CHUNK), side_lanes(CHUNK)
    for k, v, seg, first in ((k_own, v_own, seg_own, band), (k_far, v_far, seg_far, 1 - band)):
        rows = pl.ds(pl.multiple_of(first * local + i * CHUNK, CHUNK), CHUNK)
        extra = jnp.where(side < 16, jnp.where(side == seg[...], 0.0, NEG_LARGE), jnp.where(side < 19, -1.0, 0.0))
        fill_pairs(k, kaug, rows, low, extra.astype(bf16))
        fill_pairs(v, vaug, rows, low, value_extra)


def attend_fwd_kernel(fills, BQ, BK, start_ref, count_ref, band_ref, q_ref, qseg_ref, k_own, k_far, v_own, v_far,
                      seg_own, seg_far, o_ref, lse_ref, kaug, vaug, qm, s_all, mx, acc):
    i = pl.program_id(0)

    @pl.when(i < fills)
    def _():
        fill_keys(band_ref[0], i, k_own, k_far, v_own, v_far, seg_own, seg_far, kaug, vaug, jnp.ones((CHUNK, 128), bf16))

    @pl.when(i >= fills)
    def _():
        low, side = low_lanes(BQ), side_lanes(BQ)
        own = (side == qseg_ref[...]).astype(f32).astype(bf16)
        for p in range(PAIRS):
            pair = q_ref[:, p * 128 : (p + 1) * 128]
            qm[2 * p] = jnp.where(low, pair, own)
            qm[2 * p + 1] = jnp.where(low, own, pair)
        mx[...] = jnp.full(mx.shape, -3e38, f32)
        acc[...] = jnp.zeros(acc.shape, f32)
        start = start_ref[i - fills]
        count = count_ref[i - fills]

        def first(j, c):
            at = pl.multiple_of(start + j * BK, 128)
            out = pl.ds(pl.multiple_of(j * BK, BK), BK)
            for h in range(HEADS):
                s = mm(qm[h], kaug[h, pl.ds(at, BK), :], NT)
                s_all[h, :, out] = s
                m = mx[h]
                for t in range(BK // 128):
                    m = jnp.maximum(m, s[:, t * 128 : (t + 1) * 128])
                mx[h] = m
            return c

        lax.fori_loop(0, count, first, 0)
        for h in range(HEADS):
            mx[h] = jnp.broadcast_to(jnp.max(mx[h], axis=1, keepdims=True), (BQ, 128))

        def second(j, c):
            at = pl.multiple_of(start + j * BK, 128)
            src = pl.ds(pl.multiple_of(j * BK, BK), BK)
            for h in range(HEADS):
                p = jnp.exp(s_all[h, :, src] - jnp.concatenate([mx[h]] * (BK // 128), axis=1)).astype(bf16)
                acc[h] += mm(p, vaug[h, pl.ds(at, BK), :])
            return c

        lax.fori_loop(0, count, second, 0)
        lane = lax.broadcasted_iota(jnp.int32, (BQ, 128), 1)
        lse = jnp.zeros((BQ, 128), f32)
        for p in range(PAIRS):
            even, odd = acc[2 * p], acc[2 * p + 1]
            swapped = pltpu.roll(even, HEAD_DIM, 1)
            total = jnp.where(low, swapped, pltpu.roll(odd, HEAD_DIM, 1))
            o_ref[:, p * 128 : (p + 1) * 128] = (jnp.where(low, even, odd) / total).astype(bf16)
            lse = jnp.where(lane == 2 * p, mx[2 * p] + jnp.log(swapped), lse)
            lse = jnp.where(lane == 2 * p + 1, mx[2 * p + 1] + jnp.log(odd), lse)
        lse_ref[...] = lse


def attend_forward(band, q, seg_own, seg_far, k_own, k_far, v_own, v_far, start, count, BQ=256, BK=256):
    rows, width = q.shape
    fills, steps = rows // CHUNK, rows // BQ
    mine = lambda i, *_: (jnp.clip(i - fills, 0, steps - 1), 0)
    fill = lambda i, *_: (jnp.minimum(i, fills - 1), 0)
    wide = pl.BlockSpec((CHUNK, width), fill)
    thin = pl.BlockSpec((CHUNK, 1), fill)
    return pl.pallas_call(
        functools.partial(attend_fwd_kernel, fills, BQ, BK),
        out_shape=(jax.ShapeDtypeStruct((rows, width), bf16), jax.ShapeDtypeStruct((rows, 128), f32)),
        grid_spec=pltpu.PrefetchScalarGridSpec(
            num_scalar_prefetch=3,
            grid=(fills + steps,),
            in_specs=[pl.BlockSpec((BQ, width), mine), pl.BlockSpec((BQ, 1), mine), wide, wide, wide, wide, thin, thin],
            out_specs=[pl.BlockSpec((BQ, width), mine), pl.BlockSpec((BQ, 128), mine)],
            scratch_shapes=[
                pltpu.VMEM((HEADS, 2 * rows, 128), bf16),
                pltpu.VMEM((HEADS, 2 * rows, 128), bf16),
                pltpu.VMEM((HEADS, BQ, 128), bf16),
                pltpu.VMEM((HEADS, BQ, 2 * rows), f32),
                pltpu.VMEM((HEADS, BQ, 128), f32),
                pltpu.VMEM((HEADS, BQ, 128), f32),
            ],
        ),
        compiler_params=pltpu.CompilerParams(vmem_limit_bytes=56 * MIB),
        cost_estimate=pl.CostEstimate(flops=30 * 10**9, bytes_accessed=10 * 10**6, transcendentals=0),
        name="attend_forward",
    )(start, count, band, q, seg_own, k_own, k_far, v_own, v_far, seg_own, seg_far)


def attend_bwd_kernel(fills, steps, BQ, BK, start_ref, count_ref, band_ref, q_ref, do_ref, o_ref, lse_ref, qseg_ref,
                      k_own, k_far, v_own, v_far, seg_own, seg_far, dq_ref, dkt_own, dkt_far, dvt_own, dvt_far,
                      kaug, vaug, qm, dom, lqt, ldot, dq_acc, dk_acc, dv_acc):
    i = pl.program_id(0)
    band = band_ref[0]
    local = kaug.shape[1] // 2

    @pl.when(i < fills)
    def _():
        side = side_lanes(CHUNK)
        extra = jnp.where((side >= 16) & (side < 19), -1.0, 0.0).astype(bf16)
        fill_keys(band, i, k_own, k_far, v_own, v_far, seg_own, seg_far, kaug, vaug, extra)
        for part in range(2):
            cols = pl.ds(pl.multiple_of(part * local + i * CHUNK, CHUNK), CHUNK)
            for p in range(PAIRS):
                dk_acc[p, :, cols] = jnp.zeros((128, CHUNK), f32)
                dv_acc[p, :, cols] = jnp.zeros((128, CHUNK), f32)

    @pl.when((i >= fills) & (i < fills + steps))
    def _():
        low, side = low_lanes(BQ), side_lanes(BQ)
        own = (side == qseg_ref[...]).astype(f32)
        for p in range(PAIRS):
            cols = slice(p * 128, (p + 1) * 128)
            q_pair, do_pair = q_ref[:, cols], do_ref[:, cols]
            prod = do_pair.astype(f32) * o_ref[:, cols].astype(f32)
            for e in range(2):
                mine = low if e == 0 else jnp.logical_not(low)
                h = 2 * p + e
                delta = jnp.sum(jnp.where(mine, prod, 0.0), axis=1, keepdims=True)
                qm[h] = jnp.where(mine, q_pair, place(side, split3(lse_ref[:, h : h + 1]), own).astype(bf16))
                dom[h] = jnp.where(mine, do_pair, place(side, split3(delta), jnp.zeros_like(own)).astype(bf16))
            zero = jnp.zeros((HEAD_DIM, BQ), bf16)
            for pair, dst in ((q_pair, lqt), (do_pair, ldot)):
                flipped = pair.T
                dst[p, 0:HEAD_DIM, 0:BQ] = flipped[0:HEAD_DIM]
                dst[p, HEAD_DIM:128, 0:BQ] = zero
                dst[p, 0:HEAD_DIM, BQ : 2 * BQ] = zero
                dst[p, HEAD_DIM:128, BQ : 2 * BQ] = flipped[HEAD_DIM:128]
        dq_acc[...] = jnp.zeros(dq_acc.shape, f32)
        start = start_ref[i - fills]

        def step(j, c):
            window = pl.ds(pl.multiple_of(start + j * BK, 128), BK)

            def scores(h):
                return mm(qm[h], kaug[h, window, :], NT), mm(dom[h], vaug[h, window, :], NT)

            ahead = scores(0)
            kept = []
            for h in range(HEADS):
                p = h // 2
                s, dp = ahead
                if h + 1 < HEADS:
                    ahead = scores(h + 1)
                prob = jnp.exp(s)
                ds = (prob * dp).astype(bf16)
                kept.append((prob.astype(bf16), ds))
                dq_acc[h] += mm(ds, kaug[h, window, :])
                if h % 2:
                    dv_acc[p, :, window] += mm(ldot[p], jnp.concatenate([kept[0][0], kept[1][0]], axis=0))
                    dk_acc[p, :, window] += mm(lqt[p], jnp.concatenate([kept[0][1], kept[1][1]], axis=0))
                    kept = []
            return c

        lax.fori_loop(0, count_ref[i - fills], step, 0)
        for p in range(PAIRS):
            pair = jnp.where(low, dq_acc[2 * p], dq_acc[2 * p + 1]) * HEAD_DIM**-0.5
            dq_ref[:, p * 128 : (p + 1) * 128] = pair.astype(bf16)

    @pl.when(i >= fills + steps)
    def _():
        j = i - fills - steps
        for p in range(PAIRS):
            rows = slice(p * 128, (p + 1) * 128)
            for first, dk_out, dv_out in ((band, dkt_own, dvt_own), (1 - band, dkt_far, dvt_far)):
                cols = pl.ds(pl.multiple_of(first * local + j * CHUNK, CHUNK), CHUNK)
                dk_out[rows, :] = dk_acc[p, :, cols].astype(bf16)
                dv_out[rows, :] = dv_acc[p, :, cols].astype(bf16)


def attend_backward(band, q, do, o, lse, seg_own, seg_far, k_own, k_far, v_own, v_far, start, count, BQ=256, BK=256):
    rows, width = q.shape
    fills, steps = rows // CHUNK, rows // BQ
    mine = lambda i, *_: (jnp.clip(i - fills, 0, steps - 1), 0)
    fill = lambda i, *_: (jnp.minimum(i, fills - 1), 0)
    drain = lambda i, *_: (0, jnp.clip(i - fills - steps, 0, fills - 1))
    wide = pl.BlockSpec((CHUNK, width), fill)
    thin = pl.BlockSpec((CHUNK, 1), fill)
    block = pl.BlockSpec((BQ, width), mine)
    flat = jax.ShapeDtypeStruct((width, rows), bf16)
    return pl.pallas_call(
        functools.partial(attend_bwd_kernel, fills, steps, BQ, BK),
        out_shape=(jax.ShapeDtypeStruct((rows, width), bf16), flat, flat, flat, flat),
        grid_spec=pltpu.PrefetchScalarGridSpec(
            num_scalar_prefetch=3,
            grid=(fills + steps + fills,),
            in_specs=[block, block, block, pl.BlockSpec((BQ, 128), mine), pl.BlockSpec((BQ, 1), mine), wide, wide, wide, wide, thin, thin],
            out_specs=[block] + [pl.BlockSpec((width, CHUNK), drain)] * 4,
            scratch_shapes=[
                pltpu.VMEM((HEADS, 2 * rows, 128), bf16),
                pltpu.VMEM((HEADS, 2 * rows, 128), bf16),
                pltpu.VMEM((HEADS, BQ, 128), bf16),
                pltpu.VMEM((HEADS, BQ, 128), bf16),
                pltpu.VMEM((PAIRS, 128, 2 * BQ), bf16),
                pltpu.VMEM((PAIRS, 128, 2 * BQ), bf16),
                pltpu.VMEM((HEADS, BQ, 128), f32),
                pltpu.VMEM((PAIRS, 128, 2 * rows), f32),
                pltpu.VMEM((PAIRS, 128, 2 * rows), f32),
            ],
        ),
        compiler_params=pltpu.CompilerParams(vmem_limit_bytes=56 * MIB),
        cost_estimate=pl.CostEstimate(flops=45 * 10**9, bytes_accessed=20 * 10**6, transcendentals=0),
        name="attend_backward",
    )(start, count, band, q, do, o, lse, seg_own, k_own, k_far, v_own, v_far, seg_own, seg_far)


def key_windows(seg_own, seg_far, band, BQ=256, BK=256):
    keys = 2 * seg_own.shape[0]
    blocks = seg_own.reshape(-1, BQ)
    first, last = blocks[:, 0], blocks[:, -1]

    def below(limit, strict):
        def count(seg):
            return jnp.sum((seg[None, :] < limit[:, None]) if strict else (seg[None, :] <= limit[:, None]), axis=1, dtype=jnp.int32)

        return count(seg_own) + count(seg_far)

    lo = below(first, True) // 128 * 128
    count = (below(last, False) - lo + BK - 1) // BK
    return jnp.minimum(lo, keys - count * BK), count


def layer_norm(values, gain, shift):
    average = jnp.mean(values, axis=-1, keepdims=True)
    centred = values - average
    spread = jnp.mean(centred * centred, axis=-1, keepdims=True)
    return centred * lax.rsqrt(spread + EPS) * gain + shift


def gelu_exact(upper):
    return jax.nn.gelu(upper, approximate=False)


def column_sums(block):
    return jnp.sum(block.astype(f32), axis=0)


def low_dot(a, b, dims=NN):
    return mm(a, b, dims).astype(bf16)


def swap_band(x):
    return lax.ppermute(x, "band", [(0, 1), (1, 0)])


def split_band(grad):
    band = lax.axis_index("band")
    half = grad.shape[1] // 2
    return (
        lax.dynamic_slice_in_dim(grad, band * half, half, 1),
        lax.dynamic_slice_in_dim(grad, (1 - band) * half, half, 1),
    )


def pick(x, which, axis):
    return lax.dynamic_index_in_dim(x, which, axis, keepdims=False)


def halve(x, axis, bit, size):
    mine = (lax.axis_index("dp") >> bit) & 1
    arrived = lax.ppermute(pick(x, 1 - mine, axis), "dp", [(i, i ^ (1 << bit)) for i in range(size)])
    return pick(x, mine, axis).astype(f32) + arrived.astype(f32)


def reduce_dp(x, order, size):
    rows, columns = x.shape
    levels = size.bit_length() - 1
    x = x.reshape((2,) * levels + (rows // size, columns))
    left = list(range(levels - 1, -1, -1))
    for bit in order:
        axis = left.index(bit)
        x = halve(x, axis, bit, size)
        left.remove(bit)
        if left:
            x = x.astype(bf16)
    return x


def local(
    size,
    inputs,
    segment_ids,
    cotangent,
    first_gain,
    first_bias,
    w_qkv,
    query_bias,
    value_bias,
    w_proj,
    proj_bias,
    second_gain,
    second_bias,
    w_up,
    up_bias,
    w_down,
    down_bias,
):
    local_shape = inputs.shape
    width = local_shape[-1]
    levels = size.bit_length() - 1
    rising = list(range(levels))
    turned = [1, 0] + list(range(2, levels))
    band = lax.axis_index("band")
    band_at = band.astype(jnp.int32).reshape(1)
    tokens = inputs.reshape(-1, width)
    seg_own = segment_ids.reshape(-1)
    seg_far = swap_band(seg_own)
    start, count = key_windows(seg_own, seg_far, band)
    normed_one, first_pull = jax.vjp(layer_norm, tokens, first_gain, first_bias)
    normed_low = normed_one.astype(bf16)
    k_own = low_dot(normed_low, w_qkv[:, width : 2 * width])
    k_far = swap_band(k_own)
    v_own = (mm(normed_low, w_qkv[:, 2 * width :]) + value_bias).astype(bf16)
    v_far = swap_band(v_own)
    queries = (mm(normed_low, w_qkv[:, :width]) + query_bias).astype(bf16) * jnp.asarray(HEAD_DIM**-0.5, bf16)
    keys = (seg_own[:, None], seg_far[:, None], k_own, k_far, v_own, v_far, start, count)
    attended, log_totals = attend_forward(band_at, queries, *keys)
    residual = tokens + mm(attended, w_proj) + proj_bias
    normed_two, second_pull = jax.vjp(layer_norm, residual, second_gain, second_bias)
    normed_two_low = normed_two.astype(bf16)
    upper = mm(normed_two_low, w_up) + up_bias
    hidden_full, gelu_pull = jax.vjp(gelu_exact, upper)
    hidden = hidden_full.astype(bf16)
    output = residual + mm(hidden, w_down) + down_bias
    upstream = cotangent.reshape(-1, width)
    branch_grad = upstream.astype(bf16)
    down_own, down_far = split_band(low_dot(hidden.T, branch_grad))
    down_half = (down_own.astype(f32) + swap_band(down_far).astype(f32)).astype(bf16)
    down_bias_grad = column_sums(branch_grad)
    hidden_grad = mm(branch_grad, w_down.T)
    upper_grad = gelu_pull(hidden_grad)[0].astype(bf16)
    up_own, up_far = split_band(low_dot(normed_two_low.T, upper_grad))
    up_half = (up_own.astype(f32) + swap_band(up_far).astype(f32)).astype(bf16)
    up_bias_grad = column_sums(upper_grad)
    normed_two_grad = mm(upper_grad, w_up.T)
    residual_part, second_gain_grad, second_bias_grad = second_pull(normed_two_grad)
    residual_grad = upstream + residual_part
    attn_grad = residual_grad.astype(bf16)
    proj_grad = low_dot(attended.T, attn_grad)
    proj_bias_grad = column_sums(attn_grad)
    attended_grad = low_dot(attn_grad, w_proj.T)
    query_grad, dkt_own, dkt_far, dvt_own, dvt_far = attend_backward(
        band_at, queries, attended_grad, attended, log_totals, *keys
    )
    dkt = (dkt_own.astype(f32) + swap_band(dkt_far).astype(f32)).astype(bf16)
    dvt = (dvt_own.astype(f32) + swap_band(dvt_far).astype(f32)).astype(bf16)
    query_bias_grad = column_sums(query_grad)
    value_bias_grad = jnp.sum(dvt.astype(f32), axis=1)
    packed_grad = jnp.concatenate([query_grad, dkt.T, dvt.T], axis=1)
    qkv_own, qkv_far = split_band(low_dot(normed_low.T, packed_grad))
    qkv_half = (qkv_own.astype(f32) + swap_band(qkv_far).astype(f32)).astype(bf16)
    normed_one_grad = mm(packed_grad, w_qkv.T)
    input_part, first_gain_grad, first_bias_grad = first_pull(normed_one_grad)
    input_grad = residual_grad + input_part
    proj_own, proj_far = split_band(proj_grad)
    proj_half = (proj_own.astype(f32) + swap_band(proj_far).astype(f32)).astype(bf16)
    tall = (
        first_gain_grad,
        first_bias_grad,
        query_bias_grad,
        value_bias_grad,
        proj_bias_grad,
        second_gain_grad,
        second_bias_grad,
        down_bias_grad,
    )
    thin = jnp.concatenate([jnp.stack(tall, axis=1), up_bias_grad.reshape(width, -1)], axis=1)
    thin = jnp.pad(thin, ((0, 0), (0, 128 - thin.shape[1]))).astype(bf16)
    thin = (thin.astype(f32) + swap_band(thin).astype(f32)).astype(bf16)
    down_sum = reduce_dp(down_half, rising, size)
    up_sum = reduce_dp(up_half, turned, size)
    proj_sum = reduce_dp(proj_half, turned, size)
    qkv_sum = reduce_dp(qkv_half, rising, size)
    thin_sum = reduce_dp(thin, turned, size)
    vectors = [thin_sum[:, t] for t in range(len(tall))]
    return (
        output.reshape(local_shape),
        input_grad.reshape(local_shape),
        vectors[0],
        vectors[1],
        qkv_sum,
        vectors[2],
        vectors[3],
        proj_sum,
        vectors[4],
        vectors[5],
        vectors[6],
        up_sum,
        thin_sum[:, len(tall) : len(tall) + up_bias.shape[0] // width].reshape(-1),
        down_sum,
        vectors[7],
    )


def solution(mesh):
    size = mesh.shape["dp"]
    placed = (P("dp", "band", None), P("dp", "band"), P("dp", "band", None)) + (P(),) * 13
    split, thin = P("dp", "band"), P("dp")
    wide = P("dp", "band", None)
    return jax.shard_map(
        functools.partial(local, size),
        mesh=mesh,
        in_specs=placed,
        out_specs=(wide, wide, thin, thin, split, thin, thin, split, thin, thin, thin, split, thin, split, thin),
        check_vma=False,
    )
```

```python
import functools

import jax
import jax.numpy as jnp
from jax import lax
from jax.experimental import pallas as pl
from jax.experimental.pallas import tpu as pltpu
from jax.sharding import PartitionSpec as P

EPS = 1e-05
HEADS = 12
HEAD_DIM = 64
NEG_LARGE = -1e30
PAIRS = HEADS // 2
CHUNK = 256
MIB = 1 << 20
f32, bf16 = jnp.float32, jnp.bfloat16
NN = (((1,), (0,)), ((), ()))
NT = (((1,), (1,)), ((), ()))


def mm(a, b, dims=NN):
    return lax.dot_general(a, b, dims, preferred_element_type=f32)


def low_lanes(rows):
    return lax.broadcasted_iota(jnp.int32, (rows, 128), 1) < HEAD_DIM


def side_lanes(rows):
    return lax.broadcasted_iota(jnp.int32, (rows, 128), 1) & (HEAD_DIM - 1)


def split3(x):
    high = x.astype(bf16).astype(f32)
    middle = (x - high).astype(bf16).astype(f32)
    return high, middle, x - high - middle


def place(side, parts, base):
    for t, part in enumerate(parts):
        base = jnp.where(side == 16 + t, part, base)
    return base


def fill_pairs(src, dst, rows, low, extra):
    for p in range(PAIRS):
        pair = src[:, p * 128 : (p + 1) * 128]
        dst[2 * p, rows, :] = jnp.where(low, pair, extra)
        dst[2 * p + 1, rows, :] = jnp.where(low, extra, pair)


def fill_keys(band, i, k_own, k_far, v_own, v_far, seg_own, seg_far, kaug, vaug, value_extra):
    local = kaug.shape[1] // 2
    low, side = low_lanes(CHUNK), side_lanes(CHUNK)
    for k, v, seg, first in ((k_own, v_own, seg_own, band), (k_far, v_far, seg_far, 1 - band)):
        rows = pl.ds(pl.multiple_of(first * local + i * CHUNK, CHUNK), CHUNK)
        extra = jnp.where(side < 16, jnp.where(side == seg[...], 0.0, NEG_LARGE), jnp.where(side < 19, -1.0, 0.0))
        fill_pairs(k, kaug, rows, low, extra.astype(bf16))
        fill_pairs(v, vaug, rows, low, value_extra)


def attend_fwd_kernel(fills, BQ, BK, start_ref, count_ref, band_ref, q_ref, qseg_ref, k_own, k_far, v_own, v_far,
                      seg_own, seg_far, o_ref, lse_ref, kaug, vaug, qm, s_all, mx, acc):
    i = pl.program_id(0)

    @pl.when(i < fills)
    def _():
        fill_keys(band_ref[0], i, k_own, k_far, v_own, v_far, seg_own, seg_far, kaug, vaug, jnp.ones((CHUNK, 128), bf16))

    @pl.when(i >= fills)
    def _():
        low, side = low_lanes(BQ), side_lanes(BQ)
        own = (side == qseg_ref[...]).astype(f32).astype(bf16)
        for p in range(PAIRS):
            pair = q_ref[:, p * 128 : (p + 1) * 128]
            qm[2 * p] = jnp.where(low, pair, own)
            qm[2 * p + 1] = jnp.where(low, own, pair)
        mx[...] = jnp.full(mx.shape, -3e38, f32)
        acc[...] = jnp.zeros(acc.shape, f32)
        start = start_ref[i - fills]
        count = count_ref[i - fills]

        def first(j, c):
            at = pl.multiple_of(start + j * BK, 128)
            out = pl.ds(pl.multiple_of(j * BK, BK), BK)
            for h in range(HEADS):
                s = mm(qm[h], kaug[h, pl.ds(at, BK), :], NT)
                s_all[h, :, out] = s
                m = mx[h]
                for t in range(BK // 128):
                    m = jnp.maximum(m, s[:, t * 128 : (t + 1) * 128])
                mx[h] = m
            return c

        lax.fori_loop(0, count, first, 0)
        for h in range(HEADS):
            mx[h] = jnp.broadcast_to(jnp.max(mx[h], axis=1, keepdims=True), (BQ, 128))

        def second(j, c):
            at = pl.multiple_of(start + j * BK, 128)
            src = pl.ds(pl.multiple_of(j * BK, BK), BK)
            for h in range(HEADS):
                p = jnp.exp(s_all[h, :, src] - jnp.concatenate([mx[h]] * (BK // 128), axis=1)).astype(bf16)
                acc[h] += mm(p, vaug[h, pl.ds(at, BK), :])
            return c

        lax.fori_loop(0, count, second, 0)
        lane = lax.broadcasted_iota(jnp.int32, (BQ, 128), 1)
        lse = jnp.zeros((BQ, 128), f32)
        for p in range(PAIRS):
            even, odd = acc[2 * p], acc[2 * p + 1]
            swapped = pltpu.roll(even, HEAD_DIM, 1)
            total = jnp.where(low, swapped, pltpu.roll(odd, HEAD_DIM, 1))
            o_ref[:, p * 128 : (p + 1) * 128] = (jnp.where(low, even, odd) / total).astype(bf16)
            lse = jnp.where(lane == 2 * p, mx[2 * p] + jnp.log(swapped), lse)
            lse = jnp.where(lane == 2 * p + 1, mx[2 * p + 1] + jnp.log(odd), lse)
        lse_ref[...] = lse


def attend_forward(band, q, seg_own, seg_far, k_own, k_far, v_own, v_far, start, count, BQ=256, BK=256):
    rows, width = q.shape
    fills, steps = rows // CHUNK, rows // BQ
    mine = lambda i, *_: (jnp.clip(i - fills, 0, steps - 1), 0)
    fill = lambda i, *_: (jnp.minimum(i, fills - 1), 0)
    wide = pl.BlockSpec((CHUNK, width), fill)
    thin = pl.BlockSpec((CHUNK, 1), fill)
    return pl.pallas_call(
        functools.partial(attend_fwd_kernel, fills, BQ, BK),
        out_shape=(jax.ShapeDtypeStruct((rows, width), bf16), jax.ShapeDtypeStruct((rows, 128), f32)),
        grid_spec=pltpu.PrefetchScalarGridSpec(
            num_scalar_prefetch=3,
            grid=(fills + steps,),
            in_specs=[pl.BlockSpec((BQ, width), mine), pl.BlockSpec((BQ, 1), mine), wide, wide, wide, wide, thin, thin],
            out_specs=[pl.BlockSpec((BQ, width), mine), pl.BlockSpec((BQ, 128), mine)],
            scratch_shapes=[
                pltpu.VMEM((HEADS, 2 * rows, 128), bf16),
                pltpu.VMEM((HEADS, 2 * rows, 128), bf16),
                pltpu.VMEM((HEADS, BQ, 128), bf16),
                pltpu.VMEM((HEADS, BQ, 2 * rows), f32),
                pltpu.VMEM((HEADS, BQ, 128), f32),
                pltpu.VMEM((HEADS, BQ, 128), f32),
            ],
        ),
        compiler_params=pltpu.CompilerParams(vmem_limit_bytes=56 * MIB),
        cost_estimate=pl.CostEstimate(flops=30 * 10**9, bytes_accessed=10 * 10**6, transcendentals=0),
        name="attend_forward",
    )(start, count, band, q, seg_own, k_own, k_far, v_own, v_far, seg_own, seg_far)


def attend_bwd_kernel(fills, steps, BQ, BK, start_ref, count_ref, band_ref, q_ref, do_ref, o_ref, lse_ref, qseg_ref,
                      k_own, k_far, v_own, v_far, seg_own, seg_far, dq_ref, dkt_own, dkt_far, dvt_own, dvt_far,
                      kaug, vaug, qm, dom, lqt, ldot, dq_acc, dk_acc, dv_acc):
    i = pl.program_id(0)
    band = band_ref[0]
    local = kaug.shape[1] // 2

    @pl.when(i < fills)
    def _():
        side = side_lanes(CHUNK)
        extra = jnp.where((side >= 16) & (side < 19), -1.0, 0.0).astype(bf16)
        fill_keys(band, i, k_own, k_far, v_own, v_far, seg_own, seg_far, kaug, vaug, extra)
        for part in range(2):
            cols = pl.ds(pl.multiple_of(part * local + i * CHUNK, CHUNK), CHUNK)
            for p in range(PAIRS):
                dk_acc[p, :, cols] = jnp.zeros((128, CHUNK), f32)
                dv_acc[p, :, cols] = jnp.zeros((128, CHUNK), f32)

    @pl.when((i >= fills) & (i < fills + steps))
    def _():
        low, side = low_lanes(BQ), side_lanes(BQ)
        own = (side == qseg_ref[...]).astype(f32)
        for p in range(PAIRS):
            cols = slice(p * 128, (p + 1) * 128)
            q_pair, do_pair = q_ref[:, cols], do_ref[:, cols]
            prod = do_pair.astype(f32) * o_ref[:, cols].astype(f32)
            for e in range(2):
                mine = low if e == 0 else jnp.logical_not(low)
                h = 2 * p + e
                delta = jnp.sum(jnp.where(mine, prod, 0.0), axis=1, keepdims=True)
                qm[h] = jnp.where(mine, q_pair, place(side, split3(lse_ref[:, h : h + 1]), own).astype(bf16))
                dom[h] = jnp.where(mine, do_pair, place(side, split3(delta), jnp.zeros_like(own)).astype(bf16))
            zero = jnp.zeros((HEAD_DIM, BQ), bf16)
            for pair, dst in ((q_pair, lqt), (do_pair, ldot)):
                flipped = pair.T
                dst[p, 0:HEAD_DIM, 0:BQ] = flipped[0:HEAD_DIM]
                dst[p, HEAD_DIM:128, 0:BQ] = zero
                dst[p, 0:HEAD_DIM, BQ : 2 * BQ] = zero
                dst[p, HEAD_DIM:128, BQ : 2 * BQ] = flipped[HEAD_DIM:128]
        dq_acc[...] = jnp.zeros(dq_acc.shape, f32)
        start = start_ref[i - fills]

        def step(j, c):
            window = pl.ds(pl.multiple_of(start + j * BK, 128), BK)

            def scores(h):
                return mm(qm[h], kaug[h, window, :], NT), mm(dom[h], vaug[h, window, :], NT)

            ahead = scores(0)
            kept = []
            for h in range(HEADS):
                p = h // 2
                s, dp = ahead
                if h + 1 < HEADS:
                    ahead = scores(h + 1)
                prob = jnp.exp(s)
                ds = (prob * dp).astype(bf16)
                kept.append((prob.astype(bf16), ds))
                dq_acc[h] += mm(ds, kaug[h, window, :])
                if h % 2:
                    dv_acc[p, :, window] += mm(ldot[p], jnp.concatenate([kept[0][0], kept[1][0]], axis=0))
                    dk_acc[p, :, window] += mm(lqt[p], jnp.concatenate([kept[0][1], kept[1][1]], axis=0))
                    kept = []
            return c

        lax.fori_loop(0, count_ref[i - fills], step, 0)
        for p in range(PAIRS):
            pair = jnp.where(low, dq_acc[2 * p], dq_acc[2 * p + 1]) * HEAD_DIM**-0.5
            dq_ref[:, p * 128 : (p + 1) * 128] = pair.astype(bf16)

    @pl.when(i >= fills + steps)
    def _():
        j = i - fills - steps
        for p in range(PAIRS):
            rows = slice(p * 128, (p + 1) * 128)
            for first, dk_out, dv_out in ((band, dkt_own, dvt_own), (1 - band, dkt_far, dvt_far)):
                cols = pl.ds(pl.multiple_of(first * local + j * CHUNK, CHUNK), CHUNK)
                dk_out[rows, :] = dk_acc[p, :, cols].astype(bf16)
                dv_out[rows, :] = dv_acc[p, :, cols].astype(bf16)


def attend_backward(band, q, do, o, lse, seg_own, seg_far, k_own, k_far, v_own, v_far, start, count, BQ=256, BK=256):
    rows, width = q.shape
    fills, steps = rows // CHUNK, rows // BQ
    mine = lambda i, *_: (jnp.clip(i - fills, 0, steps - 1), 0)
    fill = lambda i, *_: (jnp.minimum(i, fills - 1), 0)
    drain = lambda i, *_: (0, jnp.clip(i - fills - steps, 0, fills - 1))
    wide = pl.BlockSpec((CHUNK, width), fill)
    thin = pl.BlockSpec((CHUNK, 1), fill)
    block = pl.BlockSpec((BQ, width), mine)
    flat = jax.ShapeDtypeStruct((width, rows), bf16)
    return pl.pallas_call(
        functools.partial(attend_bwd_kernel, fills, steps, BQ, BK),
        out_shape=(jax.ShapeDtypeStruct((rows, width), bf16), flat, flat, flat, flat),
        grid_spec=pltpu.PrefetchScalarGridSpec(
            num_scalar_prefetch=3,
            grid=(fills + steps + fills,),
            in_specs=[block, block, block, pl.BlockSpec((BQ, 128), mine), pl.BlockSpec((BQ, 1), mine), wide, wide, wide, wide, thin, thin],
            out_specs=[block] + [pl.BlockSpec((width, CHUNK), drain)] * 4,
            scratch_shapes=[
                pltpu.VMEM((HEADS, 2 * rows, 128), bf16),
                pltpu.VMEM((HEADS, 2 * rows, 128), bf16),
                pltpu.VMEM((HEADS, BQ, 128), bf16),
                pltpu.VMEM((HEADS, BQ, 128), bf16),
                pltpu.VMEM((PAIRS, 128, 2 * BQ), bf16),
                pltpu.VMEM((PAIRS, 128, 2 * BQ), bf16),
                pltpu.VMEM((HEADS, BQ, 128), f32),
                pltpu.VMEM((PAIRS, 128, 2 * rows), f32),
                pltpu.VMEM((PAIRS, 128, 2 * rows), f32),
            ],
        ),
        compiler_params=pltpu.CompilerParams(vmem_limit_bytes=56 * MIB),
        cost_estimate=pl.CostEstimate(flops=45 * 10**9, bytes_accessed=20 * 10**6, transcendentals=0),
        name="attend_backward",
    )(start, count, band, q, do, o, lse, seg_own, k_own, k_far, v_own, v_far, seg_own, seg_far)


def key_windows(seg_own, seg_far, band, BQ=256, BK=256):
    keys = 2 * seg_own.shape[0]
    blocks = seg_own.reshape(-1, BQ)
    first, last = blocks[:, 0], blocks[:, -1]

    def below(limit, strict):
        def count(seg):
            return jnp.sum((seg[None, :] < limit[:, None]) if strict else (seg[None, :] <= limit[:, None]), axis=1, dtype=jnp.int32)

        return count(seg_own) + count(seg_far)

    lo = below(first, True) // 128 * 128
    count = (below(last, False) - lo + BK - 1) // BK
    return jnp.minimum(lo, keys - count * BK), count


TN = (((0,), (0,)), ((), ()))
SLICE = 768
ERFC_RATE = 0.39
ERFC_TERMS = (0.23532524, 0.09138829, 0.64955972, -0.63540067, 0.88666461, -0.22753718)


def gelu_and_slope(u):
    bell = jnp.exp(u * u * -0.5)
    t = 1.0 / (1.0 + jnp.abs(u) * (ERFC_RATE * 0.5**0.5))
    total = ERFC_TERMS[-1] * 0.5
    for term in ERFC_TERMS[-2::-1]:
        total = total * t + term * 0.5
    half = total * t * bell
    below = jnp.where(u < 0, half, 1.0 - half)
    return u * below, below + u * bell * (0.5 / 3.141592653589793) ** 0.5


def normalize(rows):
    centred = rows - jnp.mean(rows, axis=-1, keepdims=True)
    scale = lax.rsqrt(jnp.mean(centred * centred, axis=-1, keepdims=True) + EPS)
    return centred * scale, scale


def add_sums(ref, row, values, first):
    sums = jnp.sum(values, axis=0, keepdims=True)
    at = slice(row, row + 1)
    ref[at, :] = jnp.where(first, sums, ref[at, :] + sums)


def mlp_kernel(blocks, rows, slices, band_ref, tok_ref, att_ref, cot_ref, wproj, wup, wdown, pbias, gain, shift, ubias, dbias,
               out_ref, rgrad_ref, agrad_ref, down_own, down_far, up_own, up_far, proj_own, proj_far, sums_ref, usums_ref,
               hid, ugr, n2s, bgs, ags, ats):
    i = pl.program_id(0)
    band = band_ref[0]
    half = down_own.shape[1]

    @pl.when(i < blocks)
    def _():
        here = pl.ds(pl.multiple_of(i * rows, rows), rows)
        first = i == 0
        att = att_ref[...]
        ats[here, :] = att
        residual = tok_ref[...] + mm(att, wproj[...]) + pbias[...]
        xhat, scale = normalize(residual)
        n2 = (xhat * gain[...] + shift[...]).astype(bf16)
        n2s[here, :] = n2
        cot = cot_ref[...]
        bg = cot.astype(bf16)
        bgs[here, :] = bg
        add_sums(sums_ref, 0, bg.astype(f32), first)
        for c in range(slices):
            cols = slice(c * SLICE, (c + 1) * SLICE)
            hidden, slope = gelu_and_slope(mm(n2, wup[:, cols]) + ubias[:, cols])
            hid[here, cols] = hidden.astype(bf16)
            grad = (mm(bg, wdown[cols, :], NT) * slope).astype(bf16)
            ugr[here, cols] = grad
            sums = jnp.sum(grad.astype(f32), axis=0, keepdims=True)
            usums_ref[0:1, cols] = jnp.where(first, sums, usums_ref[0:1, cols] + sums)
        out_ref[...] = residual + mm(hid[here, :], wdown[...]) + dbias[...]
        e = mm(ugr[here, :], wup[...], NT)
        add_sums(sums_ref, 1, e * xhat, first)
        add_sums(sums_ref, 2, e, first)
        f = e * gain[...]
        rgrad = cot + scale * (f - jnp.mean(f, axis=-1, keepdims=True) - xhat * jnp.mean(f * xhat, axis=-1, keepdims=True))
        rgrad_ref[...] = rgrad
        ag = rgrad.astype(bf16)
        ags[here, :] = ag
        add_sums(sums_ref, 3, ag.astype(f32), first)
        agrad_ref[...] = mm(ag, wproj[...], NT).astype(bf16)

    def columns(grad, own, far):
        left, right = grad[:, :half].astype(bf16), grad[:, half:].astype(bf16)
        own[...] = jnp.where(band == 0, left, right)
        far[...] = jnp.where(band == 0, right, left)

    @pl.when((i >= blocks) & (i < blocks + slices))
    def _():
        at = pl.ds(pl.multiple_of((i - blocks) * SLICE, SLICE), SLICE)
        columns(mm(hid[:, at], bgs[...], TN), down_own, down_far)

    def up_slice(which):
        at = pl.ds(pl.multiple_of(which * SLICE, SLICE), SLICE)
        return mm(n2s[...], ugr[:, at], TN).astype(bf16)

    middle = blocks + slices
    per_half = slices // 2

    @pl.when((i >= middle) & (i < middle + per_half))
    def _():
        up_far[...] = up_slice((1 - band) * per_half + i - middle)

    @pl.when((i >= middle + per_half) & (i < middle + slices))
    def _():
        up_own[...] = up_slice(band * per_half + i - middle - per_half)

    @pl.when(i == middle + slices)
    def _():
        columns(mm(ats[...], ags[...], TN), proj_own, proj_far)


def mlp(band, tokens, attended, cotangent, w_proj, w_up, w_down, proj_bias, gain, shift, up_bias, down_bias, rows=256):
    count, width = tokens.shape
    ff = w_up.shape[1]
    blocks, slices = count // rows, ff // SLICE
    half, per_half = width // 2, slices // 2
    one = pl.Buffered(1)
    mine = lambda i, *_: (jnp.minimum(i, blocks - 1), 0)
    whole = lambda i, *_: (0, 0)
    down_at = lambda i, *_: (jnp.clip(i - blocks, 0, slices - 1), 0)
    far_at = lambda i, *_: (0, jnp.clip(i - blocks - slices, 0, per_half - 1))
    own_at = lambda i, *_: (0, jnp.clip(i - blocks - slices - per_half, 0, per_half - 1))
    block = pl.BlockSpec((rows, width), mine)

    def full(a):
        return pl.BlockSpec(a.shape, whole, pipeline_mode=one)

    vectors = [v.reshape(1, -1) for v in (proj_bias, gain, shift, up_bias, down_bias)]
    shape = jax.ShapeDtypeStruct
    return pl.pallas_call(
        functools.partial(mlp_kernel, blocks, rows, slices),
        out_shape=(
            shape((count, width), f32),
            shape((count, width), f32),
            shape((count, width), bf16),
            shape((ff, half), bf16),
            shape((ff, half), bf16),
            shape((width, ff // 2), bf16),
            shape((width, ff // 2), bf16),
            shape((width, half), bf16),
            shape((width, half), bf16),
            shape((8, width), f32),
            shape((8, ff), f32),
        ),
        grid_spec=pltpu.PrefetchScalarGridSpec(
            num_scalar_prefetch=1,
            grid=(blocks + 2 * slices + 1,),
            in_specs=[block, block, block] + [full(a) for a in (w_proj, w_up, w_down, *vectors)],
            out_specs=[
                block,
                block,
                block,
                pl.BlockSpec((SLICE, half), down_at),
                pl.BlockSpec((SLICE, half), down_at),
                pl.BlockSpec((width, SLICE), own_at),
                pl.BlockSpec((width, SLICE), far_at),
                pl.BlockSpec((width, half), whole, pipeline_mode=one),
                pl.BlockSpec((width, half), whole, pipeline_mode=one),
                pl.BlockSpec((8, width), whole, pipeline_mode=one),
                pl.BlockSpec((8, ff), whole, pipeline_mode=one),
            ],
            scratch_shapes=[
                pltpu.VMEM((count, ff), bf16),
                pltpu.VMEM((count, ff), bf16),
                pltpu.VMEM((count, width), bf16),
                pltpu.VMEM((count, width), bf16),
                pltpu.VMEM((count, width), bf16),
                pltpu.VMEM((count, width), bf16),
            ],
        ),
        compiler_params=pltpu.CompilerParams(vmem_limit_bytes=58 * MIB),
        cost_estimate=pl.CostEstimate(flops=40 * 10**9, bytes_accessed=40 * 10**6, transcendentals=0),
        name="mlp",
    )(band, tokens, attended, cotangent, w_proj, w_up, w_down, *vectors)


def qkv_kernel(tok_ref, w_ref, gain, shift, qbias, vbias, q_ref, k_ref, v_ref, n_ref):
    width = tok_ref.shape[1]
    xhat, _ = normalize(tok_ref[...])
    n1 = (xhat * gain[...] + shift[...]).astype(bf16)
    n_ref[...] = n1
    k_ref[...] = mm(n1, w_ref[:, width : 2 * width]).astype(bf16)
    v_ref[...] = (mm(n1, w_ref[:, 2 * width :]) + vbias[...]).astype(bf16)
    q = (mm(n1, w_ref[:, :width]) + qbias[...]).astype(bf16)
    q_ref[...] = q * jnp.asarray(HEAD_DIM**-0.5, bf16)


def project_qkv(tokens, w_qkv, gain, shift, query_bias, value_bias, rows=256):
    count, width = tokens.shape
    one = pl.Buffered(1)
    block = pl.BlockSpec((rows, width), lambda i: (i, 0))
    vectors = [v.reshape(1, -1) for v in (gain, shift, query_bias, value_bias)]
    return pl.pallas_call(
        qkv_kernel,
        out_shape=(jax.ShapeDtypeStruct((count, width), bf16),) * 4,
        grid=(count // rows,),
        in_specs=[block] + [pl.BlockSpec(a.shape, lambda i: (0, 0), pipeline_mode=one) for a in (w_qkv, *vectors)],
        out_specs=[block] * 4,
        compiler_params=pltpu.CompilerParams(vmem_limit_bytes=32 * MIB),
        cost_estimate=pl.CostEstimate(flops=4 * 10**9, bytes_accessed=13 * 10**6, transcendentals=0),
        name="project_qkv",
    )(tokens, w_qkv, *vectors)


def qkv_grad_kernel(blocks, rows, band_ref, dq_ref, dk_own, dk_far, dv_own, dv_far, n_ref, packed_ref, own_ref, far_ref, sums_ref, packed):
    i = pl.program_id(0)
    band = band_ref[0]
    width = dq_ref.shape[1]
    half = own_ref.shape[1]

    @pl.when(i < blocks)
    def _():
        here = pl.ds(pl.multiple_of(i * rows, rows), rows)
        first = i == 0
        dq = dq_ref[...]
        packed_ref[:, :width] = dq
        packed[here, :width] = dq
        add_sums(sums_ref, 0, dq.astype(f32), first)
        for t, (own, far) in enumerate(((dk_own, dk_far), (dv_own, dv_far))):
            for p in range(width // 128):
                at = slice(p * 128, (p + 1) * 128)
                to = slice((t + 1) * width + p * 128, (t + 1) * width + (p + 1) * 128)
                turned = (own[at, :].astype(f32) + far[at, :].astype(f32)).astype(bf16).T
                packed_ref[:, to] = turned
                packed[here, to] = turned
        add_sums(sums_ref, 1, packed_ref[:, 2 * width :].astype(f32), first)

    def columns(which):
        at = pl.ds(pl.multiple_of(which * half, 128), half)
        return mm(n_ref[...], packed[:, at], TN).astype(bf16)

    @pl.when(i == blocks)
    def _():
        far_ref[...] = columns(1 - band)

    @pl.when(i == blocks + 1)
    def _():
        own_ref[...] = columns(band)


def qkv_grads(band, dq, dk_own, dk_far, dv_own, dv_far, normed, rows=256):
    count, width = dq.shape
    blocks = count // rows
    half = 3 * width // 2
    one = pl.Buffered(1)
    mine = lambda i, *_: (jnp.minimum(i, blocks - 1), 0)
    flip = lambda i, *_: (0, jnp.minimum(i, blocks - 1))
    whole = lambda i, *_: (0, 0)
    shape = jax.ShapeDtypeStruct
    return pl.pallas_call(
        functools.partial(qkv_grad_kernel, blocks, rows),
        out_shape=(shape((count, 3 * width), bf16), shape((width, half), bf16), shape((width, half), bf16), shape((8, width), f32)),
        grid_spec=pltpu.PrefetchScalarGridSpec(
            num_scalar_prefetch=1,
            grid=(blocks + 2,),
            in_specs=[pl.BlockSpec((rows, width), mine)]
            + [pl.BlockSpec((width, rows), flip)] * 4
            + [pl.BlockSpec((count, width), whole, pipeline_mode=one)],
            out_specs=[
                pl.BlockSpec((rows, 3 * width), mine),
                pl.BlockSpec((width, half), whole, pipeline_mode=one),
                pl.BlockSpec((width, half), whole, pipeline_mode=one),
                pl.BlockSpec((8, width), whole, pipeline_mode=one),
            ],
            scratch_shapes=[pltpu.VMEM((count, 3 * width), bf16)],
        ),
        compiler_params=pltpu.CompilerParams(vmem_limit_bytes=40 * MIB),
        cost_estimate=pl.CostEstimate(flops=8 * 10**9, bytes_accessed=18 * 10**6, transcendentals=0),
        name="qkv_grads",
    )(band, dq, dk_own, dk_far, dv_own, dv_far, normed)


def input_grad_kernel(packed_ref, tok_ref, rgrad_ref, w_ref, gain, out_ref, sums_ref):
    first = pl.program_id(0) == 0
    e = mm(packed_ref[...], w_ref[...], NT)
    xhat, scale = normalize(tok_ref[...])
    add_sums(sums_ref, 0, e * xhat, first)
    add_sums(sums_ref, 1, e, first)
    f = e * gain[...]
    back = scale * (f - jnp.mean(f, axis=-1, keepdims=True) - xhat * jnp.mean(f * xhat, axis=-1, keepdims=True))
    out_ref[...] = rgrad_ref[...] + back


def input_grads(packed, tokens, rgrad, w_qkv, gain, rows=256):
    count, width = tokens.shape
    one = pl.Buffered(1)
    block = pl.BlockSpec((rows, width), lambda i: (i, 0))
    return pl.pallas_call(
        input_grad_kernel,
        out_shape=(jax.ShapeDtypeStruct((count, width), f32), jax.ShapeDtypeStruct((8, width), f32)),
        grid=(count // rows,),
        in_specs=[
            pl.BlockSpec((rows, packed.shape[1]), lambda i: (i, 0)),
            block,
            block,
            pl.BlockSpec(w_qkv.shape, lambda i: (0, 0), pipeline_mode=one),
            pl.BlockSpec((1, width), lambda i: (0, 0), pipeline_mode=one),
        ],
        out_specs=[block, pl.BlockSpec((8, width), lambda i: (0, 0), pipeline_mode=one)],
        compiler_params=pltpu.CompilerParams(vmem_limit_bytes=32 * MIB),
        cost_estimate=pl.CostEstimate(flops=6 * 10**9, bytes_accessed=18 * 10**6, transcendentals=0),
        name="input_grads",
    )(packed, tokens, rgrad, w_qkv, gain.reshape(1, -1))


def swap_band(x):
    return lax.ppermute(x, "band", [(0, 1), (1, 0)])


def join_band(own, far):
    return (own.astype(f32) + swap_band(far).astype(f32)).astype(bf16)


def pick(x, which, axis):
    return lax.dynamic_index_in_dim(x, which, axis, keepdims=False)


def halve(x, axis, bit, size):
    mine = (lax.axis_index("dp") >> bit) & 1
    arrived = lax.ppermute(pick(x, 1 - mine, axis), "dp", [(i, i ^ (1 << bit)) for i in range(size)])
    return pick(x, mine, axis).astype(f32) + arrived.astype(f32)


class Reduction:
    def __init__(self, x, order, size):
        rows, columns = x.shape
        levels = size.bit_length() - 1
        self.size = size
        self.x = x.reshape((2,) * levels + (rows // size, columns))
        self.left = list(range(levels - 1, -1, -1))
        self.order = list(order)

    def step(self):
        if self.order:
            bit = self.order.pop(0)
            x = halve(self.x, self.left.index(bit), bit, self.size)
            self.left.remove(bit)
            self.x = x.astype(bf16) if self.left else x

    def finish(self):
        while self.order:
            self.step()
        return self.x


def local(
    size,
    inputs,
    segment_ids,
    cotangent,
    first_gain,
    first_bias,
    w_qkv,
    query_bias,
    value_bias,
    w_proj,
    proj_bias,
    second_gain,
    second_bias,
    w_up,
    up_bias,
    w_down,
    down_bias,
):
    local_shape = inputs.shape
    width = local_shape[-1]
    levels = size.bit_length() - 1
    rising = list(range(levels))
    turned = [1, 0] + list(range(2, levels))
    band = lax.axis_index("band")
    band_at = band.astype(jnp.int32).reshape(1)
    tokens = inputs.reshape(-1, width)
    seg_own = segment_ids.reshape(-1)
    seg_far = swap_band(seg_own)
    start, count = key_windows(seg_own, seg_far, band)
    queries, k_own, v_own, normed = project_qkv(tokens, w_qkv, first_gain, first_bias, query_bias, value_bias)
    k_far, v_far = swap_band(k_own), swap_band(v_own)
    keys = (seg_own[:, None], seg_far[:, None], k_own, k_far, v_own, v_far, start, count)
    attended, log_totals = attend_forward(band_at, queries, *keys)
    (
        output,
        residual_grad,
        attended_grad,
        down_own,
        down_far,
        up_own,
        up_far,
        proj_own,
        proj_far,
        mlp_sums,
        up_sums,
    ) = mlp(
        band_at,
        tokens,
        attended,
        cotangent.reshape(-1, width),
        w_proj,
        w_up,
        w_down,
        proj_bias,
        second_gain,
        second_bias,
        up_bias,
        down_bias,
    )
    down = Reduction(join_band(down_own, down_far), rising, size)
    up = Reduction(join_band(up_own, up_far), turned, size)
    query_grad, dk_own, dk_far, dv_own, dv_far = attend_backward(
        band_at, queries, attended_grad, attended, log_totals, *keys
    )
    packed, qkv_own, qkv_far, qkv_sums = qkv_grads(
        band_at, query_grad, dk_own, swap_band(dk_far), dv_own, swap_band(dv_far), normed
    )
    input_grad, first_sums = input_grads(packed, tokens, residual_grad, w_qkv, first_gain)
    proj = Reduction(join_band(proj_own, proj_far), turned, size)
    qkv = Reduction(join_band(qkv_own, qkv_far), rising, size)
    tall = jnp.concatenate([first_sums[:2], qkv_sums[:2], mlp_sums[:4]], axis=0)
    thin = jnp.concatenate([tall.T, up_sums[0].reshape(width, -1)], axis=1)
    thin = jnp.pad(thin, ((0, 0), (0, 128 - thin.shape[1]))).astype(bf16)
    thin_sum = Reduction(join_band(thin, thin), turned, size).finish()
    vectors = [thin_sum[:, t] for t in range(8)]
    ups = up_bias.shape[0] // width
    return (
        output.reshape(local_shape),
        input_grad.reshape(local_shape),
        vectors[0],
        vectors[1],
        qkv.finish(),
        vectors[2],
        vectors[3],
        proj.finish(),
        vectors[7],
        vectors[5],
        vectors[6],
        up.finish(),
        thin_sum[:, 8 : 8 + ups].reshape(-1),
        down.finish(),
        vectors[4],
    )


def solution(mesh):
    size = mesh.shape["dp"]
    placed = (P("dp", "band", None), P("dp", "band"), P("dp", "band", None)) + (P(),) * 13
    split, thin = P("dp", "band"), P("dp")
    wide = P("dp", "band", None)
    return jax.shard_map(
        functools.partial(local, size),
        mesh=mesh,
        in_specs=placed,
        out_specs=(wide, wide, thin, thin, split, thin, thin, split, thin, thin, thin, split, thin, split, thin),
        check_vma=False,
    )
```

```python
import functools

import jax
import jax.numpy as jnp
from jax import lax
from jax.experimental import pallas as pl
from jax.experimental.pallas import tpu as pltpu
from jax.sharding import PartitionSpec as P

EPS = 1e-05
HEADS = 12
HEAD_DIM = 64
NEG_LARGE = -1e30
PAIRS = HEADS // 2
CHUNK = 256
MIB = 1 << 20
f32, bf16 = jnp.float32, jnp.bfloat16
NN = (((1,), (0,)), ((), ()))
NT = (((1,), (1,)), ((), ()))


def mm(a, b, dims=NN):
    return lax.dot_general(a, b, dims, preferred_element_type=f32)


def low_lanes(rows):
    return lax.broadcasted_iota(jnp.int32, (rows, 128), 1) < HEAD_DIM


def side_lanes(rows):
    return lax.broadcasted_iota(jnp.int32, (rows, 128), 1) & (HEAD_DIM - 1)


def split3(x):
    high = x.astype(bf16).astype(f32)
    middle = (x - high).astype(bf16).astype(f32)
    return high, middle, x - high - middle


def place(side, parts, base):
    for t, part in enumerate(parts):
        base = jnp.where(side == 16 + t, part, base)
    return base


def fill_pairs(src, dst, rows, low, extra):
    for p in range(PAIRS):
        pair = src[:, p * 128 : (p + 1) * 128]
        dst[2 * p, rows, :] = jnp.where(low, pair, extra)
        dst[2 * p + 1, rows, :] = jnp.where(low, extra, pair)


def fill_keys(band, i, k_own, k_far, v_own, v_far, seg_own, seg_far, kaug, vaug, value_extra):
    local = kaug.shape[1] // 2
    low, side = low_lanes(CHUNK), side_lanes(CHUNK)
    for k, v, seg, first in ((k_own, v_own, seg_own, band), (k_far, v_far, seg_far, 1 - band)):
        rows = pl.ds(pl.multiple_of(first * local + i * CHUNK, CHUNK), CHUNK)
        extra = jnp.where(side < 16, jnp.where(side == seg[...], 0.0, NEG_LARGE), jnp.where(side < 19, -1.0, 0.0))
        fill_pairs(k, kaug, rows, low, extra.astype(bf16))
        fill_pairs(v, vaug, rows, low, value_extra)


def attend_fwd_kernel(fills, BQ, BK, start_ref, count_ref, band_ref, q_ref, qseg_ref, k_own, k_far, v_own, v_far,
                      seg_own, seg_far, o_ref, lse_ref, kaug, vaug, qm, s_all, mx, acc):
    i = pl.program_id(0)

    @pl.when(i < fills)
    def _():
        fill_keys(band_ref[0], i, k_own, k_far, v_own, v_far, seg_own, seg_far, kaug, vaug, jnp.ones((CHUNK, 128), bf16))

    @pl.when(i >= fills)
    def _():
        low, side = low_lanes(BQ), side_lanes(BQ)
        own = (side == qseg_ref[...]).astype(f32).astype(bf16)
        for p in range(PAIRS):
            pair = q_ref[:, p * 128 : (p + 1) * 128]
            qm[2 * p] = jnp.where(low, pair, own)
            qm[2 * p + 1] = jnp.where(low, own, pair)
        mx[...] = jnp.full(mx.shape, -3e38, f32)
        acc[...] = jnp.zeros(acc.shape, f32)
        start = start_ref[i - fills]
        count = count_ref[i - fills]

        def first(j, c):
            at = pl.multiple_of(start + j * BK, 128)
            out = pl.ds(pl.multiple_of(j * BK, BK), BK)
            for h in range(HEADS):
                s = mm(qm[h], kaug[h, pl.ds(at, BK), :], NT)
                s_all[h, :, out] = s
                m = mx[h]
                for t in range(BK // 128):
                    m = jnp.maximum(m, s[:, t * 128 : (t + 1) * 128])
                mx[h] = m
            return c

        lax.fori_loop(0, count, first, 0)
        for h in range(HEADS):
            mx[h] = jnp.broadcast_to(jnp.max(mx[h], axis=1, keepdims=True), (BQ, 128))

        def second(j, c):
            at = pl.multiple_of(start + j * BK, 128)
            src = pl.ds(pl.multiple_of(j * BK, BK), BK)
            for h in range(HEADS):
                p = jnp.exp(s_all[h, :, src] - jnp.concatenate([mx[h]] * (BK // 128), axis=1)).astype(bf16)
                acc[h] += mm(p, vaug[h, pl.ds(at, BK), :])
            return c

        lax.fori_loop(0, count, second, 0)
        lane = lax.broadcasted_iota(jnp.int32, (BQ, 128), 1)
        lse = jnp.zeros((BQ, 128), f32)
        for p in range(PAIRS):
            even, odd = acc[2 * p], acc[2 * p + 1]
            swapped = pltpu.roll(even, HEAD_DIM, 1)
            total = jnp.where(low, swapped, pltpu.roll(odd, HEAD_DIM, 1))
            o_ref[:, p * 128 : (p + 1) * 128] = (jnp.where(low, even, odd) / total).astype(bf16)
            lse = jnp.where(lane == 2 * p, mx[2 * p] + jnp.log(swapped), lse)
            lse = jnp.where(lane == 2 * p + 1, mx[2 * p + 1] + jnp.log(odd), lse)
        lse_ref[...] = lse


def attend_forward(band, q, seg_own, seg_far, k_own, k_far, v_own, v_far, start, count, BQ=256, BK=256):
    rows, width = q.shape
    fills, steps = rows // CHUNK, rows // BQ
    mine = lambda i, *_: (jnp.clip(i - fills, 0, steps - 1), 0)
    fill = lambda i, *_: (jnp.minimum(i, fills - 1), 0)
    wide = pl.BlockSpec((CHUNK, width), fill)
    thin = pl.BlockSpec((CHUNK, 1), fill)
    return pl.pallas_call(
        functools.partial(attend_fwd_kernel, fills, BQ, BK),
        out_shape=(jax.ShapeDtypeStruct((rows, width), bf16), jax.ShapeDtypeStruct((rows, 128), f32)),
        grid_spec=pltpu.PrefetchScalarGridSpec(
            num_scalar_prefetch=3,
            grid=(fills + steps,),
            in_specs=[pl.BlockSpec((BQ, width), mine), pl.BlockSpec((BQ, 1), mine), wide, wide, wide, wide, thin, thin],
            out_specs=[pl.BlockSpec((BQ, width), mine), pl.BlockSpec((BQ, 128), mine)],
            scratch_shapes=[
                pltpu.VMEM((HEADS, 2 * rows, 128), bf16),
                pltpu.VMEM((HEADS, 2 * rows, 128), bf16),
                pltpu.VMEM((HEADS, BQ, 128), bf16),
                pltpu.VMEM((HEADS, BQ, 2 * rows), f32),
                pltpu.VMEM((HEADS, BQ, 128), f32),
                pltpu.VMEM((HEADS, BQ, 128), f32),
            ],
        ),
        compiler_params=pltpu.CompilerParams(vmem_limit_bytes=56 * MIB),
        cost_estimate=pl.CostEstimate(flops=30 * 10**9, bytes_accessed=10 * 10**6, transcendentals=0),
        name="attend_forward",
    )(start, count, band, q, seg_own, k_own, k_far, v_own, v_far, seg_own, seg_far)


def attend_bwd_kernel(fills, steps, BQ, BK, start_ref, count_ref, band_ref, q_ref, do_ref, o_ref, lse_ref, qseg_ref,
                      k_own, k_far, v_own, v_far, seg_own, seg_far, dq_ref, dkt_own, dkt_far, dvt_own, dvt_far,
                      kaug, vaug, qm, dom, lqt, ldot, dq_acc, dk_acc, dv_acc):
    i = pl.program_id(0)
    band = band_ref[0]
    local = kaug.shape[1] // 2

    @pl.when(i < fills)
    def _():
        side = side_lanes(CHUNK)
        extra = jnp.where((side >= 16) & (side < 19), -1.0, 0.0).astype(bf16)
        fill_keys(band, i, k_own, k_far, v_own, v_far, seg_own, seg_far, kaug, vaug, extra)
        for part in range(2):
            cols = pl.ds(pl.multiple_of(part * local + i * CHUNK, CHUNK), CHUNK)
            for p in range(PAIRS):
                dk_acc[p, :, cols] = jnp.zeros((128, CHUNK), f32)
                dv_acc[p, :, cols] = jnp.zeros((128, CHUNK), f32)

    @pl.when((i >= fills) & (i < fills + steps))
    def _():
        low, side = low_lanes(BQ), side_lanes(BQ)
        own = (side == qseg_ref[...]).astype(f32)
        for p in range(PAIRS):
            cols = slice(p * 128, (p + 1) * 128)
            q_pair, do_pair = q_ref[:, cols], do_ref[:, cols]
            prod = do_pair.astype(f32) * o_ref[:, cols].astype(f32)
            for e in range(2):
                mine = low if e == 0 else jnp.logical_not(low)
                h = 2 * p + e
                delta = jnp.sum(jnp.where(mine, prod, 0.0), axis=1, keepdims=True)
                qm[h] = jnp.where(mine, q_pair, place(side, split3(lse_ref[:, h : h + 1]), own).astype(bf16))
                dom[h] = jnp.where(mine, do_pair, place(side, split3(delta), jnp.zeros_like(own)).astype(bf16))
            zero = jnp.zeros((HEAD_DIM, BQ), bf16)
            for pair, dst in ((q_pair, lqt), (do_pair, ldot)):
                flipped = pair.T
                dst[p, 0:HEAD_DIM, 0:BQ] = flipped[0:HEAD_DIM]
                dst[p, HEAD_DIM:128, 0:BQ] = zero
                dst[p, 0:HEAD_DIM, BQ : 2 * BQ] = zero
                dst[p, HEAD_DIM:128, BQ : 2 * BQ] = flipped[HEAD_DIM:128]
        dq_acc[...] = jnp.zeros(dq_acc.shape, f32)
        start = start_ref[i - fills]

        def step(j, c):
            window = pl.ds(pl.multiple_of(start + j * BK, 128), BK)

            def scores(h):
                return mm(qm[h], kaug[h, window, :], NT), mm(dom[h], vaug[h, window, :], NT)

            ahead = scores(0)
            kept = []
            for h in range(HEADS):
                p = h // 2
                s, dp = ahead
                if h + 1 < HEADS:
                    ahead = scores(h + 1)
                prob = jnp.exp(s)
                ds = (prob * dp).astype(bf16)
                kept.append((prob.astype(bf16), ds))
                dq_acc[h] += mm(ds, kaug[h, window, :])
                if h % 2:
                    dv_acc[p, :, window] += mm(ldot[p], jnp.concatenate([kept[0][0], kept[1][0]], axis=0))
                    dk_acc[p, :, window] += mm(lqt[p], jnp.concatenate([kept[0][1], kept[1][1]], axis=0))
                    kept = []
            return c

        lax.fori_loop(0, count_ref[i - fills], step, 0)
        for p in range(PAIRS):
            pair = jnp.where(low, dq_acc[2 * p], dq_acc[2 * p + 1]) * HEAD_DIM**-0.5
            dq_ref[:, p * 128 : (p + 1) * 128] = pair.astype(bf16)

    @pl.when(i >= fills + steps)
    def _():
        j = i - fills - steps
        for p in range(PAIRS):
            rows = slice(p * 128, (p + 1) * 128)
            for first, dk_out, dv_out in ((band, dkt_own, dvt_own), (1 - band, dkt_far, dvt_far)):
                cols = pl.ds(pl.multiple_of(first * local + j * CHUNK, CHUNK), CHUNK)
                dk_out[rows, :] = dk_acc[p, :, cols].astype(bf16)
                dv_out[rows, :] = dv_acc[p, :, cols].astype(bf16)


def attend_backward(band, q, do, o, lse, seg_own, seg_far, k_own, k_far, v_own, v_far, start, count, BQ=256, BK=256):
    rows, width = q.shape
    fills, steps = rows // CHUNK, rows // BQ
    mine = lambda i, *_: (jnp.clip(i - fills, 0, steps - 1), 0)
    fill = lambda i, *_: (jnp.minimum(i, fills - 1), 0)
    drain = lambda i, *_: (0, jnp.clip(i - fills - steps, 0, fills - 1))
    wide = pl.BlockSpec((CHUNK, width), fill)
    thin = pl.BlockSpec((CHUNK, 1), fill)
    block = pl.BlockSpec((BQ, width), mine)
    flat = jax.ShapeDtypeStruct((width, rows), bf16)
    return pl.pallas_call(
        functools.partial(attend_bwd_kernel, fills, steps, BQ, BK),
        out_shape=(jax.ShapeDtypeStruct((rows, width), bf16), flat, flat, flat, flat),
        grid_spec=pltpu.PrefetchScalarGridSpec(
            num_scalar_prefetch=3,
            grid=(fills + steps + fills,),
            in_specs=[block, block, block, pl.BlockSpec((BQ, 128), mine), pl.BlockSpec((BQ, 1), mine), wide, wide, wide, wide, thin, thin],
            out_specs=[block] + [pl.BlockSpec((width, CHUNK), drain)] * 4,
            scratch_shapes=[
                pltpu.VMEM((HEADS, 2 * rows, 128), bf16),
                pltpu.VMEM((HEADS, 2 * rows, 128), bf16),
                pltpu.VMEM((HEADS, BQ, 128), bf16),
                pltpu.VMEM((HEADS, BQ, 128), bf16),
                pltpu.VMEM((PAIRS, 128, 2 * BQ), bf16),
                pltpu.VMEM((PAIRS, 128, 2 * BQ), bf16),
                pltpu.VMEM((HEADS, BQ, 128), f32),
                pltpu.VMEM((PAIRS, 128, 2 * rows), f32),
                pltpu.VMEM((PAIRS, 128, 2 * rows), f32),
            ],
        ),
        compiler_params=pltpu.CompilerParams(vmem_limit_bytes=56 * MIB),
        cost_estimate=pl.CostEstimate(flops=45 * 10**9, bytes_accessed=20 * 10**6, transcendentals=0),
        name="attend_backward",
    )(start, count, band, q, do, o, lse, seg_own, k_own, k_far, v_own, v_far, seg_own, seg_far)


def key_windows(seg_own, seg_far, band, BQ=256, BK=256):
    keys = 2 * seg_own.shape[0]
    blocks = seg_own.reshape(-1, BQ)
    first, last = blocks[:, 0], blocks[:, -1]

    def below(limit, strict):
        def count(seg):
            return jnp.sum((seg[None, :] < limit[:, None]) if strict else (seg[None, :] <= limit[:, None]), axis=1, dtype=jnp.int32)

        return count(seg_own) + count(seg_far)

    lo = below(first, True) // 128 * 128
    count = (below(last, False) - lo + BK - 1) // BK
    return jnp.minimum(lo, keys - count * BK), count


TN = (((0,), (0,)), ((), ()))
SLICE = 768
ERFC_RATE = 0.39
ERFC_TERMS = (0.23532524, 0.09138829, 0.64955972, -0.63540067, 0.88666461, -0.22753718)


def gelu_and_slope(u):
    bell = jnp.exp(u * u * -0.5)
    t = 1.0 / (1.0 + jnp.abs(u) * (ERFC_RATE * 0.5**0.5))
    total = ERFC_TERMS[-1] * 0.5
    for term in ERFC_TERMS[-2::-1]:
        total = total * t + term * 0.5
    half = total * t * bell
    below = jnp.where(u < 0, half, 1.0 - half)
    return u * below, below + u * bell * (0.5 / 3.141592653589793) ** 0.5


def normalize(rows):
    centred = rows - jnp.mean(rows, axis=-1, keepdims=True)
    scale = lax.rsqrt(jnp.mean(centred * centred, axis=-1, keepdims=True) + EPS)
    return centred * scale, scale


def add_sums(ref, row, values, first):
    sums = jnp.sum(values, axis=0, keepdims=True)
    at = slice(row, row + 1)
    ref[at, :] = jnp.where(first, sums, ref[at, :] + sums)


def mlp_kernel(blocks, rows, slices, band_ref, tok_ref, att_ref, cot_ref, wproj, wup, wdown, pbias, gain, shift, ubias, dbias,
               out_ref, rgrad_ref, agrad_ref, down_own, down_far, up_own, up_far, proj_own, proj_far, sums_ref, usums_ref,
               hid, ugr, n2s, bgs, ags, ats):
    i = pl.program_id(0)
    band = band_ref[0]
    half = down_own.shape[1]

    @pl.when(i < blocks)
    def _():
        here = pl.ds(pl.multiple_of(i * rows, rows), rows)
        first = i == 0
        att = att_ref[...]
        ats[here, :] = att
        residual = tok_ref[...] + mm(att, wproj[...]) + pbias[...]
        xhat, scale = normalize(residual)
        n2 = (xhat * gain[...] + shift[...]).astype(bf16)
        n2s[here, :] = n2
        cot = cot_ref[...]
        bg = cot.astype(bf16)
        bgs[here, :] = bg
        add_sums(sums_ref, 0, bg.astype(f32), first)
        for c in range(slices):
            cols = slice(c * SLICE, (c + 1) * SLICE)
            hidden, slope = gelu_and_slope(mm(n2, wup[:, cols]) + ubias[:, cols])
            hid[here, cols] = hidden.astype(bf16)
            grad = (mm(bg, wdown[cols, :], NT) * slope).astype(bf16)
            ugr[here, cols] = grad
            sums = jnp.sum(grad.astype(f32), axis=0, keepdims=True)
            usums_ref[0:1, cols] = jnp.where(first, sums, usums_ref[0:1, cols] + sums)
        out_ref[...] = residual + mm(hid[here, :], wdown[...]) + dbias[...]
        e = mm(ugr[here, :], wup[...], NT)
        add_sums(sums_ref, 1, e * xhat, first)
        add_sums(sums_ref, 2, e, first)
        f = e * gain[...]
        rgrad = cot + scale * (f - jnp.mean(f, axis=-1, keepdims=True) - xhat * jnp.mean(f * xhat, axis=-1, keepdims=True))
        rgrad_ref[...] = rgrad
        ag = rgrad.astype(bf16)
        ags[here, :] = ag
        add_sums(sums_ref, 3, ag.astype(f32), first)
        agrad_ref[...] = mm(ag, wproj[...], NT).astype(bf16)

    def columns(grad, own, far):
        left, right = grad[:, :half].astype(bf16), grad[:, half:].astype(bf16)
        own[...] = jnp.where(band == 0, left, right)
        far[...] = jnp.where(band == 0, right, left)

    @pl.when((i >= blocks) & (i < blocks + slices))
    def _():
        at = pl.ds(pl.multiple_of((i - blocks) * SLICE, SLICE), SLICE)
        columns(mm(hid[:, at], bgs[...], TN), down_own, down_far)

    def up_slice(which):
        at = pl.ds(pl.multiple_of(which * SLICE, SLICE), SLICE)
        return mm(n2s[...], ugr[:, at], TN).astype(bf16)

    middle = blocks + slices
    per_half = slices // 2

    @pl.when((i >= middle) & (i < middle + per_half))
    def _():
        up_far[...] = up_slice((1 - band) * per_half + i - middle)

    @pl.when((i >= middle + per_half) & (i < middle + slices))
    def _():
        up_own[...] = up_slice(band * per_half + i - middle - per_half)

    @pl.when(i == middle + slices)
    def _():
        columns(mm(ats[...], ags[...], TN), proj_own, proj_far)


def mlp(band, tokens, attended, cotangent, w_proj, w_up, w_down, proj_bias, gain, shift, up_bias, down_bias, rows=256):
    count, width = tokens.shape
    ff = w_up.shape[1]
    blocks, slices = count // rows, ff // SLICE
    half, per_half = width // 2, slices // 2
    one = pl.Buffered(1)
    mine = lambda i, *_: (jnp.minimum(i, blocks - 1), 0)
    whole = lambda i, *_: (0, 0)
    down_at = lambda i, *_: (jnp.clip(i - blocks, 0, slices - 1), 0)
    far_at = lambda i, *_: (0, jnp.clip(i - blocks - slices, 0, per_half - 1))
    own_at = lambda i, *_: (0, jnp.clip(i - blocks - slices - per_half, 0, per_half - 1))
    block = pl.BlockSpec((rows, width), mine)

    def full(a):
        return pl.BlockSpec(a.shape, whole, pipeline_mode=one)

    vectors = [v.reshape(1, -1) for v in (proj_bias, gain, shift, up_bias, down_bias)]
    shape = jax.ShapeDtypeStruct
    return pl.pallas_call(
        functools.partial(mlp_kernel, blocks, rows, slices),
        out_shape=(
            shape((count, width), f32),
            shape((count, width), f32),
            shape((count, width), bf16),
            shape((ff, half), bf16),
            shape((ff, half), bf16),
            shape((width, ff // 2), bf16),
            shape((width, ff // 2), bf16),
            shape((width, half), bf16),
            shape((width, half), bf16),
            shape((8, width), f32),
            shape((8, ff), f32),
        ),
        grid_spec=pltpu.PrefetchScalarGridSpec(
            num_scalar_prefetch=1,
            grid=(blocks + 2 * slices + 1,),
            in_specs=[block, block, block] + [full(a) for a in (w_proj, w_up, w_down, *vectors)],
            out_specs=[
                block,
                block,
                block,
                pl.BlockSpec((SLICE, half), down_at),
                pl.BlockSpec((SLICE, half), down_at),
                pl.BlockSpec((width, SLICE), own_at),
                pl.BlockSpec((width, SLICE), far_at),
                pl.BlockSpec((width, half), whole, pipeline_mode=one),
                pl.BlockSpec((width, half), whole, pipeline_mode=one),
                pl.BlockSpec((8, width), whole, pipeline_mode=one),
                pl.BlockSpec((8, ff), whole, pipeline_mode=one),
            ],
            scratch_shapes=[
                pltpu.VMEM((count, ff), bf16),
                pltpu.VMEM((count, ff), bf16),
                pltpu.VMEM((count, width), bf16),
                pltpu.VMEM((count, width), bf16),
                pltpu.VMEM((count, width), bf16),
                pltpu.VMEM((count, width), bf16),
            ],
        ),
        compiler_params=pltpu.CompilerParams(vmem_limit_bytes=58 * MIB),
        cost_estimate=pl.CostEstimate(flops=40 * 10**9, bytes_accessed=40 * 10**6, transcendentals=0),
        name="mlp",
    )(band, tokens, attended, cotangent, w_proj, w_up, w_down, *vectors)


def qkv_kernel(tok_ref, w_ref, gain, shift, qbias, vbias, q_ref, k_ref, v_ref, n_ref):
    width = tok_ref.shape[1]
    xhat, _ = normalize(tok_ref[...])
    n1 = (xhat * gain[...] + shift[...]).astype(bf16)
    n_ref[...] = n1
    k_ref[...] = mm(n1, w_ref[:, width : 2 * width]).astype(bf16)
    v_ref[...] = (mm(n1, w_ref[:, 2 * width :]) + vbias[...]).astype(bf16)
    q = (mm(n1, w_ref[:, :width]) + qbias[...]).astype(bf16)
    q_ref[...] = q * jnp.asarray(HEAD_DIM**-0.5, bf16)


def project_qkv(tokens, w_qkv, gain, shift, query_bias, value_bias, rows=256):
    count, width = tokens.shape
    one = pl.Buffered(1)
    block = pl.BlockSpec((rows, width), lambda i: (i, 0))
    vectors = [v.reshape(1, -1) for v in (gain, shift, query_bias, value_bias)]
    return pl.pallas_call(
        qkv_kernel,
        out_shape=(jax.ShapeDtypeStruct((count, width), bf16),) * 4,
        grid=(count // rows,),
        in_specs=[block] + [pl.BlockSpec(a.shape, lambda i: (0, 0), pipeline_mode=one) for a in (w_qkv, *vectors)],
        out_specs=[block] * 4,
        compiler_params=pltpu.CompilerParams(vmem_limit_bytes=32 * MIB),
        cost_estimate=pl.CostEstimate(flops=4 * 10**9, bytes_accessed=13 * 10**6, transcendentals=0),
        name="project_qkv",
    )(tokens, w_qkv, *vectors)


def qkv_grad_kernel(blocks, rows, band_ref, dq_ref, dk_own, dk_far, dv_own, dv_far, n_ref, packed_ref, own_ref, far_ref, sums_ref, packed):
    i = pl.program_id(0)
    band = band_ref[0]
    width = dq_ref.shape[1]
    half = own_ref.shape[1]

    @pl.when(i < blocks)
    def _():
        here = pl.ds(pl.multiple_of(i * rows, rows), rows)
        first = i == 0
        dq = dq_ref[...]
        packed_ref[:, :width] = dq
        packed[here, :width] = dq
        add_sums(sums_ref, 0, dq.astype(f32), first)
        for t, (own, far) in enumerate(((dk_own, dk_far), (dv_own, dv_far))):
            for p in range(width // 128):
                at = slice(p * 128, (p + 1) * 128)
                to = slice((t + 1) * width + p * 128, (t + 1) * width + (p + 1) * 128)
                turned = (own[at, :].astype(f32) + far[at, :].astype(f32)).astype(bf16).T
                packed_ref[:, to] = turned
                packed[here, to] = turned
        add_sums(sums_ref, 1, packed_ref[:, 2 * width :].astype(f32), first)

    def columns(which):
        at = pl.ds(pl.multiple_of(which * half, 128), half)
        return mm(n_ref[...], packed[:, at], TN).astype(bf16)

    @pl.when(i == blocks)
    def _():
        far_ref[...] = columns(1 - band)

    @pl.when(i == blocks + 1)
    def _():
        own_ref[...] = columns(band)


def qkv_grads(band, dq, dk_own, dk_far, dv_own, dv_far, normed, rows=256):
    count, width = dq.shape
    blocks = count // rows
    half = 3 * width // 2
    one = pl.Buffered(1)
    mine = lambda i, *_: (jnp.minimum(i, blocks - 1), 0)
    flip = lambda i, *_: (0, jnp.minimum(i, blocks - 1))
    whole = lambda i, *_: (0, 0)
    shape = jax.ShapeDtypeStruct
    return pl.pallas_call(
        functools.partial(qkv_grad_kernel, blocks, rows),
        out_shape=(shape((count, 3 * width), bf16), shape((width, half), bf16), shape((width, half), bf16), shape((8, width), f32)),
        grid_spec=pltpu.PrefetchScalarGridSpec(
            num_scalar_prefetch=1,
            grid=(blocks + 2,),
            in_specs=[pl.BlockSpec((rows, width), mine)]
            + [pl.BlockSpec((width, rows), flip)] * 4
            + [pl.BlockSpec((count, width), whole, pipeline_mode=one)],
            out_specs=[
                pl.BlockSpec((rows, 3 * width), mine),
                pl.BlockSpec((width, half), whole, pipeline_mode=one),
                pl.BlockSpec((width, half), whole, pipeline_mode=one),
                pl.BlockSpec((8, width), whole, pipeline_mode=one),
            ],
            scratch_shapes=[pltpu.VMEM((count, 3 * width), bf16)],
        ),
        compiler_params=pltpu.CompilerParams(vmem_limit_bytes=40 * MIB),
        cost_estimate=pl.CostEstimate(flops=8 * 10**9, bytes_accessed=18 * 10**6, transcendentals=0),
        name="qkv_grads",
    )(band, dq, dk_own, dk_far, dv_own, dv_far, normed)


def input_grad_kernel(packed_ref, tok_ref, rgrad_ref, w_ref, gain, out_ref, sums_ref):
    first = pl.program_id(0) == 0
    e = mm(packed_ref[...], w_ref[...], NT)
    xhat, scale = normalize(tok_ref[...])
    add_sums(sums_ref, 0, e * xhat, first)
    add_sums(sums_ref, 1, e, first)
    f = e * gain[...]
    back = scale * (f - jnp.mean(f, axis=-1, keepdims=True) - xhat * jnp.mean(f * xhat, axis=-1, keepdims=True))
    out_ref[...] = rgrad_ref[...] + back


def input_grads(packed, tokens, rgrad, w_qkv, gain, rows=256):
    count, width = tokens.shape
    one = pl.Buffered(1)
    block = pl.BlockSpec((rows, width), lambda i: (i, 0))
    return pl.pallas_call(
        input_grad_kernel,
        out_shape=(jax.ShapeDtypeStruct((count, width), f32), jax.ShapeDtypeStruct((8, width), f32)),
        grid=(count // rows,),
        in_specs=[
            pl.BlockSpec((rows, packed.shape[1]), lambda i: (i, 0)),
            block,
            block,
            pl.BlockSpec(w_qkv.shape, lambda i: (0, 0), pipeline_mode=one),
            pl.BlockSpec((1, width), lambda i: (0, 0), pipeline_mode=one),
        ],
        out_specs=[block, pl.BlockSpec((8, width), lambda i: (0, 0), pipeline_mode=one)],
        compiler_params=pltpu.CompilerParams(vmem_limit_bytes=32 * MIB),
        cost_estimate=pl.CostEstimate(flops=6 * 10**9, bytes_accessed=18 * 10**6, transcendentals=0),
        name="input_grads",
    )(packed, tokens, rgrad, w_qkv, gain.reshape(1, -1))


MESH = pl.DeviceIdType.MESH


def add_low(dst, a, b):
    dst[...] = (a[...].astype(f32) + b[...].astype(f32)).astype(bf16)


def finish_kernel(
    dq_hbm, dko_hbm, dkf_hbm, dvo_hbm, dvf_hbm, n_hbm, tok_hbm, rgrad_hbm, w_hbm, downo_hbm, downf_hbm, upo_hbm, upf_hbm,
    projo_hbm, projf_hbm, gain, msums, usums,
    out_hbm, down_out, up_out, qkv_out, proj_out, vec_out,
    packed, dko, dko_in, dvo, dvo_in, n1, tok, rgrad, wq, down, down_in, up, up_in, proj, proj_in, far, far_in, tail,
    one_d, one_u, one_t, two_d, two_u, two_t, thr_d, thr_u, thr_t, vec, vec_band, vec_x, vec_y, vec_z,
    load_sem, store_sem, swap_send, swap_recv, send, recv, vsend, vrecv,
):
    me = lax.axis_index("dp")
    band = lax.axis_index("band")
    x, y, z = me & 1, (me >> 1) & 1, me >> 2
    rows, width = tok.shape
    half = far.shape[-1]
    peer_band = (me, 1 - band)
    peer_x = (me ^ 1, band)
    peer_y = (me ^ 2, band)
    peers_z = [(((z + d) & 3) * 4 + (me & 3), band) for d in (1, 2, 3)]

    def load(t, src, dst):
        copy = pltpu.make_async_copy(src, dst, load_sem.at[t])
        copy.start()
        return copy

    loads = {
        "down": (load(0, downo_hbm, down), load(1, downf_hbm, down_in)),
        "up": (load(2, upo_hbm, up), load(3, upf_hbm, up_in)),
        "keys": (load(4, dko_hbm, dko), load(5, dvo_hbm, dvo), load(6, dq_hbm, packed.at[:, 0:width])),
        "normed": (load(7, n_hbm, n1),),
        "proj": (load(8, projo_hbm, proj), load(9, projf_hbm, proj_in)),
        "weight": (load(10, w_hbm, wq),),
        "rows": (load(11, tok_hbm, tok), load(12, rgrad_hbm, rgrad)),
    }

    def ready(name):
        for copy in loads[name]:
            copy.wait()

    barrier = pltpu.get_barrier_semaphore()
    for peer in (peer_band, peer_x, peer_y, *peers_z):
        pl.semaphore_signal(barrier, inc=1, device_id=peer, device_id_type=MESH)
    pl.semaphore_wait(barrier, 6)

    pending = []

    def push(src, dst, peer, s, r):
        copy = pltpu.make_async_remote_copy(src_ref=src, dst_ref=dst, send_sem=s, recv_sem=r, device_id=peer, device_id_type=MESH)
        copy.start()
        pending.append(copy)
        return copy

    swap_k = push(dkf_hbm, dko_in, peer_band, swap_send.at[0], swap_recv.at[0])
    swap_v = push(dvf_hbm, dvo_in, peer_band, swap_send.at[1], swap_recv.at[1])

    def each_shard(body):
        def step(s, c):
            body(s >> 2, (s >> 1) & 1, s & 1)
            return c

        lax.fori_loop(0, 16, step, 0)

    def first_stage(t, work, one, cut):
        a, b = cut
        return (
            push(work.at[:, :, 1 - x, a[0], a[1]], one.at[0], peer_x, send.at[t, 0, 0], recv.at[t, 0, 0]),
            push(work.at[:, 1 - y, :, b[0], b[1]], one.at[1], peer_y, send.at[t, 1, 0], recv.at[t, 1, 0]),
        )

    def second_stage(t, work, one, two, cut, copies):
        a, b = cut
        copies[0].wait_recv()

        def sum_a(s, c):
            zz, yy = s >> 1, s & 1
            add_low(one.at[0, zz, yy], one.at[0, zz, yy], work.at[zz, yy, x, a[0], a[1]])
            return c

        lax.fori_loop(0, 8, sum_a, 0)
        first = push(one.at[0, :, 1 - y], two.at[0], peer_y, send.at[t, 0, 1], recv.at[t, 0, 1])
        copies[1].wait_recv()

        def sum_b(s, c):
            zz, xx = s >> 1, s & 1
            add_low(one.at[1, zz, xx], one.at[1, zz, xx], work.at[zz, y, xx, b[0], b[1]])
            return c

        lax.fori_loop(0, 8, sum_b, 0)
        return first, push(one.at[1, :, 1 - x], two.at[1], peer_x, send.at[t, 1, 1], recv.at[t, 1, 1])

    def third_stage(t, one, two, three, copies):
        out = []
        for piece, mine in ((0, y), (1, x)):
            copies[piece].wait_recv()

            def total(zz, c, piece=piece, mine=mine):
                add_low(two.at[piece, zz], two.at[piece, zz], one.at[piece, zz, mine])
                return c

            lax.fori_loop(0, 4, total, 0)
            for d in (1, 2, 3):
                out.append(
                    push(two.at[piece, (z + d) & 3], three.at[piece, d - 1], peers_z[d - 1], send.at[t, piece, 1 + d], recv.at[t, piece, 1 + d])
                )
        return out

    def last(two, three, copies, piece):
        for d in range(3):
            copies[3 * piece + d].wait_recv()
        total = two[piece, z].astype(f32)
        for d in range(3):
            total = total + three[piece, d].astype(f32)
        return total

    everything = slice(None)
    down_cut = ((slice(0, 96), everything), (slice(96, 192), everything))
    wide_cut = ((everything, slice(0, 768)), (everything, slice(768, 1536)))

    ready("down")
    each_shard(lambda i, j, k: add_low(down.at[i, j, k], down.at[i, j, k], down_in.at[i, j, k]))
    d_one = first_stage(0, down, one_d, down_cut)
    ready("up")
    each_shard(lambda i, j, k: add_low(up.at[i, j, k], up.at[i, j, k], up_in.at[i, j, k]))
    u_one = first_stage(1, up, one_u, wide_cut)

    ready("keys")
    swap_k.wait_recv()
    swap_v.wait_recv()

    def turn(i, c):
        here = pl.ds(pl.multiple_of(i * 256, 256), 256)
        for t, (own, other) in enumerate(((dko, dko_in), (dvo, dvo_in))):
            for p in range(width // 128):
                at = slice(p * 128, (p + 1) * 128)
                turned = (own[at, here].astype(f32) + other[at, here].astype(f32)).astype(bf16).T
                packed[here, (t + 1) * width + p * 128 : (t + 1) * width + (p + 1) * 128] = turned
        return c

    lax.fori_loop(0, rows // 256, turn, 0)
    ready("normed")

    def columns(which):
        at = pl.ds(pl.multiple_of(which * half, 128), half)
        return mm(n1[...], packed[:, at], TN).astype(bf16).reshape(far.shape)

    far[...] = columns(1 - band)
    swap_far = push(far, far_in, peer_band, swap_send.at[2], swap_recv.at[2])
    tail[:, :, :, :, 0:half] = columns(band)
    ready("proj")
    each_shard(lambda i, j, k: add_low(tail.at[i, j, k, :, half : 2 * width], proj.at[i, j, k], proj_in.at[i, j, k]))
    swap_far.wait_recv()
    each_shard(lambda i, j, k: add_low(tail.at[i, j, k, :, 0:half], tail.at[i, j, k, :, 0:half], far_in.at[i, j, k]))
    t_one = first_stage(2, tail, one_t, wide_cut)
    d_two = second_stage(0, down, one_d, two_d, down_cut, d_one)
    u_two = second_stage(1, up, one_u, two_u, wide_cut, u_one)

    ready("weight")
    ready("rows")
    vec[...] = jnp.zeros(vec.shape, f32)

    def rows_back(i, c):
        here = pl.ds(pl.multiple_of(i * 256, 256), 256)
        e = mm(packed[here, :], wq[...], NT)
        xhat, scale = normalize(tok[here, :])
        vec[0:1, :] = vec[0:1, :] + jnp.sum(e * xhat, axis=0, keepdims=True)
        vec[1:2, :] = vec[1:2, :] + jnp.sum(e, axis=0, keepdims=True)
        vec[2:3, :] = vec[2:3, :] + jnp.sum(packed[here, 0:width].astype(f32), axis=0, keepdims=True)
        vec[3:4, :] = vec[3:4, :] + jnp.sum(packed[here, 2 * width : 3 * width].astype(f32), axis=0, keepdims=True)
        f = e * gain[...]
        back = scale * (f - jnp.mean(f, axis=-1, keepdims=True) - xhat * jnp.mean(f * xhat, axis=-1, keepdims=True))
        rgrad[here, :] = rgrad[here, :] + back
        return c

    lax.fori_loop(0, rows // 256, rows_back, 0)
    store = pltpu.make_async_copy(rgrad, out_hbm, store_sem)
    store.start()
    vec[4:8, :] = msums[0:4, :]
    for t in range(usums.shape[1] // width):
        vec[8 + t : 9 + t, :] = usums[0:1, t * width : (t + 1) * width]
    v_band = push(vec, vec_band, peer_band, vsend.at[0], vrecv.at[0])
    d_three = third_stage(0, one_d, two_d, thr_d, d_two)
    v_band.wait()
    vec_band[...] = vec[...] + vec_band[...]
    v_x = push(vec_band, vec_x, peer_x, vsend.at[1], vrecv.at[1])
    u_three = third_stage(1, one_u, two_u, thr_u, u_two)
    v_x.wait()
    vec_x[...] = vec_band[...] + vec_x[...]
    v_y = push(vec_x, vec_y, peer_y, vsend.at[2], vrecv.at[2])
    t_two = second_stage(2, tail, one_t, two_t, wide_cut, t_one)
    v_y.wait()
    vec_y[...] = vec_x[...] + vec_y[...]
    v_z = [push(vec_y, vec_z.at[d], peers_z[d], vsend.at[3 + d], vrecv.at[3 + d]) for d in range(3)]
    t_three = third_stage(2, one_t, two_t, thr_t, t_two)
    down_out[0:96, :] = last(two_d, thr_d, d_three, 0)
    down_out[96:192, :] = last(two_d, thr_d, d_three, 1)
    up_out[:, 0:768] = last(two_u, thr_u, u_three, 0)
    up_out[:, 768:1536] = last(two_u, thr_u, u_three, 1)
    for copy in v_z:
        copy.wait_recv()
    vec_out[...] = vec_y[...] + vec_z[0] + vec_z[1] + vec_z[2]
    qkv_out[:, 0:768] = last(two_t, thr_t, t_three, 0)
    final = last(two_t, thr_t, t_three, 1)
    qkv_out[:, 768:half] = final[:, 0 : half - 768]
    proj_out[...] = final[:, half - 768 :]
    done = {id(c) for c in (v_band, v_x, v_y)}
    for copy in pending:
        if id(copy) not in done:
            copy.wait_send()
    store.wait()


def finish(dq, dk_own, dk_far, dv_own, dv_far, normed, tokens, rgrad, w_qkv, down, up, proj, gain, msums, usums):
    rows, width = tokens.shape
    ff = usums.shape[1]
    half = 3 * width // 2
    shards = (4, 2, 2)
    d_shape, u_shape, p_shape = shards + (ff // 16, width // 2), shards + (width // 16, ff // 2), shards + (width // 16, width // 2)
    q_shape = shards + (width // 16, half)
    down_own, down_far = (a.reshape(d_shape) for a in down)
    up_own, up_far = (a.reshape(u_shape) for a in up)
    proj_own, proj_far = (a.reshape(p_shape) for a in proj)
    d_piece, w_piece = (ff // 32, width // 2), (width // 16, ff // 4)
    hbm, vmem = pl.BlockSpec(memory_space=pl.ANY), pl.BlockSpec(memory_space=pltpu.VMEM)
    shape = jax.ShapeDtypeStruct
    low = lambda *s: pltpu.VMEM(s, bf16)
    dma = pltpu.SemaphoreType.DMA
    return pl.pallas_call(
        finish_kernel,
        out_shape=(
            shape((rows, width), f32),
            shape((ff // 16, width // 2), f32),
            shape((width // 16, ff // 2), f32),
            shape((width // 16, half), f32),
            shape((width // 16, width // 2), f32),
            shape((16, width), f32),
        ),
        in_specs=[hbm] * 15 + [vmem] * 3,
        out_specs=[hbm] + [vmem] * 5,
        scratch_shapes=[
            low(rows, 3 * width),
            *([low(width, rows)] * 4),
            low(rows, width),
            pltpu.VMEM((rows, width), f32),
            pltpu.VMEM((rows, width), f32),
            low(width, 3 * width),
            low(*d_shape),
            low(*d_shape),
            low(*u_shape),
            low(*u_shape),
            low(*p_shape),
            low(*p_shape),
            low(*q_shape),
            low(*q_shape),
            low(*u_shape),
            low(2, 4, 2, *d_piece),
            low(2, 4, 2, *w_piece),
            low(2, 4, 2, *w_piece),
            low(2, 4, *d_piece),
            low(2, 4, *w_piece),
            low(2, 4, *w_piece),
            low(2, 3, *d_piece),
            low(2, 3, *w_piece),
            low(2, 3, *w_piece),
            pltpu.VMEM((16, width), f32),
            pltpu.VMEM((16, width), f32),
            pltpu.VMEM((16, width), f32),
            pltpu.VMEM((16, width), f32),
            pltpu.VMEM((3, 16, width), f32),
            dma((13,)),
            dma,
            dma((3,)),
            dma((3,)),
            dma((3, 2, 5)),
            dma((3, 2, 5)),
            dma((6,)),
            dma((6,)),
        ],
        compiler_params=pltpu.CompilerParams(vmem_limit_bytes=60 * MIB, collective_id=0, has_side_effects=True),
        cost_estimate=pl.CostEstimate(flops=20 * 10**9, bytes_accessed=40 * 10**6, transcendentals=0),
        name="finish",
    )(dq, dk_own, dk_far, dv_own, dv_far, normed, tokens, rgrad, w_qkv, down_own, down_far, up_own, up_far, proj_own, proj_far,
      gain.reshape(1, -1), msums, usums)


def swap_band(x):
    return lax.ppermute(x, "band", [(0, 1), (1, 0)])


def pick(x, which, axis):
    return lax.dynamic_index_in_dim(x, which, axis, keepdims=False)


def halve(x, axis, bit, size):
    mine = (lax.axis_index("dp") >> bit) & 1
    arrived = lax.ppermute(pick(x, 1 - mine, axis), "dp", [(i, i ^ (1 << bit)) for i in range(size)])
    return pick(x, mine, axis).astype(f32) + arrived.astype(f32)


class Reduction:
    def __init__(self, x, order, size):
        rows, columns = x.shape
        levels = size.bit_length() - 1
        self.size = size
        self.x = x.reshape((2,) * levels + (rows // size, columns))
        self.left = list(range(levels - 1, -1, -1))
        self.order = list(order)

    def step(self):
        if self.order:
            bit = self.order.pop(0)
            x = halve(self.x, self.left.index(bit), bit, self.size)
            self.left.remove(bit)
            self.x = x.astype(bf16) if self.left else x

    def finish(self):
        while self.order:
            self.step()
        return self.x


def finish_any(size, band_at, query_grad, dk_own, dk_far, dv_own, dv_far, normed, tokens, residual_grad, w_qkv, down, up, proj, gain, msums, usums):
    width = tokens.shape[1]
    rising = list(range(size.bit_length() - 1))
    turned = [1, 0] + rising[2:]
    packed, qkv_own, qkv_far, qkv_sums = qkv_grads(
        band_at, query_grad, dk_own, swap_band(dk_far), dv_own, swap_band(dv_far), normed
    )
    input_grad, first_sums = input_grads(packed, tokens, residual_grad, w_qkv, gain)

    def total(own, arrived, order):
        return Reduction((own.astype(f32) + arrived.astype(f32)).astype(bf16), order, size).finish()

    tall = jnp.concatenate([first_sums[:2], qkv_sums[:2], msums[:4]], axis=0)
    thin = jnp.concatenate([tall.T, usums[0].reshape(width, -1)], axis=1)
    thin = jnp.pad(thin, ((0, 0), (0, 128 - thin.shape[1]))).astype(bf16)
    thin_sum = total(thin, swap_band(thin), turned)
    ups = usums.shape[1] // width
    return (
        input_grad,
        total(*down, rising),
        total(*up, turned),
        total(qkv_own, swap_band(qkv_far), rising),
        total(*proj, turned),
        [thin_sum[:, t] for t in range(8)],
        thin_sum[:, 8 : 8 + ups].reshape(-1),
    )


def local(
    size,
    inputs,
    segment_ids,
    cotangent,
    first_gain,
    first_bias,
    w_qkv,
    query_bias,
    value_bias,
    w_proj,
    proj_bias,
    second_gain,
    second_bias,
    w_up,
    up_bias,
    w_down,
    down_bias,
):
    local_shape = inputs.shape
    width = local_shape[-1]
    band = lax.axis_index("band")
    band_at = band.astype(jnp.int32).reshape(1)
    tokens = inputs.reshape(-1, width)
    seg_own = segment_ids.reshape(-1)
    seg_far = swap_band(seg_own)
    start, count = key_windows(seg_own, seg_far, band)
    queries, k_own, v_own, normed = project_qkv(tokens, w_qkv, first_gain, first_bias, query_bias, value_bias)
    k_far, v_far = swap_band(k_own), swap_band(v_own)
    keys = (seg_own[:, None], seg_far[:, None], k_own, k_far, v_own, v_far, start, count)
    attended, log_totals = attend_forward(band_at, queries, *keys)
    (
        output,
        residual_grad,
        attended_grad,
        down_own,
        down_far,
        up_own,
        up_far,
        proj_own,
        proj_far,
        mlp_sums,
        up_sums,
    ) = mlp(
        band_at,
        tokens,
        attended,
        cotangent.reshape(-1, width),
        w_proj,
        w_up,
        w_down,
        proj_bias,
        second_gain,
        second_bias,
        up_bias,
        down_bias,
    )
    down, up, proj = (down_own, swap_band(down_far)), (up_own, swap_band(up_far)), (proj_own, swap_band(proj_far))
    query_grad, dk_own, dk_far, dv_own, dv_far = attend_backward(
        band_at, queries, attended_grad, attended, log_totals, *keys
    )
    ups = up_bias.shape[0] // width
    if size == 16:
        input_grad, down_sum, up_sum, qkv_sum, proj_sum, vec = finish(
            query_grad, dk_own, dk_far, dv_own, dv_far, normed, tokens, residual_grad, w_qkv, down, up, proj, first_gain, mlp_sums, up_sums
        )
        shard = width // size
        mine = lax.dynamic_slice_in_dim(vec[:8], lax.axis_index("dp") * shard, shard, 1)
        vectors = [mine[t] for t in range(8)]
        up_vector = lax.dynamic_slice_in_dim(vec[8 : 8 + ups].reshape(-1), lax.axis_index("dp") * ups * shard, ups * shard, 0)
    else:
        input_grad, down_sum, up_sum, qkv_sum, proj_sum, vectors, up_vector = finish_any(
            size, band_at, query_grad, dk_own, dk_far, dv_own, dv_far, normed, tokens, residual_grad, w_qkv, down, up, proj, first_gain, mlp_sums, up_sums
        )
    return (
        output.reshape(local_shape),
        input_grad.reshape(local_shape),
        vectors[0],
        vectors[1],
        qkv_sum,
        vectors[2],
        vectors[3],
        proj_sum,
        vectors[7],
        vectors[5],
        vectors[6],
        up_sum,
        up_vector,
        down_sum,
        vectors[4],
    )


def solution(mesh):
    size = mesh.shape["dp"]
    placed = (P("dp", "band", None), P("dp", "band"), P("dp", "band", None)) + (P(),) * 13
    split, thin = P("dp", "band"), P("dp")
    wide = P("dp", "band", None)
    return jax.shard_map(
        functools.partial(local, size),
        mesh=mesh,
        in_specs=placed,
        out_specs=(wide, wide, thin, thin, split, thin, thin, split, thin, thin, thin, split, thin, split, thin),
        check_vma=False,
    )
```

```python
import functools

import jax
import jax.numpy as jnp
from jax import lax
from jax.experimental import pallas as pl
from jax.experimental.pallas import tpu as pltpu
from jax.sharding import PartitionSpec as P

EPS = 1e-05
HEADS = 12
HEAD_DIM = 64
NEG_LARGE = -1e30
PAIRS = HEADS // 2
CHUNK = 256
MIB = 1 << 20
f32, bf16 = jnp.float32, jnp.bfloat16
NN = (((1,), (0,)), ((), ()))
NT = (((1,), (1,)), ((), ()))


def mm(a, b, dims=NN):
    return lax.dot_general(a, b, dims, preferred_element_type=f32)


def low_lanes(rows):
    return lax.broadcasted_iota(jnp.int32, (rows, 128), 1) < HEAD_DIM


def side_lanes(rows):
    return lax.broadcasted_iota(jnp.int32, (rows, 128), 1) & (HEAD_DIM - 1)


def split3(x):
    high = x.astype(bf16).astype(f32)
    middle = (x - high).astype(bf16).astype(f32)
    return high, middle, x - high - middle


def place(side, parts, base):
    for t, part in enumerate(parts):
        base = jnp.where(side == 16 + t, part, base)
    return base


def fill_pairs(src, dst, rows, low, extra):
    for p in range(PAIRS):
        pair = src[:, p * 128 : (p + 1) * 128]
        dst[2 * p, rows, :] = jnp.where(low, pair, extra)
        dst[2 * p + 1, rows, :] = jnp.where(low, extra, pair)


def fill_keys(band, i, k_own, k_far, v_own, v_far, seg_own, seg_far, kaug, vaug, value_extra):
    local = kaug.shape[1] // 2
    low, side = low_lanes(CHUNK), side_lanes(CHUNK)
    for k, v, seg, first in ((k_own, v_own, seg_own, band), (k_far, v_far, seg_far, 1 - band)):
        rows = pl.ds(pl.multiple_of(first * local + i * CHUNK, CHUNK), CHUNK)
        extra = jnp.where(side < 16, jnp.where(side == seg[...], 0.0, NEG_LARGE), jnp.where(side < 19, -1.0, 0.0))
        fill_pairs(k, kaug, rows, low, extra.astype(bf16))
        fill_pairs(v, vaug, rows, low, value_extra)


def attend_fwd_kernel(fills, BQ, BK, start_ref, count_ref, band_ref, q_ref, qseg_ref, k_own, k_far, v_own, v_far,
                      seg_own, seg_far, o_ref, lse_ref, kaug, vaug, qm, s_all, mx, acc):
    i = pl.program_id(0)

    @pl.when(i < fills)
    def _():
        fill_keys(band_ref[0], i, k_own, k_far, v_own, v_far, seg_own, seg_far, kaug, vaug, jnp.ones((CHUNK, 128), bf16))

    @pl.when(i >= fills)
    def _():
        low, side = low_lanes(BQ), side_lanes(BQ)
        own = (side == qseg_ref[...]).astype(f32).astype(bf16)
        for p in range(PAIRS):
            pair = q_ref[:, p * 128 : (p + 1) * 128]
            qm[2 * p] = jnp.where(low, pair, own)
            qm[2 * p + 1] = jnp.where(low, own, pair)
        mx[...] = jnp.full(mx.shape, -3e38, f32)
        acc[...] = jnp.zeros(acc.shape, f32)
        start = start_ref[i - fills]
        count = count_ref[i - fills]

        def first(j, c):
            at = pl.multiple_of(start + j * BK, 128)
            out = pl.ds(pl.multiple_of(j * BK, BK), BK)
            for h in range(HEADS):
                s = mm(qm[h], kaug[h, pl.ds(at, BK), :], NT)
                s_all[h, :, out] = s
                m = mx[h]
                for t in range(BK // 128):
                    m = jnp.maximum(m, s[:, t * 128 : (t + 1) * 128])
                mx[h] = m
            return c

        lax.fori_loop(0, count, first, 0)
        for h in range(HEADS):
            mx[h] = jnp.broadcast_to(jnp.max(mx[h], axis=1, keepdims=True), (BQ, 128))

        def second(j, c):
            at = pl.multiple_of(start + j * BK, 128)
            src = pl.ds(pl.multiple_of(j * BK, BK), BK)
            for h in range(HEADS):
                p = jnp.exp(s_all[h, :, src] - jnp.concatenate([mx[h]] * (BK // 128), axis=1)).astype(bf16)
                acc[h] += mm(p, vaug[h, pl.ds(at, BK), :])
            return c

        lax.fori_loop(0, count, second, 0)
        lane = lax.broadcasted_iota(jnp.int32, (BQ, 128), 1)
        lse = jnp.zeros((BQ, 128), f32)
        for p in range(PAIRS):
            even, odd = acc[2 * p], acc[2 * p + 1]
            swapped = pltpu.roll(even, HEAD_DIM, 1)
            total = jnp.where(low, swapped, pltpu.roll(odd, HEAD_DIM, 1))
            o_ref[:, p * 128 : (p + 1) * 128] = (jnp.where(low, even, odd) / total).astype(bf16)
            lse = jnp.where(lane == 2 * p, mx[2 * p] + jnp.log(swapped), lse)
            lse = jnp.where(lane == 2 * p + 1, mx[2 * p + 1] + jnp.log(odd), lse)
        lse_ref[...] = lse


def attend_forward(band, q, seg_own, seg_far, k_own, k_far, v_own, v_far, start, count, BQ=256, BK=256):
    rows, width = q.shape
    fills, steps = rows // CHUNK, rows // BQ
    mine = lambda i, *_: (jnp.clip(i - fills, 0, steps - 1), 0)
    fill = lambda i, *_: (jnp.minimum(i, fills - 1), 0)
    wide = pl.BlockSpec((CHUNK, width), fill)
    thin = pl.BlockSpec((CHUNK, 1), fill)
    return pl.pallas_call(
        functools.partial(attend_fwd_kernel, fills, BQ, BK),
        out_shape=(jax.ShapeDtypeStruct((rows, width), bf16), jax.ShapeDtypeStruct((rows, 128), f32)),
        grid_spec=pltpu.PrefetchScalarGridSpec(
            num_scalar_prefetch=3,
            grid=(fills + steps,),
            in_specs=[pl.BlockSpec((BQ, width), mine), pl.BlockSpec((BQ, 1), mine), wide, wide, wide, wide, thin, thin],
            out_specs=[pl.BlockSpec((BQ, width), mine), pl.BlockSpec((BQ, 128), mine)],
            scratch_shapes=[
                pltpu.VMEM((HEADS, 2 * rows, 128), bf16),
                pltpu.VMEM((HEADS, 2 * rows, 128), bf16),
                pltpu.VMEM((HEADS, BQ, 128), bf16),
                pltpu.VMEM((HEADS, BQ, 2 * rows), f32),
                pltpu.VMEM((HEADS, BQ, 128), f32),
                pltpu.VMEM((HEADS, BQ, 128), f32),
            ],
        ),
        compiler_params=pltpu.CompilerParams(vmem_limit_bytes=56 * MIB),
        cost_estimate=pl.CostEstimate(flops=30 * 10**9, bytes_accessed=10 * 10**6, transcendentals=0),
        name="attend_forward",
    )(start, count, band, q, seg_own, k_own, k_far, v_own, v_far, seg_own, seg_far)


def attend_bwd_kernel(fills, steps, BQ, BK, start_ref, count_ref, band_ref, q_ref, do_ref, o_ref, lse_ref, qseg_ref,
                      k_own, k_far, v_own, v_far, seg_own, seg_far, dq_ref, dkt_own, dkt_far, dvt_own, dvt_far,
                      kaug, vaug, qm, dom, lqt, ldot, dq_acc, dk_acc, dv_acc):
    i = pl.program_id(0)
    band = band_ref[0]
    local = kaug.shape[1] // 2

    @pl.when(i < fills)
    def _():
        side = side_lanes(CHUNK)
        extra = jnp.where((side >= 16) & (side < 19), -1.0, 0.0).astype(bf16)
        fill_keys(band, i, k_own, k_far, v_own, v_far, seg_own, seg_far, kaug, vaug, extra)
        for part in range(2):
            cols = pl.ds(pl.multiple_of(part * local + i * CHUNK, CHUNK), CHUNK)
            for p in range(PAIRS):
                dk_acc[p, :, cols] = jnp.zeros((128, CHUNK), f32)
                dv_acc[p, :, cols] = jnp.zeros((128, CHUNK), f32)

    @pl.when((i >= fills) & (i < fills + steps))
    def _():
        low, side = low_lanes(BQ), side_lanes(BQ)
        own = (side == qseg_ref[...]).astype(f32)
        for p in range(PAIRS):
            cols = slice(p * 128, (p + 1) * 128)
            q_pair, do_pair = q_ref[:, cols], do_ref[:, cols]
            prod = do_pair.astype(f32) * o_ref[:, cols].astype(f32)
            for e in range(2):
                mine = low if e == 0 else jnp.logical_not(low)
                h = 2 * p + e
                delta = jnp.sum(jnp.where(mine, prod, 0.0), axis=1, keepdims=True)
                qm[h] = jnp.where(mine, q_pair, place(side, split3(lse_ref[:, h : h + 1]), own).astype(bf16))
                dom[h] = jnp.where(mine, do_pair, place(side, split3(delta), jnp.zeros_like(own)).astype(bf16))
            zero = jnp.zeros((HEAD_DIM, BQ), bf16)
            for pair, dst in ((q_pair, lqt), (do_pair, ldot)):
                flipped = pair.T
                dst[p, 0:HEAD_DIM, 0:BQ] = flipped[0:HEAD_DIM]
                dst[p, HEAD_DIM:128, 0:BQ] = zero
                dst[p, 0:HEAD_DIM, BQ : 2 * BQ] = zero
                dst[p, HEAD_DIM:128, BQ : 2 * BQ] = flipped[HEAD_DIM:128]
        dq_acc[...] = jnp.zeros(dq_acc.shape, f32)
        start = start_ref[i - fills]

        def step(j, c):
            window = pl.ds(pl.multiple_of(start + j * BK, 128), BK)

            def scores(h):
                return mm(qm[h], kaug[h, window, :], NT), mm(dom[h], vaug[h, window, :], NT)

            ahead = scores(0)
            kept = []
            for h in range(HEADS):
                p = h // 2
                s, dp = ahead
                if h + 1 < HEADS:
                    ahead = scores(h + 1)
                prob = jnp.exp(s)
                ds = (prob * dp).astype(bf16)
                kept.append((prob.astype(bf16), ds))
                dq_acc[h] += mm(ds, kaug[h, window, :])
                if h % 2:
                    dv_acc[p, :, window] += mm(ldot[p], jnp.concatenate([kept[0][0], kept[1][0]], axis=0))
                    dk_acc[p, :, window] += mm(lqt[p], jnp.concatenate([kept[0][1], kept[1][1]], axis=0))
                    kept = []
            return c

        lax.fori_loop(0, count_ref[i - fills], step, 0)
        for p in range(PAIRS):
            pair = jnp.where(low, dq_acc[2 * p], dq_acc[2 * p + 1]) * HEAD_DIM**-0.5
            dq_ref[:, p * 128 : (p + 1) * 128] = pair.astype(bf16)

    @pl.when(i >= fills + steps)
    def _():
        j = i - fills - steps
        for p in range(PAIRS):
            rows = slice(p * 128, (p + 1) * 128)
            for first, dk_out, dv_out in ((band, dkt_own, dvt_own), (1 - band, dkt_far, dvt_far)):
                cols = pl.ds(pl.multiple_of(first * local + j * CHUNK, CHUNK), CHUNK)
                dk_out[rows, :] = dk_acc[p, :, cols].astype(bf16)
                dv_out[rows, :] = dv_acc[p, :, cols].astype(bf16)


def attend_backward(band, q, do, o, lse, seg_own, seg_far, k_own, k_far, v_own, v_far, start, count, BQ=256, BK=256):
    rows, width = q.shape
    fills, steps = rows // CHUNK, rows // BQ
    mine = lambda i, *_: (jnp.clip(i - fills, 0, steps - 1), 0)
    fill = lambda i, *_: (jnp.minimum(i, fills - 1), 0)
    drain = lambda i, *_: (0, jnp.clip(i - fills - steps, 0, fills - 1))
    wide = pl.BlockSpec((CHUNK, width), fill)
    thin = pl.BlockSpec((CHUNK, 1), fill)
    block = pl.BlockSpec((BQ, width), mine)
    flat = jax.ShapeDtypeStruct((width, rows), bf16)
    return pl.pallas_call(
        functools.partial(attend_bwd_kernel, fills, steps, BQ, BK),
        out_shape=(jax.ShapeDtypeStruct((rows, width), bf16), flat, flat, flat, flat),
        grid_spec=pltpu.PrefetchScalarGridSpec(
            num_scalar_prefetch=3,
            grid=(fills + steps + fills,),
            in_specs=[block, block, block, pl.BlockSpec((BQ, 128), mine), pl.BlockSpec((BQ, 1), mine), wide, wide, wide, wide, thin, thin],
            out_specs=[block] + [pl.BlockSpec((width, CHUNK), drain)] * 4,
            scratch_shapes=[
                pltpu.VMEM((HEADS, 2 * rows, 128), bf16),
                pltpu.VMEM((HEADS, 2 * rows, 128), bf16),
                pltpu.VMEM((HEADS, BQ, 128), bf16),
                pltpu.VMEM((HEADS, BQ, 128), bf16),
                pltpu.VMEM((PAIRS, 128, 2 * BQ), bf16),
                pltpu.VMEM((PAIRS, 128, 2 * BQ), bf16),
                pltpu.VMEM((HEADS, BQ, 128), f32),
                pltpu.VMEM((PAIRS, 128, 2 * rows), f32),
                pltpu.VMEM((PAIRS, 128, 2 * rows), f32),
            ],
        ),
        compiler_params=pltpu.CompilerParams(vmem_limit_bytes=56 * MIB),
        cost_estimate=pl.CostEstimate(flops=45 * 10**9, bytes_accessed=20 * 10**6, transcendentals=0),
        name="attend_backward",
    )(start, count, band, q, do, o, lse, seg_own, k_own, k_far, v_own, v_far, seg_own, seg_far)


def key_windows(seg_own, seg_far, band, BQ=256, BK=256):
    keys = 2 * seg_own.shape[0]
    blocks = seg_own.reshape(-1, BQ)
    first, last = blocks[:, 0], blocks[:, -1]

    def below(limit, strict):
        def count(seg):
            return jnp.sum((seg[None, :] < limit[:, None]) if strict else (seg[None, :] <= limit[:, None]), axis=1, dtype=jnp.int32)

        return count(seg_own) + count(seg_far)

    lo = below(first, True) // 128 * 128
    count = (below(last, False) - lo + BK - 1) // BK
    return jnp.minimum(lo, keys - count * BK), count


MESH = pl.DeviceIdType.MESH
TN = (((0,), (0,)), ((), ()))
SLICE = 768
ERFC_RATE = 0.39
ERFC_TERMS = (0.23532524, 0.09138829, 0.64955972, -0.63540067, 0.88666461, -0.22753718)


def gelu_and_slope(u):
    bell = jnp.exp(u * u * -0.5)
    t = 1.0 / (1.0 + jnp.abs(u) * (ERFC_RATE * 0.5**0.5))
    total = ERFC_TERMS[-1] * 0.5
    for term in ERFC_TERMS[-2::-1]:
        total = total * t + term * 0.5
    half = total * t * bell
    below = jnp.where(u < 0, half, 1.0 - half)
    return u * below, below + u * bell * (0.5 / 3.141592653589793) ** 0.5


def normalize(rows):
    centred = rows - jnp.mean(rows, axis=-1, keepdims=True)
    scale = lax.rsqrt(jnp.mean(centred * centred, axis=-1, keepdims=True) + EPS)
    return centred * scale, scale


def add_sums(ref, row, values, first):
    sums = jnp.sum(values, axis=0, keepdims=True)
    at = slice(row, row + 1)
    ref[at, :] = jnp.where(first, sums, ref[at, :] + sums)


def add_low(dst, a, b):
    dst[...] = (a[...].astype(f32) + b[...].astype(f32)).astype(bf16)


def mlp_kernel(sorted_out, blocks, rows, slices, tok_ref, att_ref, cot_ref, wproj, wup, wdown, pbias, gain, shift, ubias, dbias,
               out_ref, rgrad_ref, agrad_ref, sums_ref, usums_ref, proj_out, *rest):
    outs, scratch = rest[: 8 if sorted_out else 2], rest[8 if sorted_out else 2 :]
    hid, ugr, n2s, bgs, ags, ats, d_own, d_far, d_in, u_in, p_own, p_far, p_in, send_sem, recv_sem = scratch
    i = pl.program_id(0)
    me, band = lax.axis_index("dp"), lax.axis_index("band")
    other = (me, 1 - band)
    width = tok_ref.shape[1]
    half, per_half = width // 2, slices // 2

    def push(t, src, dst):
        return pltpu.make_async_remote_copy(
            src_ref=src, dst_ref=dst, send_sem=send_sem.at[t], recv_sem=recv_sem.at[t], device_id=other, device_id_type=MESH
        )

    def d_copy(j):
        at = pl.ds(pl.multiple_of(j * SLICE, SLICE), SLICE)
        return push(j, d_far.at[at, :], d_in.at[at, :])

    def u_copy(c):
        return push(slices + c, hid.at[0:width, pl.ds(pl.multiple_of(c * SLICE, SLICE), SLICE)], u_in.at[c])

    def p_copy():
        return push(slices + per_half, p_far, p_in)

    @pl.when(i == 0)
    def _():
        barrier = pltpu.get_barrier_semaphore()
        pl.semaphore_signal(barrier, inc=1, device_id=other, device_id_type=MESH)
        pl.semaphore_wait(barrier, 1)

    @pl.when(i < blocks)
    def _():
        here = pl.ds(pl.multiple_of(i * rows, rows), rows)
        first = i == 0
        att = att_ref[...]
        ats[here, :] = att
        residual = tok_ref[...] + mm(att, wproj[...]) + pbias[...]
        xhat, scale = normalize(residual)
        n2 = (xhat * gain[...] + shift[...]).astype(bf16)
        n2s[here, :] = n2
        cot = cot_ref[...]
        bg = cot.astype(bf16)
        bgs[here, :] = bg
        add_sums(sums_ref, 0, bg.astype(f32), first)
        for c in range(slices):
            cols = slice(c * SLICE, (c + 1) * SLICE)
            hidden, slope = gelu_and_slope(mm(n2, wup[:, cols]) + ubias[:, cols])
            hid[here, cols] = hidden.astype(bf16)
            grad = (mm(bg, wdown[cols, :], NT) * slope).astype(bf16)
            ugr[here, cols] = grad
            sums = jnp.sum(grad.astype(f32), axis=0, keepdims=True)
            usums_ref[0:1, cols] = jnp.where(first, sums, usums_ref[0:1, cols] + sums)
        out_ref[...] = residual + mm(hid[here, :], wdown[...]) + dbias[...]
        e = mm(ugr[here, :], wup[...], NT)
        add_sums(sums_ref, 1, e * xhat, first)
        add_sums(sums_ref, 2, e, first)
        f = e * gain[...]
        rgrad = cot + scale * (f - jnp.mean(f, axis=-1, keepdims=True) - xhat * jnp.mean(f * xhat, axis=-1, keepdims=True))
        rgrad_ref[...] = rgrad
        ag = rgrad.astype(bf16)
        ags[here, :] = ag
        add_sums(sums_ref, 3, ag.astype(f32), first)
        agrad_ref[...] = mm(ag, wproj[...], NT).astype(bf16)

    def columns(grad, own, far, at):
        left, right = grad[:, :half].astype(bf16), grad[:, half:].astype(bf16)
        own[at, :] = jnp.where(band == 0, left, right)
        far[at, :] = jnp.where(band == 0, right, left)

    @pl.when((i >= blocks) & (i < blocks + slices))
    def _():
        j = i - blocks
        at = pl.ds(pl.multiple_of(j * SLICE, SLICE), SLICE)
        columns(mm(hid[:, at], bgs[...], TN), d_own, d_far, at)
        d_copy(j).start()

    def up_slice(which):
        at = pl.ds(pl.multiple_of(which * SLICE, SLICE), SLICE)
        return mm(n2s[...], ugr[:, at], TN).astype(bf16)

    x, y = me & 1, (me >> 1) & 1

    def join_down(j):
        d_copy(j).wait_recv()
        if not sorted_out:
            at = pl.ds(pl.multiple_of(j * SLICE, SLICE), SLICE)
            add_low(outs[0].at[at, :], d_own.at[at, :], d_in.at[at, :])
            return
        shard = SLICE // 4
        piece = shard // 2
        for t in range(2):
            for out, x_bit, y_bit, first in (
                (outs[0], 1 - x, t, 0),
                (outs[1], x, t, 0),
                (outs[2], t, 1 - y, piece),
                (outs[3], t, y, piece),
            ):
                at = pl.ds(pl.multiple_of(j * SLICE + y_bit * 2 * shard + x_bit * shard + first, piece), piece)
                add_low(out.at[j, t], d_own.at[at, :], d_in.at[at, :])

    def join_up(c):
        u_copy(c).wait_recv()
        own = hid.at[0:width, (per_half + c) * SLICE : (per_half + c + 1) * SLICE]
        if not sorted_out:
            add_low(outs[1].at[:, c * SLICE : (c + 1) * SLICE], own, u_in.at[c])
            return
        shard = width // 16

        def one(s, carry):
            z, t = s >> 1, s & 1
            for out, sends in ((outs[4 + 2 * c], 1), (outs[5 + 2 * c], 0)):
                bit = (y if c else x) ^ sends
                x_bit, y_bit = (t, bit) if c else (bit, t)
                at = pl.ds(pl.multiple_of((z * 4 + y_bit * 2 + x_bit) * shard, shard), shard)
                add_low(out.at[z, t], own.at[at, :], u_in.at[c, at, :])
            return carry

        lax.fori_loop(0, 8, one, 0)

    middle = blocks + slices
    for c in range(per_half):
        at = slice(c * SLICE, (c + 1) * SLICE)

        @pl.when(i == middle + c)
        def _(c=c, at=at):
            hid[0:width, at] = up_slice((1 - band) * per_half + c)
            u_copy(c).start()
            join_down(c)

        @pl.when(i == middle + per_half + c)
        def _(c=c):
            hid[0:width, (per_half + c) * SLICE : (per_half + c + 1) * SLICE] = up_slice(band * per_half + c)
            join_down(per_half + c)

    @pl.when(i == middle + slices)
    def _():
        columns(mm(ats[...], ags[...], TN), p_own, p_far, slice(None))
        p_copy().start()
        for c in range(per_half):
            join_up(c)
        p_copy().wait_recv()
        add_low(proj_out, p_own, p_in)
        for j in range(slices):
            d_copy(j).wait_send()
        for c in range(per_half):
            u_copy(c).wait_send()
        p_copy().wait_send()


def mlp(size, tokens, attended, cotangent, w_proj, w_up, w_down, proj_bias, gain, shift, up_bias, down_bias, rows=256):
    count, width = tokens.shape
    ff = w_up.shape[1]
    blocks, slices = count // rows, ff // SLICE
    half, per_half = width // 2, slices // 2
    sorted_out = size == 16
    one = pl.Buffered(1)
    mine = lambda i: (jnp.minimum(i, blocks - 1), 0)
    block = pl.BlockSpec((rows, width), mine)

    def full(a):
        return pl.BlockSpec(a.shape, lambda i: (0,) * len(a.shape), pipeline_mode=one)

    vectors = [v.reshape(1, -1) for v in (proj_bias, gain, shift, up_bias, down_bias)]
    shape = jax.ShapeDtypeStruct
    if sorted_out:
        pieces = [shape((4, 2, ff // 32, half), bf16)] * 4 + [shape((4, 2, width // 16, ff // 4), bf16)] * 4
    else:
        pieces = [shape((ff, half), bf16), shape((width, ff // 2), bf16)]
    kept = [shape((8, width), f32), shape((8, ff), f32), shape((width, half), bf16)] + pieces
    low = lambda *s: pltpu.VMEM(s, bf16)
    copies = slices + per_half + 1
    return pl.pallas_call(
        functools.partial(mlp_kernel, sorted_out, blocks, rows, slices),
        out_shape=[shape((count, width), f32), shape((count, width), f32), shape((count, width), bf16)] + kept,
        grid=(blocks + 2 * slices + 1,),
        in_specs=[block, block, block] + [full(a) for a in (w_proj, w_up, w_down, *vectors)],
        out_specs=[block, block, block] + [full(a) for a in kept],
        scratch_shapes=[
            low(count, ff),
            low(count, ff),
            *([low(count, width)] * 4),
            *([low(ff, half)] * 3),
            low(per_half, width, SLICE),
            *([low(width, half)] * 3),
            pltpu.SemaphoreType.DMA((copies,)),
            pltpu.SemaphoreType.DMA((copies,)),
        ],
        compiler_params=pltpu.CompilerParams(vmem_limit_bytes=62 * MIB, collective_id=1, has_side_effects=True),
        cost_estimate=pl.CostEstimate(flops=40 * 10**9, bytes_accessed=40 * 10**6, transcendentals=0),
        name="mlp",
    )(tokens, attended, cotangent, w_proj, w_up, w_down, *vectors)


def qkv_kernel(tok_ref, seg_ref, w_ref, gain, shift, qbias, vbias, q_ref, k_ref, v_ref, n_ref, k_far, v_far, seg_far,
               k_all, v_all, send_sem, recv_sem):
    i = pl.program_id(0)
    last = pl.num_programs(0) - 1
    other = (lax.axis_index("dp"), 1 - lax.axis_index("band"))
    rows, width = tok_ref.shape

    def push(t, src, dst):
        return pltpu.make_async_remote_copy(
            src_ref=src, dst_ref=dst, send_sem=send_sem.at[t], recv_sem=recv_sem.at[t], device_id=other, device_id_type=MESH
        )

    def copies(j):
        at = pl.ds(pl.multiple_of(j * rows, rows), rows)
        return push(2 * j, k_all.at[at, :], k_far.at[at, :]), push(2 * j + 1, v_all.at[at, :], v_far.at[at, :])

    segs = push(send_sem.shape[0] - 1, seg_ref, seg_far)

    @pl.when(i == 0)
    def _():
        barrier = pltpu.get_barrier_semaphore()
        pl.semaphore_signal(barrier, inc=1, device_id=other, device_id_type=MESH)
        pl.semaphore_wait(barrier, 1)
        segs.start()

    here = pl.ds(pl.multiple_of(i * rows, rows), rows)
    xhat, _ = normalize(tok_ref[...])
    n1 = (xhat * gain[...] + shift[...]).astype(bf16)
    n_ref[...] = n1
    k = mm(n1, w_ref[:, width : 2 * width]).astype(bf16)
    k_ref[...] = k
    k_all[here, :] = k
    v = (mm(n1, w_ref[:, 2 * width :]) + vbias[...]).astype(bf16)
    v_ref[...] = v
    v_all[here, :] = v
    for copy in copies(i):
        copy.start()
    q = (mm(n1, w_ref[:, :width]) + qbias[...]).astype(bf16)
    q_ref[...] = q * jnp.asarray(HEAD_DIM**-0.5, bf16)

    @pl.when(i == last)
    def _():
        segs.wait()
        for j in range(k_all.shape[0] // rows):
            for copy in copies(j):
                copy.wait()


def project_qkv(tokens, seg, w_qkv, gain, shift, query_bias, value_bias, rows=256):
    count, width = tokens.shape
    one = pl.Buffered(1)
    block = pl.BlockSpec((rows, width), lambda i: (i, 0))
    vectors = [v.reshape(1, -1) for v in (gain, shift, query_bias, value_bias)]
    hbm = pl.BlockSpec(memory_space=pl.ANY)
    steps = count // rows
    low = jax.ShapeDtypeStruct((count, width), bf16)
    return pl.pallas_call(
        qkv_kernel,
        out_shape=(low,) * 6 + (jax.ShapeDtypeStruct(seg.shape, seg.dtype),),
        grid=(steps,),
        in_specs=[block, hbm] + [pl.BlockSpec(a.shape, lambda i: (0, 0), pipeline_mode=one) for a in (w_qkv, *vectors)],
        out_specs=[block] * 4 + [hbm] * 3,
        scratch_shapes=[
            pltpu.VMEM((count, width), bf16),
            pltpu.VMEM((count, width), bf16),
            pltpu.SemaphoreType.DMA((2 * steps + 1,)),
            pltpu.SemaphoreType.DMA((2 * steps + 1,)),
        ],
        compiler_params=pltpu.CompilerParams(vmem_limit_bytes=60 * MIB, collective_id=2, has_side_effects=True),
        cost_estimate=pl.CostEstimate(flops=4 * 10**9, bytes_accessed=13 * 10**6, transcendentals=0),
        name="project_qkv",
    )(tokens, seg, w_qkv, *vectors)


def qkv_grad_kernel(blocks, rows, band_ref, dq_ref, dk_own, dk_far, dv_own, dv_far, n_ref, packed_ref, own_ref, far_ref, sums_ref, packed):
    i = pl.program_id(0)
    band = band_ref[0]
    width = dq_ref.shape[1]
    half = own_ref.shape[1]

    @pl.when(i < blocks)
    def _():
        here = pl.ds(pl.multiple_of(i * rows, rows), rows)
        first = i == 0
        dq = dq_ref[...]
        packed_ref[:, :width] = dq
        packed[here, :width] = dq
        add_sums(sums_ref, 0, dq.astype(f32), first)
        for t, (own, far) in enumerate(((dk_own, dk_far), (dv_own, dv_far))):
            for p in range(width // 128):
                at = slice(p * 128, (p + 1) * 128)
                to = slice((t + 1) * width + p * 128, (t + 1) * width + (p + 1) * 128)
                turned = (own[at, :].astype(f32) + far[at, :].astype(f32)).astype(bf16).T
                packed_ref[:, to] = turned
                packed[here, to] = turned
        add_sums(sums_ref, 1, packed_ref[:, 2 * width :].astype(f32), first)

    def columns(which):
        at = pl.ds(pl.multiple_of(which * half, 128), half)
        return mm(n_ref[...], packed[:, at], TN).astype(bf16)

    @pl.when(i == blocks)
    def _():
        far_ref[...] = columns(1 - band)

    @pl.when(i == blocks + 1)
    def _():
        own_ref[...] = columns(band)


def qkv_grads(band, dq, dk_own, dk_far, dv_own, dv_far, normed, rows=256):
    count, width = dq.shape
    blocks = count // rows
    half = 3 * width // 2
    one = pl.Buffered(1)
    mine = lambda i, *_: (jnp.minimum(i, blocks - 1), 0)
    flip = lambda i, *_: (0, jnp.minimum(i, blocks - 1))
    whole = lambda i, *_: (0, 0)
    shape = jax.ShapeDtypeStruct
    return pl.pallas_call(
        functools.partial(qkv_grad_kernel, blocks, rows),
        out_shape=(shape((count, 3 * width), bf16), shape((width, half), bf16), shape((width, half), bf16), shape((8, width), f32)),
        grid_spec=pltpu.PrefetchScalarGridSpec(
            num_scalar_prefetch=1,
            grid=(blocks + 2,),
            in_specs=[pl.BlockSpec((rows, width), mine)]
            + [pl.BlockSpec((width, rows), flip)] * 4
            + [pl.BlockSpec((count, width), whole, pipeline_mode=one)],
            out_specs=[
                pl.BlockSpec((rows, 3 * width), mine),
                pl.BlockSpec((width, half), whole, pipeline_mode=one),
                pl.BlockSpec((width, half), whole, pipeline_mode=one),
                pl.BlockSpec((8, width), whole, pipeline_mode=one),
            ],
            scratch_shapes=[pltpu.VMEM((count, 3 * width), bf16)],
        ),
        compiler_params=pltpu.CompilerParams(vmem_limit_bytes=40 * MIB),
        cost_estimate=pl.CostEstimate(flops=8 * 10**9, bytes_accessed=18 * 10**6, transcendentals=0),
        name="qkv_grads",
    )(band, dq, dk_own, dk_far, dv_own, dv_far, normed)


def input_grad_kernel(packed_ref, tok_ref, rgrad_ref, w_ref, gain, out_ref, sums_ref):
    first = pl.program_id(0) == 0
    e = mm(packed_ref[...], w_ref[...], NT)
    xhat, scale = normalize(tok_ref[...])
    add_sums(sums_ref, 0, e * xhat, first)
    add_sums(sums_ref, 1, e, first)
    f = e * gain[...]
    back = scale * (f - jnp.mean(f, axis=-1, keepdims=True) - xhat * jnp.mean(f * xhat, axis=-1, keepdims=True))
    out_ref[...] = rgrad_ref[...] + back


def input_grads(packed, tokens, rgrad, w_qkv, gain, rows=256):
    count, width = tokens.shape
    one = pl.Buffered(1)
    block = pl.BlockSpec((rows, width), lambda i: (i, 0))
    return pl.pallas_call(
        input_grad_kernel,
        out_shape=(jax.ShapeDtypeStruct((count, width), f32), jax.ShapeDtypeStruct((8, width), f32)),
        grid=(count // rows,),
        in_specs=[
            pl.BlockSpec((rows, packed.shape[1]), lambda i: (i, 0)),
            block,
            block,
            pl.BlockSpec(w_qkv.shape, lambda i: (0, 0), pipeline_mode=one),
            pl.BlockSpec((1, width), lambda i: (0, 0), pipeline_mode=one),
        ],
        out_specs=[block, pl.BlockSpec((8, width), lambda i: (0, 0), pipeline_mode=one)],
        compiler_params=pltpu.CompilerParams(vmem_limit_bytes=32 * MIB),
        cost_estimate=pl.CostEstimate(flops=6 * 10**9, bytes_accessed=18 * 10**6, transcendentals=0),
        name="input_grads",
    )(packed, tokens, rgrad, w_qkv, gain.reshape(1, -1))


def finish_kernel(
    dq_hbm, dko_hbm, dkf_hbm, dvo_hbm, dvf_hbm, n_hbm, tok_hbm, rgrad_hbm, w_hbm, dak_hbm, dar_hbm, dbk_hbm, dbr_hbm,
    uak_hbm, uar_hbm, ubk_hbm, ubr_hbm, proj_hbm, gain, msums, usums,
    out_hbm, down_out, up_out, qkv_out, proj_out, vec_out,
    packed, dko, dko_in, dvo, dvo_in, n1, tok, rgrad, wq, down, up, proj, far, far_in, tail,
    one_d, one_u, one_t, two_d, two_u, two_t, thr_d, thr_u, thr_t, vec, vec_band, vec_x, vec_y, vec_z,
    load_sem, store_sem, swap_send, swap_recv, send, recv, vsend, vrecv,
):
    me = lax.axis_index("dp")
    band = lax.axis_index("band")
    x, y, z = me & 1, (me >> 1) & 1, me >> 2
    rows, width = tok.shape
    half = far.shape[-1]
    peer_band = (me, 1 - band)
    peer_x = (me ^ 1, band)
    peer_y = (me ^ 2, band)
    peers_z = [(((z + d) & 3) * 4 + (me & 3), band) for d in (1, 2, 3)]

    def load(t, src, dst):
        copy = pltpu.make_async_copy(src, dst, load_sem.at[t])
        copy.start()
        return copy

    loads = {
        "down": (load(0, dak_hbm, down.at[0]), load(1, dar_hbm, one_d.at[0]), load(2, dbk_hbm, down.at[1]), load(3, dbr_hbm, one_d.at[1])),
        "up": (load(13, uak_hbm, up.at[0]), load(14, uar_hbm, one_u.at[0]), load(15, ubk_hbm, up.at[1]), load(16, ubr_hbm, one_u.at[1])),
        "keys": (load(4, dko_hbm, dko), load(5, dvo_hbm, dvo), load(6, dq_hbm, packed.at[:, 0:width])),
        "normed": (load(7, n_hbm, n1),),
        "proj": (load(8, proj_hbm, proj),),
        "weight": (load(10, w_hbm, wq),),
        "rows": (load(11, tok_hbm, tok), load(12, rgrad_hbm, rgrad)),
    }

    def ready(name):
        for copy in loads[name]:
            copy.wait()

    barrier = pltpu.get_barrier_semaphore()
    for peer in (peer_band, peer_x, peer_y, *peers_z):
        pl.semaphore_signal(barrier, inc=1, device_id=peer, device_id_type=MESH)
    pl.semaphore_wait(barrier, 6)

    pending = []

    def push(src, dst, peer, s, r):
        copy = pltpu.make_async_remote_copy(src_ref=src, dst_ref=dst, send_sem=s, recv_sem=r, device_id=peer, device_id_type=MESH)
        copy.start()
        pending.append(copy)
        return copy

    swap_k = push(dkf_hbm, dko_in, peer_band, swap_send.at[0], swap_recv.at[0])
    swap_v = push(dvf_hbm, dvo_in, peer_band, swap_send.at[1], swap_recv.at[1])

    def put(dst, src):
        dst[...] = src[...]

    def each_shard(body):
        def step(s, c):
            body(s >> 2, (s >> 1) & 1, s & 1)
            return c

        lax.fori_loop(0, 16, step, 0)

    def first_stage(t, work, one, cut):
        a, b = cut
        return (
            push(work.at[:, :, 1 - x, a[0], a[1]], one.at[0], peer_x, send.at[t, 0, 0], recv.at[t, 0, 0]),
            push(work.at[:, 1 - y, :, b[0], b[1]], one.at[1], peer_y, send.at[t, 1, 0], recv.at[t, 1, 0]),
        )

    def second_stage(t, kept, one, two, copies):
        out = []
        for piece, mine, peer in ((0, y, peer_y), (1, x, peer_x)):
            if copies is not None:
                copies[piece].wait_recv()

            def total(s, c, piece=piece):
                add_low(one.at[piece, s >> 1, s & 1], one.at[piece, s >> 1, s & 1], kept(piece, s >> 1, s & 1))
                return c

            lax.fori_loop(0, 8, total, 0)
            out.append(push(one.at[piece, :, 1 - mine], two.at[piece], peer, send.at[t, piece, 1], recv.at[t, piece, 1]))
        return out

    def third_stage(t, one, two, three, copies):
        out = []
        for piece, mine in ((0, y), (1, x)):
            copies[piece].wait_recv()

            def total(zz, c, piece=piece, mine=mine):
                add_low(two.at[piece, zz], two.at[piece, zz], one.at[piece, zz, mine])
                return c

            lax.fori_loop(0, 4, total, 0)
            for d in (1, 2, 3):
                out.append(
                    push(two.at[piece, (z + d) & 3], three.at[piece, d - 1], peers_z[d - 1], send.at[t, piece, 1 + d], recv.at[t, piece, 1 + d])
                )
        return out

    def last(two, three, copies, piece):
        for d in range(3):
            copies[3 * piece + d].wait_recv()
        total = two[piece, z].astype(f32)
        for d in range(3):
            total = total + three[piece, d].astype(f32)
        return total

    everything = slice(None)
    wide_cut = ((everything, slice(0, 768)), (everything, slice(768, 1536)))

    ready("down")
    d_two = second_stage(0, lambda p, i, j: down.at[p, i, j], one_d, two_d, None)
    ready("up")
    u_two = second_stage(1, lambda p, i, j: up.at[p, i, j], one_u, two_u, None)

    def tail_kept(piece, zz, t):
        return tail.at[zz, t, x, :, 0:768] if piece == 0 else tail.at[zz, y, t, :, 768:1536]

    ready("keys")
    swap_k.wait_recv()
    swap_v.wait_recv()

    def turn(i, c):
        here = pl.ds(pl.multiple_of(i * 256, 256), 256)
        for t, (own, other) in enumerate(((dko, dko_in), (dvo, dvo_in))):
            for p in range(width // 128):
                at = slice(p * 128, (p + 1) * 128)
                turned = (own[at, here].astype(f32) + other[at, here].astype(f32)).astype(bf16).T
                packed[here, (t + 1) * width + p * 128 : (t + 1) * width + (p + 1) * 128] = turned
        return c

    lax.fori_loop(0, rows // 256, turn, 0)
    ready("normed")

    def columns(which):
        at = pl.ds(pl.multiple_of(which * half, 128), half)
        return mm(n1[...], packed[:, at], TN).astype(bf16).reshape(far.shape)

    far[...] = columns(1 - band)
    swap_far = push(far, far_in, peer_band, swap_send.at[2], swap_recv.at[2])
    tail[:, :, :, :, 0:half] = columns(band)
    ready("proj")
    each_shard(lambda i, j, k: put(tail.at[i, j, k, :, half : 2 * width], proj.at[i, j, k]))
    swap_far.wait_recv()
    each_shard(lambda i, j, k: add_low(tail.at[i, j, k, :, 0:half], tail.at[i, j, k, :, 0:half], far_in.at[i, j, k]))
    t_one = first_stage(2, tail, one_t, wide_cut)
    d_three = third_stage(0, one_d, two_d, thr_d, d_two)
    u_three = third_stage(1, one_u, two_u, thr_u, u_two)

    ready("weight")
    ready("rows")
    vec[...] = jnp.zeros(vec.shape, f32)

    def rows_back(i, c):
        here = pl.ds(pl.multiple_of(i * 256, 256), 256)
        e = mm(packed[here, :], wq[...], NT)
        xhat, scale = normalize(tok[here, :])
        vec[0:1, :] = vec[0:1, :] + jnp.sum(e * xhat, axis=0, keepdims=True)
        vec[1:2, :] = vec[1:2, :] + jnp.sum(e, axis=0, keepdims=True)
        vec[2:3, :] = vec[2:3, :] + jnp.sum(packed[here, 0:width].astype(f32), axis=0, keepdims=True)
        vec[3:4, :] = vec[3:4, :] + jnp.sum(packed[here, 2 * width : 3 * width].astype(f32), axis=0, keepdims=True)
        f = e * gain[...]
        back = scale * (f - jnp.mean(f, axis=-1, keepdims=True) - xhat * jnp.mean(f * xhat, axis=-1, keepdims=True))
        rgrad[here, :] = rgrad[here, :] + back
        return c

    lax.fori_loop(0, rows // 256, rows_back, 0)
    store = pltpu.make_async_copy(rgrad, out_hbm, store_sem)
    store.start()
    vec[4:8, :] = msums[0:4, :]
    for t in range(usums.shape[1] // width):
        vec[8 + t : 9 + t, :] = usums[0:1, t * width : (t + 1) * width]
    v_band = push(vec, vec_band, peer_band, vsend.at[0], vrecv.at[0])
    v_band.wait()
    vec_band[...] = vec[...] + vec_band[...]
    v_x = push(vec_band, vec_x, peer_x, vsend.at[1], vrecv.at[1])
    v_x.wait()
    vec_x[...] = vec_band[...] + vec_x[...]
    v_y = push(vec_x, vec_y, peer_y, vsend.at[2], vrecv.at[2])
    t_two = second_stage(2, tail_kept, one_t, two_t, t_one)
    v_y.wait()
    vec_y[...] = vec_x[...] + vec_y[...]
    v_z = [push(vec_y, vec_z.at[d], peers_z[d], vsend.at[3 + d], vrecv.at[3 + d]) for d in range(3)]
    t_three = third_stage(2, one_t, two_t, thr_t, t_two)
    down_out[0:96, :] = last(two_d, thr_d, d_three, 0)
    down_out[96:192, :] = last(two_d, thr_d, d_three, 1)
    up_out[:, 0:768] = last(two_u, thr_u, u_three, 0)
    up_out[:, 768:1536] = last(two_u, thr_u, u_three, 1)
    for copy in v_z:
        copy.wait_recv()
    vec_out[...] = vec_y[...] + vec_z[0] + vec_z[1] + vec_z[2]
    qkv_out[:, 0:768] = last(two_t, thr_t, t_three, 0)
    final = last(two_t, thr_t, t_three, 1)
    qkv_out[:, 768:half] = final[:, 0 : half - 768]
    proj_out[...] = final[:, half - 768 :]
    done = {id(c) for c in (v_band, v_x, v_y)}
    for copy in pending:
        if id(copy) not in done:
            copy.wait_send()
    store.wait()


def finish(dq, dk_own, dk_far, dv_own, dv_far, normed, tokens, rgrad, w_qkv, pieces, proj, gain, msums, usums):
    rows, width = tokens.shape
    ff = usums.shape[1]
    half = 3 * width // 2
    shards = (4, 2, 2)
    u_shape, p_shape = shards + (width // 16, ff // 2), shards + (width // 16, width // 2)
    q_shape = shards + (width // 16, half)
    d_piece, w_piece = (ff // 32, width // 2), (width // 16, ff // 4)
    hbm, vmem = pl.BlockSpec(memory_space=pl.ANY), pl.BlockSpec(memory_space=pltpu.VMEM)
    shape = jax.ShapeDtypeStruct
    low = lambda *s: pltpu.VMEM(s, bf16)
    dma = pltpu.SemaphoreType.DMA
    return pl.pallas_call(
        finish_kernel,
        out_shape=(
            shape((rows, width), f32),
            shape((ff // 16, width // 2), f32),
            shape((width // 16, ff // 2), f32),
            shape((width // 16, half), f32),
            shape((width // 16, width // 2), f32),
            shape((16, width), f32),
        ),
        in_specs=[hbm] * 18 + [vmem] * 3,
        out_specs=[hbm] + [vmem] * 5,
        scratch_shapes=[
            low(rows, 3 * width),
            *([low(width, rows)] * 4),
            low(rows, width),
            pltpu.VMEM((rows, width), f32),
            pltpu.VMEM((rows, width), f32),
            low(width, 3 * width),
            low(2, 4, 2, *d_piece),
            low(2, 4, 2, *w_piece),
            low(*p_shape),
            low(*q_shape),
            low(*q_shape),
            low(*u_shape),
            low(2, 4, 2, *d_piece),
            low(2, 4, 2, *w_piece),
            low(2, 4, 2, *w_piece),
            low(2, 4, *d_piece),
            low(2, 4, *w_piece),
            low(2, 4, *w_piece),
            low(2, 3, *d_piece),
            low(2, 3, *w_piece),
            low(2, 3, *w_piece),
            pltpu.VMEM((16, width), f32),
            pltpu.VMEM((16, width), f32),
            pltpu.VMEM((16, width), f32),
            pltpu.VMEM((16, width), f32),
            pltpu.VMEM((3, 16, width), f32),
            dma((17,)),
            dma,
            dma((3,)),
            dma((3,)),
            dma((3, 2, 5)),
            dma((3, 2, 5)),
            dma((6,)),
            dma((6,)),
        ],
        compiler_params=pltpu.CompilerParams(vmem_limit_bytes=60 * MIB, collective_id=0, has_side_effects=True),
        cost_estimate=pl.CostEstimate(flops=20 * 10**9, bytes_accessed=40 * 10**6, transcendentals=0),
        name="finish",
    )(dq, dk_own, dk_far, dv_own, dv_far, normed, tokens, rgrad, w_qkv, *pieces, proj.reshape(p_shape),
      gain.reshape(1, -1), msums, usums)


def swap_band(x):
    return lax.ppermute(x, "band", [(0, 1), (1, 0)])


def pick(x, which, axis):
    return lax.dynamic_index_in_dim(x, which, axis, keepdims=False)


def halve(x, axis, bit, size):
    mine = (lax.axis_index("dp") >> bit) & 1
    arrived = lax.ppermute(pick(x, 1 - mine, axis), "dp", [(i, i ^ (1 << bit)) for i in range(size)])
    return pick(x, mine, axis).astype(f32) + arrived.astype(f32)


class Reduction:
    def __init__(self, x, order, size):
        rows, columns = x.shape
        levels = size.bit_length() - 1
        self.size = size
        self.x = x.reshape((2,) * levels + (rows // size, columns))
        self.left = list(range(levels - 1, -1, -1))
        self.order = list(order)

    def step(self):
        if self.order:
            bit = self.order.pop(0)
            x = halve(self.x, self.left.index(bit), bit, self.size)
            self.left.remove(bit)
            self.x = x.astype(bf16) if self.left else x

    def finish(self):
        while self.order:
            self.step()
        return self.x


def finish_any(size, band_at, query_grad, dk_own, dk_far, dv_own, dv_far, normed, tokens, residual_grad, w_qkv, pieces, proj, gain, msums, usums):
    width = tokens.shape[1]
    rising = list(range(size.bit_length() - 1))
    turned = [1, 0] + rising[2:]
    packed, qkv_own, qkv_far, qkv_sums = qkv_grads(
        band_at, query_grad, dk_own, swap_band(dk_far), dv_own, swap_band(dv_far), normed
    )
    input_grad, first_sums = input_grads(packed, tokens, residual_grad, w_qkv, gain)

    def total(x, order):
        return Reduction(x, order, size).finish()

    def join(own, far):
        return (own.astype(f32) + swap_band(far).astype(f32)).astype(bf16)

    tall = jnp.concatenate([first_sums[:2], qkv_sums[:2], msums[:4]], axis=0)
    thin = jnp.concatenate([tall.T, usums[0].reshape(width, -1)], axis=1)
    thin = jnp.pad(thin, ((0, 0), (0, 128 - thin.shape[1]))).astype(bf16)
    thin_sum = total(join(thin, thin), turned)
    ups = usums.shape[1] // width
    return (
        input_grad,
        total(pieces[0], rising),
        total(pieces[1], turned),
        total(join(qkv_own, qkv_far), rising),
        total(proj, turned),
        [thin_sum[:, t] for t in range(8)],
        thin_sum[:, 8 : 8 + ups].reshape(-1),
    )


def local(
    size,
    inputs,
    segment_ids,
    cotangent,
    first_gain,
    first_bias,
    w_qkv,
    query_bias,
    value_bias,
    w_proj,
    proj_bias,
    second_gain,
    second_bias,
    w_up,
    up_bias,
    w_down,
    down_bias,
):
    local_shape = inputs.shape
    width = local_shape[-1]
    band = lax.axis_index("band")
    band_at = band.astype(jnp.int32).reshape(1)
    tokens = inputs.reshape(-1, width)
    seg_own = segment_ids.reshape(-1)
    queries, k_own, v_own, normed, k_far, v_far, seg_far = project_qkv(
        tokens, seg_own, w_qkv, first_gain, first_bias, query_bias, value_bias
    )
    start, count = key_windows(seg_own, seg_far, band)
    keys = (seg_own[:, None], seg_far[:, None], k_own, k_far, v_own, v_far, start, count)
    attended, log_totals = attend_forward(band_at, queries, *keys)
    output, residual_grad, attended_grad, mlp_sums, up_sums, proj, *pieces = mlp(
        size,
        tokens,
        attended,
        cotangent.reshape(-1, width),
        w_proj,
        w_up,
        w_down,
        proj_bias,
        second_gain,
        second_bias,
        up_bias,
        down_bias,
    )
    if size == 16:
        turns = [[(i, i ^ bit) for i in range(size)] for bit in (1, 2)]
        pieces = [
            part
            for t in range(4)
            for part in (pieces[2 * t + 1], lax.ppermute(pieces[2 * t], "dp", turns[t % 2]))
        ]
    query_grad, dk_own, dk_far, dv_own, dv_far = attend_backward(
        band_at, queries, attended_grad, attended, log_totals, *keys
    )
    ups = up_bias.shape[0] // width
    if size == 16:
        input_grad, down_sum, up_sum, qkv_sum, proj_sum, vec = finish(
            query_grad, dk_own, dk_far, dv_own, dv_far, normed, tokens, residual_grad, w_qkv, pieces, proj, first_gain, mlp_sums, up_sums
        )
        shard = width // size
        mine = lax.dynamic_slice_in_dim(vec[:8], lax.axis_index("dp") * shard, shard, 1)
        vectors = [mine[t] for t in range(8)]
        up_vector = lax.dynamic_slice_in_dim(vec[8 : 8 + ups].reshape(-1), lax.axis_index("dp") * ups * shard, ups * shard, 0)
    else:
        input_grad, down_sum, up_sum, qkv_sum, proj_sum, vectors, up_vector = finish_any(
            size, band_at, query_grad, dk_own, dk_far, dv_own, dv_far, normed, tokens, residual_grad, w_qkv, pieces, proj, first_gain, mlp_sums, up_sums
        )
    return (
        output.reshape(local_shape),
        input_grad.reshape(local_shape),
        vectors[0],
        vectors[1],
        qkv_sum,
        vectors[2],
        vectors[3],
        proj_sum,
        vectors[7],
        vectors[5],
        vectors[6],
        up_sum,
        up_vector,
        down_sum,
        vectors[4],
    )


def solution(mesh):
    size = mesh.shape["dp"]
    placed = (P("dp", "band", None), P("dp", "band"), P("dp", "band", None)) + (P(),) * 13
    split, thin = P("dp", "band"), P("dp")
    wide = P("dp", "band", None)
    return jax.shard_map(
        functools.partial(local, size),
        mesh=mesh,
        in_specs=placed,
        out_specs=(wide, wide, thin, thin, split, thin, thin, split, thin, thin, thin, split, thin, split, thin),
        check_vma=False,
    )
```

```python
import functools

import jax
import jax.numpy as jnp
from jax import lax
from jax.experimental import pallas as pl
from jax.experimental.pallas import tpu as pltpu
from jax.sharding import PartitionSpec as P

EPS = 1e-05
HEADS = 12
HEAD_DIM = 64
NEG_LARGE = -1e30
PAIRS = HEADS // 2
CHUNK = 256
MIB = 1 << 20
f32, bf16 = jnp.float32, jnp.bfloat16
NN = (((1,), (0,)), ((), ()))
NT = (((1,), (1,)), ((), ()))


def mm(a, b, dims=NN):
    return lax.dot_general(a, b, dims, preferred_element_type=f32)


def low_lanes(rows):
    return lax.broadcasted_iota(jnp.int32, (rows, 128), 1) < HEAD_DIM


def side_lanes(rows):
    return lax.broadcasted_iota(jnp.int32, (rows, 128), 1) & (HEAD_DIM - 1)


def split3(x):
    high = x.astype(bf16).astype(f32)
    middle = (x - high).astype(bf16).astype(f32)
    return high, middle, x - high - middle


def place(side, parts, base):
    for t, part in enumerate(parts):
        base = jnp.where(side == 16 + t, part, base)
    return base


def as_column(row):
    return jnp.broadcast_to(row, (8, row.shape[1])).T[:, 0:1]


def key_window(seg_own, seg_far, block, BQ, BK):
    own, far = seg_own[...].astype(f32), seg_far[...].astype(f32)
    mine = seg_own[:, pl.ds(pl.multiple_of(block * BQ, BQ), BQ)].astype(f32)
    first, last = jnp.min(mine), jnp.max(mine)

    def count(hits_own, hits_far):
        return jnp.sum(hits_own.astype(f32) + hits_far.astype(f32)).astype(jnp.int32)

    lo = (count(own < first, far < first) // 128) * 128
    blocks = (count(own <= last, far <= last) - lo + BK - 1) // BK
    return jnp.minimum(lo, 2 * own.shape[1] - blocks * BK), blocks


def fill_pairs(src, dst, rows, low, extra):
    for p in range(PAIRS):
        pair = src[:, p * 128 : (p + 1) * 128]
        dst[2 * p, rows, :] = jnp.where(low, pair, extra)
        dst[2 * p + 1, rows, :] = jnp.where(low, extra, pair)


def fill_keys(band, i, k_own, k_far, v_own, v_far, seg_own, seg_far, kaug, vaug, value_extra):
    local = kaug.shape[1] // 2
    low, side = low_lanes(CHUNK), side_lanes(CHUNK)
    here = pl.ds(pl.multiple_of(i * CHUNK, CHUNK), CHUNK)
    for k, v, seg, first in ((k_own, v_own, seg_own, band), (k_far, v_far, seg_far, 1 - band)):
        rows = pl.ds(pl.multiple_of(first * local + i * CHUNK, CHUNK), CHUNK)
        extra = jnp.where(side < 16, jnp.where(side == as_column(seg[:, here]), 0.0, NEG_LARGE), jnp.where(side < 19, -1.0, 0.0))
        fill_pairs(k, kaug, rows, low, extra.astype(bf16))
        fill_pairs(v, vaug, rows, low, value_extra)


def attend_fwd_kernel(fills, BQ, BK, band_ref, q_ref, k_own, k_far, v_own, v_far,
                      seg_own, seg_far, o_ref, lse_ref, kaug, vaug, qm, s_all, mx, acc):
    i = pl.program_id(0)

    @pl.when(i < fills)
    def _():
        fill_keys(band_ref[0], i, k_own, k_far, v_own, v_far, seg_own, seg_far, kaug, vaug, jnp.ones((CHUNK, 128), bf16))

    @pl.when(i >= fills)
    def _():
        low, side = low_lanes(BQ), side_lanes(BQ)
        block = i - fills
        ids = as_column(seg_own[:, pl.ds(pl.multiple_of(block * BQ, BQ), BQ)])
        own = (side == ids).astype(f32).astype(bf16)
        for p in range(PAIRS):
            pair = q_ref[:, p * 128 : (p + 1) * 128]
            qm[2 * p] = jnp.where(low, pair, own)
            qm[2 * p + 1] = jnp.where(low, own, pair)
        mx[...] = jnp.full(mx.shape, -3e38, f32)
        acc[...] = jnp.zeros(acc.shape, f32)
        start, count = key_window(seg_own, seg_far, block, BQ, BK)

        def first(j, c):
            at = pl.multiple_of(start + j * BK, 128)
            out = pl.ds(pl.multiple_of(j * BK, BK), BK)
            for h in range(HEADS):
                s = mm(qm[h], kaug[h, pl.ds(at, BK), :], NT)
                s_all[h, :, out] = s
                m = mx[h]
                for t in range(BK // 128):
                    m = jnp.maximum(m, s[:, t * 128 : (t + 1) * 128])
                mx[h] = m
            return c

        lax.fori_loop(0, count, first, 0)
        for h in range(HEADS):
            mx[h] = jnp.broadcast_to(jnp.max(mx[h], axis=1, keepdims=True), (BQ, 128))

        def second(j, c):
            at = pl.multiple_of(start + j * BK, 128)
            src = pl.ds(pl.multiple_of(j * BK, BK), BK)
            for h in range(HEADS):
                p = jnp.exp(s_all[h, :, src] - jnp.concatenate([mx[h]] * (BK // 128), axis=1)).astype(bf16)
                acc[h] += mm(p, vaug[h, pl.ds(at, BK), :])
            return c

        lax.fori_loop(0, count, second, 0)
        lane = lax.broadcasted_iota(jnp.int32, (BQ, 128), 1)
        lse = jnp.zeros((BQ, 128), f32)
        for p in range(PAIRS):
            even, odd = acc[2 * p], acc[2 * p + 1]
            swapped = pltpu.roll(even, HEAD_DIM, 1)
            total = jnp.where(low, swapped, pltpu.roll(odd, HEAD_DIM, 1))
            o_ref[:, p * 128 : (p + 1) * 128] = (jnp.where(low, even, odd) / total).astype(bf16)
            lse = jnp.where(lane == 2 * p, mx[2 * p] + jnp.log(swapped), lse)
            lse = jnp.where(lane == 2 * p + 1, mx[2 * p + 1] + jnp.log(odd), lse)
        lse_ref[...] = lse


def attend_forward(band, q, seg_own, seg_far, k_own, k_far, v_own, v_far, BQ=256, BK=256):
    rows, width = q.shape
    fills, steps = rows // CHUNK, rows // BQ
    mine = lambda i, *_: (jnp.clip(i - fills, 0, steps - 1), 0)
    fill = lambda i, *_: (jnp.minimum(i, fills - 1), 0)
    wide = pl.BlockSpec((CHUNK, width), fill)
    thin = pl.BlockSpec((1, rows), lambda i, *_: (0, 0))
    return pl.pallas_call(
        functools.partial(attend_fwd_kernel, fills, BQ, BK),
        out_shape=(jax.ShapeDtypeStruct((rows, width), bf16), jax.ShapeDtypeStruct((rows, 128), f32)),
        grid_spec=pltpu.PrefetchScalarGridSpec(
            num_scalar_prefetch=1,
            grid=(fills + steps,),
            in_specs=[pl.BlockSpec((BQ, width), mine), wide, wide, wide, wide, thin, thin],
            out_specs=[pl.BlockSpec((BQ, width), mine), pl.BlockSpec((BQ, 128), mine)],
            scratch_shapes=[
                pltpu.VMEM((HEADS, 2 * rows, 128), bf16),
                pltpu.VMEM((HEADS, 2 * rows, 128), bf16),
                pltpu.VMEM((HEADS, BQ, 128), bf16),
                pltpu.VMEM((HEADS, BQ, 2 * rows), f32),
                pltpu.VMEM((HEADS, BQ, 128), f32),
                pltpu.VMEM((HEADS, BQ, 128), f32),
            ],
        ),
        compiler_params=pltpu.CompilerParams(vmem_limit_bytes=56 * MIB),
        cost_estimate=pl.CostEstimate(flops=30 * 10**9, bytes_accessed=10 * 10**6, transcendentals=0),
        name="attend_forward",
    )(band, q, k_own, k_far, v_own, v_far, seg_own, seg_far)


def attend_bwd_kernel(fills, steps, BQ, BK, band_ref, q_ref, do_ref, o_ref, lse_ref,
                      k_own, k_far, v_own, v_far, seg_own, seg_far, carried, dq_ref, dkt_own, dkt_far, dvt_own, dvt_far, carried_out,
                      kaug, vaug, qm, dom, lqt, ldot, dq_acc, dk_acc, dv_acc):
    i = pl.program_id(0)
    band = band_ref[0]
    local = kaug.shape[1] // 2

    @pl.when(i < fills)
    def _():
        side = side_lanes(CHUNK)
        extra = jnp.where((side >= 16) & (side < 19), -1.0, 0.0).astype(bf16)
        fill_keys(band, i, k_own, k_far, v_own, v_far, seg_own, seg_far, kaug, vaug, extra)
        for part in range(2):
            cols = pl.ds(pl.multiple_of(part * local + i * CHUNK, CHUNK), CHUNK)
            for p in range(PAIRS):
                dk_acc[p, :, cols] = jnp.zeros((128, CHUNK), f32)
                dv_acc[p, :, cols] = jnp.zeros((128, CHUNK), f32)

    @pl.when((i >= fills) & (i < fills + steps))
    def _():
        low, side = low_lanes(BQ), side_lanes(BQ)
        block = i - fills
        carried_out[...] = carried[...]
        ids = as_column(seg_own[:, pl.ds(pl.multiple_of(block * BQ, BQ), BQ)])
        own = (side == ids).astype(f32)
        for p in range(PAIRS):
            cols = slice(p * 128, (p + 1) * 128)
            q_pair, do_pair = q_ref[:, cols], do_ref[:, cols]
            prod = do_pair.astype(f32) * o_ref[:, cols].astype(f32)
            for e in range(2):
                mine = low if e == 0 else jnp.logical_not(low)
                h = 2 * p + e
                delta = jnp.sum(jnp.where(mine, prod, 0.0), axis=1, keepdims=True)
                qm[h] = jnp.where(mine, q_pair, place(side, split3(lse_ref[:, h : h + 1]), own).astype(bf16))
                dom[h] = jnp.where(mine, do_pair, place(side, split3(delta), jnp.zeros_like(own)).astype(bf16))
            zero = jnp.zeros((HEAD_DIM, BQ), bf16)
            for pair, dst in ((q_pair, lqt), (do_pair, ldot)):
                flipped = pair.T
                dst[p, 0:HEAD_DIM, 0:BQ] = flipped[0:HEAD_DIM]
                dst[p, HEAD_DIM:128, 0:BQ] = zero
                dst[p, 0:HEAD_DIM, BQ : 2 * BQ] = zero
                dst[p, HEAD_DIM:128, BQ : 2 * BQ] = flipped[HEAD_DIM:128]
        dq_acc[...] = jnp.zeros(dq_acc.shape, f32)
        start, count = key_window(seg_own, seg_far, block, BQ, BK)

        def step(j, c):
            window = pl.ds(pl.multiple_of(start + j * BK, 128), BK)

            def scores(h):
                return mm(qm[h], kaug[h, window, :], NT), mm(dom[h], vaug[h, window, :], NT)

            ahead = scores(0)
            kept = []
            for h in range(HEADS):
                p = h // 2
                s, dp = ahead
                if h + 1 < HEADS:
                    ahead = scores(h + 1)
                prob = jnp.exp(s)
                ds = (prob * dp).astype(bf16)
                kept.append((prob.astype(bf16), ds))
                dq_acc[h] += mm(ds, kaug[h, window, :])
                if h % 2:
                    dv_acc[p, :, window] += mm(ldot[p], jnp.concatenate([kept[0][0], kept[1][0]], axis=0))
                    dk_acc[p, :, window] += mm(lqt[p], jnp.concatenate([kept[0][1], kept[1][1]], axis=0))
                    kept = []
            return c

        lax.fori_loop(0, count, step, 0)
        for p in range(PAIRS):
            pair = jnp.where(low, dq_acc[2 * p], dq_acc[2 * p + 1]) * HEAD_DIM**-0.5
            dq_ref[:, p * 128 : (p + 1) * 128] = pair.astype(bf16)

    @pl.when(i >= fills + steps)
    def _():
        j = i - fills - steps
        for p in range(PAIRS):
            rows = slice(p * 128, (p + 1) * 128)
            for first, dk_out, dv_out in ((band, dkt_own, dvt_own), (1 - band, dkt_far, dvt_far)):
                cols = pl.ds(pl.multiple_of(first * local + j * CHUNK, CHUNK), CHUNK)
                dk_out[rows, :] = dk_acc[p, :, cols].astype(bf16)
                dv_out[rows, :] = dv_acc[p, :, cols].astype(bf16)


def attend_backward(band, carried, q, do, o, lse, seg_own, seg_far, k_own, k_far, v_own, v_far, BQ=256, BK=256):
    rows, width = q.shape
    fills, steps = rows // CHUNK, rows // BQ
    mine = lambda i, *_: (jnp.clip(i - fills, 0, steps - 1), 0)
    fill = lambda i, *_: (jnp.minimum(i, fills - 1), 0)
    drain = lambda i, *_: (0, jnp.clip(i - fills - steps, 0, fills - 1))
    wide = pl.BlockSpec((CHUNK, width), fill)
    thin = pl.BlockSpec((1, rows), lambda i, *_: (0, 0))
    block = pl.BlockSpec((BQ, width), mine)
    flat = jax.ShapeDtypeStruct((width, rows), bf16)
    return pl.pallas_call(
        functools.partial(attend_bwd_kernel, fills, steps, BQ, BK),
        out_shape=(jax.ShapeDtypeStruct((rows, width), bf16), flat, flat, flat, flat, jax.ShapeDtypeStruct(carried.shape, carried.dtype)),
        grid_spec=pltpu.PrefetchScalarGridSpec(
            num_scalar_prefetch=1,
            grid=(fills + steps + fills,),
            in_specs=[block, block, block, pl.BlockSpec((BQ, 128), mine), wide, wide, wide, wide, thin, thin, block],
            out_specs=[block] + [pl.BlockSpec((width, CHUNK), drain)] * 4 + [block],
            scratch_shapes=[
                pltpu.VMEM((HEADS, 2 * rows, 128), bf16),
                pltpu.VMEM((HEADS, 2 * rows, 128), bf16),
                pltpu.VMEM((HEADS, BQ, 128), bf16),
                pltpu.VMEM((HEADS, BQ, 128), bf16),
                pltpu.VMEM((PAIRS, 128, 2 * BQ), bf16),
                pltpu.VMEM((PAIRS, 128, 2 * BQ), bf16),
                pltpu.VMEM((HEADS, BQ, 128), f32),
                pltpu.VMEM((PAIRS, 128, 2 * rows), f32),
                pltpu.VMEM((PAIRS, 128, 2 * rows), f32),
            ],
        ),
        compiler_params=pltpu.CompilerParams(vmem_limit_bytes=56 * MIB),
        cost_estimate=pl.CostEstimate(flops=45 * 10**9, bytes_accessed=20 * 10**6, transcendentals=0),
        name="attend_backward",
    )(band, q, do, o, lse, k_own, k_far, v_own, v_far, seg_own, seg_far, carried)


MESH = pl.DeviceIdType.MESH
TN = (((0,), (0,)), ((), ()))
SLICE = 768


def gelu_and_slope(u):
    below = 0.5 + 0.5 * lax.erf(u * 0.5**0.5)
    return u * below, below + u * jnp.exp(u * u * -0.5) * (0.5 / 3.141592653589793) ** 0.5


def normalize(rows):
    centred = rows - jnp.mean(rows, axis=-1, keepdims=True)
    scale = lax.rsqrt(jnp.mean(centred * centred, axis=-1, keepdims=True) + EPS)
    return centred * scale, scale


def add_sums(ref, row, values, first):
    sums = jnp.sum(values, axis=0, keepdims=True)
    at = slice(row, row + 1)
    ref[at, :] = jnp.where(first, sums, ref[at, :] + sums)


def as_row(ref):
    return ref[...].reshape(1, -1)


def add_low(dst, a, b):
    dst[...] = (a[...].astype(f32) + b[...].astype(f32)).astype(bf16)


def mlp_kernel(sorted_out, blocks, rows, slices, tok_ref, att_ref, cot_ref, wproj, wup, wdown, pbias, gain, shift, ubias, dbias,
               out_ref, rgrad_ref, agrad_ref, sums_ref, usums_ref, proj_out, *rest):
    outs, scratch = rest[: 4 if sorted_out else 2], rest[4 if sorted_out else 2 :]
    hid, ugr, n2s, bgs, ags, ats, d_own, d_far, d_in, u_in, p_own, p_far, p_in, send_sem, recv_sem = scratch
    i = pl.program_id(0)
    me, band = lax.axis_index("dp"), lax.axis_index("band")
    other = (me, 1 - band)
    width = tok_ref.shape[1]
    half, per_half = width // 2, slices // 2

    def push(t, src, dst):
        return pltpu.make_async_remote_copy(
            src_ref=src, dst_ref=dst, send_sem=send_sem.at[t], recv_sem=recv_sem.at[t], device_id=other, device_id_type=MESH
        )

    def d_copy(j):
        at = pl.ds(pl.multiple_of(j * SLICE, SLICE), SLICE)
        return push(j, d_far.at[at, :], d_in.at[at, :])

    def u_copy(c):
        return push(slices + c, hid.at[0:width, pl.ds(pl.multiple_of(c * SLICE, SLICE), SLICE)], u_in.at[c])

    def p_copy():
        return push(slices + per_half, p_far, p_in)

    @pl.when(i == 0)
    def _():
        barrier = pltpu.get_barrier_semaphore()
        pl.semaphore_signal(barrier, inc=1, device_id=other, device_id_type=MESH)
        pl.semaphore_wait(barrier, 1)

    @pl.when(i < blocks)
    def _():
        here = pl.ds(pl.multiple_of(i * rows, rows), rows)
        first = i == 0
        att = att_ref[...]
        ats[here, :] = att
        residual = tok_ref[...] + mm(att, wproj[...]) + as_row(pbias)
        xhat, scale = normalize(residual)
        n2 = (xhat * as_row(gain) + as_row(shift)).astype(bf16)
        n2s[here, :] = n2
        cot = cot_ref[...]
        bg = cot.astype(bf16)
        bgs[here, :] = bg
        add_sums(sums_ref, 0, bg.astype(f32), first)
        for c in range(slices):
            cols = slice(c * SLICE, (c + 1) * SLICE)
            hidden, slope = gelu_and_slope(mm(n2, wup[:, cols]) + ubias[cols].reshape(1, -1))
            hid[here, cols] = hidden.astype(bf16)
            grad = (mm(bg, wdown[cols, :], NT) * slope).astype(bf16)
            ugr[here, cols] = grad
            sums = jnp.sum(grad.astype(f32), axis=0, keepdims=True)
            usums_ref[0:1, cols] = jnp.where(first, sums, usums_ref[0:1, cols] + sums)
        out_ref[...] = residual + mm(hid[here, :], wdown[...]) + as_row(dbias)
        e = mm(ugr[here, :], wup[...], NT)
        add_sums(sums_ref, 1, e * xhat, first)
        add_sums(sums_ref, 2, e, first)
        f = e * as_row(gain)
        rgrad = cot + scale * (f - jnp.mean(f, axis=-1, keepdims=True) - xhat * jnp.mean(f * xhat, axis=-1, keepdims=True))
        rgrad_ref[...] = rgrad
        ag = rgrad.astype(bf16)
        ags[here, :] = ag
        add_sums(sums_ref, 3, ag.astype(f32), first)
        agrad_ref[...] = mm(ag, wproj[...], NT).astype(bf16)

    def columns(grad, own, far, at):
        left, right = grad[:, :half].astype(bf16), grad[:, half:].astype(bf16)
        own[at, :] = jnp.where(band == 0, left, right)
        far[at, :] = jnp.where(band == 0, right, left)

    @pl.when((i >= blocks) & (i < blocks + slices))
    def _():
        j = i - blocks
        at = pl.ds(pl.multiple_of(j * SLICE, SLICE), SLICE)
        columns(mm(hid[:, at], bgs[...], TN), d_own, d_far, at)
        d_copy(j).start()

    def up_slice(which):
        at = pl.ds(pl.multiple_of(which * SLICE, SLICE), SLICE)
        return mm(n2s[...], ugr[:, at], TN).astype(bf16)

    x, y = me & 1, (me >> 1) & 1

    def join_down(j):
        d_copy(j).wait_recv()
        if not sorted_out:
            at = pl.ds(pl.multiple_of(j * SLICE, SLICE), SLICE)
            add_low(outs[0].at[at, :], d_own.at[at, :], d_in.at[at, :])
            return
        shard = SLICE // 4
        piece = shard // 2
        for t in range(2):
            for out, x_bit, y_bit, first in (
                (outs[0], 1 - x, t, 0),
                (outs[1], x, t, 0),
                (outs[2], t, 1 - y, piece),
                (outs[3], t, y, piece),
            ):
                at = pl.ds(pl.multiple_of(j * SLICE + y_bit * 2 * shard + x_bit * shard + first, piece), piece)
                add_low(out.at[j, t, 0:piece], d_own.at[at, :], d_in.at[at, :])

    def join_up(c):
        u_copy(c).wait_recv()
        own = hid.at[0:width, (per_half + c) * SLICE : (per_half + c + 1) * SLICE]
        if not sorted_out:
            add_low(outs[1].at[:, c * SLICE : (c + 1) * SLICE], own, u_in.at[c])
            return
        shard = width // 16

        def one(s, carry):
            z, t = s >> 1, s & 1
            for out, sends in ((outs[2 * c], 1), (outs[2 * c + 1], 0)):
                bit = (y if c else x) ^ sends
                x_bit, y_bit = (t, bit) if c else (bit, t)
                at = pl.ds(pl.multiple_of((z * 4 + y_bit * 2 + x_bit) * shard, shard), shard)
                for part in range(2):
                    cols = slice(part * half, (part + 1) * half)
                    to = slice((2 + part) * shard, (3 + part) * shard)
                    add_low(out.at[z, t, to], own.at[at, cols], u_in.at[c, at, cols])
            return carry

        lax.fori_loop(0, 8, one, 0)

    middle = blocks + slices
    for c in range(per_half):
        at = slice(c * SLICE, (c + 1) * SLICE)

        @pl.when(i == middle + c)
        def _(c=c, at=at):
            hid[0:width, at] = up_slice((1 - band) * per_half + c)
            u_copy(c).start()
            join_down(c)

        @pl.when(i == middle + per_half + c)
        def _(c=c):
            hid[0:width, (per_half + c) * SLICE : (per_half + c + 1) * SLICE] = up_slice(band * per_half + c)
            join_down(per_half + c)

    @pl.when(i == middle + slices)
    def _():
        columns(mm(ats[...], ags[...], TN), p_own, p_far, slice(None))
        p_copy().start()
        for c in range(per_half):
            join_up(c)
        p_copy().wait_recv()
        add_low(proj_out, p_own, p_in)
        for j in range(slices):
            d_copy(j).wait_send()
        for c in range(per_half):
            u_copy(c).wait_send()
        p_copy().wait_send()


def mlp(size, tokens, attended, cotangent, w_proj, w_up, w_down, proj_bias, gain, shift, up_bias, down_bias, rows=256):
    count, width = tokens.shape
    ff = w_up.shape[1]
    blocks, slices = count // rows, ff // SLICE
    half, per_half = width // 2, slices // 2
    sorted_out = size == 16
    one = pl.Buffered(1)
    mine = lambda i: (jnp.minimum(i, blocks - 1), 0)
    block = pl.BlockSpec((rows, width), mine)

    def full(a):
        return pl.BlockSpec(a.shape, lambda i: (0,) * len(a.shape), pipeline_mode=one)

    vectors = (proj_bias, gain, shift, up_bias, down_bias)
    shape = jax.ShapeDtypeStruct
    if sorted_out:
        pieces = [shape((4, 2, ff // 16, half), bf16)] * 4
    else:
        pieces = [shape((ff, half), bf16), shape((width, ff // 2), bf16)]
    kept = [shape((8, width), f32), shape((8, ff), f32), shape((width, half), bf16)] + pieces
    low = lambda *s: pltpu.VMEM(s, bf16)
    copies = slices + per_half + 1
    return pl.pallas_call(
        functools.partial(mlp_kernel, sorted_out, blocks, rows, slices),
        out_shape=[shape((count, width), f32), shape((count, width), f32), shape((count, width), bf16)] + kept,
        grid=(blocks + 2 * slices + 1,),
        in_specs=[block, block, block] + [full(a) for a in (w_proj, w_up, w_down, *vectors)],
        out_specs=[block, block, block] + [full(a) for a in kept],
        scratch_shapes=[
            low(count, ff),
            low(count, ff),
            *([low(count, width)] * 4),
            *([low(ff, half)] * 3),
            low(per_half, width, SLICE),
            *([low(width, half)] * 3),
            pltpu.SemaphoreType.DMA((copies,)),
            pltpu.SemaphoreType.DMA((copies,)),
        ],
        compiler_params=pltpu.CompilerParams(vmem_limit_bytes=62 * MIB, collective_id=1, has_side_effects=True),
        cost_estimate=pl.CostEstimate(flops=40 * 10**9, bytes_accessed=40 * 10**6, transcendentals=0),
        name="mlp",
    )(tokens, attended, cotangent, w_proj, w_up, w_down, *vectors)


def qkv_kernel(steps, tok_ref, seg_ref, w_ref, gain, shift, qbias, vbias, q_ref, k_ref, v_ref, n_ref, k_far, v_far, seg_far,
               n_all, k_all, v_all, send_sem, recv_sem):
    i = pl.program_id(0)
    last = pl.num_programs(0) - 1
    other = (lax.axis_index("dp"), 1 - lax.axis_index("band"))
    rows, width = tok_ref.shape

    def push(t, src, dst):
        return pltpu.make_async_remote_copy(
            src_ref=src, dst_ref=dst, send_sem=send_sem.at[t], recv_sem=recv_sem.at[t], device_id=other, device_id_type=MESH
        )

    def copies(j):
        at = pl.ds(pl.multiple_of(j * rows, rows), rows)
        return push(2 * j, k_all.at[at, :], k_far.at[at, :]), push(2 * j + 1, v_all.at[at, :], v_far.at[at, :])

    segs = push(send_sem.shape[0] - 1, seg_ref, seg_far)

    @pl.when(i == 0)
    def _():
        barrier = pltpu.get_barrier_semaphore()
        pl.semaphore_signal(barrier, inc=1, device_id=other, device_id_type=MESH)
        pl.semaphore_wait(barrier, 1)
        segs.start()

    @pl.when(i < steps)
    def _():
        here = pl.ds(pl.multiple_of(i * rows, rows), rows)
        xhat, _ = normalize(tok_ref[...])
        n1 = (xhat * as_row(gain) + as_row(shift)).astype(bf16)
        n_ref[...] = n1
        n_all[here, :] = n1
        k = mm(n1, w_ref[:, width : 2 * width]).astype(bf16)
        k_ref[...] = k
        k_all[here, :] = k
        copies(i)[0].start()
        v = (mm(n1, w_ref[:, 2 * width :]) + as_row(vbias)).astype(bf16)
        v_ref[...] = v
        v_all[here, :] = v
        copies(i)[1].start()

    @pl.when(i >= steps)
    def _():
        here = pl.ds(pl.multiple_of((i - steps) * rows, rows), rows)
        q = (mm(n_all[here, :], w_ref[:, :width]) + as_row(qbias)).astype(bf16)
        q_ref[...] = q * jnp.asarray(HEAD_DIM**-0.5, bf16)

    @pl.when(i == last)
    def _():
        segs.wait()
        for j in range(k_all.shape[0] // rows):
            for copy in copies(j):
                copy.wait()


def project_qkv(tokens, seg, w_qkv, gain, shift, query_bias, value_bias, rows=256):
    count, width = tokens.shape
    one = pl.Buffered(1)
    steps = count // rows
    block = pl.BlockSpec((rows, width), lambda i: (jnp.minimum(i, steps - 1), 0))
    late = pl.BlockSpec((rows, width), lambda i: (jnp.maximum(i - steps, 0), 0))
    vectors = (gain, shift, query_bias, value_bias)
    hbm = pl.BlockSpec(memory_space=pl.ANY)
    low = jax.ShapeDtypeStruct((count, width), bf16)
    return pl.pallas_call(
        functools.partial(qkv_kernel, steps),
        out_shape=(low,) * 6 + (jax.ShapeDtypeStruct(seg.shape, seg.dtype),),
        grid=(2 * steps,),
        in_specs=[block, hbm] + [pl.BlockSpec(a.shape, lambda i, n=a.ndim: (0,) * n, pipeline_mode=one) for a in (w_qkv, *vectors)],
        out_specs=[late] + [block] * 3 + [hbm] * 3,
        scratch_shapes=[
            pltpu.VMEM((count, width), bf16),
            pltpu.VMEM((count, width), bf16),
            pltpu.VMEM((count, width), bf16),
            pltpu.SemaphoreType.DMA((2 * steps + 1,)),
            pltpu.SemaphoreType.DMA((2 * steps + 1,)),
        ],
        compiler_params=pltpu.CompilerParams(vmem_limit_bytes=60 * MIB, collective_id=2, has_side_effects=True),
        cost_estimate=pl.CostEstimate(flops=4 * 10**9, bytes_accessed=13 * 10**6, transcendentals=0),
        name="project_qkv",
    )(tokens, seg, w_qkv, *vectors)


def qkv_grad_kernel(blocks, rows, band_ref, dq_ref, dk_own, dk_far, dv_own, dv_far, n_ref, packed_ref, own_ref, far_ref, sums_ref, packed):
    i = pl.program_id(0)
    band = band_ref[0]
    width = dq_ref.shape[1]
    half = own_ref.shape[1]

    @pl.when(i < blocks)
    def _():
        here = pl.ds(pl.multiple_of(i * rows, rows), rows)
        first = i == 0
        dq = dq_ref[...]
        packed_ref[:, :width] = dq
        packed[here, :width] = dq
        add_sums(sums_ref, 0, dq.astype(f32), first)
        for t, (own, far) in enumerate(((dk_own, dk_far), (dv_own, dv_far))):
            for p in range(width // 128):
                at = slice(p * 128, (p + 1) * 128)
                to = slice((t + 1) * width + p * 128, (t + 1) * width + (p + 1) * 128)
                turned = (own[at, :].astype(f32) + far[at, :].astype(f32)).astype(bf16).T
                packed_ref[:, to] = turned
                packed[here, to] = turned
        add_sums(sums_ref, 1, packed_ref[:, 2 * width :].astype(f32), first)

    def columns(which):
        at = pl.ds(pl.multiple_of(which * half, 128), half)
        return mm(n_ref[...], packed[:, at], TN).astype(bf16)

    @pl.when(i == blocks)
    def _():
        far_ref[...] = columns(1 - band)

    @pl.when(i == blocks + 1)
    def _():
        own_ref[...] = columns(band)


def qkv_grads(band, dq, dk_own, dk_far, dv_own, dv_far, normed, rows=256):
    count, width = dq.shape
    blocks = count // rows
    half = 3 * width // 2
    one = pl.Buffered(1)
    mine = lambda i, *_: (jnp.minimum(i, blocks - 1), 0)
    flip = lambda i, *_: (0, jnp.minimum(i, blocks - 1))
    whole = lambda i, *_: (0, 0)
    shape = jax.ShapeDtypeStruct
    return pl.pallas_call(
        functools.partial(qkv_grad_kernel, blocks, rows),
        out_shape=(shape((count, 3 * width), bf16), shape((width, half), bf16), shape((width, half), bf16), shape((8, width), f32)),
        grid_spec=pltpu.PrefetchScalarGridSpec(
            num_scalar_prefetch=1,
            grid=(blocks + 2,),
            in_specs=[pl.BlockSpec((rows, width), mine)]
            + [pl.BlockSpec((width, rows), flip)] * 4
            + [pl.BlockSpec((count, width), whole, pipeline_mode=one)],
            out_specs=[
                pl.BlockSpec((rows, 3 * width), mine),
                pl.BlockSpec((width, half), whole, pipeline_mode=one),
                pl.BlockSpec((width, half), whole, pipeline_mode=one),
                pl.BlockSpec((8, width), whole, pipeline_mode=one),
            ],
            scratch_shapes=[pltpu.VMEM((count, 3 * width), bf16)],
        ),
        compiler_params=pltpu.CompilerParams(vmem_limit_bytes=40 * MIB),
        cost_estimate=pl.CostEstimate(flops=8 * 10**9, bytes_accessed=18 * 10**6, transcendentals=0),
        name="qkv_grads",
    )(band, dq, dk_own, dk_far, dv_own, dv_far, normed)


def input_grad_kernel(packed_ref, tok_ref, rgrad_ref, w_ref, gain, out_ref, sums_ref):
    first = pl.program_id(0) == 0
    e = mm(packed_ref[...], w_ref[...], NT)
    xhat, scale = normalize(tok_ref[...])
    add_sums(sums_ref, 0, e * xhat, first)
    add_sums(sums_ref, 1, e, first)
    f = e * gain[...]
    back = scale * (f - jnp.mean(f, axis=-1, keepdims=True) - xhat * jnp.mean(f * xhat, axis=-1, keepdims=True))
    out_ref[...] = rgrad_ref[...] + back


def input_grads(packed, tokens, rgrad, w_qkv, gain, rows=256):
    count, width = tokens.shape
    one = pl.Buffered(1)
    block = pl.BlockSpec((rows, width), lambda i: (i, 0))
    return pl.pallas_call(
        input_grad_kernel,
        out_shape=(jax.ShapeDtypeStruct((count, width), f32), jax.ShapeDtypeStruct((8, width), f32)),
        grid=(count // rows,),
        in_specs=[
            pl.BlockSpec((rows, packed.shape[1]), lambda i: (i, 0)),
            block,
            block,
            pl.BlockSpec(w_qkv.shape, lambda i: (0, 0), pipeline_mode=one),
            pl.BlockSpec((1, width), lambda i: (0, 0), pipeline_mode=one),
        ],
        out_specs=[block, pl.BlockSpec((8, width), lambda i: (0, 0), pipeline_mode=one)],
        compiler_params=pltpu.CompilerParams(vmem_limit_bytes=32 * MIB),
        cost_estimate=pl.CostEstimate(flops=6 * 10**9, bytes_accessed=18 * 10**6, transcendentals=0),
        name="input_grads",
    )(packed, tokens, rgrad, w_qkv, gain.reshape(1, -1))


def finish_kernel(
    dq_hbm, dko_hbm, dkf_hbm, dvo_hbm, dvf_hbm, n_hbm, tok_hbm, rgrad_hbm, w_hbm, ak_hbm, ar_hbm, bk_hbm, br_hbm, proj_hbm, gain, msums, usums,
    out, down_out, up_out, qkv_out, proj_out, vec_out, usum_out,
    packed, dko, dko_in, dvo, dvo_in, n1, tok, wq, early, proj, cols, far_in, tail,
    one_e, one_t, two_e, two_t, thr_e, thr_t, vec, vec_band, vec_x, vec_y, vec_z,
    load_sem, swap_send, swap_recv, send, recv, vsend, vrecv,
):
    me = lax.axis_index("dp")
    band = lax.axis_index("band")
    x, y, z = me & 1, (me >> 1) & 1, me >> 2
    rows, width = tok.shape
    half = far_in.shape[-1]
    peer_band = (me, 1 - band)
    peer_x = (me ^ 1, band)
    peer_y = (me ^ 2, band)
    peers_z = [(((z + d) & 3) * 4 + (me & 3), band) for d in (1, 2, 3)]

    def load(t, src, dst):
        copy = pltpu.make_async_copy(src, dst, load_sem.at[t])
        copy.start()
        return copy

    loads = {
        "early": (load(0, ak_hbm, early.at[0]), load(1, ar_hbm, one_e.at[0]), load(2, bk_hbm, early.at[1]), load(3, br_hbm, one_e.at[1])),
        "queries": (load(6, dq_hbm, packed.at[:, 0:width]),),
        "normed": (load(7, n_hbm, n1),),
        "keys": (load(4, dko_hbm, dko), load(5, dvo_hbm, dvo)),
        "proj": (load(8, proj_hbm, proj),),
        "weight": (load(10, w_hbm, wq),),
        "rows": (load(11, tok_hbm, tok), load(12, rgrad_hbm, out)),
    }

    def ready(name):
        for copy in loads[name]:
            copy.wait()

    barrier = pltpu.get_barrier_semaphore()
    for peer in (peer_band, peer_x, peer_y, *peers_z):
        pl.semaphore_signal(barrier, inc=1, device_id=peer, device_id_type=MESH)
    pl.semaphore_wait(barrier, 6)

    pending = []

    def push(src, dst, peer, s, r):
        copy = pltpu.make_async_remote_copy(src_ref=src, dst_ref=dst, send_sem=s, recv_sem=r, device_id=peer, device_id_type=MESH)
        copy.start()
        pending.append(copy)
        return copy

    swap_k = push(dkf_hbm, dko_in, peer_band, swap_send.at[0], swap_recv.at[0])
    swap_v = push(dvf_hbm, dvo_in, peer_band, swap_send.at[1], swap_recv.at[1])

    def put(dst, src):
        dst[...] = src[...]

    def each_shard(body):
        def step(s, c):
            body(s >> 2, (s >> 1) & 1, s & 1)
            return c

        lax.fori_loop(0, 16, step, 0)

    def first_stage(t, work, one, cut):
        a, b = cut
        return (
            push(work.at[:, :, 1 - x, a[0], a[1]], one.at[0], peer_x, send.at[t, 0, 0], recv.at[t, 0, 0]),
            push(work.at[:, 1 - y, :, b[0], b[1]], one.at[1], peer_y, send.at[t, 1, 0], recv.at[t, 1, 0]),
        )

    def second_stage(t, kept, one, two, copies):
        out = []
        for piece, mine, peer in ((0, y, peer_y), (1, x, peer_x)):
            if copies is not None:
                copies[piece].wait_recv()

            def total(s, c, piece=piece):
                add_low(one.at[piece, s >> 1, s & 1], one.at[piece, s >> 1, s & 1], kept(piece, s >> 1, s & 1))
                return c

            lax.fori_loop(0, 8, total, 0)
            out.append(push(one.at[piece, :, 1 - mine], two.at[piece], peer, send.at[t, piece, 1], recv.at[t, piece, 1]))
        return out

    def third_stage(t, one, two, three, copies):
        out = []
        for piece, mine in ((0, y), (1, x)):
            copies[piece].wait_recv()

            def total(zz, c, piece=piece, mine=mine):
                add_low(two.at[piece, zz], two.at[piece, zz], one.at[piece, zz, mine])
                return c

            lax.fori_loop(0, 4, total, 0)
            for d in (1, 2, 3):
                out.append(
                    push(two.at[piece, (z + d) & 3], three.at[piece, d - 1], peers_z[d - 1], send.at[t, piece, 1 + d], recv.at[t, piece, 1 + d])
                )
        return out

    def last(two, three, copies, piece):
        for d in range(3):
            copies[3 * piece + d].wait_recv()
        total = two[piece, z].astype(f32)
        for d in range(3):
            total = total + three[piece, d].astype(f32)
        return total

    everything = slice(None)
    wide_cut = ((everything, slice(0, 768)), (everything, slice(768, 1536)))

    ready("early")
    e_two = second_stage(0, lambda p, i, j: early.at[p, i, j], one_e, two_e, None)

    def tail_kept(piece, zz, t):
        return tail.at[zz, t, x, :, 0:768] if piece == 0 else tail.at[zz, y, t, :, 768:1536]

    def columns(t):
        cols[:, :, :, :, t * width : (t + 1) * width] = (
            mm(n1[...], packed[:, t * width : (t + 1) * width], TN).astype(bf16).reshape(cols.shape[:-1] + (width,))
        )

    def turn(t, own, other):
        def step(i, c):
            here = pl.ds(pl.multiple_of(i * 256, 256), 256)
            for p in range(width // 128):
                at = slice(p * 128, (p + 1) * 128)
                turned = (own[at, here].astype(f32) + other[at, here].astype(f32)).astype(bf16).T
                packed[here, t * width + p * 128 : t * width + (p + 1) * 128] = turned
            return c

        lax.fori_loop(0, rows // 256, step, 0)

    def swap(t, start, size, to):
        return pltpu.make_async_remote_copy(
            src_ref=cols.at[:, :, :, :, pl.ds(pl.multiple_of(start, 128), size)],
            dst_ref=far_in.at[:, :, :, :, pl.ds(pl.multiple_of(to, 128), size)],
            send_sem=swap_send.at[t],
            recv_sem=swap_recv.at[t],
            device_id=peer_band,
            device_id_type=MESH,
        )

    third = width // 2
    swap_near = swap(2, (3 - band) * third, third, band * width)
    swap_wide = swap(3, (1 - band) * 2 * width, width, (1 - band) * third)
    ready("queries")
    ready("normed")
    columns(0)

    @pl.when(band == 1)
    def _():
        swap_wide.start()

    ready("keys")
    swap_k.wait_recv()
    turn(1, dko, dko_in)
    columns(1)
    swap_near.start()
    swap_v.wait_recv()
    turn(2, dvo, dvo_in)
    columns(2)

    @pl.when(band == 0)
    def _():
        swap_wide.start()

    ready("proj")
    each_shard(lambda i, j, k: put(tail.at[i, j, k, :, half : 2 * width], proj.at[i, j, k]))
    e_three = third_stage(0, one_e, two_e, thr_e, e_two)
    swap_near.wait()
    swap_wide.wait()
    mine = pl.ds(pl.multiple_of(band * half, 128), half)
    each_shard(lambda i, j, k: add_low(tail.at[i, j, k, :, 0:half], cols.at[i, j, k, :, mine], far_in.at[i, j, k]))
    t_one = first_stage(2, tail, one_t, wide_cut)

    ready("weight")
    ready("rows")
    vec[...] = jnp.zeros(vec.shape, f32)

    def rows_back(i, c):
        here = pl.ds(pl.multiple_of(i * 256, 256), 256)
        e = mm(packed[here, :], wq[...], NT)
        xhat, scale = normalize(tok[here, :])
        vec[0:1, :] = vec[0:1, :] + jnp.sum(e * xhat, axis=0, keepdims=True)
        vec[1:2, :] = vec[1:2, :] + jnp.sum(e, axis=0, keepdims=True)
        vec[2:3, :] = vec[2:3, :] + jnp.sum(packed[here, 0:width].astype(f32), axis=0, keepdims=True)
        vec[3:4, :] = vec[3:4, :] + jnp.sum(packed[here, 2 * width : 3 * width].astype(f32), axis=0, keepdims=True)
        f = e * as_row(gain)
        back = scale * (f - jnp.mean(f, axis=-1, keepdims=True) - xhat * jnp.mean(f * xhat, axis=-1, keepdims=True))
        out[here, :] = out[here, :] + back
        return c

    lax.fori_loop(0, rows // 256, rows_back, 0)
    vec[4:8, :] = msums[0:4, :]
    for t in range(usums.shape[1] // width):
        vec[8 + t : 9 + t, :] = usums[0:1, t * width : (t + 1) * width]
    v_band = push(vec, vec_band, peer_band, vsend.at[0], vrecv.at[0])
    t_two = second_stage(2, tail_kept, one_t, two_t, t_one)
    v_band.wait()
    vec_band[...] = vec[...] + vec_band[...]
    v_x = push(vec_band, vec_x, peer_x, vsend.at[1], vrecv.at[1])
    v_x.wait()
    vec_x[...] = vec_band[...] + vec_x[...]
    v_y = push(vec_x, vec_y, peer_y, vsend.at[2], vrecv.at[2])
    v_y.wait()
    vec_y[...] = vec_x[...] + vec_y[...]
    v_z = [push(vec_y, vec_z.at[d], peers_z[d], vsend.at[3 + d], vrecv.at[3 + d]) for d in range(3)]
    t_three = third_stage(2, one_t, two_t, thr_t, t_two)
    for copy in v_z:
        copy.wait_recv()
    vec[...] = vec_y[...] + vec_z[0] + vec_z[1] + vec_z[2]
    shard = vec_out.shape[1]
    vec_out[...] = pltpu.roll(vec[0:8, :], width - me * shard, 1)[:, 0:shard]
    wide = usum_out.shape[1]
    per_row = width // wide
    row = vec[pl.ds(8 + me // per_row, 1), :]
    usum_out[...] = pltpu.roll(jnp.broadcast_to(row, (8, width)), width - (me % per_row) * wide, 1)[0:1, 0:wide]
    shard = width // 16
    for piece in range(2):
        early_sum = last(two_e, thr_e, e_three, piece)
        down_out[piece * 2 * shard : (piece + 1) * 2 * shard, :] = early_sum[0 : 2 * shard]
        for part in range(2):
            at = (2 * piece + part) * third
            up_out[:, at : at + third] = early_sum[(2 + part) * shard : (3 + part) * shard]
    qkv_out[:, 0:768] = last(two_t, thr_t, t_three, 0)
    final = last(two_t, thr_t, t_three, 1)
    qkv_out[:, 768:half] = final[:, 0 : half - 768]
    proj_out[...] = final[:, half - 768 :]
    done = {id(c) for c in (v_band, v_x, v_y)}
    for copy in pending:
        if id(copy) not in done:
            copy.wait_send()


def finish(dq, dk_own, dk_far, dv_own, dv_far, normed, tokens, rgrad, w_qkv, pieces, proj, gain, msums, usums):
    rows, width = tokens.shape
    ff = usums.shape[1]
    half = 3 * width // 2
    shards = (4, 2, 2)
    u_shape, p_shape = shards + (width // 16, ff // 2), shards + (width // 16, width // 2)
    q_shape = shards + (width // 16, half)
    e_piece, w_piece = (ff // 16, width // 2), (width // 16, ff // 4)
    hbm, vmem = pl.BlockSpec(memory_space=pl.ANY), pl.BlockSpec(memory_space=pltpu.VMEM)
    shape = jax.ShapeDtypeStruct
    low = lambda *s: pltpu.VMEM(s, bf16)
    dma = pltpu.SemaphoreType.DMA
    return pl.pallas_call(
        finish_kernel,
        out_shape=(
            shape((rows, width), f32),
            shape((ff // 16, width // 2), f32),
            shape((width // 16, ff // 2), f32),
            shape((width // 16, half), f32),
            shape((width // 16, width // 2), f32),
            shape((8, width // 16), f32),
            shape((1, ff // 16), f32),
        ),
        in_specs=[hbm] * 14 + [vmem] * 3,
        out_specs=[vmem] * 7,
        scratch_shapes=[
            low(rows, 3 * width),
            *([low(width, rows)] * 4),
            low(rows, width),
            pltpu.VMEM((rows, width), f32),
            low(width, 3 * width),
            low(2, 4, 2, *e_piece),
            low(*p_shape),
            low(*shards, width // 16, 3 * width),
            low(*q_shape),
            low(*u_shape),
            low(2, 4, 2, *e_piece),
            low(2, 4, 2, *w_piece),
            low(2, 4, *e_piece),
            low(2, 4, *w_piece),
            low(2, 3, *e_piece),
            low(2, 3, *w_piece),
            pltpu.VMEM((16, width), f32),
            pltpu.VMEM((16, width), f32),
            pltpu.VMEM((16, width), f32),
            pltpu.VMEM((16, width), f32),
            pltpu.VMEM((3, 16, width), f32),
            dma((13,)),
            dma((4,)),
            dma((4,)),
            dma((3, 2, 5)),
            dma((3, 2, 5)),
            dma((6,)),
            dma((6,)),
        ],
        compiler_params=pltpu.CompilerParams(vmem_limit_bytes=52 * MIB, collective_id=0, has_side_effects=True),
        cost_estimate=pl.CostEstimate(flops=20 * 10**9, bytes_accessed=40 * 10**6, transcendentals=0),
        name="finish",
    )(dq, dk_own, dk_far, dv_own, dv_far, normed, tokens, rgrad, w_qkv, *pieces, proj.reshape(p_shape),
      gain, msums, usums)


def swap_band(x):
    return lax.ppermute(x, "band", [(0, 1), (1, 0)])


def pick(x, which, axis):
    return lax.dynamic_index_in_dim(x, which, axis, keepdims=False)


def halve(x, axis, bit, size):
    mine = (lax.axis_index("dp") >> bit) & 1
    arrived = lax.ppermute(pick(x, 1 - mine, axis), "dp", [(i, i ^ (1 << bit)) for i in range(size)])
    return pick(x, mine, axis).astype(f32) + arrived.astype(f32)


class Reduction:
    def __init__(self, x, order, size):
        rows, columns = x.shape
        levels = size.bit_length() - 1
        self.size = size
        self.x = x.reshape((2,) * levels + (rows // size, columns))
        self.left = list(range(levels - 1, -1, -1))
        self.order = list(order)

    def step(self):
        if self.order:
            bit = self.order.pop(0)
            x = halve(self.x, self.left.index(bit), bit, self.size)
            self.left.remove(bit)
            self.x = x.astype(bf16) if self.left else x

    def finish(self):
        while self.order:
            self.step()
        return self.x


def finish_any(size, band_at, query_grad, dk_own, dk_far, dv_own, dv_far, normed, tokens, residual_grad, w_qkv, pieces, proj, gain, msums, usums):
    width = tokens.shape[1]
    rising = list(range(size.bit_length() - 1))
    turned = [1, 0] + rising[2:]
    packed, qkv_own, qkv_far, qkv_sums = qkv_grads(
        band_at, query_grad, dk_own, swap_band(dk_far), dv_own, swap_band(dv_far), normed
    )
    input_grad, first_sums = input_grads(packed, tokens, residual_grad, w_qkv, gain)

    def total(x, order):
        return Reduction(x, order, size).finish()

    def join(own, far):
        return (own.astype(f32) + swap_band(far).astype(f32)).astype(bf16)

    tall = jnp.concatenate([first_sums[:2], qkv_sums[:2], msums[:4]], axis=0)
    thin = jnp.concatenate([tall.T, usums[0].reshape(width, -1)], axis=1)
    thin = jnp.pad(thin, ((0, 0), (0, 128 - thin.shape[1]))).astype(bf16)
    thin_sum = total(join(thin, thin), turned)
    ups = usums.shape[1] // width
    return (
        input_grad,
        total(pieces[0], rising),
        total(pieces[1], turned),
        total(join(qkv_own, qkv_far), rising),
        total(proj, turned),
        [thin_sum[:, t] for t in range(8)],
        thin_sum[:, 8 : 8 + ups].reshape(-1),
    )


def local(
    size,
    inputs,
    segment_ids,
    cotangent,
    first_gain,
    first_bias,
    w_qkv,
    query_bias,
    value_bias,
    w_proj,
    proj_bias,
    second_gain,
    second_bias,
    w_up,
    up_bias,
    w_down,
    down_bias,
):
    local_shape = inputs.shape
    width = local_shape[-1]
    band = lax.axis_index("band")
    band_at = band.astype(jnp.int32).reshape(1)
    tokens = inputs.reshape(-1, width)
    seg_own = segment_ids
    queries, k_own, v_own, normed, k_far, v_far, seg_far = project_qkv(
        tokens, seg_own, w_qkv, first_gain, first_bias, query_bias, value_bias
    )
    keys = (seg_own, seg_far, k_own, k_far, v_own, v_far)
    attended, log_totals = attend_forward(band_at, queries, *keys)
    output, residual_grad, attended_grad, mlp_sums, up_sums, proj, *pieces = mlp(
        size,
        tokens,
        attended,
        cotangent.reshape(-1, width),
        w_proj,
        w_up,
        w_down,
        proj_bias,
        second_gain,
        second_bias,
        up_bias,
        down_bias,
    )
    if size == 16:
        turns = [[(i, i ^ bit) for i in range(size)] for bit in (1, 2)]
        pieces = [
            part
            for t in range(2)
            for part in (pieces[2 * t + 1], lax.ppermute(pieces[2 * t], "dp", turns[t]))
        ]
    query_grad, dk_own, dk_far, dv_own, dv_far, output = attend_backward(
        band_at, output, queries, attended_grad, attended, log_totals, *keys
    )
    if size == 16:
        input_grad, down_sum, up_sum, qkv_sum, proj_sum, vec, up_vec = finish(
            query_grad, dk_own, dk_far, dv_own, dv_far, normed, tokens, residual_grad, w_qkv, pieces, proj, first_gain, mlp_sums, up_sums
        )
        vectors, up_vector = [vec[t] for t in range(8)], up_vec.reshape(-1)
    else:
        input_grad, down_sum, up_sum, qkv_sum, proj_sum, vectors, up_vector = finish_any(
            size, band_at, query_grad, dk_own, dk_far, dv_own, dv_far, normed, tokens, residual_grad, w_qkv, pieces, proj, first_gain, mlp_sums, up_sums
        )
    return (
        output.reshape(local_shape),
        input_grad.reshape(local_shape),
        vectors[0],
        vectors[1],
        qkv_sum,
        vectors[2],
        vectors[3],
        proj_sum,
        vectors[7],
        vectors[5],
        vectors[6],
        up_sum,
        up_vector,
        down_sum,
        vectors[4],
    )


def solution(mesh):
    size = mesh.shape["dp"]
    placed = (P("dp", "band", None), P("dp", "band"), P("dp", "band", None)) + (P(),) * 13
    split, thin = P("dp", "band"), P("dp")
    wide = P("dp", "band", None)
    return jax.shard_map(
        functools.partial(local, size),
        mesh=mesh,
        in_specs=placed,
        out_specs=(wide, wide, thin, thin, split, thin, thin, split, thin, thin, thin, split, thin, split, thin),
        check_vma=False,
    )
```

```python
import functools

import jax
import jax.numpy as jnp
from jax import lax
from jax.experimental import pallas as pl
from jax.experimental.pallas import tpu as pltpu
from jax.sharding import PartitionSpec as P

EPS = 1e-05
HEADS = 12
HEAD_DIM = 64
NEG_LARGE = -1e30
PAIRS = HEADS // 2
CHUNK = 256
EDGE = 64
MIB = 1 << 20
f32, bf16 = jnp.float32, jnp.bfloat16
NN = (((1,), (0,)), ((), ()))
NT = (((1,), (1,)), ((), ()))


def mm(a, b, dims=NN):
    return lax.dot_general(a, b, dims, preferred_element_type=f32)


def low_lanes(rows):
    return lax.broadcasted_iota(jnp.int32, (rows, 128), 1) < HEAD_DIM


def side_lanes(rows):
    return lax.broadcasted_iota(jnp.int32, (rows, 128), 1) & (HEAD_DIM - 1)


def split3(x):
    high = x.astype(bf16).astype(f32)
    middle = (x - high).astype(bf16).astype(f32)
    return high, middle, x - high - middle


def place(side, parts, base):
    for t, part in enumerate(parts):
        base = jnp.where(side == 16 + t, part, base)
    return base


def as_column(row):
    return jnp.broadcast_to(row, (8, row.shape[1])).T[:, 0:1]


def key_window(seg_own, seg_far, block, BQ, BK):
    own, far = seg_own[...].astype(f32), seg_far[...].astype(f32)

    def below(limit):
        return jnp.sum((own < limit).astype(f32) + (far < limit).astype(f32)).astype(jnp.int32)

    mine = seg_own[:, pl.ds(pl.multiple_of(block * BQ, BQ), BQ)].astype(f32)
    row = lax.broadcasted_iota(jnp.int32, mine.shape, 1)
    lo = (below(jnp.min(mine)) // 128) * 128
    blocks = (below(jnp.max(mine) + 1.0) - lo + BK - 1) // BK
    start = jnp.minimum(lo, 2 * own.shape[1] - blocks * BK)
    early_end = below(jnp.min(jnp.where(row >= EDGE, mine, 99.0)))
    late_start = below(jnp.max(jnp.where(row < BQ - EDGE, mine, -1.0)) + 1.0)
    early = jnp.clip((early_end - start) // BK, 0, blocks)
    late = jnp.clip((start + blocks * BK - late_start) // BK, 0, blocks - early)
    return start, blocks, early, late


def over_blocks(count, early, late, rows, body):
    for first, end, part in (
        (0, early, slice(0, EDGE)),
        (early, count - late, slice(0, rows)),
        (count - late, count, slice(rows - EDGE, rows)),
    ):

        def step(j, c, part=part):
            body(j, part)
            return c

        lax.fori_loop(first, end, step, 0)


def fill_pairs(src, dst, rows, low, extra):
    for p in range(PAIRS):
        pair = src[:, p * 128 : (p + 1) * 128]
        dst[2 * p, rows, :] = jnp.where(low, pair, extra)
        dst[2 * p + 1, rows, :] = jnp.where(low, extra, pair)


def fill_keys(band, i, k_own, k_far, v_own, v_far, seg_own, seg_far, kaug, vaug, value_extra):
    local = kaug.shape[1] // 2
    low, side = low_lanes(CHUNK), side_lanes(CHUNK)
    here = pl.ds(pl.multiple_of(i * CHUNK, CHUNK), CHUNK)
    for k, v, seg, first in ((k_own, v_own, seg_own, band), (k_far, v_far, seg_far, 1 - band)):
        rows = pl.ds(pl.multiple_of(first * local + i * CHUNK, CHUNK), CHUNK)
        extra = jnp.where(side < 16, jnp.where(side == as_column(seg[:, here]), 0.0, NEG_LARGE), jnp.where(side < 19, -1.0, 0.0))
        fill_pairs(k, kaug, rows, low, extra.astype(bf16))
        fill_pairs(v, vaug, rows, low, value_extra)


def attend_fwd_kernel(fills, BQ, BK, band_ref, q_ref, k_own, k_far, v_own, v_far,
                      seg_own, seg_far, o_ref, lse_ref, kaug, vaug, qm, s_all, mx, acc):
    i = pl.program_id(0)

    @pl.when(i < fills)
    def _():
        fill_keys(band_ref[0], i, k_own, k_far, v_own, v_far, seg_own, seg_far, kaug, vaug, jnp.ones((CHUNK, 128), bf16))

    @pl.when(i >= fills)
    def _():
        low, side = low_lanes(BQ), side_lanes(BQ)
        block = i - fills
        ids = as_column(seg_own[:, pl.ds(pl.multiple_of(block * BQ, BQ), BQ)])
        own = (side == ids).astype(f32).astype(bf16)
        for p in range(PAIRS):
            pair = q_ref[:, p * 128 : (p + 1) * 128]
            qm[2 * p] = jnp.where(low, pair, own)
            qm[2 * p + 1] = jnp.where(low, own, pair)
        mx[...] = jnp.full(mx.shape, -3e38, f32)
        acc[...] = jnp.zeros(acc.shape, f32)
        start, count, early, late = key_window(seg_own, seg_far, block, BQ, BK)

        def first(j, part):
            at = pl.multiple_of(start + j * BK, 128)
            out = pl.ds(pl.multiple_of(j * BK, BK), BK)
            for h in range(HEADS):
                s = mm(qm[h, part, :], kaug[h, pl.ds(at, BK), :], NT)
                s_all[h, part, out] = s
                m = mx[h, part, :]
                for t in range(BK // 128):
                    m = jnp.maximum(m, s[:, t * 128 : (t + 1) * 128])
                mx[h, part, :] = m

        over_blocks(count, early, late, BQ, first)
        for h in range(HEADS):
            mx[h] = jnp.broadcast_to(jnp.max(mx[h], axis=1, keepdims=True), (BQ, 128))

        def second(j, part):
            at = pl.multiple_of(start + j * BK, 128)
            src = pl.ds(pl.multiple_of(j * BK, BK), BK)
            for h in range(HEADS):
                p = jnp.exp(s_all[h, part, src] - jnp.concatenate([mx[h, part, :]] * (BK // 128), axis=1)).astype(bf16)
                acc[h, part, :] += mm(p, vaug[h, pl.ds(at, BK), :])

        over_blocks(count, early, late, BQ, second)
        lane = lax.broadcasted_iota(jnp.int32, (BQ, 128), 1)
        lse = jnp.zeros((BQ, 128), f32)
        for p in range(PAIRS):
            even, odd = acc[2 * p], acc[2 * p + 1]
            swapped = pltpu.roll(even, HEAD_DIM, 1)
            total = jnp.where(low, swapped, pltpu.roll(odd, HEAD_DIM, 1))
            o_ref[:, p * 128 : (p + 1) * 128] = (jnp.where(low, even, odd) / total).astype(bf16)
            lse = jnp.where(lane == 2 * p, mx[2 * p] + jnp.log(swapped), lse)
            lse = jnp.where(lane == 2 * p + 1, mx[2 * p + 1] + jnp.log(odd), lse)
        lse_ref[...] = lse


def attend_forward(band, q, seg_own, seg_far, k_own, k_far, v_own, v_far, BQ=256, BK=256):
    rows, width = q.shape
    fills, steps = rows // CHUNK, rows // BQ
    mine = lambda i, *_: (jnp.clip(i - fills, 0, steps - 1), 0)
    fill = lambda i, *_: (jnp.minimum(i, fills - 1), 0)
    wide = pl.BlockSpec((CHUNK, width), fill)
    thin = pl.BlockSpec((1, rows), lambda i, *_: (0, 0))
    return pl.pallas_call(
        functools.partial(attend_fwd_kernel, fills, BQ, BK),
        out_shape=(jax.ShapeDtypeStruct((rows, width), bf16), jax.ShapeDtypeStruct((rows, 128), f32)),
        grid_spec=pltpu.PrefetchScalarGridSpec(
            num_scalar_prefetch=1,
            grid=(fills + steps,),
            in_specs=[pl.BlockSpec((BQ, width), mine), wide, wide, wide, wide, thin, thin],
            out_specs=[pl.BlockSpec((BQ, width), mine), pl.BlockSpec((BQ, 128), mine)],
            scratch_shapes=[
                pltpu.VMEM((HEADS, 2 * rows, 128), bf16),
                pltpu.VMEM((HEADS, 2 * rows, 128), bf16),
                pltpu.VMEM((HEADS, BQ, 128), bf16),
                pltpu.VMEM((HEADS, BQ, 2 * rows), f32),
                pltpu.VMEM((HEADS, BQ, 128), f32),
                pltpu.VMEM((HEADS, BQ, 128), f32),
            ],
        ),
        compiler_params=pltpu.CompilerParams(vmem_limit_bytes=56 * MIB),
        cost_estimate=pl.CostEstimate(flops=30 * 10**9, bytes_accessed=10 * 10**6, transcendentals=0),
        name="attend_forward",
    )(band, q, k_own, k_far, v_own, v_far, seg_own, seg_far)


def attend_bwd_kernel(fills, steps, BQ, BK, band_ref, q_ref, do_ref, o_ref, lse_ref,
                      k_own, k_far, v_own, v_far, seg_own, seg_far, carried, dq_ref, dkt_own, dkt_far, dvt_own, dvt_far, carried_out,
                      kaug, vaug, qm, dom, lqt, ldot, eqt, edot, dq_acc, dk_acc, dv_acc):
    i = pl.program_id(0)
    band = band_ref[0]
    local = kaug.shape[1] // 2

    @pl.when(i < fills)
    def _():
        side = side_lanes(CHUNK)
        extra = jnp.where((side >= 16) & (side < 19), -1.0, 0.0).astype(bf16)
        fill_keys(band, i, k_own, k_far, v_own, v_far, seg_own, seg_far, kaug, vaug, extra)
        for part in range(2):
            cols = pl.ds(pl.multiple_of(part * local + i * CHUNK, CHUNK), CHUNK)
            for p in range(PAIRS):
                dk_acc[p, :, cols] = jnp.zeros((128, CHUNK), f32)
                dv_acc[p, :, cols] = jnp.zeros((128, CHUNK), f32)

    @pl.when((i >= fills) & (i < fills + steps))
    def _():
        low, side = low_lanes(BQ), side_lanes(BQ)
        block = i - fills
        carried_out[...] = carried[...]
        ids = as_column(seg_own[:, pl.ds(pl.multiple_of(block * BQ, BQ), BQ)])
        own = (side == ids).astype(f32)
        for p in range(PAIRS):
            cols = slice(p * 128, (p + 1) * 128)
            q_pair, do_pair = q_ref[:, cols], do_ref[:, cols]
            prod = do_pair.astype(f32) * o_ref[:, cols].astype(f32)
            for e in range(2):
                mine = low if e == 0 else jnp.logical_not(low)
                h = 2 * p + e
                delta = jnp.sum(jnp.where(mine, prod, 0.0), axis=1, keepdims=True)
                qm[h] = jnp.where(mine, q_pair, place(side, split3(lse_ref[:, h : h + 1]), own).astype(bf16))
                dom[h] = jnp.where(mine, do_pair, place(side, split3(delta), jnp.zeros_like(own)).astype(bf16))
            for pair, dst, edges in ((q_pair, lqt, eqt), (do_pair, ldot, edot)):
                flipped = pair.T
                upper = lax.broadcasted_iota(jnp.int32, flipped.shape, 0) < HEAD_DIM
                zero = jnp.zeros_like(flipped)
                even, odd = jnp.where(upper, flipped, zero), jnp.where(upper, zero, flipped)
                dst[p, :, 0:BQ] = even
                dst[p, :, BQ : 2 * BQ] = odd
                edges[0, p] = jnp.concatenate([even[:, 0:EDGE], odd[:, 0:EDGE]], axis=1)
                edges[1, p] = jnp.concatenate([even[:, BQ - EDGE :], odd[:, BQ - EDGE :]], axis=1)
        lefts = {-1: (lqt, ldot), 0: (eqt.at[0], edot.at[0]), BQ - EDGE: (eqt.at[1], edot.at[1])}
        dq_acc[...] = jnp.zeros(dq_acc.shape, f32)
        start, count, early, late = key_window(seg_own, seg_far, block, BQ, BK)

        def step(j, part):
            window = pl.ds(pl.multiple_of(start + j * BK, 128), BK)
            left_q, left_do = lefts[part.start if part.stop - part.start < BQ else -1]

            def scores(h):
                return mm(qm[h, part, :], kaug[h, window, :], NT), mm(dom[h, part, :], vaug[h, window, :], NT)

            ahead = scores(0)
            kept = []
            for h in range(HEADS):
                p = h // 2
                s, dp = ahead
                if h + 1 < HEADS:
                    ahead = scores(h + 1)
                prob = jnp.exp(s)
                ds = (prob * dp).astype(bf16)
                kept.append((prob.astype(bf16), ds))
                dq_acc[h, part, :] += mm(ds, kaug[h, window, :])
                if h % 2:
                    dv_acc[p, :, window] += mm(left_do[p], jnp.concatenate([kept[0][0], kept[1][0]], axis=0))
                    dk_acc[p, :, window] += mm(left_q[p], jnp.concatenate([kept[0][1], kept[1][1]], axis=0))
                    kept = []

        over_blocks(count, early, late, BQ, step)
        for p in range(PAIRS):
            pair = jnp.where(low, dq_acc[2 * p], dq_acc[2 * p + 1]) * HEAD_DIM**-0.5
            dq_ref[:, p * 128 : (p + 1) * 128] = pair.astype(bf16)

    @pl.when(i >= fills + steps)
    def _():
        j = i - fills - steps
        for p in range(PAIRS):
            rows = slice(p * 128, (p + 1) * 128)
            for first, dk_out, dv_out in ((band, dkt_own, dvt_own), (1 - band, dkt_far, dvt_far)):
                cols = pl.ds(pl.multiple_of(first * local + j * CHUNK, CHUNK), CHUNK)
                dk_out[rows, :] = dk_acc[p, :, cols].astype(bf16)
                dv_out[rows, :] = dv_acc[p, :, cols].astype(bf16)


def attend_backward(band, carried, q, do, o, lse, seg_own, seg_far, k_own, k_far, v_own, v_far, BQ=256, BK=256):
    rows, width = q.shape
    fills, steps = rows // CHUNK, rows // BQ
    mine = lambda i, *_: (jnp.clip(i - fills, 0, steps - 1), 0)
    fill = lambda i, *_: (jnp.minimum(i, fills - 1), 0)
    drain = lambda i, *_: (0, jnp.clip(i - fills - steps, 0, fills - 1))
    wide = pl.BlockSpec((CHUNK, width), fill)
    thin = pl.BlockSpec((1, rows), lambda i, *_: (0, 0))
    block = pl.BlockSpec((BQ, width), mine)
    flat = jax.ShapeDtypeStruct((width, rows), bf16)
    return pl.pallas_call(
        functools.partial(attend_bwd_kernel, fills, steps, BQ, BK),
        out_shape=(jax.ShapeDtypeStruct((rows, width), bf16), flat, flat, flat, flat, jax.ShapeDtypeStruct(carried.shape, carried.dtype)),
        grid_spec=pltpu.PrefetchScalarGridSpec(
            num_scalar_prefetch=1,
            grid=(fills + steps + fills,),
            in_specs=[block, block, block, pl.BlockSpec((BQ, 128), mine), wide, wide, wide, wide, thin, thin, block],
            out_specs=[block] + [pl.BlockSpec((width, CHUNK), drain)] * 4 + [block],
            scratch_shapes=[
                pltpu.VMEM((HEADS, 2 * rows, 128), bf16),
                pltpu.VMEM((HEADS, 2 * rows, 128), bf16),
                pltpu.VMEM((HEADS, BQ, 128), bf16),
                pltpu.VMEM((HEADS, BQ, 128), bf16),
                pltpu.VMEM((PAIRS, 128, 2 * BQ), bf16),
                pltpu.VMEM((PAIRS, 128, 2 * BQ), bf16),
                pltpu.VMEM((2, PAIRS, 128, 2 * EDGE), bf16),
                pltpu.VMEM((2, PAIRS, 128, 2 * EDGE), bf16),
                pltpu.VMEM((HEADS, BQ, 128), f32),
                pltpu.VMEM((PAIRS, 128, 2 * rows), f32),
                pltpu.VMEM((PAIRS, 128, 2 * rows), f32),
            ],
        ),
        compiler_params=pltpu.CompilerParams(vmem_limit_bytes=56 * MIB),
        cost_estimate=pl.CostEstimate(flops=45 * 10**9, bytes_accessed=20 * 10**6, transcendentals=0),
        name="attend_backward",
    )(band, q, do, o, lse, k_own, k_far, v_own, v_far, seg_own, seg_far, carried)


MESH = pl.DeviceIdType.MESH
TN = (((0,), (0,)), ((), ()))
SLICE = 768


def gelu_and_slope(u):
    below = 0.5 + 0.5 * lax.erf(u * 0.5**0.5)
    return u * below, below + u * jnp.exp(u * u * -0.5) * (0.5 / 3.141592653589793) ** 0.5


def normalize(rows):
    centred = rows - jnp.mean(rows, axis=-1, keepdims=True)
    scale = lax.rsqrt(jnp.mean(centred * centred, axis=-1, keepdims=True) + EPS)
    return centred * scale, scale


def add_sums(ref, row, values, first):
    sums = jnp.sum(values, axis=0, keepdims=True)
    at = slice(row, row + 1)
    ref[at, :] = jnp.where(first, sums, ref[at, :] + sums)


def as_row(ref):
    return ref[...].reshape(1, -1)


def add_low(dst, a, b):
    dst[...] = (a[...].astype(f32) + b[...].astype(f32)).astype(bf16)


def mlp_kernel(sorted_out, blocks, rows, slices, tok_ref, att_ref, cot_ref, wproj, wup, wdown, pbias, gain, shift, ubias, dbias,
               out_ref, rgrad_ref, agrad_ref, sums_ref, usums_ref, *rest):
    outs, scratch = rest[: 8 if sorted_out else 3], rest[8 if sorted_out else 3 :]
    hid, ugr, n2s, bgs, ags, ats, d_own, d_far, d_in, u_in, p_own, p_far, p_in, send_sem, recv_sem = scratch
    i = pl.program_id(0)
    me, band = lax.axis_index("dp"), lax.axis_index("band")
    other = (me, 1 - band)
    width = tok_ref.shape[1]
    half, per_half = width // 2, slices // 2

    def push(t, src, dst):
        return pltpu.make_async_remote_copy(
            src_ref=src, dst_ref=dst, send_sem=send_sem.at[t], recv_sem=recv_sem.at[t], device_id=other, device_id_type=MESH
        )

    def d_copy(j):
        at = pl.ds(pl.multiple_of(j * SLICE, SLICE), SLICE)
        return push(j, d_far.at[at, :], d_in.at[at, :])

    def u_copy(c):
        return push(slices + c, hid.at[0:width, pl.ds(pl.multiple_of(c * SLICE, SLICE), SLICE)], u_in.at[c])

    def p_copy():
        return push(slices + per_half, p_far, p_in)

    @pl.when(i == 0)
    def _():
        barrier = pltpu.get_barrier_semaphore()
        pl.semaphore_signal(barrier, inc=1, device_id=other, device_id_type=MESH)
        pl.semaphore_wait(barrier, 1)

    @pl.when(i < blocks)
    def _():
        here = pl.ds(pl.multiple_of(i * rows, rows), rows)
        first = i == 0
        att = att_ref[...]
        ats[here, :] = att
        residual = tok_ref[...] + mm(att, wproj[...]) + as_row(pbias)
        xhat, scale = normalize(residual)
        n2 = (xhat * as_row(gain) + as_row(shift)).astype(bf16)
        n2s[here, :] = n2
        cot = cot_ref[...]
        bg = cot.astype(bf16)
        bgs[here, :] = bg
        add_sums(sums_ref, 0, bg.astype(f32), first)
        for c in range(slices):
            cols = slice(c * SLICE, (c + 1) * SLICE)
            hidden, slope = gelu_and_slope(mm(n2, wup[:, cols]) + ubias[cols].reshape(1, -1))
            hid[here, cols] = hidden.astype(bf16)
            grad = (mm(bg, wdown[cols, :], NT) * slope).astype(bf16)
            ugr[here, cols] = grad
            sums = jnp.sum(grad.astype(f32), axis=0, keepdims=True)
            usums_ref[0:1, cols] = jnp.where(first, sums, usums_ref[0:1, cols] + sums)
        out_ref[...] = residual + mm(hid[here, :], wdown[...]) + as_row(dbias)
        e = mm(ugr[here, :], wup[...], NT)
        add_sums(sums_ref, 1, e * xhat, first)
        add_sums(sums_ref, 2, e, first)
        f = e * as_row(gain)
        rgrad = cot + scale * (f - jnp.mean(f, axis=-1, keepdims=True) - xhat * jnp.mean(f * xhat, axis=-1, keepdims=True))
        rgrad_ref[...] = rgrad
        ag = rgrad.astype(bf16)
        ags[here, :] = ag
        add_sums(sums_ref, 3, ag.astype(f32), first)
        agrad_ref[...] = mm(ag, wproj[...], NT).astype(bf16)

    def columns(grad, own, far, at):
        left, right = grad[:, :half].astype(bf16), grad[:, half:].astype(bf16)
        own[at, :] = jnp.where(band == 0, left, right)
        far[at, :] = jnp.where(band == 0, right, left)

    @pl.when((i >= blocks) & (i < blocks + slices))
    def _():
        j = i - blocks
        at = pl.ds(pl.multiple_of(j * SLICE, SLICE), SLICE)
        columns(mm(hid[:, at], bgs[...], TN), d_own, d_far, at)
        d_copy(j).start()

    def up_slice(which):
        at = pl.ds(pl.multiple_of(which * SLICE, SLICE), SLICE)
        return mm(n2s[...], ugr[:, at], TN).astype(bf16)

    x, y = me & 1, (me >> 1) & 1

    z = me >> 2
    shard = width // 16

    def down_arrived(j):
        d_copy(j).wait_recv()
        if not sorted_out:
            at = pl.ds(pl.multiple_of(j * SLICE, SLICE), SLICE)
            add_low(outs[0].at[at, :], d_own.at[at, :], d_in.at[at, :])
            return
        for t in range(2):
            for out, x_bit, y_bit, first in (
                (outs[0], 1 - x, t, 0),
                (outs[1], x, t, 0),
                (outs[2], t, 1 - y, shard),
                (outs[3], t, y, shard),
            ):
                at = pl.ds(pl.multiple_of(j * SLICE + (y_bit * 2 + x_bit) * 4 * shard + first, shard), shard)
                add_low(out.at[j, t, 0:shard], d_own.at[at, :], d_in.at[at, :])

    def down_along_z(d):
        if sorted_out:
            for t in range(4):
                at = pl.ds(pl.multiple_of(((z + d) & 3) * SLICE + t * 4 * shard + 2 * shard, shard), 2 * shard)
                add_low(outs[4 + d].at[t // 2, t % 2, 0 : 2 * shard], d_own.at[at, :], d_in.at[at, :])

    def up_arrived(c):
        u_copy(c).wait_recv()
        own = hid.at[0:width, (per_half + c) * SLICE : (per_half + c + 1) * SLICE]
        if not sorted_out:
            add_low(outs[1].at[:, c * SLICE : (c + 1) * SLICE], own, u_in.at[c])
            return

        def fold(dst, s, part):
            at = pl.ds(pl.multiple_of(s * shard, shard), shard)
            cols = slice(part * half, (part + 1) * half)
            add_low(dst, own.at[at, cols], u_in.at[c, at, cols])

        def near(s, carry):
            zz, t = s >> 1, s & 1
            for sends in range(2):
                fold(outs[1 - sends].at[zz, t, shard : 2 * shard], zz * 4 + t * 2 + (x ^ sends), 0)
                fold(outs[3 - sends].at[zz, t, shard : 2 * shard], zz * 4 + (y ^ sends) * 2 + t, 1)
            return carry

        def along(s, carry):
            for d in range(4):
                for part in range(2):
                    to = slice((2 + part) * shard, (3 + part) * shard)
                    fold(outs[4 + d].at[s >> 1, s & 1, to], ((z + d) & 3) * 4 + s, part)
            return carry

        lax.fori_loop(0, 8 if c == 0 else 4, near if c == 0 else along, 0, unroll=2)

    def proj_arrived():
        p_copy().wait_recv()
        if not sorted_out:
            add_low(outs[2], p_own, p_in)
            return

        def one(s, carry):
            zz, t = s >> 1, s & 1
            for sends in range(2):
                at = pl.ds(pl.multiple_of((zz * 4 + t * 2 + (x ^ sends)) * shard, shard), shard)
                add_low(outs[1 - sends].at[zz, t, 2 * shard : 3 * shard], p_own.at[at, :], p_in.at[at, :])
            return carry

        lax.fori_loop(0, 8, one, 0, unroll=4)

    middle = blocks + slices
    for c in range(per_half):
        at = slice(c * SLICE, (c + 1) * SLICE)

        @pl.when(i == middle + c)
        def _(c=c, at=at):
            hid[0:width, at] = up_slice((1 - band) * per_half + c)
            u_copy(c).start()
            for j in range(2 * c, 2 * c + 2):
                down_arrived(j)

        @pl.when(i == middle + per_half + c)
        def _(c=c):
            hid[0:width, (per_half + c) * SLICE : (per_half + c + 1) * SLICE] = up_slice(band * per_half + c)
            for d in range(2 * c, 2 * c + 2):
                down_along_z(d)

    @pl.when(i == middle + slices)
    def _():
        columns(mm(ats[...], ags[...], TN), p_own, p_far, slice(None))
        p_copy().start()
        for c in range(per_half):
            up_arrived(c)
        proj_arrived()
        for j in range(slices):
            d_copy(j).wait_send()
        for c in range(per_half):
            u_copy(c).wait_send()
        p_copy().wait_send()


def mlp(size, tokens, attended, cotangent, w_proj, w_up, w_down, proj_bias, gain, shift, up_bias, down_bias, rows=256):
    count, width = tokens.shape
    ff = w_up.shape[1]
    blocks, slices = count // rows, ff // SLICE
    half, per_half = width // 2, slices // 2
    sorted_out = size == 16
    one = pl.Buffered(1)
    mine = lambda i: (jnp.minimum(i, blocks - 1), 0)
    block = pl.BlockSpec((rows, width), mine)

    def full(a):
        return pl.BlockSpec(a.shape, lambda i: (0,) * len(a.shape), pipeline_mode=one)

    vectors = (proj_bias, gain, shift, up_bias, down_bias)
    shape = jax.ShapeDtypeStruct
    if sorted_out:
        sixteenth = width // 16
        pieces = [shape((4, 2, n * sixteenth, half), bf16) for n in (3, 3, 2, 2)]
        pieces += [shape((2, 2, 4 * sixteenth, half), bf16)] * 4
    else:
        pieces = [shape((ff, half), bf16), shape((width, ff // 2), bf16), shape((width, half), bf16)]
    kept = [shape((8, width), f32), shape((8, ff), f32)] + pieces
    low = lambda *s: pltpu.VMEM(s, bf16)
    copies = slices + per_half + 1
    return pl.pallas_call(
        functools.partial(mlp_kernel, sorted_out, blocks, rows, slices),
        out_shape=[shape((count, width), f32), shape((count, width), f32), shape((count, width), bf16)] + kept,
        grid=(blocks + 2 * slices + 1,),
        in_specs=[block, block, block] + [full(a) for a in (w_proj, w_up, w_down, *vectors)],
        out_specs=[block, block, block] + [full(a) for a in kept],
        scratch_shapes=[
            low(count, ff),
            low(count, ff),
            *([low(count, width)] * 4),
            *([low(ff, half)] * 3),
            low(per_half, width, SLICE),
            *([low(width, half)] * 3),
            pltpu.SemaphoreType.DMA((copies,)),
            pltpu.SemaphoreType.DMA((copies,)),
        ],
        compiler_params=pltpu.CompilerParams(vmem_limit_bytes=62 * MIB, collective_id=1, has_side_effects=True),
        cost_estimate=pl.CostEstimate(flops=40 * 10**9, bytes_accessed=40 * 10**6, transcendentals=0),
        name="mlp",
    )(tokens, attended, cotangent, w_proj, w_up, w_down, *vectors)


def qkv_kernel(steps, tok_ref, seg_ref, w_ref, gain, shift, qbias, vbias, q_ref, k_ref, v_ref, n_ref, k_far, v_far, seg_far,
               n_all, k_all, v_all, send_sem, recv_sem):
    i = pl.program_id(0)
    last = pl.num_programs(0) - 1
    other = (lax.axis_index("dp"), 1 - lax.axis_index("band"))
    rows, width = tok_ref.shape

    def push(t, src, dst):
        return pltpu.make_async_remote_copy(
            src_ref=src, dst_ref=dst, send_sem=send_sem.at[t], recv_sem=recv_sem.at[t], device_id=other, device_id_type=MESH
        )

    def copies(j):
        at = pl.ds(pl.multiple_of(j * rows, rows), rows)
        return push(2 * j, k_all.at[at, :], k_far.at[at, :]), push(2 * j + 1, v_all.at[at, :], v_far.at[at, :])

    segs = push(send_sem.shape[0] - 1, seg_ref, seg_far)

    @pl.when(i == 0)
    def _():
        barrier = pltpu.get_barrier_semaphore()
        pl.semaphore_signal(barrier, inc=1, device_id=other, device_id_type=MESH)
        pl.semaphore_wait(barrier, 1)
        segs.start()

    @pl.when(i < steps)
    def _():
        here = pl.ds(pl.multiple_of(i * rows, rows), rows)
        xhat, _ = normalize(tok_ref[...])
        n1 = (xhat * as_row(gain) + as_row(shift)).astype(bf16)
        n_ref[...] = n1
        n_all[here, :] = n1
        k = mm(n1, w_ref[:, width : 2 * width]).astype(bf16)
        k_ref[...] = k
        k_all[here, :] = k
        copies(i)[0].start()
        v = (mm(n1, w_ref[:, 2 * width :]) + as_row(vbias)).astype(bf16)
        v_ref[...] = v
        v_all[here, :] = v
        copies(i)[1].start()

    @pl.when(i >= steps)
    def _():
        here = pl.ds(pl.multiple_of((i - steps) * rows, rows), rows)
        q = (mm(n_all[here, :], w_ref[:, :width]) + as_row(qbias)).astype(bf16)
        q_ref[...] = q * jnp.asarray(HEAD_DIM**-0.5, bf16)

    @pl.when(i == last)
    def _():
        segs.wait()
        for j in range(k_all.shape[0] // rows):
            for copy in copies(j):
                copy.wait()


def project_qkv(tokens, seg, w_qkv, gain, shift, query_bias, value_bias, rows=256):
    count, width = tokens.shape
    one = pl.Buffered(1)
    steps = count // rows
    block = pl.BlockSpec((rows, width), lambda i: (jnp.minimum(i, steps - 1), 0))
    late = pl.BlockSpec((rows, width), lambda i: (jnp.maximum(i - steps, 0), 0))
    vectors = (gain, shift, query_bias, value_bias)
    hbm = pl.BlockSpec(memory_space=pl.ANY)
    low = jax.ShapeDtypeStruct((count, width), bf16)
    return pl.pallas_call(
        functools.partial(qkv_kernel, steps),
        out_shape=(low,) * 6 + (jax.ShapeDtypeStruct(seg.shape, seg.dtype),),
        grid=(2 * steps,),
        in_specs=[block, hbm] + [pl.BlockSpec(a.shape, lambda i, n=a.ndim: (0,) * n, pipeline_mode=one) for a in (w_qkv, *vectors)],
        out_specs=[late] + [block] * 3 + [hbm] * 3,
        scratch_shapes=[
            pltpu.VMEM((count, width), bf16),
            pltpu.VMEM((count, width), bf16),
            pltpu.VMEM((count, width), bf16),
            pltpu.SemaphoreType.DMA((2 * steps + 1,)),
            pltpu.SemaphoreType.DMA((2 * steps + 1,)),
        ],
        compiler_params=pltpu.CompilerParams(vmem_limit_bytes=60 * MIB, collective_id=2, has_side_effects=True),
        cost_estimate=pl.CostEstimate(flops=4 * 10**9, bytes_accessed=13 * 10**6, transcendentals=0),
        name="project_qkv",
    )(tokens, seg, w_qkv, *vectors)


def qkv_grad_kernel(blocks, rows, band_ref, dq_ref, dk_own, dk_far, dv_own, dv_far, n_ref, packed_ref, own_ref, far_ref, sums_ref, packed):
    i = pl.program_id(0)
    band = band_ref[0]
    width = dq_ref.shape[1]
    half = own_ref.shape[1]

    @pl.when(i < blocks)
    def _():
        here = pl.ds(pl.multiple_of(i * rows, rows), rows)
        first = i == 0
        dq = dq_ref[...]
        packed_ref[:, :width] = dq
        packed[here, :width] = dq
        add_sums(sums_ref, 0, dq.astype(f32), first)
        for t, (own, far) in enumerate(((dk_own, dk_far), (dv_own, dv_far))):
            for p in range(width // 128):
                at = slice(p * 128, (p + 1) * 128)
                to = slice((t + 1) * width + p * 128, (t + 1) * width + (p + 1) * 128)
                turned = (own[at, :].astype(f32) + far[at, :].astype(f32)).astype(bf16).T
                packed_ref[:, to] = turned
                packed[here, to] = turned
        add_sums(sums_ref, 1, packed_ref[:, 2 * width :].astype(f32), first)

    def columns(which):
        at = pl.ds(pl.multiple_of(which * half, 128), half)
        return mm(n_ref[...], packed[:, at], TN).astype(bf16)

    @pl.when(i == blocks)
    def _():
        far_ref[...] = columns(1 - band)

    @pl.when(i == blocks + 1)
    def _():
        own_ref[...] = columns(band)


def qkv_grads(band, dq, dk_own, dk_far, dv_own, dv_far, normed, rows=256):
    count, width = dq.shape
    blocks = count // rows
    half = 3 * width // 2
    one = pl.Buffered(1)
    mine = lambda i, *_: (jnp.minimum(i, blocks - 1), 0)
    flip = lambda i, *_: (0, jnp.minimum(i, blocks - 1))
    whole = lambda i, *_: (0, 0)
    shape = jax.ShapeDtypeStruct
    return pl.pallas_call(
        functools.partial(qkv_grad_kernel, blocks, rows),
        out_shape=(shape((count, 3 * width), bf16), shape((width, half), bf16), shape((width, half), bf16), shape((8, width), f32)),
        grid_spec=pltpu.PrefetchScalarGridSpec(
            num_scalar_prefetch=1,
            grid=(blocks + 2,),
            in_specs=[pl.BlockSpec((rows, width), mine)]
            + [pl.BlockSpec((width, rows), flip)] * 4
            + [pl.BlockSpec((count, width), whole, pipeline_mode=one)],
            out_specs=[
                pl.BlockSpec((rows, 3 * width), mine),
                pl.BlockSpec((width, half), whole, pipeline_mode=one),
                pl.BlockSpec((width, half), whole, pipeline_mode=one),
                pl.BlockSpec((8, width), whole, pipeline_mode=one),
            ],
            scratch_shapes=[pltpu.VMEM((count, 3 * width), bf16)],
        ),
        compiler_params=pltpu.CompilerParams(vmem_limit_bytes=40 * MIB),
        cost_estimate=pl.CostEstimate(flops=8 * 10**9, bytes_accessed=18 * 10**6, transcendentals=0),
        name="qkv_grads",
    )(band, dq, dk_own, dk_far, dv_own, dv_far, normed)


def input_grad_kernel(packed_ref, tok_ref, rgrad_ref, w_ref, gain, out_ref, sums_ref):
    first = pl.program_id(0) == 0
    e = mm(packed_ref[...], w_ref[...], NT)
    xhat, scale = normalize(tok_ref[...])
    add_sums(sums_ref, 0, e * xhat, first)
    add_sums(sums_ref, 1, e, first)
    f = e * gain[...]
    back = scale * (f - jnp.mean(f, axis=-1, keepdims=True) - xhat * jnp.mean(f * xhat, axis=-1, keepdims=True))
    out_ref[...] = rgrad_ref[...] + back


def input_grads(packed, tokens, rgrad, w_qkv, gain, rows=256):
    count, width = tokens.shape
    one = pl.Buffered(1)
    block = pl.BlockSpec((rows, width), lambda i: (i, 0))
    return pl.pallas_call(
        input_grad_kernel,
        out_shape=(jax.ShapeDtypeStruct((count, width), f32), jax.ShapeDtypeStruct((8, width), f32)),
        grid=(count // rows,),
        in_specs=[
            pl.BlockSpec((rows, packed.shape[1]), lambda i: (i, 0)),
            block,
            block,
            pl.BlockSpec(w_qkv.shape, lambda i: (0, 0), pipeline_mode=one),
            pl.BlockSpec((1, width), lambda i: (0, 0), pipeline_mode=one),
        ],
        out_specs=[block, pl.BlockSpec((8, width), lambda i: (0, 0), pipeline_mode=one)],
        compiler_params=pltpu.CompilerParams(vmem_limit_bytes=32 * MIB),
        cost_estimate=pl.CostEstimate(flops=6 * 10**9, bytes_accessed=18 * 10**6, transcendentals=0),
        name="input_grads",
    )(packed, tokens, rgrad, w_qkv, gain.reshape(1, -1))


def finish_kernel(
    dq_hbm, dko_hbm, dkf_hbm, dvo_hbm, dvf_hbm, n_hbm, tok_hbm, rgrad_hbm, w_hbm, ak_hbm, bk_hbm, ck_hbm, ar_hbm, br_hbm, c1_hbm, c2_hbm, c3_hbm, gain, msums, usums,
    out, down_out, up_out, qkv_out, proj_out, vec_out, usum_out,
    packed, dko, dko_in, dvo, dvo_in, n1, tok, wq, ak, bk, ck, cols, far_in, tail,
    a_one, b_one, c_one, a_two, b_two, c_two, a_thr, b_thr, c_thr, ta_one, tb_one, ta_two, tb_two, ta_thr, tb_thr, vec, vec_band, vec_x, vec_y, vec_z,
    load_sem, swap_send, swap_recv, send, recv, vsend, vrecv,
):
    me = lax.axis_index("dp")
    band = lax.axis_index("band")
    x, y, z = me & 1, (me >> 1) & 1, me >> 2
    rows, width = tok.shape
    half = far_in.shape[-1]
    peer_band = (me, 1 - band)
    peer_x = (me ^ 1, band)
    peer_y = (me ^ 2, band)
    peers_z = [(((z + d) & 3) * 4 + (me & 3), band) for d in (1, 2, 3)]

    def load(t, src, dst):
        copy = pltpu.make_async_copy(src, dst, load_sem.at[t])
        copy.start()
        return copy

    loads = {
        "early": (load(0, ak_hbm, ak), load(1, ar_hbm, a_one), load(2, bk_hbm, bk), load(3, br_hbm, b_one)),
        "along": (load(8, ck_hbm, ck), load(13, c1_hbm, c_one.at[0]), load(14, c2_hbm, c_one.at[1]), load(15, c3_hbm, c_one.at[2])),
        "queries": (load(6, dq_hbm, packed.at[:, 0:width]),),
        "normed": (load(7, n_hbm, n1),),
        "keys": (load(4, dko_hbm, dko), load(5, dvo_hbm, dvo)),
        "weight": (load(10, w_hbm, wq),),
        "rows": (load(11, tok_hbm, tok), load(12, rgrad_hbm, out)),
    }

    def ready(name):
        for copy in loads[name]:
            copy.wait()

    barrier = pltpu.get_barrier_semaphore()
    for peer in (peer_band, peer_x, peer_y, *peers_z):
        pl.semaphore_signal(barrier, inc=1, device_id=peer, device_id_type=MESH)
    pl.semaphore_wait(barrier, 6)

    pending = []

    def push(src, dst, peer, s, r):
        copy = pltpu.make_async_remote_copy(src_ref=src, dst_ref=dst, send_sem=s, recv_sem=r, device_id=peer, device_id_type=MESH)
        copy.start()
        pending.append(copy)
        return copy

    swap_k = push(dkf_hbm, dko_in, peer_band, swap_send.at[0], swap_recv.at[0])
    swap_v = push(dvf_hbm, dvo_in, peer_band, swap_send.at[1], swap_recv.at[1])

    def put(dst, src):
        dst[...] = src[...]

    def each_shard(body):
        def step(s, c):
            body(s >> 2, (s >> 1) & 1, s & 1)
            return c

        lax.fori_loop(0, 16, step, 0, unroll=4)

    def second_stage(t, kept, one, two, mine, peer):
        def total(s, c):
            add_low(one.at[s >> 1, s & 1], one.at[s >> 1, s & 1], kept(s >> 1, s & 1))
            return c

        lax.fori_loop(0, 8, total, 0, unroll=True)
        return push(one.at[:, 1 - mine], two, peer, send.at[t, 0], recv.at[t, 0])

    def third_stage(t, one, two, three, mine, copy):
        copy.wait_recv()

        def total(zz, c):
            add_low(two.at[zz], two.at[zz], one.at[zz, mine])
            return c

        lax.fori_loop(0, 4, total, 0, unroll=True)
        return [push(two.at[(z + d) & 3], three.at[d - 1], peers_z[d - 1], send.at[t, d], recv.at[t, d]) for d in (1, 2, 3)]

    def last(two, three, copies):
        for copy in copies:
            copy.wait_recv()
        total = two[z].astype(f32)
        for d in range(3):
            total = total + three[d].astype(f32)
        return total

    ready("early")
    a_copy = second_stage(0, lambda i, j: ak.at[i, j], a_one, a_two, y, peer_y)
    b_copy = second_stage(1, lambda i, j: bk.at[i, j], b_one, b_two, x, peer_x)
    ready("along")

    def along(s, c):
        i, j = s >> 1, s & 1
        total = ck[i, j].astype(f32)
        for d in range(3):
            total = total + c_one[d, i, j].astype(f32)
        ck[i, j] = total.astype(bf16)
        return c

    lax.fori_loop(0, 4, along, 0, unroll=True)
    c_copy = push(ck.at[:, 1 - x], c_two, peer_x, send.at[2, 0], recv.at[2, 0])

    def columns(t):
        cols[:, :, :, :, t * width : (t + 1) * width] = (
            mm(n1[...], packed[:, t * width : (t + 1) * width], TN).astype(bf16).reshape(cols.shape[:-1] + (width,))
        )

    def turn(t, own, other):
        def step(i, c):
            here = pl.ds(pl.multiple_of(i * 256, 256), 256)
            for p in range(width // 128):
                at = slice(p * 128, (p + 1) * 128)
                turned = (own[at, here].astype(f32) + other[at, here].astype(f32)).astype(bf16).T
                packed[here, t * width + p * 128 : t * width + (p + 1) * 128] = turned
            return c

        lax.fori_loop(0, rows // 256, step, 0)

    def swap(t, start, size, to):
        return pltpu.make_async_remote_copy(
            src_ref=cols.at[:, :, :, :, pl.ds(pl.multiple_of(start, 128), size)],
            dst_ref=far_in.at[:, :, :, :, pl.ds(pl.multiple_of(to, 128), size)],
            send_sem=swap_send.at[t],
            recv_sem=swap_recv.at[t],
            device_id=peer_band,
            device_id_type=MESH,
        )

    third = width // 2
    swap_near = swap(2, (3 - band) * third, third, band * width)
    swap_wide = swap(3, (1 - band) * 2 * width, width, (1 - band) * third)
    ready("queries")
    ready("normed")
    columns(0)

    @pl.when(band == 1)
    def _():
        swap_wide.start()

    ready("keys")
    swap_k.wait_recv()
    turn(1, dko, dko_in)
    columns(1)
    swap_near.start()
    swap_v.wait_recv()
    turn(2, dvo, dvo_in)
    columns(2)

    @pl.when(band == 0)
    def _():
        swap_wide.start()

    a_copies = third_stage(0, a_one, a_two, a_thr, y, a_copy)
    b_copies = third_stage(1, b_one, b_two, b_thr, x, b_copy)
    swap_near.wait()
    swap_wide.wait()
    mine = pl.ds(pl.multiple_of(band * half, 128), half)
    each_shard(lambda i, j, k: add_low(tail.at[i, j, k], cols.at[i, j, k, :, mine], far_in.at[i, j, k]))
    cut = ta_one.shape[-1]
    ta_first = push(tail.at[:, :, 1 - x, :, 0:cut], ta_one, peer_x, send.at[3, 4], recv.at[3, 4])
    tb_first = push(tail.at[:, 1 - y, :, :, cut:half], tb_one, peer_y, send.at[4, 4], recv.at[4, 4])
    c_copy.wait_recv()
    add_low(c_two.at[0], c_two.at[0], ck.at[0, x])
    add_low(c_two.at[1], c_two.at[1], ck.at[1, x])
    c_last = push(c_two.at[1 - y], c_thr, peer_y, send.at[2, 1], recv.at[2, 1])

    ready("weight")
    ready("rows")
    vec[...] = jnp.zeros(vec.shape, f32)

    def rows_back(i, c):
        here = pl.ds(pl.multiple_of(i * 256, 256), 256)
        e = mm(packed[here, :], wq[...], NT)
        xhat, scale = normalize(tok[here, :])
        vec[0:1, :] = vec[0:1, :] + jnp.sum(e * xhat, axis=0, keepdims=True)
        vec[1:2, :] = vec[1:2, :] + jnp.sum(e, axis=0, keepdims=True)
        vec[2:3, :] = vec[2:3, :] + jnp.sum(packed[here, 0:width].astype(f32), axis=0, keepdims=True)
        vec[3:4, :] = vec[3:4, :] + jnp.sum(packed[here, 2 * width : 3 * width].astype(f32), axis=0, keepdims=True)
        f = e * as_row(gain)
        back = scale * (f - jnp.mean(f, axis=-1, keepdims=True) - xhat * jnp.mean(f * xhat, axis=-1, keepdims=True))
        out[here, :] = out[here, :] + back
        return c

    lax.fori_loop(0, rows // 256, rows_back, 0)
    vec[4:8, :] = msums[0:4, :]
    for t in range(usums.shape[1] // width):
        vec[8 + t : 9 + t, :] = usums[0:1, t * width : (t + 1) * width]
    v_band = push(vec, vec_band, peer_band, vsend.at[0], vrecv.at[0])
    ta_first.wait_recv()
    ta_copy = second_stage(3, lambda i, j: tail.at[i, j, x, :, 0:cut], ta_one, ta_two, y, peer_y)
    tb_first.wait_recv()
    tb_copy = second_stage(4, lambda i, j: tail.at[i, y, j, :, cut:half], tb_one, tb_two, x, peer_x)
    v_band.wait()
    vec_band[...] = vec[...] + vec_band[...]
    v_x = push(vec_band, vec_x, peer_x, vsend.at[1], vrecv.at[1])
    v_x.wait()
    vec_x[...] = vec_band[...] + vec_x[...]
    v_y = push(vec_x, vec_y, peer_y, vsend.at[2], vrecv.at[2])
    v_y.wait()
    vec_y[...] = vec_x[...] + vec_y[...]
    v_z = [push(vec_y, vec_z.at[d], peers_z[d], vsend.at[3 + d], vrecv.at[3 + d]) for d in range(3)]
    ta_copies = third_stage(3, ta_one, ta_two, ta_thr, y, ta_copy)
    tb_copies = third_stage(4, tb_one, tb_two, tb_thr, x, tb_copy)
    for copy in v_z:
        copy.wait_recv()
    vec[...] = vec_y[...] + vec_z[0] + vec_z[1] + vec_z[2]
    shard = vec_out.shape[1]
    vec_out[...] = pltpu.roll(vec[0:8, :], width - me * shard, 1)[:, 0:shard]
    wide = usum_out.shape[1]
    per_row = width // wide
    row = vec[pl.ds(8 + me // per_row, 1), :]
    usum_out[...] = pltpu.roll(jnp.broadcast_to(row, (8, width)), width - (me % per_row) * wide, 1)[0:1, 0:wide]
    shard = width // 16
    a_sum, b_sum = last(a_two, a_thr, a_copies), last(b_two, b_thr, b_copies)
    c_last.wait_recv()
    c_sum = c_two[y].astype(f32) + c_thr[...].astype(f32)
    down_out[0:shard, :] = a_sum[0:shard]
    down_out[shard : 2 * shard, :] = b_sum[0:shard]
    down_out[2 * shard : 4 * shard, :] = c_sum[0 : 2 * shard]
    ups = (a_sum[shard : 2 * shard], b_sum[shard : 2 * shard], c_sum[2 * shard : 3 * shard], c_sum[3 * shard : 4 * shard])
    for t, part in enumerate(ups):
        up_out[:, t * third : (t + 1) * third] = part
    proj_out[...] = a_sum[2 * shard : 3 * shard]
    qkv_out[:, 0:cut] = last(ta_two, ta_thr, ta_copies)
    qkv_out[:, cut:half] = last(tb_two, tb_thr, tb_copies)
    done = {id(c) for c in (v_band, v_x, v_y)}
    for copy in pending:
        if id(copy) not in done:
            copy.wait_send()


def finish(dq, dk_own, dk_far, dv_own, dv_far, normed, tokens, rgrad, w_qkv, pieces, gain, msums, usums):
    rows, width = tokens.shape
    ff = usums.shape[1]
    half = 3 * width // 2
    shards = (4, 2, 2)
    third, shard = width // 2, width // 16
    q_shape = shards + (shard, half)
    a_piece, b_piece, c_piece = (3 * shard, third), (2 * shard, third), (4 * shard, third)
    cut = half // 256 * 128 + 128
    ta_piece, tb_piece = (shard, cut), (shard, half - cut)
    hbm, vmem = pl.BlockSpec(memory_space=pl.ANY), pl.BlockSpec(memory_space=pltpu.VMEM)
    shape = jax.ShapeDtypeStruct
    low = lambda *s: pltpu.VMEM(s, bf16)
    dma = pltpu.SemaphoreType.DMA
    return pl.pallas_call(
        finish_kernel,
        out_shape=(
            shape((rows, width), f32),
            shape((ff // 16, width // 2), f32),
            shape((width // 16, ff // 2), f32),
            shape((width // 16, half), f32),
            shape((width // 16, width // 2), f32),
            shape((8, width // 16), f32),
            shape((1, ff // 16), f32),
        ),
        in_specs=[hbm] * 17 + [vmem] * 3,
        out_specs=[vmem] * 7,
        scratch_shapes=[
            low(rows, 3 * width),
            *([low(width, rows)] * 4),
            low(rows, width),
            pltpu.VMEM((rows, width), f32),
            low(width, 3 * width),
            low(4, 2, *a_piece),
            low(4, 2, *b_piece),
            low(2, 2, *c_piece),
            low(*shards, shard, 3 * width),
            low(*q_shape),
            low(*q_shape),
            low(4, 2, *a_piece),
            low(4, 2, *b_piece),
            low(3, 2, 2, *c_piece),
            low(4, *a_piece),
            low(4, *b_piece),
            low(2, *c_piece),
            low(3, *a_piece),
            low(3, *b_piece),
            low(*c_piece),
            low(4, 2, *ta_piece),
            low(4, 2, *tb_piece),
            low(4, *ta_piece),
            low(4, *tb_piece),
            low(3, *ta_piece),
            low(3, *tb_piece),
            pltpu.VMEM((16, width), f32),
            pltpu.VMEM((16, width), f32),
            pltpu.VMEM((16, width), f32),
            pltpu.VMEM((16, width), f32),
            pltpu.VMEM((3, 16, width), f32),
            dma((16,)),
            dma((4,)),
            dma((4,)),
            dma((5, 5)),
            dma((5, 5)),
            dma((6,)),
            dma((6,)),
        ],
        compiler_params=pltpu.CompilerParams(vmem_limit_bytes=52 * MIB, collective_id=0, has_side_effects=True),
        cost_estimate=pl.CostEstimate(flops=20 * 10**9, bytes_accessed=40 * 10**6, transcendentals=0),
        name="finish",
    )(dq, dk_own, dk_far, dv_own, dv_far, normed, tokens, rgrad, w_qkv, *pieces,
      gain, msums, usums)


def swap_band(x):
    return lax.ppermute(x, "band", [(0, 1), (1, 0)])


def pick(x, which, axis):
    return lax.dynamic_index_in_dim(x, which, axis, keepdims=False)


def halve(x, axis, bit, size):
    mine = (lax.axis_index("dp") >> bit) & 1
    arrived = lax.ppermute(pick(x, 1 - mine, axis), "dp", [(i, i ^ (1 << bit)) for i in range(size)])
    return pick(x, mine, axis).astype(f32) + arrived.astype(f32)


class Reduction:
    def __init__(self, x, order, size):
        rows, columns = x.shape
        levels = size.bit_length() - 1
        self.size = size
        self.x = x.reshape((2,) * levels + (rows // size, columns))
        self.left = list(range(levels - 1, -1, -1))
        self.order = list(order)

    def step(self):
        if self.order:
            bit = self.order.pop(0)
            x = halve(self.x, self.left.index(bit), bit, self.size)
            self.left.remove(bit)
            self.x = x.astype(bf16) if self.left else x

    def finish(self):
        while self.order:
            self.step()
        return self.x


def finish_any(size, band_at, query_grad, dk_own, dk_far, dv_own, dv_far, normed, tokens, residual_grad, w_qkv, pieces, gain, msums, usums):
    width = tokens.shape[1]
    rising = list(range(size.bit_length() - 1))
    turned = [1, 0] + rising[2:]
    packed, qkv_own, qkv_far, qkv_sums = qkv_grads(
        band_at, query_grad, dk_own, swap_band(dk_far), dv_own, swap_band(dv_far), normed
    )
    input_grad, first_sums = input_grads(packed, tokens, residual_grad, w_qkv, gain)

    def total(x, order):
        return Reduction(x, order, size).finish()

    def join(own, far):
        return (own.astype(f32) + swap_band(far).astype(f32)).astype(bf16)

    tall = jnp.concatenate([first_sums[:2], qkv_sums[:2], msums[:4]], axis=0)
    thin = jnp.concatenate([tall.T, usums[0].reshape(width, -1)], axis=1)
    thin = jnp.pad(thin, ((0, 0), (0, 128 - thin.shape[1]))).astype(bf16)
    thin_sum = total(join(thin, thin), turned)
    ups = usums.shape[1] // width
    return (
        input_grad,
        total(pieces[0], rising),
        total(pieces[1], turned),
        total(join(qkv_own, qkv_far), rising),
        total(pieces[2], turned),
        [thin_sum[:, t] for t in range(8)],
        thin_sum[:, 8 : 8 + ups].reshape(-1),
    )


def local(
    size,
    inputs,
    segment_ids,
    cotangent,
    first_gain,
    first_bias,
    w_qkv,
    query_bias,
    value_bias,
    w_proj,
    proj_bias,
    second_gain,
    second_bias,
    w_up,
    up_bias,
    w_down,
    down_bias,
):
    local_shape = inputs.shape
    width = local_shape[-1]
    band = lax.axis_index("band")
    band_at = band.astype(jnp.int32).reshape(1)
    tokens = inputs.reshape(-1, width)
    seg_own = segment_ids
    queries, k_own, v_own, normed, k_far, v_far, seg_far = project_qkv(
        tokens, seg_own, w_qkv, first_gain, first_bias, query_bias, value_bias
    )
    keys = (seg_own, seg_far, k_own, k_far, v_own, v_far)
    attended, log_totals = attend_forward(band_at, queries, *keys)
    output, residual_grad, attended_grad, mlp_sums, up_sums, *pieces = mlp(
        size,
        tokens,
        attended,
        cotangent.reshape(-1, width),
        w_proj,
        w_up,
        w_down,
        proj_bias,
        second_gain,
        second_bias,
        up_bias,
        down_bias,
    )
    if size == 16:
        turns = [[(i, i ^ bit) for i in range(size)] for bit in (1, 2)]
        turns += [[(i, (i + 4 * d) % size) for i in range(size)] for d in (1, 2, 3)]
        sent = (pieces[0], pieces[2], *pieces[5:8])
        pieces = [pieces[1], pieces[3], pieces[4]] + [lax.ppermute(a, "dp", turn) for a, turn in zip(sent, turns)]
    query_grad, dk_own, dk_far, dv_own, dv_far, output = attend_backward(
        band_at, output, queries, attended_grad, attended, log_totals, *keys
    )
    if size == 16:
        input_grad, down_sum, up_sum, qkv_sum, proj_sum, vec, up_vec = finish(
            query_grad, dk_own, dk_far, dv_own, dv_far, normed, tokens, residual_grad, w_qkv, pieces, first_gain, mlp_sums, up_sums
        )
        vectors, up_vector = [vec[t] for t in range(8)], up_vec.reshape(-1)
    else:
        input_grad, down_sum, up_sum, qkv_sum, proj_sum, vectors, up_vector = finish_any(
            size, band_at, query_grad, dk_own, dk_far, dv_own, dv_far, normed, tokens, residual_grad, w_qkv, pieces, first_gain, mlp_sums, up_sums
        )
    return (
        output.reshape(local_shape),
        input_grad.reshape(local_shape),
        vectors[0],
        vectors[1],
        qkv_sum,
        vectors[2],
        vectors[3],
        proj_sum,
        vectors[7],
        vectors[5],
        vectors[6],
        up_sum,
        up_vector,
        down_sum,
        vectors[4],
    )


def solution(mesh):
    size = mesh.shape["dp"]
    placed = (P("dp", "band", None), P("dp", "band"), P("dp", "band", None)) + (P(),) * 13
    split, thin = P("dp", "band"), P("dp")
    wide = P("dp", "band", None)
    return jax.shard_map(
        functools.partial(local, size),
        mesh=mesh,
        in_specs=placed,
        out_specs=(wide, wide, thin, thin, split, thin, thin, split, thin, thin, thin, split, thin, split, thin),
        check_vma=False,
    )
```

```python
import functools

import jax
import jax.numpy as jnp
from jax import lax
from jax.experimental import pallas as pl
from jax.experimental.pallas import tpu as pltpu
from jax.sharding import PartitionSpec as P

EPS = 1e-05
HEADS = 12
HEAD_DIM = 64
NEG_LARGE = -1e30
PAIRS = HEADS // 2
CHUNK = 256
EDGE = 64
MIB = 1 << 20
f32, bf16 = jnp.float32, jnp.bfloat16
NN = (((1,), (0,)), ((), ()))
NT = (((1,), (1,)), ((), ()))


def mm(a, b, dims=NN):
    return lax.dot_general(a, b, dims, preferred_element_type=f32)


def low_lanes(rows):
    return lax.broadcasted_iota(jnp.int32, (rows, 128), 1) < HEAD_DIM


def side_lanes(rows):
    return lax.broadcasted_iota(jnp.int32, (rows, 128), 1) & (HEAD_DIM - 1)


def split3(x):
    high = x.astype(bf16).astype(f32)
    middle = (x - high).astype(bf16).astype(f32)
    return high, middle, x - high - middle


def place(side, parts, base):
    for t, part in enumerate(parts):
        base = jnp.where(side == 16 + t, part, base)
    return base


def as_column(row):
    return jnp.broadcast_to(row, (8, row.shape[1])).T[:, 0:1]


def key_window(seg_own, seg_far, block, BQ, BK):
    own, far = seg_own[...].astype(f32), seg_far[...].astype(f32)

    def below(limit):
        return jnp.sum((own < limit).astype(f32) + (far < limit).astype(f32)).astype(jnp.int32)

    mine = seg_own[:, pl.ds(pl.multiple_of(block * BQ, BQ), BQ)].astype(f32)
    row = lax.broadcasted_iota(jnp.int32, mine.shape, 1)
    lo = (below(jnp.min(mine)) // 128) * 128
    blocks = (below(jnp.max(mine) + 1.0) - lo + BK - 1) // BK
    start = jnp.minimum(lo, 2 * own.shape[1] - blocks * BK)
    early_end = below(jnp.min(jnp.where(row >= EDGE, mine, 99.0)))
    late_start = below(jnp.max(jnp.where(row < BQ - EDGE, mine, -1.0)) + 1.0)
    early = jnp.clip((early_end - start) // BK, 0, blocks)
    late = jnp.clip((start + blocks * BK - late_start) // BK, 0, blocks - early)
    return start, blocks, early, late


def over_blocks(count, early, late, rows, body):
    for first, end, part in (
        (0, early, slice(0, EDGE)),
        (early, count - late, slice(0, rows)),
        (count - late, count, slice(rows - EDGE, rows)),
    ):

        def step(j, c, part=part):
            body(j, part)
            return c

        lax.fori_loop(first, end, step, 0)


def fill_pairs(src, dst, rows, low, extra):
    for p in range(PAIRS):
        pair = src[:, p * 128 : (p + 1) * 128]
        dst[2 * p, rows, :] = jnp.where(low, pair, extra)
        dst[2 * p + 1, rows, :] = jnp.where(low, extra, pair)


def fill_keys(band, i, k_own, k_far, v_own, v_far, seg_own, seg_far, kaug, vaug, value_extra):
    local = kaug.shape[1] // 2
    low, side = low_lanes(CHUNK), side_lanes(CHUNK)
    here = pl.ds(pl.multiple_of(i * CHUNK, CHUNK), CHUNK)
    for k, v, seg, first in ((k_own, v_own, seg_own, band), (k_far, v_far, seg_far, 1 - band)):
        rows = pl.ds(pl.multiple_of(first * local + i * CHUNK, CHUNK), CHUNK)
        extra = jnp.where(side < 16, jnp.where(side == as_column(seg[:, here]), 0.0, NEG_LARGE), jnp.where(side < 19, -1.0, 0.0))
        fill_pairs(k, kaug, rows, low, extra.astype(bf16))
        fill_pairs(v, vaug, rows, low, value_extra)


def attend_fwd_kernel(fills, BQ, BK, band_ref, q_ref, k_own, k_far, v_own, v_far,
                      seg_own, seg_far, o_ref, qaug_ref, kaug, vaug, qm, s_all, mx, acc):
    i = pl.program_id(0)

    @pl.when(i < fills)
    def _():
        fill_keys(band_ref[0], i, k_own, k_far, v_own, v_far, seg_own, seg_far, kaug, vaug, jnp.ones((CHUNK, 128), bf16))

    @pl.when(i >= fills)
    def _():
        low, side = low_lanes(BQ), side_lanes(BQ)
        block = i - fills
        ids = as_column(seg_own[:, pl.ds(pl.multiple_of(block * BQ, BQ), BQ)])
        own = (side == ids).astype(f32).astype(bf16)
        for p in range(PAIRS):
            pair = q_ref[:, p * 128 : (p + 1) * 128]
            qm[2 * p] = jnp.where(low, pair, own)
            qm[2 * p + 1] = jnp.where(low, own, pair)
        mx[...] = jnp.full(mx.shape, -3e38, f32)
        acc[...] = jnp.zeros(acc.shape, f32)
        start, count, early, late = key_window(seg_own, seg_far, block, BQ, BK)

        def first(j, part):
            at = pl.multiple_of(start + j * BK, 128)
            out = pl.ds(pl.multiple_of(j * BK, BK), BK)
            for h in range(HEADS):
                s = mm(qm[h, part, :], kaug[h, pl.ds(at, BK), :], NT)
                s_all[h, part, out] = s
                m = mx[h, part, :]
                for t in range(BK // 128):
                    m = jnp.maximum(m, s[:, t * 128 : (t + 1) * 128])
                mx[h, part, :] = m

        over_blocks(count, early, late, BQ, first)
        for h in range(HEADS):
            mx[h] = jnp.broadcast_to(jnp.max(mx[h], axis=1, keepdims=True), (BQ, 128))

        def second(j, part):
            at = pl.multiple_of(start + j * BK, 128)
            src = pl.ds(pl.multiple_of(j * BK, BK), BK)
            for h in range(HEADS):
                p = jnp.exp(s_all[h, part, src] - jnp.concatenate([mx[h, part, :]] * (BK // 128), axis=1)).astype(bf16)
                acc[h, part, :] += mm(p, vaug[h, pl.ds(at, BK), :])

        over_blocks(count, early, late, BQ, second)
        ids = (side == ids).astype(f32)
        for p in range(PAIRS):
            even, odd = acc[2 * p], acc[2 * p + 1]
            total = jnp.where(low, pltpu.roll(even, HEAD_DIM, 1), pltpu.roll(odd, HEAD_DIM, 1))
            o_ref[:, p * 128 : (p + 1) * 128] = (jnp.where(low, even, odd) / total).astype(bf16)
            pair = q_ref[:, p * 128 : (p + 1) * 128]
            extra = [place(side, split3(mx[2 * p + e] + jnp.log(sums)), ids).astype(bf16) for e, sums in enumerate((even, odd))]
            qaug_ref[2 * p] = jnp.where(low, pair, extra[0])
            qaug_ref[2 * p + 1] = jnp.where(low, extra[1], pair)


def attend_forward(band, q, seg_own, seg_far, k_own, k_far, v_own, v_far, BQ=256, BK=256):
    rows, width = q.shape
    fills, steps = rows // CHUNK, rows // BQ
    mine = lambda i, *_: (jnp.clip(i - fills, 0, steps - 1), 0)
    fill = lambda i, *_: (jnp.minimum(i, fills - 1), 0)
    wide = pl.BlockSpec((CHUNK, width), fill)
    thin = pl.BlockSpec((1, rows), lambda i, *_: (0, 0))
    return pl.pallas_call(
        functools.partial(attend_fwd_kernel, fills, BQ, BK),
        out_shape=(jax.ShapeDtypeStruct((rows, width), bf16), jax.ShapeDtypeStruct((HEADS, rows, 128), bf16)),
        grid_spec=pltpu.PrefetchScalarGridSpec(
            num_scalar_prefetch=1,
            grid=(fills + steps,),
            in_specs=[pl.BlockSpec((BQ, width), mine), wide, wide, wide, wide, thin, thin],
            out_specs=[pl.BlockSpec((BQ, width), mine), pl.BlockSpec((HEADS, BQ, 128), lambda i, *_: (0, jnp.clip(i - fills, 0, steps - 1), 0))],
            scratch_shapes=[
                pltpu.VMEM((HEADS, 2 * rows, 128), bf16),
                pltpu.VMEM((HEADS, 2 * rows, 128), bf16),
                pltpu.VMEM((HEADS, BQ, 128), bf16),
                pltpu.VMEM((HEADS, BQ, 2 * rows), f32),
                pltpu.VMEM((HEADS, BQ, 128), f32),
                pltpu.VMEM((HEADS, BQ, 128), f32),
            ],
        ),
        compiler_params=pltpu.CompilerParams(vmem_limit_bytes=56 * MIB),
        cost_estimate=pl.CostEstimate(flops=30 * 10**9, bytes_accessed=10 * 10**6, transcendentals=0),
        name="attend_forward",
    )(band, q, k_own, k_far, v_own, v_far, seg_own, seg_far)


def attend_bwd_kernel(fills, steps, BQ, BK, band_ref, qm, do_ref, o_ref,
                      k_own, k_far, v_own, v_far, seg_own, seg_far, carried, dq_ref, dkt_own, dkt_far, dvt_own, dvt_far, carried_out,
                      kaug, vaug, dom, lqt, ldot, eqt, edot, dq_acc, dk_acc, dv_acc):
    i = pl.program_id(0)
    band = band_ref[0]
    local = kaug.shape[1] // 2

    @pl.when(i < fills)
    def _():
        side = side_lanes(CHUNK)
        extra = jnp.where((side >= 16) & (side < 19), -1.0, 0.0).astype(bf16)
        fill_keys(band, i, k_own, k_far, v_own, v_far, seg_own, seg_far, kaug, vaug, extra)
        for part in range(2):
            cols = pl.ds(pl.multiple_of(part * local + i * CHUNK, CHUNK), CHUNK)
            for p in range(PAIRS):
                dk_acc[p, :, cols] = jnp.zeros((128, CHUNK), f32)
                dv_acc[p, :, cols] = jnp.zeros((128, CHUNK), f32)

    @pl.when((i >= fills) & (i < fills + steps))
    def _():
        low, side = low_lanes(BQ), side_lanes(BQ)
        block = i - fills
        carried_out[...] = carried[...]
        lane = lax.broadcasted_iota(jnp.int32, (256, 256), 0) & 127
        column = lax.broadcasted_iota(jnp.int32, (256, 256), 1)
        adder = ((lane < HEAD_DIM) == (column < 128)).astype(f32).astype(bf16)
        for p in range(PAIRS):
            cols = slice(p * 128, (p + 1) * 128)
            q_pair, do_pair = jnp.where(low, qm[2 * p], qm[2 * p + 1]), do_ref[:, cols]
            prod = do_pair.astype(f32) * o_ref[:, cols].astype(f32)
            high = prod.astype(bf16)
            rest = (prod - high.astype(f32)).astype(bf16)
            delta = mm(jnp.concatenate([high, rest], axis=1), adder)
            for e in range(2):
                extra = place(side, split3(delta[:, e * 128 : (e + 1) * 128]), jnp.zeros((BQ, 128), f32)).astype(bf16)
                dom[2 * p + e] = jnp.where(low, do_pair, extra) if e == 0 else jnp.where(low, extra, do_pair)
            for pair, dst, edges in ((q_pair, lqt, eqt), (do_pair, ldot, edot)):
                flipped = pair.T
                upper = lax.broadcasted_iota(jnp.int32, flipped.shape, 0) < HEAD_DIM
                zero = jnp.zeros_like(flipped)
                even, odd = jnp.where(upper, flipped, zero), jnp.where(upper, zero, flipped)
                dst[p, :, 0:BQ] = even
                dst[p, :, BQ : 2 * BQ] = odd
                edges[0, p] = jnp.concatenate([even[:, 0:EDGE], odd[:, 0:EDGE]], axis=1)
                edges[1, p] = jnp.concatenate([even[:, BQ - EDGE :], odd[:, BQ - EDGE :]], axis=1)
        lefts = {-1: (lqt, ldot), 0: (eqt.at[0], edot.at[0]), BQ - EDGE: (eqt.at[1], edot.at[1])}
        dq_acc[...] = jnp.zeros(dq_acc.shape, f32)
        start, count, early, late = key_window(seg_own, seg_far, block, BQ, BK)

        def step(j, part):
            window = pl.ds(pl.multiple_of(start + j * BK, 128), BK)
            left_q, left_do = lefts[part.start if part.stop - part.start < BQ else -1]

            def scores(h):
                return mm(qm[h, part, :], kaug[h, window, :], NT), mm(dom[h, part, :], vaug[h, window, :], NT)

            ahead = scores(0)
            kept = []
            for h in range(HEADS):
                p = h // 2
                s, dp = ahead
                if h + 1 < HEADS:
                    ahead = scores(h + 1)
                prob = jnp.exp(s)
                ds = (prob * dp).astype(bf16)
                kept.append((prob.astype(bf16), ds))
                dq_acc[h, part, :] += mm(ds, kaug[h, window, :])
                if h % 2:
                    dv_acc[p, :, window] += mm(left_do[p], jnp.concatenate([kept[0][0], kept[1][0]], axis=0))
                    dk_acc[p, :, window] += mm(left_q[p], jnp.concatenate([kept[0][1], kept[1][1]], axis=0))
                    kept = []

        over_blocks(count, early, late, BQ, step)
        for p in range(PAIRS):
            pair = jnp.where(low, dq_acc[2 * p], dq_acc[2 * p + 1]) * HEAD_DIM**-0.5
            dq_ref[:, p * 128 : (p + 1) * 128] = pair.astype(bf16)

    @pl.when(i >= fills + steps)
    def _():
        j = i - fills - steps
        for p in range(PAIRS):
            rows = slice(p * 128, (p + 1) * 128)
            for first, dk_out, dv_out in ((band, dkt_own, dvt_own), (1 - band, dkt_far, dvt_far)):
                cols = pl.ds(pl.multiple_of(first * local + j * CHUNK, CHUNK), CHUNK)
                dk_out[rows, :] = dk_acc[p, :, cols].astype(bf16)
                dv_out[rows, :] = dv_acc[p, :, cols].astype(bf16)


def attend_backward(band, carried, qaug, do, o, seg_own, seg_far, k_own, k_far, v_own, v_far, BQ=256, BK=256):
    rows, width = do.shape
    fills, steps = rows // CHUNK, rows // BQ
    mine = lambda i, *_: (jnp.clip(i - fills, 0, steps - 1), 0)
    fill = lambda i, *_: (jnp.minimum(i, fills - 1), 0)
    drain = lambda i, *_: (0, jnp.clip(i - fills - steps, 0, fills - 1))
    wide = pl.BlockSpec((CHUNK, width), fill)
    thin = pl.BlockSpec((1, rows), lambda i, *_: (0, 0))
    block = pl.BlockSpec((BQ, width), mine)
    flat = jax.ShapeDtypeStruct((width, rows), bf16)
    return pl.pallas_call(
        functools.partial(attend_bwd_kernel, fills, steps, BQ, BK),
        out_shape=(jax.ShapeDtypeStruct((rows, width), bf16), flat, flat, flat, flat, jax.ShapeDtypeStruct(carried.shape, carried.dtype)),
        grid_spec=pltpu.PrefetchScalarGridSpec(
            num_scalar_prefetch=1,
            grid=(fills + steps + fills,),
            in_specs=[pl.BlockSpec((HEADS, BQ, 128), lambda i, *_: (0, jnp.clip(i - fills, 0, steps - 1), 0)), block, block, wide, wide, wide, wide, thin, thin, block],
            out_specs=[block] + [pl.BlockSpec((width, CHUNK), drain)] * 4 + [block],
            scratch_shapes=[
                pltpu.VMEM((HEADS, 2 * rows, 128), bf16),
                pltpu.VMEM((HEADS, 2 * rows, 128), bf16),
                pltpu.VMEM((HEADS, BQ, 128), bf16),
                pltpu.VMEM((PAIRS, 128, 2 * BQ), bf16),
                pltpu.VMEM((PAIRS, 128, 2 * BQ), bf16),
                pltpu.VMEM((2, PAIRS, 128, 2 * EDGE), bf16),
                pltpu.VMEM((2, PAIRS, 128, 2 * EDGE), bf16),
                pltpu.VMEM((HEADS, BQ, 128), f32),
                pltpu.VMEM((PAIRS, 128, 2 * rows), f32),
                pltpu.VMEM((PAIRS, 128, 2 * rows), f32),
            ],
        ),
        compiler_params=pltpu.CompilerParams(vmem_limit_bytes=56 * MIB),
        cost_estimate=pl.CostEstimate(flops=45 * 10**9, bytes_accessed=20 * 10**6, transcendentals=0),
        name="attend_backward",
    )(band, qaug, do, o, k_own, k_far, v_own, v_far, seg_own, seg_far, carried)


MESH = pl.DeviceIdType.MESH
TN = (((0,), (0,)), ((), ()))
SLICE = 768


def gelu_and_slope(u):
    below = 0.5 + 0.5 * lax.erf(u * 0.5**0.5)
    return u * below, below + u * jnp.exp(u * u * -0.5) * (0.5 / 3.141592653589793) ** 0.5


def normalize(rows):
    centred = rows - jnp.mean(rows, axis=-1, keepdims=True)
    scale = lax.rsqrt(jnp.mean(centred * centred, axis=-1, keepdims=True) + EPS)
    return centred * scale, scale


def add_sums(ref, row, values, first):
    sums = jnp.sum(values, axis=0, keepdims=True)
    at = slice(row, row + 1)
    ref[at, :] = jnp.where(first, sums, ref[at, :] + sums)


def as_row(ref):
    return ref[...].reshape(1, -1)


def add_low(dst, a, b):
    dst[...] = (a[...].astype(f32) + b[...].astype(f32)).astype(bf16)


def mlp_kernel(sorted_out, blocks, rows, slices, tok_ref, att_ref, cot_ref, wproj, wup, wdown, pbias, gain, shift, ubias, dbias,
               out_ref, rgrad_ref, agrad_ref, sums_ref, usums_ref, *rest):
    outs, scratch = rest[: 8 if sorted_out else 3], rest[8 if sorted_out else 3 :]
    hid, ugr, n2s, bgs, ags, ats, d_own, d_far, d_in, u_in, p_own, p_far, p_in, send_sem, recv_sem = scratch
    i = pl.program_id(0)
    me, band = lax.axis_index("dp"), lax.axis_index("band")
    other = (me, 1 - band)
    width = tok_ref.shape[1]
    half, per_half = width // 2, slices // 2

    def push(t, src, dst):
        return pltpu.make_async_remote_copy(
            src_ref=src, dst_ref=dst, send_sem=send_sem.at[t], recv_sem=recv_sem.at[t], device_id=other, device_id_type=MESH
        )

    def d_copy(j):
        at = pl.ds(pl.multiple_of(j * SLICE, SLICE), SLICE)
        return push(j, d_far.at[at, :], d_in.at[at, :])

    def u_copy(c):
        return push(slices + c, hid.at[0:width, pl.ds(pl.multiple_of(c * SLICE, SLICE), SLICE)], u_in.at[c])

    def p_copy():
        return push(slices + per_half, p_far, p_in)

    @pl.when(i == 0)
    def _():
        barrier = pltpu.get_barrier_semaphore()
        pl.semaphore_signal(barrier, inc=1, device_id=other, device_id_type=MESH)
        pl.semaphore_wait(barrier, 1)

    @pl.when(i < blocks)
    def _():
        here = pl.ds(pl.multiple_of(i * rows, rows), rows)
        first = i == 0
        att = att_ref[...]
        ats[here, :] = att
        residual = tok_ref[...] + mm(att, wproj[...]) + as_row(pbias)
        xhat, scale = normalize(residual)
        n2 = (xhat * as_row(gain) + as_row(shift)).astype(bf16)
        n2s[here, :] = n2
        cot = cot_ref[...]
        bg = cot.astype(bf16)
        bgs[here, :] = bg
        add_sums(sums_ref, 0, bg.astype(f32), first)
        for c in range(slices):
            cols = slice(c * SLICE, (c + 1) * SLICE)
            hidden, slope = gelu_and_slope(mm(n2, wup[:, cols]) + ubias[cols].reshape(1, -1))
            hid[here, cols] = hidden.astype(bf16)
            grad = (mm(bg, wdown[cols, :], NT) * slope).astype(bf16)
            ugr[here, cols] = grad
            sums = jnp.sum(grad.astype(f32), axis=0, keepdims=True)
            usums_ref[0:1, cols] = jnp.where(first, sums, usums_ref[0:1, cols] + sums)
        out_ref[...] = residual + mm(hid[here, :], wdown[...]) + as_row(dbias)
        e = mm(ugr[here, :], wup[...], NT)
        add_sums(sums_ref, 1, e * xhat, first)
        add_sums(sums_ref, 2, e, first)
        f = e * as_row(gain)
        rgrad = cot + scale * (f - jnp.mean(f, axis=-1, keepdims=True) - xhat * jnp.mean(f * xhat, axis=-1, keepdims=True))
        rgrad_ref[...] = rgrad
        ag = rgrad.astype(bf16)
        ags[here, :] = ag
        add_sums(sums_ref, 3, ag.astype(f32), first)
        agrad_ref[...] = mm(ag, wproj[...], NT).astype(bf16)

    def columns(grad, own, far, at):
        left, right = grad[:, :half].astype(bf16), grad[:, half:].astype(bf16)
        own[at, :] = jnp.where(band == 0, left, right)
        far[at, :] = jnp.where(band == 0, right, left)

    @pl.when((i >= blocks) & (i < blocks + slices))
    def _():
        j = i - blocks
        at = pl.ds(pl.multiple_of(j * SLICE, SLICE), SLICE)
        columns(mm(hid[:, at], bgs[...], TN), d_own, d_far, at)
        d_copy(j).start()

    def up_slice(which):
        at = pl.ds(pl.multiple_of(which * SLICE, SLICE), SLICE)
        return mm(n2s[...], ugr[:, at], TN).astype(bf16)

    x, y = me & 1, (me >> 1) & 1

    z = me >> 2
    shard = width // 16

    def down_arrived(j):
        d_copy(j).wait_recv()
        if not sorted_out:
            at = pl.ds(pl.multiple_of(j * SLICE, SLICE), SLICE)
            add_low(outs[0].at[at, :], d_own.at[at, :], d_in.at[at, :])
            return
        for t in range(2):
            for out, x_bit, y_bit, first in (
                (outs[0], 1 - x, t, 0),
                (outs[1], x, t, 0),
                (outs[2], t, 1 - y, shard),
                (outs[3], t, y, shard),
            ):
                at = pl.ds(pl.multiple_of(j * SLICE + (y_bit * 2 + x_bit) * 4 * shard + first, shard), shard)
                add_low(out.at[j, t, 0:shard], d_own.at[at, :], d_in.at[at, :])

    def down_along_z(d):
        if sorted_out:
            for t in range(4):
                at = pl.ds(pl.multiple_of(((z + d) & 3) * SLICE + t * 4 * shard + 2 * shard, shard), 2 * shard)
                add_low(outs[4 + d].at[t // 2, t % 2, 0 : 2 * shard], d_own.at[at, :], d_in.at[at, :])

    def up_arrived(c):
        u_copy(c).wait_recv()
        own = hid.at[0:width, (per_half + c) * SLICE : (per_half + c + 1) * SLICE]
        if not sorted_out:
            add_low(outs[1].at[:, c * SLICE : (c + 1) * SLICE], own, u_in.at[c])
            return

        def fold(dst, s, part):
            at = pl.ds(pl.multiple_of(s * shard, shard), shard)
            cols = slice(part * half, (part + 1) * half)
            add_low(dst, own.at[at, cols], u_in.at[c, at, cols])

        def near(s, carry):
            zz, t = s >> 1, s & 1
            for sends in range(2):
                fold(outs[1 - sends].at[zz, t, shard : 2 * shard], zz * 4 + t * 2 + (x ^ sends), 0)
                fold(outs[3 - sends].at[zz, t, shard : 2 * shard], zz * 4 + (y ^ sends) * 2 + t, 1)
            return carry

        def along(s, carry):
            for d in range(4):
                for part in range(2):
                    to = slice((2 + part) * shard, (3 + part) * shard)
                    fold(outs[4 + d].at[s >> 1, s & 1, to], ((z + d) & 3) * 4 + s, part)
            return carry

        lax.fori_loop(0, 8 if c == 0 else 4, near if c == 0 else along, 0, unroll=2)

    def proj_arrived():
        p_copy().wait_recv()
        if not sorted_out:
            add_low(outs[2], p_own, p_in)
            return

        def one(s, carry):
            zz, t = s >> 1, s & 1
            for sends in range(2):
                at = pl.ds(pl.multiple_of((zz * 4 + t * 2 + (x ^ sends)) * shard, shard), shard)
                add_low(outs[1 - sends].at[zz, t, 2 * shard : 3 * shard], p_own.at[at, :], p_in.at[at, :])
            return carry

        lax.fori_loop(0, 8, one, 0, unroll=4)

    middle = blocks + slices
    for c in range(per_half):
        at = slice(c * SLICE, (c + 1) * SLICE)

        @pl.when(i == middle + c)
        def _(c=c, at=at):
            hid[0:width, at] = up_slice((1 - band) * per_half + c)
            u_copy(c).start()
            for j in range(2 * c, 2 * c + 2):
                down_arrived(j)

        @pl.when(i == middle + per_half + c)
        def _(c=c):
            hid[0:width, (per_half + c) * SLICE : (per_half + c + 1) * SLICE] = up_slice(band * per_half + c)
            for d in range(2 * c, 2 * c + 2):
                down_along_z(d)

    @pl.when(i == middle + slices)
    def _():
        columns(mm(ats[...], ags[...], TN), p_own, p_far, slice(None))
        p_copy().start()
        for c in range(per_half):
            up_arrived(c)
        proj_arrived()
        for j in range(slices):
            d_copy(j).wait_send()
        for c in range(per_half):
            u_copy(c).wait_send()
        p_copy().wait_send()


def mlp(size, tokens, attended, cotangent, w_proj, w_up, w_down, proj_bias, gain, shift, up_bias, down_bias, rows=256):
    count, width = tokens.shape
    ff = w_up.shape[1]
    blocks, slices = count // rows, ff // SLICE
    half, per_half = width // 2, slices // 2
    sorted_out = size == 16
    one = pl.Buffered(1)
    mine = lambda i: (jnp.minimum(i, blocks - 1), 0)
    block = pl.BlockSpec((rows, width), mine)

    def full(a):
        return pl.BlockSpec(a.shape, lambda i: (0,) * len(a.shape), pipeline_mode=one)

    vectors = (proj_bias, gain, shift, up_bias, down_bias)
    shape = jax.ShapeDtypeStruct
    if sorted_out:
        sixteenth = width // 16
        pieces = [shape((4, 2, n * sixteenth, half), bf16) for n in (3, 3, 2, 2)]
        pieces += [shape((2, 2, 4 * sixteenth, half), bf16)] * 4
    else:
        pieces = [shape((ff, half), bf16), shape((width, ff // 2), bf16), shape((width, half), bf16)]
    kept = [shape((8, width), f32), shape((8, ff), f32)] + pieces
    low = lambda *s: pltpu.VMEM(s, bf16)
    copies = slices + per_half + 1
    return pl.pallas_call(
        functools.partial(mlp_kernel, sorted_out, blocks, rows, slices),
        out_shape=[shape((count, width), f32), shape((count, width), f32), shape((count, width), bf16)] + kept,
        grid=(blocks + 2 * slices + 1,),
        in_specs=[block, block, block] + [full(a) for a in (w_proj, w_up, w_down, *vectors)],
        out_specs=[block, block, block] + [full(a) for a in kept],
        scratch_shapes=[
            low(count, ff),
            low(count, ff),
            *([low(count, width)] * 4),
            *([low(ff, half)] * 3),
            low(per_half, width, SLICE),
            *([low(width, half)] * 3),
            pltpu.SemaphoreType.DMA((copies,)),
            pltpu.SemaphoreType.DMA((copies,)),
        ],
        compiler_params=pltpu.CompilerParams(vmem_limit_bytes=62 * MIB, collective_id=1, has_side_effects=True),
        cost_estimate=pl.CostEstimate(flops=40 * 10**9, bytes_accessed=40 * 10**6, transcendentals=0),
        name="mlp",
    )(tokens, attended, cotangent, w_proj, w_up, w_down, *vectors)


def qkv_kernel(steps, tok_ref, seg_ref, w_ref, gain, shift, qbias, vbias, q_ref, k_ref, v_ref, n_ref, k_far, v_far, seg_far,
               n_all, k_all, v_all, send_sem, recv_sem):
    i = pl.program_id(0)
    last = pl.num_programs(0) - 1
    other = (lax.axis_index("dp"), 1 - lax.axis_index("band"))
    rows, width = tok_ref.shape

    def push(t, src, dst):
        return pltpu.make_async_remote_copy(
            src_ref=src, dst_ref=dst, send_sem=send_sem.at[t], recv_sem=recv_sem.at[t], device_id=other, device_id_type=MESH
        )

    def copies(j):
        at = pl.ds(pl.multiple_of(j * rows, rows), rows)
        return push(2 * j, k_all.at[at, :], k_far.at[at, :]), push(2 * j + 1, v_all.at[at, :], v_far.at[at, :])

    segs = push(send_sem.shape[0] - 1, seg_ref, seg_far)

    @pl.when(i == 0)
    def _():
        barrier = pltpu.get_barrier_semaphore()
        pl.semaphore_signal(barrier, inc=1, device_id=other, device_id_type=MESH)

    @pl.when(i == 1)
    def _():
        pl.semaphore_wait(pltpu.get_barrier_semaphore(), 1)
        segs.start()
        for copy in copies(0):
            copy.start()

    @pl.when(i < steps)
    def _():
        here = pl.ds(pl.multiple_of(i * rows, rows), rows)
        xhat, _ = normalize(tok_ref[...])
        n1 = (xhat * as_row(gain) + as_row(shift)).astype(bf16)
        n_ref[...] = n1
        n_all[here, :] = n1
        k = mm(n1, w_ref[:, width : 2 * width]).astype(bf16)
        k_ref[...] = k
        k_all[here, :] = k
        v = (mm(n1, w_ref[:, 2 * width :]) + as_row(vbias)).astype(bf16)
        v_ref[...] = v
        v_all[here, :] = v

    @pl.when((i >= 1) & (i < steps))
    def _():
        for copy in copies(i):
            copy.start()

    @pl.when(i >= steps)
    def _():
        here = pl.ds(pl.multiple_of((i - steps) * rows, rows), rows)
        q = (mm(n_all[here, :], w_ref[:, :width]) + as_row(qbias)).astype(bf16)
        q_ref[...] = q * jnp.asarray(HEAD_DIM**-0.5, bf16)

    @pl.when(i == last)
    def _():
        segs.wait()
        for j in range(k_all.shape[0] // rows):
            for copy in copies(j):
                copy.wait()


def project_qkv(tokens, seg, w_qkv, gain, shift, query_bias, value_bias, rows=256):
    count, width = tokens.shape
    one = pl.Buffered(1)
    steps = count // rows
    block = pl.BlockSpec((rows, width), lambda i: (jnp.minimum(i, steps - 1), 0))
    late = pl.BlockSpec((rows, width), lambda i: (jnp.maximum(i - steps, 0), 0))
    vectors = (gain, shift, query_bias, value_bias)
    hbm = pl.BlockSpec(memory_space=pl.ANY)
    low = jax.ShapeDtypeStruct((count, width), bf16)
    return pl.pallas_call(
        functools.partial(qkv_kernel, steps),
        out_shape=(low,) * 6 + (jax.ShapeDtypeStruct(seg.shape, seg.dtype),),
        grid=(2 * steps,),
        in_specs=[block, hbm] + [pl.BlockSpec(a.shape, lambda i, n=a.ndim: (0,) * n, pipeline_mode=one) for a in (w_qkv, *vectors)],
        out_specs=[late] + [block] * 3 + [hbm] * 3,
        scratch_shapes=[
            pltpu.VMEM((count, width), bf16),
            pltpu.VMEM((count, width), bf16),
            pltpu.VMEM((count, width), bf16),
            pltpu.SemaphoreType.DMA((2 * steps + 1,)),
            pltpu.SemaphoreType.DMA((2 * steps + 1,)),
        ],
        compiler_params=pltpu.CompilerParams(vmem_limit_bytes=60 * MIB, collective_id=2, has_side_effects=True),
        cost_estimate=pl.CostEstimate(flops=4 * 10**9, bytes_accessed=13 * 10**6, transcendentals=0),
        name="project_qkv",
    )(tokens, seg, w_qkv, *vectors)


def qkv_grad_kernel(blocks, rows, band_ref, dq_ref, dk_own, dk_far, dv_own, dv_far, n_ref, packed_ref, own_ref, far_ref, sums_ref, packed):
    i = pl.program_id(0)
    band = band_ref[0]
    width = dq_ref.shape[1]
    half = own_ref.shape[1]

    @pl.when(i < blocks)
    def _():
        here = pl.ds(pl.multiple_of(i * rows, rows), rows)
        first = i == 0
        dq = dq_ref[...]
        packed_ref[:, :width] = dq
        packed[here, :width] = dq
        add_sums(sums_ref, 0, dq.astype(f32), first)
        for t, (own, far) in enumerate(((dk_own, dk_far), (dv_own, dv_far))):
            for p in range(width // 128):
                at = slice(p * 128, (p + 1) * 128)
                to = slice((t + 1) * width + p * 128, (t + 1) * width + (p + 1) * 128)
                turned = (own[at, :].astype(f32) + far[at, :].astype(f32)).astype(bf16).T
                packed_ref[:, to] = turned
                packed[here, to] = turned
        add_sums(sums_ref, 1, packed_ref[:, 2 * width :].astype(f32), first)

    def columns(which):
        at = pl.ds(pl.multiple_of(which * half, 128), half)
        return mm(n_ref[...], packed[:, at], TN).astype(bf16)

    @pl.when(i == blocks)
    def _():
        far_ref[...] = columns(1 - band)

    @pl.when(i == blocks + 1)
    def _():
        own_ref[...] = columns(band)


def qkv_grads(band, dq, dk_own, dk_far, dv_own, dv_far, normed, rows=256):
    count, width = dq.shape
    blocks = count // rows
    half = 3 * width // 2
    one = pl.Buffered(1)
    mine = lambda i, *_: (jnp.minimum(i, blocks - 1), 0)
    flip = lambda i, *_: (0, jnp.minimum(i, blocks - 1))
    whole = lambda i, *_: (0, 0)
    shape = jax.ShapeDtypeStruct
    return pl.pallas_call(
        functools.partial(qkv_grad_kernel, blocks, rows),
        out_shape=(shape((count, 3 * width), bf16), shape((width, half), bf16), shape((width, half), bf16), shape((8, width), f32)),
        grid_spec=pltpu.PrefetchScalarGridSpec(
            num_scalar_prefetch=1,
            grid=(blocks + 2,),
            in_specs=[pl.BlockSpec((rows, width), mine)]
            + [pl.BlockSpec((width, rows), flip)] * 4
            + [pl.BlockSpec((count, width), whole, pipeline_mode=one)],
            out_specs=[
                pl.BlockSpec((rows, 3 * width), mine),
                pl.BlockSpec((width, half), whole, pipeline_mode=one),
                pl.BlockSpec((width, half), whole, pipeline_mode=one),
                pl.BlockSpec((8, width), whole, pipeline_mode=one),
            ],
            scratch_shapes=[pltpu.VMEM((count, 3 * width), bf16)],
        ),
        compiler_params=pltpu.CompilerParams(vmem_limit_bytes=40 * MIB),
        cost_estimate=pl.CostEstimate(flops=8 * 10**9, bytes_accessed=18 * 10**6, transcendentals=0),
        name="qkv_grads",
    )(band, dq, dk_own, dk_far, dv_own, dv_far, normed)


def input_grad_kernel(packed_ref, tok_ref, rgrad_ref, w_ref, gain, out_ref, sums_ref):
    first = pl.program_id(0) == 0
    e = mm(packed_ref[...], w_ref[...], NT)
    xhat, scale = normalize(tok_ref[...])
    add_sums(sums_ref, 0, e * xhat, first)
    add_sums(sums_ref, 1, e, first)
    f = e * gain[...]
    back = scale * (f - jnp.mean(f, axis=-1, keepdims=True) - xhat * jnp.mean(f * xhat, axis=-1, keepdims=True))
    out_ref[...] = rgrad_ref[...] + back


def input_grads(packed, tokens, rgrad, w_qkv, gain, rows=256):
    count, width = tokens.shape
    one = pl.Buffered(1)
    block = pl.BlockSpec((rows, width), lambda i: (i, 0))
    return pl.pallas_call(
        input_grad_kernel,
        out_shape=(jax.ShapeDtypeStruct((count, width), f32), jax.ShapeDtypeStruct((8, width), f32)),
        grid=(count // rows,),
        in_specs=[
            pl.BlockSpec((rows, packed.shape[1]), lambda i: (i, 0)),
            block,
            block,
            pl.BlockSpec(w_qkv.shape, lambda i: (0, 0), pipeline_mode=one),
            pl.BlockSpec((1, width), lambda i: (0, 0), pipeline_mode=one),
        ],
        out_specs=[block, pl.BlockSpec((8, width), lambda i: (0, 0), pipeline_mode=one)],
        compiler_params=pltpu.CompilerParams(vmem_limit_bytes=32 * MIB),
        cost_estimate=pl.CostEstimate(flops=6 * 10**9, bytes_accessed=18 * 10**6, transcendentals=0),
        name="input_grads",
    )(packed, tokens, rgrad, w_qkv, gain.reshape(1, -1))


def finish_kernel(
    dq_hbm, dko_hbm, dkf_hbm, dvo_hbm, dvf_hbm, n_hbm, tok_hbm, rgrad_hbm, w_hbm, ak_hbm, bk_hbm, ck_hbm, ar_hbm, br_hbm, c1_hbm, c2_hbm, c3_hbm, gain, msums, usums,
    out, down_out, wide_out, vec_out, usum_out,
    packed, dko, dko_in, dvo, dvo_in, n1, tok, wq, ak, bk, ck, cols, far_in, tail,
    a_one, b_one, c_one, a_two, b_two, c_two, a_thr, b_thr, c_thr, ta_one, tb_one, ta_two, tb_two, ta_thr, tb_thr, vec, vec_band, vec_x, vec_y, vec_z,
    load_sem, swap_send, swap_recv, send, recv, vsend, vrecv,
):
    me = lax.axis_index("dp")
    band = lax.axis_index("band")
    x, y, z = me & 1, (me >> 1) & 1, me >> 2
    rows, width = tok.shape
    half = far_in.shape[-1]
    peer_band = (me, 1 - band)
    peer_x = (me ^ 1, band)
    peer_y = (me ^ 2, band)
    peers_z = [(((z + d) & 3) * 4 + (me & 3), band) for d in (1, 2, 3)]

    def load(t, src, dst):
        copy = pltpu.make_async_copy(src, dst, load_sem.at[t])
        copy.start()
        return copy

    loads = {
        "early": (load(0, ak_hbm, ak), load(1, ar_hbm, a_one), load(2, bk_hbm, bk), load(3, br_hbm, b_one)),
        "along": (load(8, ck_hbm, ck), load(13, c1_hbm, c_one.at[0]), load(14, c2_hbm, c_one.at[1]), load(15, c3_hbm, c_one.at[2])),
        "queries": (load(6, dq_hbm, packed.at[:, 0:width]),),
        "normed": (load(7, n_hbm, n1),),
        "keys": (load(4, dko_hbm, dko), load(5, dvo_hbm, dvo)),
        "weight": (load(10, w_hbm, wq),),
        "rows": (load(11, tok_hbm, tok), load(12, rgrad_hbm, out)),
    }

    def ready(name):
        for copy in loads[name]:
            copy.wait()

    barrier = pltpu.get_barrier_semaphore()
    for peer in (peer_band, peer_x, peer_y, *peers_z):
        pl.semaphore_signal(barrier, inc=1, device_id=peer, device_id_type=MESH)
    pl.semaphore_wait(barrier, 6)

    pending = []

    def push(src, dst, peer, s, r):
        copy = pltpu.make_async_remote_copy(src_ref=src, dst_ref=dst, send_sem=s, recv_sem=r, device_id=peer, device_id_type=MESH)
        copy.start()
        pending.append(copy)
        return copy

    swap_k = push(dkf_hbm, dko_in, peer_band, swap_send.at[0], swap_recv.at[0])
    swap_v = push(dvf_hbm, dvo_in, peer_band, swap_send.at[1], swap_recv.at[1])

    def put(dst, src):
        dst[...] = src[...]

    def each_shard(body):
        def step(s, c):
            body(s >> 2, (s >> 1) & 1, s & 1)
            return c

        lax.fori_loop(0, 16, step, 0, unroll=4)

    def second_stage(t, kept, one, two, mine, peer):
        def total(s, c):
            add_low(one.at[s >> 1, s & 1], one.at[s >> 1, s & 1], kept(s >> 1, s & 1))
            return c

        lax.fori_loop(0, 8, total, 0, unroll=True)
        return push(one.at[:, 1 - mine], two, peer, send.at[t, 0], recv.at[t, 0])

    def third_stage(t, one, two, three, mine, copy):
        copy.wait_recv()

        def total(zz, c):
            add_low(two.at[zz], two.at[zz], one.at[zz, mine])
            return c

        lax.fori_loop(0, 4, total, 0, unroll=True)
        return [push(two.at[(z + d) & 3], three.at[d - 1], peers_z[d - 1], send.at[t, d], recv.at[t, d]) for d in (1, 2, 3)]

    def last(two, three, copies):
        for copy in copies:
            copy.wait_recv()
        total = two[z].astype(f32)
        for d in range(3):
            total = total + three[d].astype(f32)
        return total

    ready("early")
    a_copy = second_stage(0, lambda i, j: ak.at[i, j], a_one, a_two, y, peer_y)
    b_copy = second_stage(1, lambda i, j: bk.at[i, j], b_one, b_two, x, peer_x)
    ready("along")

    def along(s, c):
        i, j = s >> 1, s & 1
        total = ck[i, j].astype(f32)
        for d in range(3):
            total = total + c_one[d, i, j].astype(f32)
        ck[i, j] = total.astype(bf16)
        return c

    lax.fori_loop(0, 4, along, 0, unroll=True)
    c_copy = push(ck.at[:, 1 - x], c_two, peer_x, send.at[2, 0], recv.at[2, 0])

    def columns(t):
        cols[:, :, :, :, t * width : (t + 1) * width] = (
            mm(n1[...], packed[:, t * width : (t + 1) * width], TN).astype(bf16).reshape(cols.shape[:-1] + (width,))
        )

    def turn(t, own, other):
        def step(i, c):
            here = pl.ds(pl.multiple_of(i * 256, 256), 256)
            for p in range(width // 128):
                at = slice(p * 128, (p + 1) * 128)
                turned = (own[at, here].astype(f32) + other[at, here].astype(f32)).astype(bf16).T
                packed[here, t * width + p * 128 : t * width + (p + 1) * 128] = turned
            return c

        lax.fori_loop(0, rows // 256, step, 0)

    def swap(t, start, size, to):
        return pltpu.make_async_remote_copy(
            src_ref=cols.at[:, :, :, :, pl.ds(pl.multiple_of(start, 128), size)],
            dst_ref=far_in.at[:, :, :, :, pl.ds(pl.multiple_of(to, 128), size)],
            send_sem=swap_send.at[t],
            recv_sem=swap_recv.at[t],
            device_id=peer_band,
            device_id_type=MESH,
        )

    third = width // 2
    swap_near = swap(2, (3 - band) * third, third, band * width)
    swap_wide = swap(3, (1 - band) * 2 * width, width, (1 - band) * third)
    ready("queries")
    ready("normed")
    columns(0)

    @pl.when(band == 1)
    def _():
        swap_wide.start()

    ready("keys")
    swap_k.wait_recv()
    turn(1, dko, dko_in)
    columns(1)
    swap_near.start()
    swap_v.wait_recv()
    turn(2, dvo, dvo_in)
    columns(2)

    @pl.when(band == 0)
    def _():
        swap_wide.start()

    a_copies = third_stage(0, a_one, a_two, a_thr, y, a_copy)
    b_copies = third_stage(1, b_one, b_two, b_thr, x, b_copy)
    swap_near.wait()
    swap_wide.wait()
    mine = pl.ds(pl.multiple_of(band * half, 128), half)
    each_shard(lambda i, j, k: add_low(tail.at[i, j, k], cols.at[i, j, k, :, mine], far_in.at[i, j, k]))
    cut = ta_one.shape[-1]
    ta_first = push(tail.at[:, :, 1 - x, :, 0:cut], ta_one, peer_x, send.at[3, 4], recv.at[3, 4])
    tb_first = push(tail.at[:, 1 - y, :, :, cut:half], tb_one, peer_y, send.at[4, 4], recv.at[4, 4])
    c_copy.wait_recv()
    add_low(c_two.at[0], c_two.at[0], ck.at[0, x])
    add_low(c_two.at[1], c_two.at[1], ck.at[1, x])
    c_last = push(c_two.at[1 - y], c_thr, peer_y, send.at[2, 1], recv.at[2, 1])

    ready("weight")
    ready("rows")
    vec[...] = jnp.zeros(vec.shape, f32)

    def rows_back(i, c):
        here = pl.ds(pl.multiple_of(i * 256, 256), 256)
        e = mm(packed[here, :], wq[...], NT)
        xhat, scale = normalize(tok[here, :])
        vec[0:1, :] = vec[0:1, :] + jnp.sum(e * xhat, axis=0, keepdims=True)
        vec[1:2, :] = vec[1:2, :] + jnp.sum(e, axis=0, keepdims=True)
        vec[2:3, :] = vec[2:3, :] + jnp.sum(packed[here, 0:width].astype(f32), axis=0, keepdims=True)
        vec[3:4, :] = vec[3:4, :] + jnp.sum(packed[here, 2 * width : 3 * width].astype(f32), axis=0, keepdims=True)
        f = e * as_row(gain)
        back = scale * (f - jnp.mean(f, axis=-1, keepdims=True) - xhat * jnp.mean(f * xhat, axis=-1, keepdims=True))
        out[here, :] = out[here, :] + back
        return c

    lax.fori_loop(0, rows // 256, rows_back, 0)
    vec[4:8, :] = msums[0:4, :]
    for t in range(usums.shape[1] // width):
        vec[8 + t : 9 + t, :] = usums[0:1, t * width : (t + 1) * width]
    v_band = push(vec, vec_band, peer_band, vsend.at[0], vrecv.at[0])
    ta_first.wait_recv()
    ta_copy = second_stage(3, lambda i, j: tail.at[i, j, x, :, 0:cut], ta_one, ta_two, y, peer_y)
    tb_first.wait_recv()
    tb_copy = second_stage(4, lambda i, j: tail.at[i, y, j, :, cut:half], tb_one, tb_two, x, peer_x)
    v_band.wait()
    vec_band[...] = vec[...] + vec_band[...]
    v_x = push(vec_band, vec_x, peer_x, vsend.at[1], vrecv.at[1])
    ta_copies = third_stage(3, ta_one, ta_two, ta_thr, y, ta_copy)
    tb_copies = third_stage(4, tb_one, tb_two, tb_thr, x, tb_copy)
    v_x.wait()
    vec_x[...] = vec_band[...] + vec_x[...]
    v_y = push(vec_x, vec_y, peer_y, vsend.at[2], vrecv.at[2])
    v_y.wait()
    vec_y[...] = vec_x[...] + vec_y[...]
    v_z = [push(vec_y, vec_z.at[d], peers_z[d], vsend.at[3 + d], vrecv.at[3 + d]) for d in range(3)]
    for copy in v_z:
        copy.wait_recv()
    vec[...] = vec_y[...] + vec_z[0] + vec_z[1] + vec_z[2]
    shard = vec_out.shape[1]
    vec_out[...] = pltpu.roll(vec[0:8, :], width - me * shard, 1)[:, 0:shard]
    wide = usum_out.shape[1]
    per_row = width // wide
    row = vec[pl.ds(8 + me // per_row, 1), :]
    usum_out[...] = pltpu.roll(jnp.broadcast_to(row, (8, width)), width - (me % per_row) * wide, 1)[0:1, 0:wide]
    shard = width // 16
    a_sum, b_sum = last(a_two, a_thr, a_copies), last(b_two, b_thr, b_copies)
    c_last.wait_recv()
    c_sum = c_two[y].astype(f32) + c_thr[...].astype(f32)
    down_out[0:shard, :] = a_sum[0:shard]
    down_out[shard : 2 * shard, :] = b_sum[0:shard]
    down_out[2 * shard : 4 * shard, :] = c_sum[0 : 2 * shard]
    ups = (a_sum[shard : 2 * shard], b_sum[shard : 2 * shard], c_sum[2 * shard : 3 * shard], c_sum[3 * shard : 4 * shard])
    for t, part in enumerate(ups):
        wide_out[:, half + t * third : half + (t + 1) * third] = part
    wide_out[:, half + 4 * third :] = a_sum[2 * shard : 3 * shard]
    wide_out[:, 0:cut] = last(ta_two, ta_thr, ta_copies)
    wide_out[:, cut:half] = last(tb_two, tb_thr, tb_copies)
    done = {id(c) for c in (v_band, v_x, v_y)}
    for copy in pending:
        if id(copy) not in done:
            copy.wait_send()


def finish(dq, dk_own, dk_far, dv_own, dv_far, normed, tokens, rgrad, w_qkv, pieces, gain, msums, usums):
    rows, width = tokens.shape
    ff = usums.shape[1]
    half = 3 * width // 2
    shards = (4, 2, 2)
    third, shard = width // 2, width // 16
    q_shape = shards + (shard, half)
    a_piece, b_piece, c_piece = (3 * shard, third), (2 * shard, third), (4 * shard, third)
    cut = half // 256 * 128 + 128
    ta_piece, tb_piece = (shard, cut), (shard, half - cut)
    hbm, vmem = pl.BlockSpec(memory_space=pl.ANY), pl.BlockSpec(memory_space=pltpu.VMEM)
    shape = jax.ShapeDtypeStruct
    low = lambda *s: pltpu.VMEM(s, bf16)
    dma = pltpu.SemaphoreType.DMA
    return pl.pallas_call(
        finish_kernel,
        out_shape=(
            shape((rows, width), f32),
            shape((ff // 16, width // 2), f32),
            shape((width // 16, half + ff // 2 + width // 2), f32),
            shape((8, width // 16), f32),
            shape((1, ff // 16), f32),
        ),
        in_specs=[hbm] * 17 + [vmem] * 3,
        out_specs=[vmem] * 5,
        scratch_shapes=[
            low(rows, 3 * width),
            *([low(width, rows)] * 4),
            low(rows, width),
            pltpu.VMEM((rows, width), f32),
            low(width, 3 * width),
            low(4, 2, *a_piece),
            low(4, 2, *b_piece),
            low(2, 2, *c_piece),
            low(*shards, shard, 3 * width),
            low(*q_shape),
            low(*q_shape),
            low(4, 2, *a_piece),
            low(4, 2, *b_piece),
            low(3, 2, 2, *c_piece),
            low(4, *a_piece),
            low(4, *b_piece),
            low(2, *c_piece),
            low(3, *a_piece),
            low(3, *b_piece),
            low(*c_piece),
            low(4, 2, *ta_piece),
            low(4, 2, *tb_piece),
            low(4, *ta_piece),
            low(4, *tb_piece),
            low(3, *ta_piece),
            low(3, *tb_piece),
            pltpu.VMEM((16, width), f32),
            pltpu.VMEM((16, width), f32),
            pltpu.VMEM((16, width), f32),
            pltpu.VMEM((16, width), f32),
            pltpu.VMEM((3, 16, width), f32),
            dma((16,)),
            dma((4,)),
            dma((4,)),
            dma((5, 5)),
            dma((5, 5)),
            dma((6,)),
            dma((6,)),
        ],
        compiler_params=pltpu.CompilerParams(vmem_limit_bytes=52 * MIB, collective_id=0, has_side_effects=True),
        cost_estimate=pl.CostEstimate(flops=20 * 10**9, bytes_accessed=40 * 10**6, transcendentals=0),
        name="finish",
    )(dq, dk_own, dk_far, dv_own, dv_far, normed, tokens, rgrad, w_qkv, *pieces,
      gain, msums, usums)


def swap_band(x):
    return lax.ppermute(x, "band", [(0, 1), (1, 0)])


def pick(x, which, axis):
    return lax.dynamic_index_in_dim(x, which, axis, keepdims=False)


def halve(x, axis, bit, size):
    mine = (lax.axis_index("dp") >> bit) & 1
    arrived = lax.ppermute(pick(x, 1 - mine, axis), "dp", [(i, i ^ (1 << bit)) for i in range(size)])
    return pick(x, mine, axis).astype(f32) + arrived.astype(f32)


class Reduction:
    def __init__(self, x, order, size):
        rows, columns = x.shape
        levels = size.bit_length() - 1
        self.size = size
        self.x = x.reshape((2,) * levels + (rows // size, columns))
        self.left = list(range(levels - 1, -1, -1))
        self.order = list(order)

    def step(self):
        if self.order:
            bit = self.order.pop(0)
            x = halve(self.x, self.left.index(bit), bit, self.size)
            self.left.remove(bit)
            self.x = x.astype(bf16) if self.left else x

    def finish(self):
        while self.order:
            self.step()
        return self.x


def finish_any(size, band_at, query_grad, dk_own, dk_far, dv_own, dv_far, normed, tokens, residual_grad, w_qkv, pieces, gain, msums, usums):
    width = tokens.shape[1]
    rising = list(range(size.bit_length() - 1))
    turned = [1, 0] + rising[2:]
    packed, qkv_own, qkv_far, qkv_sums = qkv_grads(
        band_at, query_grad, dk_own, swap_band(dk_far), dv_own, swap_band(dv_far), normed
    )
    input_grad, first_sums = input_grads(packed, tokens, residual_grad, w_qkv, gain)

    def total(x, order):
        return Reduction(x, order, size).finish()

    def join(own, far):
        return (own.astype(f32) + swap_band(far).astype(f32)).astype(bf16)

    tall = jnp.concatenate([first_sums[:2], qkv_sums[:2], msums[:4]], axis=0)
    thin = jnp.concatenate([tall.T, usums[0].reshape(width, -1)], axis=1)
    thin = jnp.pad(thin, ((0, 0), (0, 128 - thin.shape[1]))).astype(bf16)
    thin_sum = total(join(thin, thin), turned)
    ups = usums.shape[1] // width
    return (
        input_grad,
        total(pieces[0], rising),
        total(pieces[1], turned),
        total(join(qkv_own, qkv_far), rising),
        total(pieces[2], turned),
        [thin_sum[:, t] for t in range(8)],
        thin_sum[:, 8 : 8 + ups].reshape(-1),
    )


def local(
    size,
    inputs,
    segment_ids,
    cotangent,
    first_gain,
    first_bias,
    w_qkv,
    query_bias,
    value_bias,
    w_proj,
    proj_bias,
    second_gain,
    second_bias,
    w_up,
    up_bias,
    w_down,
    down_bias,
):
    local_shape = inputs.shape
    width = local_shape[-1]
    band = lax.axis_index("band")
    band_at = band.astype(jnp.int32).reshape(1)
    tokens = inputs.reshape(-1, width)
    seg_own = segment_ids
    queries, k_own, v_own, normed, k_far, v_far, seg_far = project_qkv(
        tokens, seg_own, w_qkv, first_gain, first_bias, query_bias, value_bias
    )
    keys = (seg_own, seg_far, k_own, k_far, v_own, v_far)
    attended, query_lanes = attend_forward(band_at, queries, *keys)
    output, residual_grad, attended_grad, mlp_sums, up_sums, *pieces = mlp(
        size,
        tokens,
        attended,
        cotangent.reshape(-1, width),
        w_proj,
        w_up,
        w_down,
        proj_bias,
        second_gain,
        second_bias,
        up_bias,
        down_bias,
    )
    if size == 16:
        turns = [[(i, i ^ bit) for i in range(size)] for bit in (1, 2)]
        turns += [[(i, (i + 4 * d) % size) for i in range(size)] for d in (1, 2, 3)]
        sent = (pieces[0], pieces[2], *pieces[5:8])
        pieces = [pieces[1], pieces[3], pieces[4]] + [lax.ppermute(a, "dp", turn) for a, turn in zip(sent, turns)]
    query_grad, dk_own, dk_far, dv_own, dv_far, output = attend_backward(
        band_at, output, query_lanes, attended_grad, attended, *keys
    )
    if size == 16:
        input_grad, down_sum, wide_sum, vec, up_vec = finish(
            query_grad, dk_own, dk_far, dv_own, dv_far, normed, tokens, residual_grad, w_qkv, pieces, first_gain, mlp_sums, up_sums
        )
        first, second = 3 * width // 2, 3 * width // 2 + w_up.shape[1] // 2
        qkv_sum, up_sum, proj_sum = wide_sum[:, :first], wide_sum[:, first:second], wide_sum[:, second:]
        vectors, up_vector = [vec[t] for t in range(8)], up_vec.reshape(-1)
    else:
        input_grad, down_sum, up_sum, qkv_sum, proj_sum, vectors, up_vector = finish_any(
            size, band_at, query_grad, dk_own, dk_far, dv_own, dv_far, normed, tokens, residual_grad, w_qkv, pieces, first_gain, mlp_sums, up_sums
        )
    return (
        output.reshape(local_shape),
        input_grad.reshape(local_shape),
        vectors[0],
        vectors[1],
        qkv_sum,
        vectors[2],
        vectors[3],
        proj_sum,
        vectors[7],
        vectors[5],
        vectors[6],
        up_sum,
        up_vector,
        down_sum,
        vectors[4],
    )


def solution(mesh):
    size = mesh.shape["dp"]
    placed = (P("dp", "band", None), P("dp", "band"), P("dp", "band", None)) + (P(),) * 13
    split, thin = P("dp", "band"), P("dp")
    wide = P("dp", "band", None)
    return jax.shard_map(
        functools.partial(local, size),
        mesh=mesh,
        in_specs=placed,
        out_specs=(wide, wide, thin, thin, split, thin, thin, split, thin, thin, thin, split, thin, split, thin),
        check_vma=False,
    )
```

```python
import functools

import jax
import jax.numpy as jnp
from jax import lax
from jax.experimental import pallas as pl
from jax.experimental.pallas import tpu as pltpu
from jax.sharding import PartitionSpec as P

EPS = 1e-05
HEADS = 12
HEAD_DIM = 64
NEG_LARGE = -1e30
PAIRS = HEADS // 2
CHUNK = 256
EDGE = 64
MIB = 1 << 20
f32, bf16 = jnp.float32, jnp.bfloat16
NN = (((1,), (0,)), ((), ()))
NT = (((1,), (1,)), ((), ()))


def mm(a, b, dims=NN):
    return lax.dot_general(a, b, dims, preferred_element_type=f32)


def low_lanes(rows):
    return lax.broadcasted_iota(jnp.int32, (rows, 128), 1) < HEAD_DIM


def side_lanes(rows):
    return lax.broadcasted_iota(jnp.int32, (rows, 128), 1) & (HEAD_DIM - 1)


def split3(x):
    high = x.astype(bf16).astype(f32)
    middle = (x - high).astype(bf16).astype(f32)
    return high, middle, x - high - middle


def place(side, parts, base):
    for t, part in enumerate(parts):
        base = jnp.where(side == 16 + t, part, base)
    return base


def as_column(row):
    return jnp.broadcast_to(row, (8, row.shape[1])).T[:, 0:1]


def key_window(seg_own, seg_far, block, BQ, BK):
    own, far = seg_own[...].astype(f32), seg_far[...].astype(f32)

    def below(limit):
        return jnp.sum((own < limit).astype(f32) + (far < limit).astype(f32)).astype(jnp.int32)

    mine = seg_own[:, pl.ds(pl.multiple_of(block * BQ, BQ), BQ)].astype(f32)
    row = lax.broadcasted_iota(jnp.int32, mine.shape, 1)
    lo = (below(jnp.min(mine)) // 128) * 128
    blocks = (below(jnp.max(mine) + 1.0) - lo + BK - 1) // BK
    start = jnp.minimum(lo, 2 * own.shape[1] - blocks * BK)
    early_end = below(jnp.min(jnp.where(row >= EDGE, mine, 99.0)))
    late_start = below(jnp.max(jnp.where(row < BQ - EDGE, mine, -1.0)) + 1.0)
    early = jnp.clip((early_end - start) // BK, 0, blocks)
    late = jnp.clip((start + blocks * BK - late_start) // BK, 0, blocks - early)
    return start, blocks, early, late


def over_blocks(count, early, late, rows, body):
    for first, end, part in (
        (0, early, slice(0, EDGE)),
        (early, count - late, slice(0, rows)),
        (count - late, count, slice(rows - EDGE, rows)),
    ):

        def step(j, c, part=part):
            body(j, part)
            return c

        lax.fori_loop(first, end, step, 0)


def fill_pairs(src, dst, rows, low, extra):
    for p in range(PAIRS):
        pair = src[:, p * 128 : (p + 1) * 128]
        dst[2 * p, rows, :] = jnp.where(low, pair, extra)
        dst[2 * p + 1, rows, :] = jnp.where(low, extra, pair)


def fill_keys(band, i, k_own, k_far, v_own, v_far, seg_own, seg_far, kaug, vaug, value_extra):
    local = kaug.shape[1] // 2
    low, side = low_lanes(CHUNK), side_lanes(CHUNK)
    here = pl.ds(pl.multiple_of(i * CHUNK, CHUNK), CHUNK)
    for k, v, seg, first in ((k_own, v_own, seg_own, band), (k_far, v_far, seg_far, 1 - band)):
        rows = pl.ds(pl.multiple_of(first * local + i * CHUNK, CHUNK), CHUNK)
        extra = jnp.where(side < 16, jnp.where(side == as_column(seg[:, here]), 0.0, NEG_LARGE), jnp.where(side < 19, -1.0, 0.0))
        fill_pairs(k, kaug, rows, low, extra.astype(bf16))
        fill_pairs(v, vaug, rows, low, value_extra)


def attend_fwd_kernel(fills, BQ, BK, band_ref, q_ref, k_own, k_far, v_own, v_far,
                      seg_own, seg_far, o_ref, qaug_ref, kaug, vaug, qm, s_all, mx, acc):
    i = pl.program_id(0)

    @pl.when(i < fills)
    def _():
        fill_keys(band_ref[0], i, k_own, k_far, v_own, v_far, seg_own, seg_far, kaug, vaug, jnp.ones((CHUNK, 128), bf16))

    @pl.when(i >= fills)
    def _():
        low, side = low_lanes(BQ), side_lanes(BQ)
        block = i - fills
        ids = as_column(seg_own[:, pl.ds(pl.multiple_of(block * BQ, BQ), BQ)])
        own = (side == ids).astype(f32).astype(bf16)
        for p in range(PAIRS):
            pair = q_ref[:, p * 128 : (p + 1) * 128]
            qm[2 * p] = jnp.where(low, pair, own)
            qm[2 * p + 1] = jnp.where(low, own, pair)
        mx[...] = jnp.full(mx.shape, -3e38, f32)
        acc[...] = jnp.zeros(acc.shape, f32)
        start, count, early, late = key_window(seg_own, seg_far, block, BQ, BK)

        def first(j, part):
            at = pl.multiple_of(start + j * BK, 128)
            out = pl.ds(pl.multiple_of(j * BK, BK), BK)
            for h in range(HEADS):
                s = mm(qm[h, part, :], kaug[h, pl.ds(at, BK), :], NT)
                s_all[h, part, out] = s
                m = mx[h, part, :]
                for t in range(BK // 128):
                    m = jnp.maximum(m, s[:, t * 128 : (t + 1) * 128])
                mx[h, part, :] = m

        over_blocks(count, early, late, BQ, first)
        for h in range(HEADS):
            mx[h] = jnp.broadcast_to(jnp.max(mx[h], axis=1, keepdims=True), (BQ, 128))

        def second(j, part):
            at = pl.multiple_of(start + j * BK, 128)
            src = pl.ds(pl.multiple_of(j * BK, BK), BK)
            for h in range(HEADS):
                p = jnp.exp(s_all[h, part, src] - jnp.concatenate([mx[h, part, :]] * (BK // 128), axis=1)).astype(bf16)
                acc[h, part, :] += mm(p, vaug[h, pl.ds(at, BK), :])

        over_blocks(count, early, late, BQ, second)
        ids = (side == ids).astype(f32)
        for p in range(PAIRS):
            even, odd = acc[2 * p], acc[2 * p + 1]
            total = jnp.where(low, pltpu.roll(even, HEAD_DIM, 1), pltpu.roll(odd, HEAD_DIM, 1))
            o_ref[:, p * 128 : (p + 1) * 128] = (jnp.where(low, even, odd) / total).astype(bf16)
            pair = q_ref[:, p * 128 : (p + 1) * 128]
            extra = [place(side, split3(mx[2 * p + e] + jnp.log(sums)), ids).astype(bf16) for e, sums in enumerate((even, odd))]
            qaug_ref[2 * p] = jnp.where(low, pair, extra[0])
            qaug_ref[2 * p + 1] = jnp.where(low, extra[1], pair)


def attend_forward(band, q, seg_own, seg_far, k_own, k_far, v_own, v_far, BQ=256, BK=256):
    rows, width = q.shape
    fills, steps = rows // CHUNK, rows // BQ
    mine = lambda i, *_: (jnp.clip(i - fills, 0, steps - 1), 0)
    fill = lambda i, *_: (jnp.minimum(i, fills - 1), 0)
    wide = pl.BlockSpec((CHUNK, width), fill)
    thin = pl.BlockSpec((1, rows), lambda i, *_: (0, 0))
    return pl.pallas_call(
        functools.partial(attend_fwd_kernel, fills, BQ, BK),
        out_shape=(jax.ShapeDtypeStruct((rows, width), bf16), jax.ShapeDtypeStruct((HEADS, rows, 128), bf16)),
        grid_spec=pltpu.PrefetchScalarGridSpec(
            num_scalar_prefetch=1,
            grid=(fills + steps,),
            in_specs=[pl.BlockSpec((BQ, width), mine), wide, wide, wide, wide, thin, thin],
            out_specs=[pl.BlockSpec((BQ, width), mine), pl.BlockSpec((HEADS, BQ, 128), lambda i, *_: (0, jnp.clip(i - fills, 0, steps - 1), 0))],
            scratch_shapes=[
                pltpu.VMEM((HEADS, 2 * rows, 128), bf16),
                pltpu.VMEM((HEADS, 2 * rows, 128), bf16),
                pltpu.VMEM((HEADS, BQ, 128), bf16),
                pltpu.VMEM((HEADS, BQ, 2 * rows), f32),
                pltpu.VMEM((HEADS, BQ, 128), f32),
                pltpu.VMEM((HEADS, BQ, 128), f32),
            ],
        ),
        compiler_params=pltpu.CompilerParams(vmem_limit_bytes=56 * MIB),
        cost_estimate=pl.CostEstimate(flops=30 * 10**9, bytes_accessed=10 * 10**6, transcendentals=0),
        name="attend_forward",
    )(band, q, k_own, k_far, v_own, v_far, seg_own, seg_far)


def attend_bwd_kernel(fills, steps, BQ, BK, band_ref, qm, do_ref, o_ref,
                      k_own, k_far, v_own, v_far, seg_own, seg_far, carried, dq_ref, dkt_own, dkt_far, dvt_own, dvt_far, carried_out,
                      kaug, vaug, dom, lqt, ldot, eqt, edot, dq_acc, dk_acc, dv_acc):
    i = pl.program_id(0)
    band = band_ref[0]
    local = kaug.shape[1] // 2

    @pl.when(i < fills)
    def _():
        side = side_lanes(CHUNK)
        extra = jnp.where((side >= 16) & (side < 19), -1.0, 0.0).astype(bf16)
        fill_keys(band, i, k_own, k_far, v_own, v_far, seg_own, seg_far, kaug, vaug, extra)
        for part in range(2):
            cols = pl.ds(pl.multiple_of(part * local + i * CHUNK, CHUNK), CHUNK)
            for p in range(PAIRS):
                dk_acc[p, :, cols] = jnp.zeros((128, CHUNK), f32)
                dv_acc[p, :, cols] = jnp.zeros((128, CHUNK), f32)

    @pl.when((i >= fills) & (i < fills + steps))
    def _():
        low, side = low_lanes(BQ), side_lanes(BQ)
        block = i - fills
        carried_out[...] = carried[...]
        lane = lax.broadcasted_iota(jnp.int32, (256, 256), 0) & 127
        column = lax.broadcasted_iota(jnp.int32, (256, 256), 1)
        adder = ((lane < HEAD_DIM) == (column < 128)).astype(f32).astype(bf16)
        for p in range(PAIRS):
            cols = slice(p * 128, (p + 1) * 128)
            q_pair, do_pair = jnp.where(low, qm[2 * p], qm[2 * p + 1]), do_ref[:, cols]
            prod = do_pair.astype(f32) * o_ref[:, cols].astype(f32)
            high = prod.astype(bf16)
            rest = (prod - high.astype(f32)).astype(bf16)
            delta = mm(jnp.concatenate([high, rest], axis=1), adder)
            for e in range(2):
                extra = place(side, split3(delta[:, e * 128 : (e + 1) * 128]), jnp.zeros((BQ, 128), f32)).astype(bf16)
                dom[2 * p + e] = jnp.where(low, do_pair, extra) if e == 0 else jnp.where(low, extra, do_pair)
            for pair, dst, edges in ((q_pair, lqt, eqt), (do_pair, ldot, edot)):
                flipped = pair.T
                upper = lax.broadcasted_iota(jnp.int32, flipped.shape, 0) < HEAD_DIM
                zero = jnp.zeros_like(flipped)
                even, odd = jnp.where(upper, flipped, zero), jnp.where(upper, zero, flipped)
                dst[p, :, 0:BQ] = even
                dst[p, :, BQ : 2 * BQ] = odd
                edges[0, p] = jnp.concatenate([even[:, 0:EDGE], odd[:, 0:EDGE]], axis=1)
                edges[1, p] = jnp.concatenate([even[:, BQ - EDGE :], odd[:, BQ - EDGE :]], axis=1)
        lefts = {-1: (lqt, ldot), 0: (eqt.at[0], edot.at[0]), BQ - EDGE: (eqt.at[1], edot.at[1])}
        dq_acc[...] = jnp.zeros(dq_acc.shape, f32)
        start, count, early, late = key_window(seg_own, seg_far, block, BQ, BK)

        def step(j, part):
            window = pl.ds(pl.multiple_of(start + j * BK, 128), BK)
            left_q, left_do = lefts[part.start if part.stop - part.start < BQ else -1]

            def scores(h):
                return mm(qm[h, part, :], kaug[h, window, :], NT), mm(dom[h, part, :], vaug[h, window, :], NT)

            ahead = scores(0)
            kept = []
            for h in range(HEADS):
                p = h // 2
                s, dp = ahead
                if h + 1 < HEADS:
                    ahead = scores(h + 1)
                prob = jnp.exp(s)
                ds = (prob * dp).astype(bf16)
                kept.append((prob.astype(bf16), ds))
                dq_acc[h, part, :] += mm(ds, kaug[h, window, :])
                if h % 2:
                    dv_acc[p, :, window] += mm(left_do[p], jnp.concatenate([kept[0][0], kept[1][0]], axis=0))
                    dk_acc[p, :, window] += mm(left_q[p], jnp.concatenate([kept[0][1], kept[1][1]], axis=0))
                    kept = []

        over_blocks(count, early, late, BQ, step)
        for p in range(PAIRS):
            pair = jnp.where(low, dq_acc[2 * p], dq_acc[2 * p + 1]) * HEAD_DIM**-0.5
            dq_ref[:, p * 128 : (p + 1) * 128] = pair.astype(bf16)

    @pl.when(i >= fills + steps)
    def _():
        j = i - fills - steps
        for p in range(PAIRS):
            rows = slice(p * 128, (p + 1) * 128)
            for first, dk_out, dv_out in ((band, dkt_own, dvt_own), (1 - band, dkt_far, dvt_far)):
                cols = pl.ds(pl.multiple_of(first * local + j * CHUNK, CHUNK), CHUNK)
                dk_out[rows, :] = dk_acc[p, :, cols].astype(bf16)
                dv_out[rows, :] = dv_acc[p, :, cols].astype(bf16)


def attend_backward(band, carried, qaug, do, o, seg_own, seg_far, k_own, k_far, v_own, v_far, BQ=256, BK=256):
    rows, width = do.shape
    fills, steps = rows // CHUNK, rows // BQ
    mine = lambda i, *_: (jnp.clip(i - fills, 0, steps - 1), 0)
    fill = lambda i, *_: (jnp.minimum(i, fills - 1), 0)
    drain = lambda i, *_: (0, jnp.clip(i - fills - steps, 0, fills - 1))
    wide = pl.BlockSpec((CHUNK, width), fill)
    thin = pl.BlockSpec((1, rows), lambda i, *_: (0, 0))
    block = pl.BlockSpec((BQ, width), mine)
    flat = jax.ShapeDtypeStruct((width, rows), bf16)
    return pl.pallas_call(
        functools.partial(attend_bwd_kernel, fills, steps, BQ, BK),
        out_shape=(jax.ShapeDtypeStruct((rows, width), bf16), flat, flat, flat, flat, jax.ShapeDtypeStruct(carried.shape, carried.dtype)),
        grid_spec=pltpu.PrefetchScalarGridSpec(
            num_scalar_prefetch=1,
            grid=(fills + steps + fills,),
            in_specs=[pl.BlockSpec((HEADS, BQ, 128), lambda i, *_: (0, jnp.clip(i - fills, 0, steps - 1), 0)), block, block, wide, wide, wide, wide, thin, thin, block],
            out_specs=[block] + [pl.BlockSpec((width, CHUNK), drain)] * 4 + [block],
            scratch_shapes=[
                pltpu.VMEM((HEADS, 2 * rows, 128), bf16),
                pltpu.VMEM((HEADS, 2 * rows, 128), bf16),
                pltpu.VMEM((HEADS, BQ, 128), bf16),
                pltpu.VMEM((PAIRS, 128, 2 * BQ), bf16),
                pltpu.VMEM((PAIRS, 128, 2 * BQ), bf16),
                pltpu.VMEM((2, PAIRS, 128, 2 * EDGE), bf16),
                pltpu.VMEM((2, PAIRS, 128, 2 * EDGE), bf16),
                pltpu.VMEM((HEADS, BQ, 128), f32),
                pltpu.VMEM((PAIRS, 128, 2 * rows), f32),
                pltpu.VMEM((PAIRS, 128, 2 * rows), f32),
            ],
        ),
        compiler_params=pltpu.CompilerParams(vmem_limit_bytes=56 * MIB),
        cost_estimate=pl.CostEstimate(flops=45 * 10**9, bytes_accessed=20 * 10**6, transcendentals=0),
        name="attend_backward",
    )(band, qaug, do, o, k_own, k_far, v_own, v_far, seg_own, seg_far, carried)


MESH = pl.DeviceIdType.MESH
TN = (((0,), (0,)), ((), ()))
SLICE = 768


def gelu_and_slope(u):
    below = 0.5 + 0.5 * lax.erf(u * 0.5**0.5)
    return u * below, below + u * jnp.exp(u * u * -0.5) * (0.5 / 3.141592653589793) ** 0.5


def normalize(rows):
    centred = rows - jnp.mean(rows, axis=-1, keepdims=True)
    scale = lax.rsqrt(jnp.mean(centred * centred, axis=-1, keepdims=True) + EPS)
    return centred * scale, scale


def add_sums(ref, row, values, first):
    sums = jnp.sum(values, axis=0, keepdims=True)
    at = slice(row, row + 1)
    ref[at, :] = jnp.where(first, sums, ref[at, :] + sums)


def as_row(ref):
    return ref[...].reshape(1, -1)


def add_low(dst, a, b):
    dst[...] = (a[...].astype(f32) + b[...].astype(f32)).astype(bf16)


def mlp_kernel(sorted_out, blocks, rows, slices, tok_ref, att_ref, cot_ref, wproj, wup, wdown, pbias, gain, shift, ubias, dbias,
               out_ref, rgrad_ref, agrad_ref, sums_ref, usums_ref, *rest):
    outs, scratch = rest[: 8 if sorted_out else 3], rest[8 if sorted_out else 3 :]
    hid, ugr, n2s, bgs, ags, ats, d_own, d_far, d_in, u_in, p_own, p_far, p_in, send_sem, recv_sem = scratch
    i = pl.program_id(0)
    me, band = lax.axis_index("dp"), lax.axis_index("band")
    other = (me, 1 - band)
    width = tok_ref.shape[1]
    half, per_half = width // 2, slices // 2

    def push(t, src, dst):
        return pltpu.make_async_remote_copy(
            src_ref=src, dst_ref=dst, send_sem=send_sem.at[t], recv_sem=recv_sem.at[t], device_id=other, device_id_type=MESH
        )

    def d_copy(j):
        at = pl.ds(pl.multiple_of(j * SLICE, SLICE), SLICE)
        return push(j, d_far.at[at, :], d_in.at[at, :])

    def u_copy(c):
        return push(slices + c, hid.at[0:width, pl.ds(pl.multiple_of(c * SLICE, SLICE), SLICE)], u_in.at[c])

    def p_copy():
        return push(slices + per_half, p_far, p_in)

    @pl.when(i == 0)
    def _():
        barrier = pltpu.get_barrier_semaphore()
        pl.semaphore_signal(barrier, inc=1, device_id=other, device_id_type=MESH)
        pl.semaphore_wait(barrier, 1)

    @pl.when(i < blocks)
    def _():
        here = pl.ds(pl.multiple_of(i * rows, rows), rows)
        first = i == 0
        att = att_ref[...]
        ats[here, :] = att
        residual = tok_ref[...] + mm(att, wproj[...]) + as_row(pbias)
        xhat, scale = normalize(residual)
        n2 = (xhat * as_row(gain) + as_row(shift)).astype(bf16)
        n2s[here, :] = n2
        cot = cot_ref[...]
        bg = cot.astype(bf16)
        bgs[here, :] = bg
        add_sums(sums_ref, 0, bg.astype(f32), first)
        for c in range(slices):
            cols = slice(c * SLICE, (c + 1) * SLICE)
            hidden, slope = gelu_and_slope(mm(n2, wup[:, cols]) + ubias[cols].reshape(1, -1))
            hid[here, cols] = hidden.astype(bf16)
            grad = (mm(bg, wdown[cols, :], NT) * slope).astype(bf16)
            ugr[here, cols] = grad
            sums = jnp.sum(grad.astype(f32), axis=0, keepdims=True)
            usums_ref[0:1, cols] = jnp.where(first, sums, usums_ref[0:1, cols] + sums)
        out_ref[...] = residual + mm(hid[here, :], wdown[...]) + as_row(dbias)
        e = mm(ugr[here, :], wup[...], NT)
        add_sums(sums_ref, 1, e * xhat, first)
        add_sums(sums_ref, 2, e, first)
        f = e * as_row(gain)
        rgrad = cot + scale * (f - jnp.mean(f, axis=-1, keepdims=True) - xhat * jnp.mean(f * xhat, axis=-1, keepdims=True))
        rgrad_ref[...] = rgrad
        ag = rgrad.astype(bf16)
        ags[here, :] = ag
        add_sums(sums_ref, 3, ag.astype(f32), first)
        agrad_ref[...] = mm(ag, wproj[...], NT).astype(bf16)

    def columns(grad, own, far, at):
        left, right = grad[:, :half].astype(bf16), grad[:, half:].astype(bf16)
        own[at, :] = jnp.where(band == 0, left, right)
        far[at, :] = jnp.where(band == 0, right, left)

    @pl.when((i >= blocks) & (i < blocks + slices))
    def _():
        j = i - blocks
        at = pl.ds(pl.multiple_of(j * SLICE, SLICE), SLICE)
        columns(mm(hid[:, at], bgs[...], TN), d_own, d_far, at)
        d_copy(j).start()

    def up_slice(which):
        at = pl.ds(pl.multiple_of(which * SLICE, SLICE), SLICE)
        return mm(n2s[...], ugr[:, at], TN).astype(bf16)

    x, y = me & 1, (me >> 1) & 1

    z = me >> 2
    shard = width // 16

    corners = [(y ^ (q >> 1)) * 2 + (x ^ (q & 1)) for q in range(4)]

    def down_arrived(j):
        d_copy(j).wait_recv()
        if not sorted_out:
            at = pl.ds(pl.multiple_of(j * SLICE, SLICE), SLICE)
            add_low(outs[0].at[at, :], d_own.at[at, :], d_in.at[at, :])
            return
        for q in range(4):
            at = pl.ds(pl.multiple_of(j * SLICE + corners[q] * 4 * shard, shard), 2 * shard)
            add_low(outs[q].at[j, 0 : 2 * shard], d_own.at[at, :], d_in.at[at, :])

    def down_along_z(d):
        if sorted_out:
            for t in range(4):
                at = pl.ds(pl.multiple_of((z ^ d) * SLICE + t * 4 * shard + 2 * shard, shard), 2 * shard)
                add_low(outs[4 + d].at[t // 2, t % 2, 0 : 2 * shard], d_own.at[at, :], d_in.at[at, :])

    def up_arrived(c):
        u_copy(c).wait_recv()
        own = hid.at[0:width, (per_half + c) * SLICE : (per_half + c + 1) * SLICE]
        if not sorted_out:
            add_low(outs[1].at[:, c * SLICE : (c + 1) * SLICE], own, u_in.at[c])
            return

        def fold(dst, s, part):
            at = pl.ds(pl.multiple_of(s * shard, shard), shard)
            cols = slice(part * half, (part + 1) * half)
            add_low(dst.at[(2 + part) * shard : (3 + part) * shard], own.at[at, cols], u_in.at[c, at, cols])

        def near(zz, carry):
            for q in range(4):
                for part in range(2):
                    fold(outs[q].at[zz], zz * 4 + corners[q], part)
            return carry

        def along(s, carry):
            for d in range(4):
                for part in range(2):
                    fold(outs[4 + d].at[s >> 1, s & 1], (z ^ d) * 4 + s, part)
            return carry

        lax.fori_loop(0, 4, near if c == 0 else along, 0, unroll=2)

    def proj_arrived():
        p_copy().wait_recv()
        if not sorted_out:
            add_low(outs[2], p_own, p_in)
            return

        def one(zz, carry):
            for q in range(4):
                at = pl.ds(pl.multiple_of((zz * 4 + corners[q]) * shard, shard), shard)
                add_low(outs[q].at[zz, 4 * shard : 5 * shard], p_own.at[at, :], p_in.at[at, :])
            return carry

        lax.fori_loop(0, 4, one, 0, unroll=2)

    middle = blocks + slices
    for c in range(per_half):
        at = slice(c * SLICE, (c + 1) * SLICE)

        @pl.when(i == middle + c)
        def _(c=c, at=at):
            hid[0:width, at] = up_slice((1 - band) * per_half + c)
            u_copy(c).start()
            for j in range(2 * c, 2 * c + 2):
                down_arrived(j)

        @pl.when(i == middle + per_half + c)
        def _(c=c):
            hid[0:width, (per_half + c) * SLICE : (per_half + c + 1) * SLICE] = up_slice(band * per_half + c)
            for d in range(2 * c, 2 * c + 2):
                down_along_z(d)

    @pl.when(i == middle + slices)
    def _():
        columns(mm(ats[...], ags[...], TN), p_own, p_far, slice(None))
        p_copy().start()
        for c in range(per_half):
            up_arrived(c)
        proj_arrived()
        for j in range(slices):
            d_copy(j).wait_send()
        for c in range(per_half):
            u_copy(c).wait_send()
        p_copy().wait_send()


def mlp(size, tokens, attended, cotangent, w_proj, w_up, w_down, proj_bias, gain, shift, up_bias, down_bias, rows=256):
    count, width = tokens.shape
    ff = w_up.shape[1]
    blocks, slices = count // rows, ff // SLICE
    half, per_half = width // 2, slices // 2
    sorted_out = size == 16
    one = pl.Buffered(1)
    mine = lambda i: (jnp.minimum(i, blocks - 1), 0)
    block = pl.BlockSpec((rows, width), mine)

    def full(a):
        return pl.BlockSpec(a.shape, lambda i: (0,) * len(a.shape), pipeline_mode=one)

    vectors = (proj_bias, gain, shift, up_bias, down_bias)
    shape = jax.ShapeDtypeStruct
    if sorted_out:
        sixteenth = width // 16
        pieces = [shape((4, 5 * sixteenth, half), bf16)] * 4
        pieces += [shape((2, 2, 4 * sixteenth, half), bf16)] * 4
    else:
        pieces = [shape((ff, half), bf16), shape((width, ff // 2), bf16), shape((width, half), bf16)]
    kept = [shape((8, width), f32), shape((8, ff), f32)] + pieces
    low = lambda *s: pltpu.VMEM(s, bf16)
    copies = slices + per_half + 1
    return pl.pallas_call(
        functools.partial(mlp_kernel, sorted_out, blocks, rows, slices),
        out_shape=[shape((count, width), f32), shape((count, width), f32), shape((count, width), bf16)] + kept,
        grid=(blocks + 2 * slices + 1,),
        in_specs=[block, block, block] + [full(a) for a in (w_proj, w_up, w_down, *vectors)],
        out_specs=[block, block, block] + [full(a) for a in kept],
        scratch_shapes=[
            low(count, ff),
            low(count, ff),
            *([low(count, width)] * 4),
            *([low(ff, half)] * 3),
            low(per_half, width, SLICE),
            *([low(width, half)] * 3),
            pltpu.SemaphoreType.DMA((copies,)),
            pltpu.SemaphoreType.DMA((copies,)),
        ],
        compiler_params=pltpu.CompilerParams(vmem_limit_bytes=62 * MIB, collective_id=1, has_side_effects=True),
        cost_estimate=pl.CostEstimate(flops=40 * 10**9, bytes_accessed=40 * 10**6, transcendentals=0),
        name="mlp",
    )(tokens, attended, cotangent, w_proj, w_up, w_down, *vectors)


def qkv_kernel(steps, tok_ref, seg_ref, w_ref, gain, shift, qbias, vbias, q_ref, k_ref, v_ref, n_ref, k_far, v_far, seg_far,
               n_all, k_all, v_all, send_sem, recv_sem):
    i = pl.program_id(0)
    last = pl.num_programs(0) - 1
    other = (lax.axis_index("dp"), 1 - lax.axis_index("band"))
    rows, width = tok_ref.shape

    def push(t, src, dst):
        return pltpu.make_async_remote_copy(
            src_ref=src, dst_ref=dst, send_sem=send_sem.at[t], recv_sem=recv_sem.at[t], device_id=other, device_id_type=MESH
        )

    def copies(j):
        at = pl.ds(pl.multiple_of(j * rows, rows), rows)
        return push(2 * j, k_all.at[at, :], k_far.at[at, :]), push(2 * j + 1, v_all.at[at, :], v_far.at[at, :])

    segs = push(send_sem.shape[0] - 1, seg_ref, seg_far)

    @pl.when(i == 0)
    def _():
        barrier = pltpu.get_barrier_semaphore()
        pl.semaphore_signal(barrier, inc=1, device_id=other, device_id_type=MESH)

    @pl.when(i == 1)
    def _():
        pl.semaphore_wait(pltpu.get_barrier_semaphore(), 1)
        segs.start()
        for copy in copies(0):
            copy.start()

    @pl.when(i < steps)
    def _():
        here = pl.ds(pl.multiple_of(i * rows, rows), rows)
        xhat, _ = normalize(tok_ref[...])
        n1 = (xhat * as_row(gain) + as_row(shift)).astype(bf16)
        n_ref[...] = n1
        n_all[here, :] = n1
        k = mm(n1, w_ref[:, width : 2 * width]).astype(bf16)
        k_ref[...] = k
        k_all[here, :] = k
        v = (mm(n1, w_ref[:, 2 * width :]) + as_row(vbias)).astype(bf16)
        v_ref[...] = v
        v_all[here, :] = v

    @pl.when((i >= 1) & (i < steps))
    def _():
        for copy in copies(i):
            copy.start()

    @pl.when(i >= steps)
    def _():
        here = pl.ds(pl.multiple_of((i - steps) * rows, rows), rows)
        q = (mm(n_all[here, :], w_ref[:, :width]) + as_row(qbias)).astype(bf16)
        q_ref[...] = q * jnp.asarray(HEAD_DIM**-0.5, bf16)

    @pl.when(i == last)
    def _():
        segs.wait()
        for j in range(k_all.shape[0] // rows):
            for copy in copies(j):
                copy.wait()


def project_qkv(tokens, seg, w_qkv, gain, shift, query_bias, value_bias, rows=256):
    count, width = tokens.shape
    one = pl.Buffered(1)
    steps = count // rows
    block = pl.BlockSpec((rows, width), lambda i: (jnp.minimum(i, steps - 1), 0))
    late = pl.BlockSpec((rows, width), lambda i: (jnp.maximum(i - steps, 0), 0))
    vectors = (gain, shift, query_bias, value_bias)
    hbm = pl.BlockSpec(memory_space=pl.ANY)
    low = jax.ShapeDtypeStruct((count, width), bf16)
    return pl.pallas_call(
        functools.partial(qkv_kernel, steps),
        out_shape=(low,) * 6 + (jax.ShapeDtypeStruct(seg.shape, seg.dtype),),
        grid=(2 * steps,),
        in_specs=[block, hbm] + [pl.BlockSpec(a.shape, lambda i, n=a.ndim: (0,) * n, pipeline_mode=one) for a in (w_qkv, *vectors)],
        out_specs=[late] + [block] * 3 + [hbm] * 3,
        scratch_shapes=[
            pltpu.VMEM((count, width), bf16),
            pltpu.VMEM((count, width), bf16),
            pltpu.VMEM((count, width), bf16),
            pltpu.SemaphoreType.DMA((2 * steps + 1,)),
            pltpu.SemaphoreType.DMA((2 * steps + 1,)),
        ],
        compiler_params=pltpu.CompilerParams(vmem_limit_bytes=60 * MIB, collective_id=2, has_side_effects=True),
        cost_estimate=pl.CostEstimate(flops=4 * 10**9, bytes_accessed=13 * 10**6, transcendentals=0),
        name="project_qkv",
    )(tokens, seg, w_qkv, *vectors)


def qkv_grad_kernel(blocks, rows, band_ref, dq_ref, dk_own, dk_far, dv_own, dv_far, n_ref, packed_ref, own_ref, far_ref, sums_ref, packed):
    i = pl.program_id(0)
    band = band_ref[0]
    width = dq_ref.shape[1]
    half = own_ref.shape[1]

    @pl.when(i < blocks)
    def _():
        here = pl.ds(pl.multiple_of(i * rows, rows), rows)
        first = i == 0
        dq = dq_ref[...]
        packed_ref[:, :width] = dq
        packed[here, :width] = dq
        add_sums(sums_ref, 0, dq.astype(f32), first)
        for t, (own, far) in enumerate(((dk_own, dk_far), (dv_own, dv_far))):
            for p in range(width // 128):
                at = slice(p * 128, (p + 1) * 128)
                to = slice((t + 1) * width + p * 128, (t + 1) * width + (p + 1) * 128)
                turned = (own[at, :].astype(f32) + far[at, :].astype(f32)).astype(bf16).T
                packed_ref[:, to] = turned
                packed[here, to] = turned
        add_sums(sums_ref, 1, packed_ref[:, 2 * width :].astype(f32), first)

    def columns(which):
        at = pl.ds(pl.multiple_of(which * half, 128), half)
        return mm(n_ref[...], packed[:, at], TN).astype(bf16)

    @pl.when(i == blocks)
    def _():
        far_ref[...] = columns(1 - band)

    @pl.when(i == blocks + 1)
    def _():
        own_ref[...] = columns(band)


def qkv_grads(band, dq, dk_own, dk_far, dv_own, dv_far, normed, rows=256):
    count, width = dq.shape
    blocks = count // rows
    half = 3 * width // 2
    one = pl.Buffered(1)
    mine = lambda i, *_: (jnp.minimum(i, blocks - 1), 0)
    flip = lambda i, *_: (0, jnp.minimum(i, blocks - 1))
    whole = lambda i, *_: (0, 0)
    shape = jax.ShapeDtypeStruct
    return pl.pallas_call(
        functools.partial(qkv_grad_kernel, blocks, rows),
        out_shape=(shape((count, 3 * width), bf16), shape((width, half), bf16), shape((width, half), bf16), shape((8, width), f32)),
        grid_spec=pltpu.PrefetchScalarGridSpec(
            num_scalar_prefetch=1,
            grid=(blocks + 2,),
            in_specs=[pl.BlockSpec((rows, width), mine)]
            + [pl.BlockSpec((width, rows), flip)] * 4
            + [pl.BlockSpec((count, width), whole, pipeline_mode=one)],
            out_specs=[
                pl.BlockSpec((rows, 3 * width), mine),
                pl.BlockSpec((width, half), whole, pipeline_mode=one),
                pl.BlockSpec((width, half), whole, pipeline_mode=one),
                pl.BlockSpec((8, width), whole, pipeline_mode=one),
            ],
            scratch_shapes=[pltpu.VMEM((count, 3 * width), bf16)],
        ),
        compiler_params=pltpu.CompilerParams(vmem_limit_bytes=40 * MIB),
        cost_estimate=pl.CostEstimate(flops=8 * 10**9, bytes_accessed=18 * 10**6, transcendentals=0),
        name="qkv_grads",
    )(band, dq, dk_own, dk_far, dv_own, dv_far, normed)


def input_grad_kernel(packed_ref, tok_ref, rgrad_ref, w_ref, gain, out_ref, sums_ref):
    first = pl.program_id(0) == 0
    e = mm(packed_ref[...], w_ref[...], NT)
    xhat, scale = normalize(tok_ref[...])
    add_sums(sums_ref, 0, e * xhat, first)
    add_sums(sums_ref, 1, e, first)
    f = e * gain[...]
    back = scale * (f - jnp.mean(f, axis=-1, keepdims=True) - xhat * jnp.mean(f * xhat, axis=-1, keepdims=True))
    out_ref[...] = rgrad_ref[...] + back


def input_grads(packed, tokens, rgrad, w_qkv, gain, rows=256):
    count, width = tokens.shape
    one = pl.Buffered(1)
    block = pl.BlockSpec((rows, width), lambda i: (i, 0))
    return pl.pallas_call(
        input_grad_kernel,
        out_shape=(jax.ShapeDtypeStruct((count, width), f32), jax.ShapeDtypeStruct((8, width), f32)),
        grid=(count // rows,),
        in_specs=[
            pl.BlockSpec((rows, packed.shape[1]), lambda i: (i, 0)),
            block,
            block,
            pl.BlockSpec(w_qkv.shape, lambda i: (0, 0), pipeline_mode=one),
            pl.BlockSpec((1, width), lambda i: (0, 0), pipeline_mode=one),
        ],
        out_specs=[block, pl.BlockSpec((8, width), lambda i: (0, 0), pipeline_mode=one)],
        compiler_params=pltpu.CompilerParams(vmem_limit_bytes=32 * MIB),
        cost_estimate=pl.CostEstimate(flops=6 * 10**9, bytes_accessed=18 * 10**6, transcendentals=0),
        name="input_grads",
    )(packed, tokens, rgrad, w_qkv, gain.reshape(1, -1))


def finish_kernel(
    dq_hbm, dko_hbm, dkf_hbm, dvo_hbm, dvf_hbm, n_hbm, tok_hbm, rgrad_hbm, w_hbm, pk_hbm, ck_hbm, c1_hbm, px_hbm, py_hbm, pd_hbm, c2_hbm, c3_hbm, gain, msums, usums,
    out_hbm, down_out, wide_out, vec_out, usum_out,
    packed, dko, dko_in, dvo, dvo_in, n1, tok, out, wq, pk, p_one, ck, cols, far_in, tail,
    c_one, c_two, p_thr, c_thr, ta_one, tb_one, ta_two, tb_two, ta_thr, tb_thr, vec, vec_band, vec_x, vec_y, vec_z,
    load_sem, store_sem, swap_send, swap_recv, send, recv, vsend, vrecv,
):
    me = lax.axis_index("dp")
    band = lax.axis_index("band")
    x, y, z = me & 1, (me >> 1) & 1, me >> 2
    rows, width = tok.shape
    half = far_in.shape[-1]
    peer_band = (me, 1 - band)
    peer_x = (me ^ 1, band)
    peer_y = (me ^ 2, band)
    peers_z = [(((z + d) & 3) * 4 + (me & 3), band) for d in (1, 2, 3)]

    def load(t, src, dst):
        return pltpu.make_async_copy(src, dst, load_sem.at[t])

    loads = {
        "queries": (load(6, dq_hbm, packed.at[:, 0:width]), load(7, n_hbm, n1)),
        "keys": (load(4, dko_hbm, dko), load(5, dvo_hbm, dvo)),
        "early": (load(0, pk_hbm, pk), load(1, px_hbm, p_one.at[0]), load(2, py_hbm, p_one.at[1]), load(3, pd_hbm, p_one.at[2])),
        "along": (load(8, ck_hbm, ck), load(13, c2_hbm, c_one.at[1]), load(14, c3_hbm, c_one.at[2])),
        "rows": (load(10, w_hbm, wq), load(11, tok_hbm, tok), load(12, rgrad_hbm, out)),
    }

    def fetch(name):
        for copy in loads[name]:
            copy.start()

    def ready(name):
        for copy in loads[name]:
            copy.wait()

    for name in ("queries", "keys", "early"):
        fetch(name)

    barrier = pltpu.get_barrier_semaphore()
    for peer in (peer_band, peer_x, peer_y, *peers_z):
        pl.semaphore_signal(barrier, inc=1, device_id=peer, device_id_type=MESH)
    pl.semaphore_wait(barrier, 6)

    pending = []

    def push(src, dst, peer, s, r):
        copy = pltpu.make_async_remote_copy(src_ref=src, dst_ref=dst, send_sem=s, recv_sem=r, device_id=peer, device_id_type=MESH)
        copy.start()
        pending.append(copy)
        return copy

    swap_k = push(dkf_hbm, dko_in, peer_band, swap_send.at[0], swap_recv.at[0])
    swap_v = push(dvf_hbm, dvo_in, peer_band, swap_send.at[1], swap_recv.at[1])
    c_near = push(c1_hbm, c_one.at[0], (me ^ 4, band), send.at[2, 2], recv.at[2, 2])

    def put(dst, src):
        dst[...] = src[...]

    def each_shard(body):
        def step(s, c):
            body(s >> 2, (s >> 1) & 1, s & 1)
            return c

        lax.fori_loop(0, 16, step, 0, unroll=4)

    def second_stage(t, kept, one, two, mine, peer):
        def total(s, c):
            add_low(one.at[s >> 1, s & 1], one.at[s >> 1, s & 1], kept(s >> 1, s & 1))
            return c

        lax.fori_loop(0, 8, total, 0, unroll=True)
        return push(one.at[:, 1 - mine], two, peer, send.at[t, 0], recv.at[t, 0])

    def third_stage(t, one, two, three, mine, copy):
        copy.wait_recv()

        def total(zz, c):
            add_low(two.at[zz], two.at[zz], one.at[zz, mine])
            return c

        lax.fori_loop(0, 4, total, 0, unroll=True)
        return [push(two.at[(z + d) & 3], three.at[d - 1], peers_z[d - 1], send.at[t, d], recv.at[t, d]) for d in (1, 2, 3)]

    def last(two, three, copies):
        for copy in copies:
            copy.wait_recv()
        total = two[z].astype(f32)
        for d in range(3):
            total = total + three[d].astype(f32)
        return total

    def columns(t):
        cols[:, :, :, :, t * width : (t + 1) * width] = (
            mm(n1[...], packed[:, t * width : (t + 1) * width], TN).astype(bf16).reshape(cols.shape[:-1] + (width,))
        )

    def turn(t, own, other):
        def step(i, c):
            here = pl.ds(pl.multiple_of(i * 256, 256), 256)
            for p in range(width // 128):
                at = slice(p * 128, (p + 1) * 128)
                turned = (own[at, here].astype(f32) + other[at, here].astype(f32)).astype(bf16).T
                packed[here, t * width + p * 128 : t * width + (p + 1) * 128] = turned
            return c

        lax.fori_loop(0, rows // 256, step, 0, unroll=2)

    def swap(t, start, size, to):
        return pltpu.make_async_remote_copy(
            src_ref=cols.at[:, :, :, :, pl.ds(pl.multiple_of(start, 128), size)],
            dst_ref=far_in.at[:, :, :, :, pl.ds(pl.multiple_of(to, 128), size)],
            send_sem=swap_send.at[t],
            recv_sem=swap_recv.at[t],
            device_id=peer_band,
            device_id_type=MESH,
        )

    third = width // 2
    swap_near = swap(2, (3 - band) * third, third, band * width)
    swap_wide = swap(3, (1 - band) * 2 * width, width, (1 - band) * third)
    ready("queries")
    columns(0)
    fetch("along")
    fetch("rows")

    @pl.when(band == 1)
    def _():
        swap_wide.start()

    ready("early")

    def plane(zz, c):
        total = pk[zz].astype(f32)
        for t in range(3):
            total = total + p_one[t, zz].astype(f32)
        pk[zz] = total.astype(bf16)
        return c

    lax.fori_loop(0, 4, plane, 0)
    p_copies = [push(pk.at[(z + d) & 3], p_thr.at[d - 1], peers_z[d - 1], send.at[0, d], recv.at[0, d]) for d in (1, 2, 3)]
    ready("keys")
    swap_k.wait_recv()
    turn(1, dko, dko_in)
    columns(1)
    swap_near.start()
    swap_v.wait_recv()
    turn(2, dvo, dvo_in)
    columns(2)

    @pl.when(band == 0)
    def _():
        swap_wide.start()

    swap_near.wait()
    swap_wide.wait()
    mine = pl.ds(pl.multiple_of(band * half, 128), half)
    each_shard(lambda i, j, k: add_low(tail.at[i, j, k], cols.at[i, j, k, :, mine], far_in.at[i, j, k]))
    cut = ta_one.shape[-1]
    ta_first = push(tail.at[:, :, 1 - x, :, 0:cut], ta_one, peer_x, send.at[3, 4], recv.at[3, 4])
    tb_first = push(tail.at[:, 1 - y, :, :, cut:half], tb_one, peer_y, send.at[4, 4], recv.at[4, 4])

    ready("rows")
    vec[...] = jnp.zeros(vec.shape, f32)

    def rows_back(i, c):
        here = pl.ds(pl.multiple_of(i * 256, 256), 256)
        e = mm(packed[here, :], wq[...], NT)
        xhat, scale = normalize(tok[here, :])
        vec[0:1, :] = vec[0:1, :] + jnp.sum(e * xhat, axis=0, keepdims=True)
        vec[1:2, :] = vec[1:2, :] + jnp.sum(e, axis=0, keepdims=True)
        vec[2:3, :] = vec[2:3, :] + jnp.sum(packed[here, 0:width].astype(f32), axis=0, keepdims=True)
        vec[3:4, :] = vec[3:4, :] + jnp.sum(packed[here, 2 * width : 3 * width].astype(f32), axis=0, keepdims=True)
        f = e * as_row(gain)
        back = scale * (f - jnp.mean(f, axis=-1, keepdims=True) - xhat * jnp.mean(f * xhat, axis=-1, keepdims=True))
        out[here, :] = out[here, :] + back
        return c

    lax.fori_loop(0, rows // 256, rows_back, 0)
    store = pltpu.make_async_copy(out, out_hbm, store_sem)
    store.start()
    vec[4:8, :] = msums[0:4, :]
    for t in range(usums.shape[1] // width):
        vec[8 + t : 9 + t, :] = usums[0:1, t * width : (t + 1) * width]
    v_band = push(vec, vec_band, peer_band, vsend.at[0], vrecv.at[0])
    v_band.wait()
    vec_band[...] = vec[...] + vec_band[...]
    v_z = [push(vec_band, vec_z.at[d], peers_z[d], vsend.at[3 + d], vrecv.at[3 + d]) for d in range(3)]
    ta_first.wait_recv()
    ta_copy = second_stage(3, lambda i, j: tail.at[i, j, x, :, 0:cut], ta_one, ta_two, y, peer_y)
    tb_first.wait_recv()
    tb_copy = second_stage(4, lambda i, j: tail.at[i, y, j, :, cut:half], tb_one, tb_two, x, peer_x)
    for copy in v_z:
        copy.wait()
    vec_z[0] = vec_band[...] + vec_z[0] + vec_z[1] + vec_z[2]
    v_x = push(vec_z.at[0], vec_x, peer_x, vsend.at[1], vrecv.at[1])
    c_near.wait_recv()
    ready("along")

    def along(s, c):
        i, j = s >> 1, s & 1
        total = ck[i, j].astype(f32)
        for d in range(3):
            total = total + c_one[d, i, j].astype(f32)
        ck[i, j] = total.astype(bf16)
        return c

    lax.fori_loop(0, 4, along, 0, unroll=True)
    c_copy = push(ck.at[:, 1 - x], c_two, peer_x, send.at[2, 0], recv.at[2, 0])

    ta_copies = third_stage(3, ta_one, ta_two, ta_thr, y, ta_copy)
    tb_copies = third_stage(4, tb_one, tb_two, tb_thr, x, tb_copy)
    v_x.wait()
    vec_x[...] = vec_z[0] + vec_x[...]
    v_y = push(vec_x, vec_y, peer_y, vsend.at[2], vrecv.at[2])
    c_copy.wait_recv()
    add_low(c_two.at[0], c_two.at[0], ck.at[0, x])
    add_low(c_two.at[1], c_two.at[1], ck.at[1, x])
    c_last = push(c_two.at[1 - y], c_thr, peer_y, send.at[2, 1], recv.at[2, 1])
    v_y.wait()
    vec[...] = vec_x[...] + vec_y[...]
    shard = vec_out.shape[1]
    vec_out[...] = pltpu.roll(vec[0:8, :], width - me * shard, 1)[:, 0:shard]
    wide = usum_out.shape[1]
    per_row = width // wide
    row = vec[pl.ds(8 + me // per_row, 1), :]
    usum_out[...] = pltpu.roll(jnp.broadcast_to(row, (8, width)), width - (me % per_row) * wide, 1)[0:1, 0:wide]
    shard = width // 16
    p_sum = last(pk, p_thr, p_copies)
    c_last.wait_recv()
    c_sum = c_two[y].astype(f32) + c_thr[...].astype(f32)
    down_out[0 : 2 * shard, :] = p_sum[0 : 2 * shard]
    down_out[2 * shard : 4 * shard, :] = c_sum[0 : 2 * shard]
    ups = [part[t * shard : (t + 1) * shard] for part in (p_sum, c_sum) for t in (2, 3)]
    for t, part in enumerate(ups):
        wide_out[:, half + t * third : half + (t + 1) * third] = part
    wide_out[:, half + 4 * third :] = p_sum[4 * shard : 5 * shard]
    wide_out[:, 0:cut] = last(ta_two, ta_thr, ta_copies)
    wide_out[:, cut:half] = last(tb_two, tb_thr, tb_copies)
    done = {id(c) for c in (v_band, v_x, v_y, *v_z)}
    for copy in pending:
        if id(copy) not in done:
            copy.wait_send()
    store.wait()


def finish(dq, dk_own, dk_far, dv_own, dv_far, normed, tokens, rgrad, w_qkv, pieces, gain, msums, usums):
    rows, width = tokens.shape
    ff = usums.shape[1]
    half = 3 * width // 2
    shards = (4, 2, 2)
    third, shard = width // 2, width // 16
    q_shape = shards + (shard, half)
    p_piece, c_piece = (5 * shard, third), (4 * shard, third)
    cut = half // 256 * 128 + 128
    ta_piece, tb_piece = (shard, cut), (shard, half - cut)
    hbm, vmem = pl.BlockSpec(memory_space=pl.ANY), pl.BlockSpec(memory_space=pltpu.VMEM)
    shape = jax.ShapeDtypeStruct
    low = lambda *s: pltpu.VMEM(s, bf16)
    dma = pltpu.SemaphoreType.DMA
    return pl.pallas_call(
        finish_kernel,
        out_shape=(
            shape((rows, width), f32),
            shape((ff // 16, width // 2), f32),
            shape((width // 16, half + ff // 2 + width // 2), f32),
            shape((8, width // 16), f32),
            shape((1, ff // 16), f32),
        ),
        in_specs=[hbm] * 17 + [vmem] * 3,
        out_specs=[hbm] + [vmem] * 4,
        scratch_shapes=[
            low(rows, 3 * width),
            *([low(width, rows)] * 4),
            low(rows, width),
            pltpu.VMEM((rows, width), f32),
            pltpu.VMEM((rows, width), f32),
            low(width, 3 * width),
            low(4, *p_piece),
            low(3, 4, *p_piece),
            low(2, 2, *c_piece),
            low(*shards, shard, 3 * width),
            low(*q_shape),
            low(*q_shape),
            low(3, 2, 2, *c_piece),
            low(2, *c_piece),
            low(3, *p_piece),
            low(*c_piece),
            low(4, 2, *ta_piece),
            low(4, 2, *tb_piece),
            low(4, *ta_piece),
            low(4, *tb_piece),
            low(3, *ta_piece),
            low(3, *tb_piece),
            pltpu.VMEM((16, width), f32),
            pltpu.VMEM((16, width), f32),
            pltpu.VMEM((16, width), f32),
            pltpu.VMEM((16, width), f32),
            pltpu.VMEM((3, 16, width), f32),
            dma((16,)),
            dma,
            dma((4,)),
            dma((4,)),
            dma((5, 5)),
            dma((5, 5)),
            dma((6,)),
            dma((6,)),
        ],
        compiler_params=pltpu.CompilerParams(vmem_limit_bytes=52 * MIB, collective_id=0, has_side_effects=True),
        cost_estimate=pl.CostEstimate(flops=20 * 10**9, bytes_accessed=40 * 10**6, transcendentals=0),
        name="finish",
    )(dq, dk_own, dk_far, dv_own, dv_far, normed, tokens, rgrad, w_qkv, *pieces,
      gain, msums, usums)


def swap_band(x):
    return lax.ppermute(x, "band", [(0, 1), (1, 0)])


def pick(x, which, axis):
    return lax.dynamic_index_in_dim(x, which, axis, keepdims=False)


def halve(x, axis, bit, size):
    mine = (lax.axis_index("dp") >> bit) & 1
    arrived = lax.ppermute(pick(x, 1 - mine, axis), "dp", [(i, i ^ (1 << bit)) for i in range(size)])
    return pick(x, mine, axis).astype(f32) + arrived.astype(f32)


class Reduction:
    def __init__(self, x, order, size):
        rows, columns = x.shape
        levels = size.bit_length() - 1
        self.size = size
        self.x = x.reshape((2,) * levels + (rows // size, columns))
        self.left = list(range(levels - 1, -1, -1))
        self.order = list(order)

    def step(self):
        if self.order:
            bit = self.order.pop(0)
            x = halve(self.x, self.left.index(bit), bit, self.size)
            self.left.remove(bit)
            self.x = x.astype(bf16) if self.left else x

    def finish(self):
        while self.order:
            self.step()
        return self.x


def finish_any(size, band_at, query_grad, dk_own, dk_far, dv_own, dv_far, normed, tokens, residual_grad, w_qkv, pieces, gain, msums, usums):
    width = tokens.shape[1]
    rising = list(range(size.bit_length() - 1))
    turned = [1, 0] + rising[2:]
    packed, qkv_own, qkv_far, qkv_sums = qkv_grads(
        band_at, query_grad, dk_own, swap_band(dk_far), dv_own, swap_band(dv_far), normed
    )
    input_grad, first_sums = input_grads(packed, tokens, residual_grad, w_qkv, gain)

    def total(x, order):
        return Reduction(x, order, size).finish()

    def join(own, far):
        return (own.astype(f32) + swap_band(far).astype(f32)).astype(bf16)

    tall = jnp.concatenate([first_sums[:2], qkv_sums[:2], msums[:4]], axis=0)
    thin = jnp.concatenate([tall.T, usums[0].reshape(width, -1)], axis=1)
    thin = jnp.pad(thin, ((0, 0), (0, 128 - thin.shape[1]))).astype(bf16)
    thin_sum = total(join(thin, thin), turned)
    ups = usums.shape[1] // width
    return (
        input_grad,
        total(pieces[0], rising),
        total(pieces[1], turned),
        total(join(qkv_own, qkv_far), rising),
        total(pieces[2], turned),
        [thin_sum[:, t] for t in range(8)],
        thin_sum[:, 8 : 8 + ups].reshape(-1),
    )


def local(
    size,
    inputs,
    segment_ids,
    cotangent,
    first_gain,
    first_bias,
    w_qkv,
    query_bias,
    value_bias,
    w_proj,
    proj_bias,
    second_gain,
    second_bias,
    w_up,
    up_bias,
    w_down,
    down_bias,
):
    local_shape = inputs.shape
    width = local_shape[-1]
    band = lax.axis_index("band")
    band_at = band.astype(jnp.int32).reshape(1)
    tokens = inputs.reshape(-1, width)
    seg_own = segment_ids
    queries, k_own, v_own, normed, k_far, v_far, seg_far = project_qkv(
        tokens, seg_own, w_qkv, first_gain, first_bias, query_bias, value_bias
    )
    keys = (seg_own, seg_far, k_own, k_far, v_own, v_far)
    attended, query_lanes = attend_forward(band_at, queries, *keys)
    output, residual_grad, attended_grad, mlp_sums, up_sums, *pieces = mlp(
        size,
        tokens,
        attended,
        cotangent.reshape(-1, width),
        w_proj,
        w_up,
        w_down,
        proj_bias,
        second_gain,
        second_bias,
        up_bias,
        down_bias,
    )
    if size == 16:
        turns = [[(i, i ^ bits) for i in range(size)] for bits in (1, 2, 3, 8, 12)]
        sent = (*pieces[1:4], *pieces[6:8])
        pieces = [pieces[0], *pieces[4:6]] + [lax.ppermute(a, "dp", turn) for a, turn in zip(sent, turns)]
    query_grad, dk_own, dk_far, dv_own, dv_far, output = attend_backward(
        band_at, output, query_lanes, attended_grad, attended, *keys
    )
    if size == 16:
        input_grad, down_sum, wide_sum, vec, up_vec = finish(
            query_grad, dk_own, dk_far, dv_own, dv_far, normed, tokens, residual_grad, w_qkv, pieces, first_gain, mlp_sums, up_sums
        )
        first, second = 3 * width // 2, 3 * width // 2 + w_up.shape[1] // 2
        qkv_sum, up_sum, proj_sum = wide_sum[:, :first], wide_sum[:, first:second], wide_sum[:, second:]
        vectors, up_vector = [vec[t] for t in range(8)], up_vec.reshape(-1)
    else:
        input_grad, down_sum, up_sum, qkv_sum, proj_sum, vectors, up_vector = finish_any(
            size, band_at, query_grad, dk_own, dk_far, dv_own, dv_far, normed, tokens, residual_grad, w_qkv, pieces, first_gain, mlp_sums, up_sums
        )
    return (
        output.reshape(local_shape),
        input_grad.reshape(local_shape),
        vectors[0],
        vectors[1],
        qkv_sum,
        vectors[2],
        vectors[3],
        proj_sum,
        vectors[7],
        vectors[5],
        vectors[6],
        up_sum,
        up_vector,
        down_sum,
        vectors[4],
    )


def solution(mesh):
    size = mesh.shape["dp"]
    placed = (P("dp", "band", None), P("dp", "band"), P("dp", "band", None)) + (P(),) * 13
    split, thin = P("dp", "band"), P("dp")
    wide = P("dp", "band", None)
    return jax.shard_map(
        functools.partial(local, size),
        mesh=mesh,
        in_specs=placed,
        out_specs=(wide, wide, thin, thin, split, thin, thin, split, thin, thin, thin, split, thin, split, thin),
        check_vma=False,
    )
```

```python
import functools

import jax
import jax.numpy as jnp
from jax import lax
from jax.experimental import pallas as pl
from jax.experimental.pallas import tpu as pltpu
from jax.sharding import PartitionSpec as P

EPS = 1e-05
HEADS = 12
HEAD_DIM = 64
NEG_LARGE = -1e30
PAIRS = HEADS // 2
CHUNK = 256
EDGE = 64
MIB = 1 << 20
f32, bf16 = jnp.float32, jnp.bfloat16
NN = (((1,), (0,)), ((), ()))
NT = (((1,), (1,)), ((), ()))


def mm(a, b, dims=NN):
    return lax.dot_general(a, b, dims, preferred_element_type=f32)


def low_lanes(rows):
    return lax.broadcasted_iota(jnp.int32, (rows, 128), 1) < HEAD_DIM


def side_lanes(rows):
    return lax.broadcasted_iota(jnp.int32, (rows, 128), 1) & (HEAD_DIM - 1)


def split3(x):
    high = x.astype(bf16).astype(f32)
    middle = (x - high).astype(bf16).astype(f32)
    return high, middle, x - high - middle


def place(side, parts, base):
    for t, part in enumerate(parts):
        base = jnp.where(side == 16 + t, part, base)
    return base


def as_column(row):
    return jnp.broadcast_to(row, (8, row.shape[1])).T[:, 0:1]


def key_window(seg_own, seg_far, block, BQ, BK):
    own, far = seg_own[...].astype(f32), seg_far[...].astype(f32)

    def below(limit):
        return jnp.sum((own < limit).astype(f32) + (far < limit).astype(f32)).astype(jnp.int32)

    mine = seg_own[:, pl.ds(pl.multiple_of(block * BQ, BQ), BQ)].astype(f32)
    row = lax.broadcasted_iota(jnp.int32, mine.shape, 1)
    lo = (below(jnp.min(mine)) // 128) * 128
    blocks = (below(jnp.max(mine) + 1.0) - lo + BK - 1) // BK
    start = jnp.minimum(lo, 2 * own.shape[1] - blocks * BK)
    early_end = below(jnp.min(jnp.where(row >= EDGE, mine, 99.0)))
    late_start = below(jnp.max(jnp.where(row < BQ - EDGE, mine, -1.0)) + 1.0)
    early = jnp.clip((early_end - start) // BK, 0, blocks)
    late = jnp.clip((start + blocks * BK - late_start) // BK, 0, blocks - early)
    return start, blocks, early, late


def over_blocks(count, early, late, rows, body, paired=False):
    for first, end, part in (
        (0, early, slice(0, EDGE)),
        (early, count - late, slice(0, rows)),
        (count - late, count, slice(rows - EDGE, rows)),
    ):

        def step(j, c, part=part):
            body(j, part)
            return c

        if paired and part == slice(0, rows):

            def two(j, c, first=first, part=part):
                body(first + 2 * j, part)
                body(first + 2 * j + 1, part)
                return c

            pairs = (end - first) // 2
            lax.fori_loop(0, pairs, two, 0)
            first = first + 2 * pairs
        lax.fori_loop(first, end, step, 0)


def fill_pairs(src, dst, rows, low, extra):
    for p in range(PAIRS):
        pair = src[:, p * 128 : (p + 1) * 128]
        dst[2 * p, rows, :] = jnp.where(low, pair, extra)
        dst[2 * p + 1, rows, :] = jnp.where(low, extra, pair)


def fill_keys(band, i, k_own, k_far, v_own, v_far, seg_own, seg_far, kaug, vaug, value_extra):
    local = kaug.shape[1] // 2
    low, side = low_lanes(CHUNK), side_lanes(CHUNK)
    here = pl.ds(pl.multiple_of(i * CHUNK, CHUNK), CHUNK)
    for k, v, seg, first in ((k_own, v_own, seg_own, band), (k_far, v_far, seg_far, 1 - band)):
        rows = pl.ds(pl.multiple_of(first * local + i * CHUNK, CHUNK), CHUNK)
        extra = jnp.where(side < 16, jnp.where(side == as_column(seg[:, here]), 0.0, NEG_LARGE), jnp.where(side < 19, -1.0, 0.0))
        fill_pairs(k, kaug, rows, low, extra.astype(bf16))
        fill_pairs(v, vaug, rows, low, value_extra)


def attend_fwd_kernel(fills, BQ, BK, band_ref, q_ref, k_own, k_far, v_own, v_far,
                      seg_own, seg_far, o_ref, qaug_ref, kaug, vaug, qm, s_all, mx, acc):
    i = pl.program_id(0)

    @pl.when(i < fills)
    def _():
        fill_keys(band_ref[0], i, k_own, k_far, v_own, v_far, seg_own, seg_far, kaug, vaug, jnp.ones((CHUNK, 128), bf16))

    @pl.when(i >= fills)
    def _():
        low, side = low_lanes(BQ), side_lanes(BQ)
        block = i - fills
        ids = as_column(seg_own[:, pl.ds(pl.multiple_of(block * BQ, BQ), BQ)])
        own = (side == ids).astype(f32).astype(bf16)
        for p in range(PAIRS):
            pair = q_ref[:, p * 128 : (p + 1) * 128]
            qm[2 * p] = jnp.where(low, pair, own)
            qm[2 * p + 1] = jnp.where(low, own, pair)
        mx[...] = jnp.full(mx.shape, -3e38, f32)
        acc[...] = jnp.zeros(acc.shape, f32)
        start, count, early, late = key_window(seg_own, seg_far, block, BQ, BK)

        def first(j, part):
            at = pl.multiple_of(start + j * BK, 128)
            out = pl.ds(pl.multiple_of(j * BK, BK), BK)
            for h in range(HEADS):
                s = mm(qm[h, part, :], kaug[h, pl.ds(at, BK), :], NT)
                s_all[h, part, out] = s
                m = mx[h, part, :]
                for t in range(BK // 128):
                    m = jnp.maximum(m, s[:, t * 128 : (t + 1) * 128])
                mx[h, part, :] = m

        over_blocks(count, early, late, BQ, first, True)
        for h in range(HEADS):
            mx[h] = jnp.broadcast_to(jnp.max(mx[h], axis=1, keepdims=True), (BQ, 128))

        def second(j, part):
            at = pl.multiple_of(start + j * BK, 128)
            src = pl.ds(pl.multiple_of(j * BK, BK), BK)
            for h in range(HEADS):
                p = jnp.exp(s_all[h, part, src] - jnp.concatenate([mx[h, part, :]] * (BK // 128), axis=1)).astype(bf16)
                acc[h, part, :] += mm(p, vaug[h, pl.ds(at, BK), :])

        over_blocks(count, early, late, BQ, second)
        ids = (side == ids).astype(f32)
        for p in range(PAIRS):
            even, odd = acc[2 * p], acc[2 * p + 1]
            total = jnp.where(low, pltpu.roll(even, HEAD_DIM, 1), pltpu.roll(odd, HEAD_DIM, 1))
            o_ref[:, p * 128 : (p + 1) * 128] = (jnp.where(low, even, odd) / total).astype(bf16)
            pair = q_ref[:, p * 128 : (p + 1) * 128]
            extra = [place(side, split3(mx[2 * p + e] + jnp.log(sums)), ids).astype(bf16) for e, sums in enumerate((even, odd))]
            qaug_ref[2 * p] = jnp.where(low, pair, extra[0])
            qaug_ref[2 * p + 1] = jnp.where(low, extra[1], pair)


def attend_forward(band, q, seg_own, seg_far, k_own, k_far, v_own, v_far, BQ=256, BK=256):
    rows, width = q.shape
    fills, steps = rows // CHUNK, rows // BQ
    mine = lambda i, *_: (jnp.clip(i - fills, 0, steps - 1), 0)
    fill = lambda i, *_: (jnp.minimum(i, fills - 1), 0)
    wide = pl.BlockSpec((CHUNK, width), fill)
    thin = pl.BlockSpec((1, rows), lambda i, *_: (0, 0))
    return pl.pallas_call(
        functools.partial(attend_fwd_kernel, fills, BQ, BK),
        out_shape=(jax.ShapeDtypeStruct((rows, width), bf16), jax.ShapeDtypeStruct((HEADS, rows, 128), bf16)),
        grid_spec=pltpu.PrefetchScalarGridSpec(
            num_scalar_prefetch=1,
            grid=(fills + steps,),
            in_specs=[pl.BlockSpec((BQ, width), mine), wide, wide, wide, wide, thin, thin],
            out_specs=[pl.BlockSpec((BQ, width), mine), pl.BlockSpec((HEADS, BQ, 128), lambda i, *_: (0, jnp.clip(i - fills, 0, steps - 1), 0))],
            scratch_shapes=[
                pltpu.VMEM((HEADS, 2 * rows, 128), bf16),
                pltpu.VMEM((HEADS, 2 * rows, 128), bf16),
                pltpu.VMEM((HEADS, BQ, 128), bf16),
                pltpu.VMEM((HEADS, BQ, 2 * rows), f32),
                pltpu.VMEM((HEADS, BQ, 128), f32),
                pltpu.VMEM((HEADS, BQ, 128), f32),
            ],
        ),
        compiler_params=pltpu.CompilerParams(vmem_limit_bytes=56 * MIB),
        cost_estimate=pl.CostEstimate(flops=30 * 10**9, bytes_accessed=10 * 10**6, transcendentals=0),
        name="attend_forward",
    )(band, q, k_own, k_far, v_own, v_far, seg_own, seg_far)


def attend_bwd_kernel(fills, steps, BQ, BK, band_ref, qm, do_ref, o_ref,
                      k_own, k_far, v_own, v_far, seg_own, seg_far, carried, dq_ref, dkt_own, dkt_far, dvt_own, dvt_far, carried_out,
                      kaug, vaug, dom, lqt, ldot, eqt, edot, dq_acc, dk_acc, dv_acc):
    i = pl.program_id(0)
    band = band_ref[0]
    local = kaug.shape[1] // 2

    @pl.when(i < fills)
    def _():
        side = side_lanes(CHUNK)
        extra = jnp.where((side >= 16) & (side < 19), -1.0, 0.0).astype(bf16)
        fill_keys(band, i, k_own, k_far, v_own, v_far, seg_own, seg_far, kaug, vaug, extra)
        for part in range(2):
            cols = pl.ds(pl.multiple_of(part * local + i * CHUNK, CHUNK), CHUNK)
            for p in range(PAIRS):
                dk_acc[p, :, cols] = jnp.zeros((128, CHUNK), f32)
                dv_acc[p, :, cols] = jnp.zeros((128, CHUNK), f32)

    @pl.when((i >= fills) & (i < fills + steps))
    def _():
        low, side = low_lanes(BQ), side_lanes(BQ)
        block = i - fills
        carried_out[...] = carried[...]
        lane = lax.broadcasted_iota(jnp.int32, (256, 256), 0) & 127
        column = lax.broadcasted_iota(jnp.int32, (256, 256), 1)
        adder = ((lane < HEAD_DIM) == (column < 128)).astype(f32).astype(bf16)
        for p in range(PAIRS):
            cols = slice(p * 128, (p + 1) * 128)
            q_pair, do_pair = jnp.where(low, qm[2 * p], qm[2 * p + 1]), do_ref[:, cols]
            prod = do_pair.astype(f32) * o_ref[:, cols].astype(f32)
            high = prod.astype(bf16)
            rest = (prod - high.astype(f32)).astype(bf16)
            delta = mm(jnp.concatenate([high, rest], axis=1), adder)
            for e in range(2):
                extra = place(side, split3(delta[:, e * 128 : (e + 1) * 128]), jnp.zeros((BQ, 128), f32)).astype(bf16)
                dom[2 * p + e] = jnp.where(low, do_pair, extra) if e == 0 else jnp.where(low, extra, do_pair)
            for pair, dst, edges in ((q_pair, lqt, eqt), (do_pair, ldot, edot)):
                flipped = pair.T
                upper = lax.broadcasted_iota(jnp.int32, flipped.shape, 0) < HEAD_DIM
                zero = jnp.zeros_like(flipped)
                even, odd = jnp.where(upper, flipped, zero), jnp.where(upper, zero, flipped)
                dst[p, :, 0:BQ] = even
                dst[p, :, BQ : 2 * BQ] = odd
                edges[0, p] = jnp.concatenate([even[:, 0:EDGE], odd[:, 0:EDGE]], axis=1)
                edges[1, p] = jnp.concatenate([even[:, BQ - EDGE :], odd[:, BQ - EDGE :]], axis=1)
        lefts = {-1: (lqt, ldot), 0: (eqt.at[0], edot.at[0]), BQ - EDGE: (eqt.at[1], edot.at[1])}
        dq_acc[...] = jnp.zeros(dq_acc.shape, f32)
        start, count, early, late = key_window(seg_own, seg_far, block, BQ, BK)

        def step(j, part):
            window = pl.ds(pl.multiple_of(start + j * BK, 128), BK)
            left_q, left_do = lefts[part.start if part.stop - part.start < BQ else -1]

            def scores(h):
                return mm(qm[h, part, :], kaug[h, window, :], NT), mm(dom[h, part, :], vaug[h, window, :], NT)

            ahead = scores(0)
            kept = []
            for h in range(HEADS):
                p = h // 2
                s, dp = ahead
                if h + 1 < HEADS:
                    ahead = scores(h + 1)
                prob = jnp.exp(s)
                ds = (prob * dp).astype(bf16)
                kept.append((prob.astype(bf16), ds))
                dq_acc[h, part, :] += mm(ds, kaug[h, window, :])
                if h % 2:
                    dv_acc[p, :, window] += mm(left_do[p], jnp.concatenate([kept[0][0], kept[1][0]], axis=0))
                    dk_acc[p, :, window] += mm(left_q[p], jnp.concatenate([kept[0][1], kept[1][1]], axis=0))
                    kept = []

        over_blocks(count, early, late, BQ, step)
        for p in range(PAIRS):
            pair = jnp.where(low, dq_acc[2 * p], dq_acc[2 * p + 1]) * HEAD_DIM**-0.5
            dq_ref[:, p * 128 : (p + 1) * 128] = pair.astype(bf16)

    @pl.when(i >= fills + steps)
    def _():
        j = i - fills - steps
        for p in range(PAIRS):
            rows = slice(p * 128, (p + 1) * 128)
            for first, dk_out, dv_out in ((band, dkt_own, dvt_own), (1 - band, dkt_far, dvt_far)):
                cols = pl.ds(pl.multiple_of(first * local + j * CHUNK, CHUNK), CHUNK)
                dk_out[rows, :] = dk_acc[p, :, cols].astype(bf16)
                dv_out[rows, :] = dv_acc[p, :, cols].astype(bf16)


def attend_backward(band, carried, qaug, do, o, seg_own, seg_far, k_own, k_far, v_own, v_far, BQ=256, BK=256):
    rows, width = do.shape
    fills, steps = rows // CHUNK, rows // BQ
    mine = lambda i, *_: (jnp.clip(i - fills, 0, steps - 1), 0)
    fill = lambda i, *_: (jnp.minimum(i, fills - 1), 0)
    drain = lambda i, *_: (0, jnp.clip(i - fills - steps, 0, fills - 1))
    wide = pl.BlockSpec((CHUNK, width), fill)
    thin = pl.BlockSpec((1, rows), lambda i, *_: (0, 0))
    block = pl.BlockSpec((BQ, width), mine)
    flat = jax.ShapeDtypeStruct((width, rows), bf16)
    return pl.pallas_call(
        functools.partial(attend_bwd_kernel, fills, steps, BQ, BK),
        out_shape=(jax.ShapeDtypeStruct((rows, width), bf16), flat, flat, flat, flat, jax.ShapeDtypeStruct(carried.shape, carried.dtype)),
        grid_spec=pltpu.PrefetchScalarGridSpec(
            num_scalar_prefetch=1,
            grid=(fills + steps + fills,),
            in_specs=[pl.BlockSpec((HEADS, BQ, 128), lambda i, *_: (0, jnp.clip(i - fills, 0, steps - 1), 0)), block, block, wide, wide, wide, wide, thin, thin, block],
            out_specs=[block] + [pl.BlockSpec((width, CHUNK), drain)] * 4 + [block],
            scratch_shapes=[
                pltpu.VMEM((HEADS, 2 * rows, 128), bf16),
                pltpu.VMEM((HEADS, 2 * rows, 128), bf16),
                pltpu.VMEM((HEADS, BQ, 128), bf16),
                pltpu.VMEM((PAIRS, 128, 2 * BQ), bf16),
                pltpu.VMEM((PAIRS, 128, 2 * BQ), bf16),
                pltpu.VMEM((2, PAIRS, 128, 2 * EDGE), bf16),
                pltpu.VMEM((2, PAIRS, 128, 2 * EDGE), bf16),
                pltpu.VMEM((HEADS, BQ, 128), f32),
                pltpu.VMEM((PAIRS, 128, 2 * rows), f32),
                pltpu.VMEM((PAIRS, 128, 2 * rows), f32),
            ],
        ),
        compiler_params=pltpu.CompilerParams(vmem_limit_bytes=56 * MIB),
        cost_estimate=pl.CostEstimate(flops=45 * 10**9, bytes_accessed=20 * 10**6, transcendentals=0),
        name="attend_backward",
    )(band, qaug, do, o, k_own, k_far, v_own, v_far, seg_own, seg_far, carried)


MESH = pl.DeviceIdType.MESH
TN = (((0,), (0,)), ((), ()))
SLICE = 768


def gelu_and_slope(u):
    below = 0.5 + 0.5 * lax.erf(u * 0.5**0.5)
    return u * below, below + u * jnp.exp(u * u * -0.5) * (0.5 / 3.141592653589793) ** 0.5


def normalize(rows):
    centred = rows - jnp.mean(rows, axis=-1, keepdims=True)
    scale = lax.rsqrt(jnp.mean(centred * centred, axis=-1, keepdims=True) + EPS)
    return centred * scale, scale


def add_sums(ref, row, values, first):
    sums = jnp.sum(values, axis=0, keepdims=True)
    at = slice(row, row + 1)
    ref[at, :] = jnp.where(first, sums, ref[at, :] + sums)


def as_row(ref):
    return ref[...].reshape(1, -1)


def add_low(dst, a, b):
    dst[...] = (a[...].astype(f32) + b[...].astype(f32)).astype(bf16)


def mlp_kernel(sorted_out, blocks, rows, slices, tok_ref, att_ref, cot_ref, wproj, wup, wdown, pbias, gain, shift, ubias, dbias,
               out_ref, rgrad_ref, agrad_ref, sums_ref, usums_ref, *rest):
    outs, scratch = rest[: 8 if sorted_out else 3], rest[8 if sorted_out else 3 :]
    hid, ugr, n2s, bgs, ags, ats, d_own, d_far, d_in, u_in, p_own, p_far, p_in, send_sem, recv_sem = scratch
    i = pl.program_id(0)
    me, band = lax.axis_index("dp"), lax.axis_index("band")
    other = (me, 1 - band)
    width = tok_ref.shape[1]
    half, per_half = width // 2, slices // 2

    def push(t, src, dst):
        return pltpu.make_async_remote_copy(
            src_ref=src, dst_ref=dst, send_sem=send_sem.at[t], recv_sem=recv_sem.at[t], device_id=other, device_id_type=MESH
        )

    def d_copy(j):
        at = pl.ds(pl.multiple_of(j * SLICE, SLICE), SLICE)
        return push(j, d_far.at[at, :], d_in.at[at, :])

    def u_copy(c):
        return push(slices + c, hid.at[0:width, pl.ds(pl.multiple_of(c * SLICE, SLICE), SLICE)], u_in.at[c])

    def p_copy():
        return push(slices + per_half, p_far, p_in)

    @pl.when(i == 0)
    def _():
        barrier = pltpu.get_barrier_semaphore()
        pl.semaphore_signal(barrier, inc=1, device_id=other, device_id_type=MESH)
        pl.semaphore_wait(barrier, 1)

    @pl.when(i < blocks)
    def _():
        here = pl.ds(pl.multiple_of(i * rows, rows), rows)
        first = i == 0
        att = att_ref[...]
        ats[here, :] = att
        residual = tok_ref[...] + mm(att, wproj[...]) + as_row(pbias)
        xhat, scale = normalize(residual)
        n2 = (xhat * as_row(gain) + as_row(shift)).astype(bf16)
        n2s[here, :] = n2
        cot = cot_ref[...]
        bg = cot.astype(bf16)
        bgs[here, :] = bg
        add_sums(sums_ref, 0, bg.astype(f32), first)
        for c in range(slices):
            cols = slice(c * SLICE, (c + 1) * SLICE)
            hidden, slope = gelu_and_slope(mm(n2, wup[:, cols]) + ubias[cols].reshape(1, -1))
            hid[here, cols] = hidden.astype(bf16)
            grad = (mm(bg, wdown[cols, :], NT) * slope).astype(bf16)
            ugr[here, cols] = grad
            sums = jnp.sum(grad.astype(f32), axis=0, keepdims=True)
            usums_ref[0:1, cols] = jnp.where(first, sums, usums_ref[0:1, cols] + sums)
        out_ref[...] = residual + mm(hid[here, :], wdown[...]) + as_row(dbias)
        e = mm(ugr[here, :], wup[...], NT)
        add_sums(sums_ref, 1, e * xhat, first)
        add_sums(sums_ref, 2, e, first)
        f = e * as_row(gain)
        rgrad = cot + scale * (f - jnp.mean(f, axis=-1, keepdims=True) - xhat * jnp.mean(f * xhat, axis=-1, keepdims=True))
        rgrad_ref[...] = rgrad
        ag = rgrad.astype(bf16)
        ags[here, :] = ag
        add_sums(sums_ref, 3, ag.astype(f32), first)
        agrad_ref[...] = mm(ag, wproj[...], NT).astype(bf16)

    def columns(grad, own, far, at):
        left, right = grad[:, :half].astype(bf16), grad[:, half:].astype(bf16)
        own[at, :] = jnp.where(band == 0, left, right)
        far[at, :] = jnp.where(band == 0, right, left)

    @pl.when((i >= blocks) & (i < blocks + slices))
    def _():
        j = i - blocks
        at = pl.ds(pl.multiple_of(j * SLICE, SLICE), SLICE)
        columns(mm(hid[:, at], bgs[...], TN), d_own, d_far, at)
        d_copy(j).start()

    def up_slice(which):
        at = pl.ds(pl.multiple_of(which * SLICE, SLICE), SLICE)
        return mm(n2s[...], ugr[:, at], TN).astype(bf16)

    x, y = me & 1, (me >> 1) & 1

    z = me >> 2
    shard = width // 16

    corners = [(y ^ (q >> 1)) * 2 + (x ^ (q & 1)) for q in range(4)]

    def down_arrived(j):
        d_copy(j).wait_recv()
        if not sorted_out:
            at = pl.ds(pl.multiple_of(j * SLICE, SLICE), SLICE)
            add_low(outs[0].at[at, :], d_own.at[at, :], d_in.at[at, :])
            return
        for q in range(4):
            at = pl.ds(pl.multiple_of(j * SLICE + corners[q] * 4 * shard, shard), 2 * shard)
            add_low(outs[q].at[j, 0 : 2 * shard], d_own.at[at, :], d_in.at[at, :])

    def down_along_z(d):
        if sorted_out:
            for t in range(4):
                at = pl.ds(pl.multiple_of((z ^ d) * SLICE + t * 4 * shard + 2 * shard, shard), 2 * shard)
                add_low(outs[4 + d].at[t // 2, t % 2, 0 : 2 * shard], d_own.at[at, :], d_in.at[at, :])

    def up_arrived(c):
        u_copy(c).wait_recv()
        own = hid.at[0:width, (per_half + c) * SLICE : (per_half + c + 1) * SLICE]
        if not sorted_out:
            add_low(outs[1].at[:, c * SLICE : (c + 1) * SLICE], own, u_in.at[c])
            return

        def fold(dst, s, part):
            at = pl.ds(pl.multiple_of(s * shard, shard), shard)
            cols = slice(part * half, (part + 1) * half)
            add_low(dst.at[(2 + part) * shard : (3 + part) * shard], own.at[at, cols], u_in.at[c, at, cols])

        def near(zz, carry):
            for q in range(4):
                for part in range(2):
                    fold(outs[q].at[zz], zz * 4 + corners[q], part)
            return carry

        def along(s, carry):
            for d in range(4):
                for part in range(2):
                    fold(outs[4 + d].at[s >> 1, s & 1], (z ^ d) * 4 + s, part)
            return carry

        lax.fori_loop(0, 4, near if c == 0 else along, 0, unroll=2)

    def proj_arrived():
        p_copy().wait_recv()
        if not sorted_out:
            add_low(outs[2], p_own, p_in)
            return

        def one(zz, carry):
            for q in range(4):
                at = pl.ds(pl.multiple_of((zz * 4 + corners[q]) * shard, shard), shard)
                add_low(outs[q].at[zz, 4 * shard : 5 * shard], p_own.at[at, :], p_in.at[at, :])
            return carry

        lax.fori_loop(0, 4, one, 0, unroll=2)

    middle = blocks + slices
    @pl.when(i == middle)
    def _():
        columns(mm(ats[...], ags[...], TN), p_own, p_far, slice(None))
        p_copy().start()

    for c in range(per_half):
        at = slice(c * SLICE, (c + 1) * SLICE)

        @pl.when(i == middle + 1 + c)
        def _(c=c, at=at):
            hid[0:width, at] = up_slice((1 - band) * per_half + c)
            u_copy(c).start()
            for j in range(2 * c, 2 * c + 2):
                down_arrived(j)

        @pl.when(i == middle + 1 + per_half + c)
        def _(c=c):
            hid[0:width, (per_half + c) * SLICE : (per_half + c + 1) * SLICE] = up_slice(band * per_half + c)
            for d in range(2 * c, 2 * c + 2):
                down_along_z(d)
            if c == 0:
                proj_arrived()
            else:
                up_arrived(c - 1)

    @pl.when(i == middle + slices)
    def _():
        up_arrived(per_half - 1)
        for j in range(slices):
            d_copy(j).wait_send()
        for c in range(per_half):
            u_copy(c).wait_send()
        p_copy().wait_send()


def mlp(size, tokens, attended, cotangent, w_proj, w_up, w_down, proj_bias, gain, shift, up_bias, down_bias, rows=256):
    count, width = tokens.shape
    ff = w_up.shape[1]
    blocks, slices = count // rows, ff // SLICE
    half, per_half = width // 2, slices // 2
    sorted_out = size == 16
    one = pl.Buffered(1)
    mine = lambda i: (jnp.minimum(i, blocks - 1), 0)
    block = pl.BlockSpec((rows, width), mine)

    def full(a):
        return pl.BlockSpec(a.shape, lambda i: (0,) * len(a.shape), pipeline_mode=one)

    vectors = (proj_bias, gain, shift, up_bias, down_bias)
    shape = jax.ShapeDtypeStruct
    if sorted_out:
        sixteenth = width // 16
        pieces = [shape((4, 5 * sixteenth, half), bf16)] * 4
        pieces += [shape((2, 2, 4 * sixteenth, half), bf16)] * 4
    else:
        pieces = [shape((ff, half), bf16), shape((width, ff // 2), bf16), shape((width, half), bf16)]
    kept = [shape((8, width), f32), shape((8, ff), f32)] + pieces
    low = lambda *s: pltpu.VMEM(s, bf16)
    copies = slices + per_half + 1
    return pl.pallas_call(
        functools.partial(mlp_kernel, sorted_out, blocks, rows, slices),
        out_shape=[shape((count, width), f32), shape((count, width), f32), shape((count, width), bf16)] + kept,
        grid=(blocks + 2 * slices + 1,),
        in_specs=[block, block, block] + [full(a) for a in (w_proj, w_up, w_down, *vectors)],
        out_specs=[block, block, block] + [full(a) for a in kept],
        scratch_shapes=[
            low(count, ff),
            low(count, ff),
            *([low(count, width)] * 4),
            *([low(ff, half)] * 3),
            low(per_half, width, SLICE),
            *([low(width, half)] * 3),
            pltpu.SemaphoreType.DMA((copies,)),
            pltpu.SemaphoreType.DMA((copies,)),
        ],
        compiler_params=pltpu.CompilerParams(vmem_limit_bytes=62 * MIB, collective_id=1, has_side_effects=True),
        cost_estimate=pl.CostEstimate(flops=40 * 10**9, bytes_accessed=40 * 10**6, transcendentals=0),
        name="mlp",
    )(tokens, attended, cotangent, w_proj, w_up, w_down, *vectors)


def qkv_kernel(steps, tok_ref, seg_ref, w_ref, gain, shift, qbias, vbias, q_ref, k_ref, v_ref, n_ref, k_far, v_far, seg_far,
               n_all, k_all, v_all, send_sem, recv_sem):
    i = pl.program_id(0)
    last = pl.num_programs(0) - 1
    other = (lax.axis_index("dp"), 1 - lax.axis_index("band"))
    rows, width = tok_ref.shape

    def push(t, src, dst):
        return pltpu.make_async_remote_copy(
            src_ref=src, dst_ref=dst, send_sem=send_sem.at[t], recv_sem=recv_sem.at[t], device_id=other, device_id_type=MESH
        )

    def copies(j):
        at = pl.ds(pl.multiple_of(j * rows, rows), rows)
        return push(2 * j, k_all.at[at, :], k_far.at[at, :]), push(2 * j + 1, v_all.at[at, :], v_far.at[at, :])

    segs = push(send_sem.shape[0] - 1, seg_ref, seg_far)

    @pl.when(i == 0)
    def _():
        barrier = pltpu.get_barrier_semaphore()
        pl.semaphore_signal(barrier, inc=1, device_id=other, device_id_type=MESH)

    @pl.when(i == 1)
    def _():
        pl.semaphore_wait(pltpu.get_barrier_semaphore(), 1)
        segs.start()
        for copy in copies(0):
            copy.start()

    @pl.when(i < steps)
    def _():
        here = pl.ds(pl.multiple_of(i * rows, rows), rows)
        xhat, _ = normalize(tok_ref[...])
        n1 = (xhat * as_row(gain) + as_row(shift)).astype(bf16)
        n_ref[...] = n1
        n_all[here, :] = n1
        k = mm(n1, w_ref[:, width : 2 * width]).astype(bf16)
        k_ref[...] = k
        k_all[here, :] = k
        v = (mm(n1, w_ref[:, 2 * width :]) + as_row(vbias)).astype(bf16)
        v_ref[...] = v
        v_all[here, :] = v

    @pl.when((i >= 1) & (i < steps))
    def _():
        for copy in copies(i):
            copy.start()

    @pl.when(i >= steps)
    def _():
        here = pl.ds(pl.multiple_of((i - steps) * rows, rows), rows)
        q = (mm(n_all[here, :], w_ref[:, :width]) + as_row(qbias)).astype(bf16)
        q_ref[...] = q * jnp.asarray(HEAD_DIM**-0.5, bf16)

    @pl.when(i == last)
    def _():
        segs.wait()
        for j in range(k_all.shape[0] // rows):
            for copy in copies(j):
                copy.wait()


def project_qkv(tokens, seg, w_qkv, gain, shift, query_bias, value_bias, rows=256):
    count, width = tokens.shape
    one = pl.Buffered(1)
    steps = count // rows
    block = pl.BlockSpec((rows, width), lambda i: (jnp.minimum(i, steps - 1), 0))
    late = pl.BlockSpec((rows, width), lambda i: (jnp.maximum(i - steps, 0), 0))
    vectors = (gain, shift, query_bias, value_bias)
    hbm = pl.BlockSpec(memory_space=pl.ANY)
    low = jax.ShapeDtypeStruct((count, width), bf16)
    return pl.pallas_call(
        functools.partial(qkv_kernel, steps),
        out_shape=(low,) * 6 + (jax.ShapeDtypeStruct(seg.shape, seg.dtype),),
        grid=(2 * steps,),
        in_specs=[block, hbm] + [pl.BlockSpec(a.shape, lambda i, n=a.ndim: (0,) * n, pipeline_mode=one) for a in (w_qkv, *vectors)],
        out_specs=[late] + [block] * 3 + [hbm] * 3,
        scratch_shapes=[
            pltpu.VMEM((count, width), bf16),
            pltpu.VMEM((count, width), bf16),
            pltpu.VMEM((count, width), bf16),
            pltpu.SemaphoreType.DMA((2 * steps + 1,)),
            pltpu.SemaphoreType.DMA((2 * steps + 1,)),
        ],
        compiler_params=pltpu.CompilerParams(vmem_limit_bytes=60 * MIB, collective_id=2, has_side_effects=True),
        cost_estimate=pl.CostEstimate(flops=4 * 10**9, bytes_accessed=13 * 10**6, transcendentals=0),
        name="project_qkv",
    )(tokens, seg, w_qkv, *vectors)


def qkv_grad_kernel(blocks, rows, band_ref, dq_ref, dk_own, dk_far, dv_own, dv_far, n_ref, packed_ref, own_ref, far_ref, sums_ref, packed):
    i = pl.program_id(0)
    band = band_ref[0]
    width = dq_ref.shape[1]
    half = own_ref.shape[1]

    @pl.when(i < blocks)
    def _():
        here = pl.ds(pl.multiple_of(i * rows, rows), rows)
        first = i == 0
        dq = dq_ref[...]
        packed_ref[:, :width] = dq
        packed[here, :width] = dq
        add_sums(sums_ref, 0, dq.astype(f32), first)
        for t, (own, far) in enumerate(((dk_own, dk_far), (dv_own, dv_far))):
            for p in range(width // 128):
                at = slice(p * 128, (p + 1) * 128)
                to = slice((t + 1) * width + p * 128, (t + 1) * width + (p + 1) * 128)
                turned = (own[at, :].astype(f32) + far[at, :].astype(f32)).astype(bf16).T
                packed_ref[:, to] = turned
                packed[here, to] = turned
        add_sums(sums_ref, 1, packed_ref[:, 2 * width :].astype(f32), first)

    def columns(which):
        at = pl.ds(pl.multiple_of(which * half, 128), half)
        return mm(n_ref[...], packed[:, at], TN).astype(bf16)

    @pl.when(i == blocks)
    def _():
        far_ref[...] = columns(1 - band)

    @pl.when(i == blocks + 1)
    def _():
        own_ref[...] = columns(band)


def qkv_grads(band, dq, dk_own, dk_far, dv_own, dv_far, normed, rows=256):
    count, width = dq.shape
    blocks = count // rows
    half = 3 * width // 2
    one = pl.Buffered(1)
    mine = lambda i, *_: (jnp.minimum(i, blocks - 1), 0)
    flip = lambda i, *_: (0, jnp.minimum(i, blocks - 1))
    whole = lambda i, *_: (0, 0)
    shape = jax.ShapeDtypeStruct
    return pl.pallas_call(
        functools.partial(qkv_grad_kernel, blocks, rows),
        out_shape=(shape((count, 3 * width), bf16), shape((width, half), bf16), shape((width, half), bf16), shape((8, width), f32)),
        grid_spec=pltpu.PrefetchScalarGridSpec(
            num_scalar_prefetch=1,
            grid=(blocks + 2,),
            in_specs=[pl.BlockSpec((rows, width), mine)]
            + [pl.BlockSpec((width, rows), flip)] * 4
            + [pl.BlockSpec((count, width), whole, pipeline_mode=one)],
            out_specs=[
                pl.BlockSpec((rows, 3 * width), mine),
                pl.BlockSpec((width, half), whole, pipeline_mode=one),
                pl.BlockSpec((width, half), whole, pipeline_mode=one),
                pl.BlockSpec((8, width), whole, pipeline_mode=one),
            ],
            scratch_shapes=[pltpu.VMEM((count, 3 * width), bf16)],
        ),
        compiler_params=pltpu.CompilerParams(vmem_limit_bytes=40 * MIB),
        cost_estimate=pl.CostEstimate(flops=8 * 10**9, bytes_accessed=18 * 10**6, transcendentals=0),
        name="qkv_grads",
    )(band, dq, dk_own, dk_far, dv_own, dv_far, normed)


def input_grad_kernel(packed_ref, tok_ref, rgrad_ref, w_ref, gain, out_ref, sums_ref):
    first = pl.program_id(0) == 0
    e = mm(packed_ref[...], w_ref[...], NT)
    xhat, scale = normalize(tok_ref[...])
    add_sums(sums_ref, 0, e * xhat, first)
    add_sums(sums_ref, 1, e, first)
    f = e * gain[...]
    back = scale * (f - jnp.mean(f, axis=-1, keepdims=True) - xhat * jnp.mean(f * xhat, axis=-1, keepdims=True))
    out_ref[...] = rgrad_ref[...] + back


def input_grads(packed, tokens, rgrad, w_qkv, gain, rows=256):
    count, width = tokens.shape
    one = pl.Buffered(1)
    block = pl.BlockSpec((rows, width), lambda i: (i, 0))
    return pl.pallas_call(
        input_grad_kernel,
        out_shape=(jax.ShapeDtypeStruct((count, width), f32), jax.ShapeDtypeStruct((8, width), f32)),
        grid=(count // rows,),
        in_specs=[
            pl.BlockSpec((rows, packed.shape[1]), lambda i: (i, 0)),
            block,
            block,
            pl.BlockSpec(w_qkv.shape, lambda i: (0, 0), pipeline_mode=one),
            pl.BlockSpec((1, width), lambda i: (0, 0), pipeline_mode=one),
        ],
        out_specs=[block, pl.BlockSpec((8, width), lambda i: (0, 0), pipeline_mode=one)],
        compiler_params=pltpu.CompilerParams(vmem_limit_bytes=32 * MIB),
        cost_estimate=pl.CostEstimate(flops=6 * 10**9, bytes_accessed=18 * 10**6, transcendentals=0),
        name="input_grads",
    )(packed, tokens, rgrad, w_qkv, gain.reshape(1, -1))


def finish_kernel(
    dq_hbm, dko_hbm, dkf_hbm, dvo_hbm, dvf_hbm, n_hbm, tok_hbm, rgrad_hbm, w_hbm, pk_hbm, ck_hbm, c1_hbm, px_hbm, py_hbm, pd_hbm, c2_hbm, c3_hbm, gain, msums, usums,
    out_hbm, down_out, wide_out, vec_out, usum_out,
    packed, dko, dko_in, dvo, dvo_in, n1, tok, out, wq, pk, p_one, ck, cols, far_in, tail,
    c_one, c_two, p_thr, c_thr, ta_one, tb_one, ta_two, tb_two, ta_thr, tb_thr, vec, vec_band, vec_x, vec_y, vec_z,
    load_sem, store_sem, swap_send, swap_recv, send, recv, vsend, vrecv,
):
    me = lax.axis_index("dp")
    band = lax.axis_index("band")
    x, y, z = me & 1, (me >> 1) & 1, me >> 2
    rows, width = tok.shape
    half = far_in.shape[-1]
    peer_band = (me, 1 - band)
    peer_x = (me ^ 1, band)
    peer_y = (me ^ 2, band)
    peers_z = [(((z + d) & 3) * 4 + (me & 3), band) for d in (1, 2, 3)]

    def load(t, src, dst):
        return pltpu.make_async_copy(src, dst, load_sem.at[t])

    loads = {
        "queries": (load(6, dq_hbm, packed.at[:, 0:width]), load(7, n_hbm, n1)),
        "keys": (load(4, dko_hbm, dko), load(5, dvo_hbm, dvo)),
        "early": (load(0, pk_hbm, pk), load(1, px_hbm, p_one.at[0]), load(2, py_hbm, p_one.at[1]), load(3, pd_hbm, p_one.at[2])),
        "along": (load(8, ck_hbm, ck), load(13, c2_hbm, c_one.at[1]), load(14, c3_hbm, c_one.at[2])),
        "rows": (load(10, w_hbm, wq), load(11, tok_hbm, tok), load(12, rgrad_hbm, out)),
    }

    def fetch(name):
        for copy in loads[name]:
            copy.start()

    def ready(name):
        for copy in loads[name]:
            copy.wait()

    for name in ("queries", "keys", "early"):
        fetch(name)

    barrier = pltpu.get_barrier_semaphore()
    for peer in (peer_band, peer_x, peer_y, *peers_z):
        pl.semaphore_signal(barrier, inc=1, device_id=peer, device_id_type=MESH)
    pl.semaphore_wait(barrier, 6)

    pending = []

    def push(src, dst, peer, s, r):
        copy = pltpu.make_async_remote_copy(src_ref=src, dst_ref=dst, send_sem=s, recv_sem=r, device_id=peer, device_id_type=MESH)
        copy.start()
        pending.append(copy)
        return copy

    swap_k = push(dkf_hbm, dko_in, peer_band, swap_send.at[0], swap_recv.at[0])
    swap_v = push(dvf_hbm, dvo_in, peer_band, swap_send.at[1], swap_recv.at[1])
    c_near = push(c1_hbm, c_one.at[0], (me ^ 4, band), send.at[2, 2], recv.at[2, 2])

    def put(dst, src):
        dst[...] = src[...]

    def each_shard(body):
        def step(s, c):
            body(s >> 2, (s >> 1) & 1, s & 1)
            return c

        lax.fori_loop(0, 16, step, 0, unroll=4)

    def second_stage(t, kept, one, two, mine, peer):
        def total(s, c):
            add_low(one.at[s >> 1, s & 1], one.at[s >> 1, s & 1], kept(s >> 1, s & 1))
            return c

        lax.fori_loop(0, 8, total, 0, unroll=True)
        return push(one.at[:, 1 - mine], two, peer, send.at[t, 0], recv.at[t, 0])

    def third_stage(t, one, two, three, mine, copy):
        copy.wait_recv()

        def total(zz, c):
            add_low(two.at[zz], two.at[zz], one.at[zz, mine])
            return c

        lax.fori_loop(0, 4, total, 0, unroll=True)
        return [push(two.at[(z + d) & 3], three.at[d - 1], peers_z[d - 1], send.at[t, d], recv.at[t, d]) for d in (1, 2, 3)]

    def last(two, three, copies):
        for copy in copies:
            copy.wait_recv()
        total = two[z].astype(f32)
        for d in range(3):
            total = total + three[d].astype(f32)
        return total

    def columns(t):
        cols[:, :, :, :, t * width : (t + 1) * width] = (
            mm(n1[...], packed[:, t * width : (t + 1) * width], TN).astype(bf16).reshape(cols.shape[:-1] + (width,))
        )

    def turn(t, own, other):
        def step(i, c):
            here = pl.ds(pl.multiple_of(i * 256, 256), 256)
            for p in range(width // 128):
                at = slice(p * 128, (p + 1) * 128)
                turned = (own[at, here].astype(f32) + other[at, here].astype(f32)).astype(bf16).T
                packed[here, t * width + p * 128 : t * width + (p + 1) * 128] = turned
            return c

        lax.fori_loop(0, rows // 256, step, 0, unroll=2)

    def swap(t, start, size, to):
        return pltpu.make_async_remote_copy(
            src_ref=cols.at[:, :, :, :, pl.ds(pl.multiple_of(start, 128), size)],
            dst_ref=far_in.at[:, :, :, :, pl.ds(pl.multiple_of(to, 128), size)],
            send_sem=swap_send.at[t],
            recv_sem=swap_recv.at[t],
            device_id=peer_band,
            device_id_type=MESH,
        )

    third = width // 2
    swap_near = swap(2, (3 - band) * third, third, band * width)
    swap_wide = swap(3, (1 - band) * 2 * width, width, (1 - band) * third)
    ready("queries")
    columns(0)
    fetch("along")
    fetch("rows")

    @pl.when(band == 1)
    def _():
        swap_wide.start()

    ready("early")

    def plane(zz, c):
        total = pk[zz].astype(f32)
        for t in range(3):
            total = total + p_one[t, zz].astype(f32)
        pk[zz] = total.astype(bf16)
        return c

    lax.fori_loop(0, 4, plane, 0, unroll=True)
    p_copies = [push(pk.at[(z + d) & 3], p_thr.at[d - 1], peers_z[d - 1], send.at[0, d], recv.at[0, d]) for d in (1, 2, 3)]
    ready("keys")
    swap_k.wait_recv()
    turn(1, dko, dko_in)
    columns(1)
    swap_near.start()
    swap_v.wait_recv()
    turn(2, dvo, dvo_in)
    columns(2)

    @pl.when(band == 0)
    def _():
        swap_wide.start()

    swap_near.wait()
    swap_wide.wait()
    mine = pl.ds(pl.multiple_of(band * half, 128), half)
    each_shard(lambda i, j, k: add_low(tail.at[i, j, k], cols.at[i, j, k, :, mine], far_in.at[i, j, k]))
    cut = ta_one.shape[-1]
    ta_first = push(tail.at[:, :, 1 - x, :, 0:cut], ta_one, peer_x, send.at[3, 4], recv.at[3, 4])
    tb_first = push(tail.at[:, 1 - y, :, :, cut:half], tb_one, peer_y, send.at[4, 4], recv.at[4, 4])

    ready("rows")
    vec[...] = jnp.zeros(vec.shape, f32)

    def rows_back(i, c):
        here = pl.ds(pl.multiple_of(i * 256, 256), 256)
        e = mm(packed[here, :], wq[...], NT)
        xhat, scale = normalize(tok[here, :])
        vec[0:1, :] = vec[0:1, :] + jnp.sum(e * xhat, axis=0, keepdims=True)
        vec[1:2, :] = vec[1:2, :] + jnp.sum(e, axis=0, keepdims=True)
        vec[2:3, :] = vec[2:3, :] + jnp.sum(packed[here, 0:width].astype(f32), axis=0, keepdims=True)
        vec[3:4, :] = vec[3:4, :] + jnp.sum(packed[here, 2 * width : 3 * width].astype(f32), axis=0, keepdims=True)
        f = e * as_row(gain)
        back = scale * (f - jnp.mean(f, axis=-1, keepdims=True) - xhat * jnp.mean(f * xhat, axis=-1, keepdims=True))
        out[here, :] = out[here, :] + back
        return c

    lax.fori_loop(0, rows // 256, rows_back, 0)
    store = pltpu.make_async_copy(out, out_hbm, store_sem)
    store.start()
    vec[4:8, :] = msums[0:4, :]
    for t in range(usums.shape[1] // width):
        vec[8 + t : 9 + t, :] = usums[0:1, t * width : (t + 1) * width]
    v_band = push(vec, vec_band, peer_band, vsend.at[0], vrecv.at[0])
    v_band.wait()
    vec_band[...] = vec[...] + vec_band[...]
    v_z = [push(vec_band, vec_z.at[d], peers_z[d], vsend.at[3 + d], vrecv.at[3 + d]) for d in range(3)]
    ta_first.wait_recv()
    ta_copy = second_stage(3, lambda i, j: tail.at[i, j, x, :, 0:cut], ta_one, ta_two, y, peer_y)
    tb_first.wait_recv()
    tb_copy = second_stage(4, lambda i, j: tail.at[i, y, j, :, cut:half], tb_one, tb_two, x, peer_x)
    for copy in v_z:
        copy.wait()
    vec_z[0] = vec_band[...] + vec_z[0] + vec_z[1] + vec_z[2]
    v_x = push(vec_z.at[0], vec_x, peer_x, vsend.at[1], vrecv.at[1])
    c_near.wait_recv()
    ready("along")

    def along(s, c):
        i, j = s >> 1, s & 1
        total = ck[i, j].astype(f32)
        for d in range(3):
            total = total + c_one[d, i, j].astype(f32)
        ck[i, j] = total.astype(bf16)
        return c

    lax.fori_loop(0, 4, along, 0, unroll=True)
    c_copy = push(ck.at[:, 1 - x], c_two, peer_x, send.at[2, 0], recv.at[2, 0])

    ta_copies = third_stage(3, ta_one, ta_two, ta_thr, y, ta_copy)
    tb_copies = third_stage(4, tb_one, tb_two, tb_thr, x, tb_copy)
    v_x.wait()
    vec_x[...] = vec_z[0] + vec_x[...]
    v_y = push(vec_x, vec_y, peer_y, vsend.at[2], vrecv.at[2])
    c_copy.wait_recv()
    add_low(c_two.at[0], c_two.at[0], ck.at[0, x])
    add_low(c_two.at[1], c_two.at[1], ck.at[1, x])
    c_last = push(c_two.at[1 - y], c_thr, peer_y, send.at[2, 1], recv.at[2, 1])
    v_y.wait()
    vec[...] = vec_x[...] + vec_y[...]
    shard = vec_out.shape[1]
    vec_out[...] = pltpu.roll(vec[0:8, :], width - me * shard, 1)[:, 0:shard]
    wide = usum_out.shape[1]
    per_row = width // wide
    row = vec[pl.ds(8 + me // per_row, 1), :]
    usum_out[...] = pltpu.roll(jnp.broadcast_to(row, (8, width)), width - (me % per_row) * wide, 1)[0:1, 0:wide]
    shard = width // 16
    p_sum = last(pk, p_thr, p_copies)
    c_last.wait_recv()
    c_sum = c_two[y].astype(f32) + c_thr[...].astype(f32)
    down_out[0 : 2 * shard, :] = p_sum[0 : 2 * shard]
    down_out[2 * shard : 4 * shard, :] = c_sum[0 : 2 * shard]
    ups = [part[t * shard : (t + 1) * shard] for part in (p_sum, c_sum) for t in (2, 3)]
    for t, part in enumerate(ups):
        wide_out[:, half + t * third : half + (t + 1) * third] = part
    wide_out[:, half + 4 * third :] = p_sum[4 * shard : 5 * shard]
    wide_out[:, 0:cut] = last(ta_two, ta_thr, ta_copies)
    wide_out[:, cut:half] = last(tb_two, tb_thr, tb_copies)
    done = {id(c) for c in (v_band, v_x, v_y, *v_z)}
    for copy in pending:
        if id(copy) not in done:
            copy.wait_send()
    store.wait()


def finish(dq, dk_own, dk_far, dv_own, dv_far, normed, tokens, rgrad, w_qkv, pieces, gain, msums, usums):
    rows, width = tokens.shape
    ff = usums.shape[1]
    half = 3 * width // 2
    shards = (4, 2, 2)
    third, shard = width // 2, width // 16
    q_shape = shards + (shard, half)
    p_piece, c_piece = (5 * shard, third), (4 * shard, third)
    cut = half // 256 * 128 + 128
    ta_piece, tb_piece = (shard, cut), (shard, half - cut)
    hbm, vmem = pl.BlockSpec(memory_space=pl.ANY), pl.BlockSpec(memory_space=pltpu.VMEM)
    shape = jax.ShapeDtypeStruct
    low = lambda *s: pltpu.VMEM(s, bf16)
    dma = pltpu.SemaphoreType.DMA
    return pl.pallas_call(
        finish_kernel,
        out_shape=(
            shape((rows, width), f32),
            shape((ff // 16, width // 2), f32),
            shape((width // 16, half + ff // 2 + width // 2), f32),
            shape((8, width // 16), f32),
            shape((1, ff // 16), f32),
        ),
        in_specs=[hbm] * 17 + [vmem] * 3,
        out_specs=[hbm] + [vmem] * 4,
        scratch_shapes=[
            low(rows, 3 * width),
            *([low(width, rows)] * 4),
            low(rows, width),
            pltpu.VMEM((rows, width), f32),
            pltpu.VMEM((rows, width), f32),
            low(width, 3 * width),
            low(4, *p_piece),
            low(3, 4, *p_piece),
            low(2, 2, *c_piece),
            low(*shards, shard, 3 * width),
            low(*q_shape),
            low(*q_shape),
            low(3, 2, 2, *c_piece),
            low(2, *c_piece),
            low(3, *p_piece),
            low(*c_piece),
            low(4, 2, *ta_piece),
            low(4, 2, *tb_piece),
            low(4, *ta_piece),
            low(4, *tb_piece),
            low(3, *ta_piece),
            low(3, *tb_piece),
            pltpu.VMEM((16, width), f32),
            pltpu.VMEM((16, width), f32),
            pltpu.VMEM((16, width), f32),
            pltpu.VMEM((16, width), f32),
            pltpu.VMEM((3, 16, width), f32),
            dma((16,)),
            dma,
            dma((4,)),
            dma((4,)),
            dma((5, 5)),
            dma((5, 5)),
            dma((6,)),
            dma((6,)),
        ],
        compiler_params=pltpu.CompilerParams(vmem_limit_bytes=52 * MIB, collective_id=0, has_side_effects=True),
        cost_estimate=pl.CostEstimate(flops=20 * 10**9, bytes_accessed=40 * 10**6, transcendentals=0),
        name="finish",
    )(dq, dk_own, dk_far, dv_own, dv_far, normed, tokens, rgrad, w_qkv, *pieces,
      gain, msums, usums)


def swap_band(x):
    return lax.ppermute(x, "band", [(0, 1), (1, 0)])


def pick(x, which, axis):
    return lax.dynamic_index_in_dim(x, which, axis, keepdims=False)


def halve(x, axis, bit, size):
    mine = (lax.axis_index("dp") >> bit) & 1
    arrived = lax.ppermute(pick(x, 1 - mine, axis), "dp", [(i, i ^ (1 << bit)) for i in range(size)])
    return pick(x, mine, axis).astype(f32) + arrived.astype(f32)


class Reduction:
    def __init__(self, x, order, size):
        rows, columns = x.shape
        levels = size.bit_length() - 1
        self.size = size
        self.x = x.reshape((2,) * levels + (rows // size, columns))
        self.left = list(range(levels - 1, -1, -1))
        self.order = list(order)

    def step(self):
        if self.order:
            bit = self.order.pop(0)
            x = halve(self.x, self.left.index(bit), bit, self.size)
            self.left.remove(bit)
            self.x = x.astype(bf16) if self.left else x

    def finish(self):
        while self.order:
            self.step()
        return self.x


def finish_any(size, band_at, query_grad, dk_own, dk_far, dv_own, dv_far, normed, tokens, residual_grad, w_qkv, pieces, gain, msums, usums):
    width = tokens.shape[1]
    rising = list(range(size.bit_length() - 1))
    turned = [1, 0] + rising[2:]
    packed, qkv_own, qkv_far, qkv_sums = qkv_grads(
        band_at, query_grad, dk_own, swap_band(dk_far), dv_own, swap_band(dv_far), normed
    )
    input_grad, first_sums = input_grads(packed, tokens, residual_grad, w_qkv, gain)

    def total(x, order):
        return Reduction(x, order, size).finish()

    def join(own, far):
        return (own.astype(f32) + swap_band(far).astype(f32)).astype(bf16)

    tall = jnp.concatenate([first_sums[:2], qkv_sums[:2], msums[:4]], axis=0)
    thin = jnp.concatenate([tall.T, usums[0].reshape(width, -1)], axis=1)
    thin = jnp.pad(thin, ((0, 0), (0, 128 - thin.shape[1]))).astype(bf16)
    thin_sum = total(join(thin, thin), turned)
    ups = usums.shape[1] // width
    return (
        input_grad,
        total(pieces[0], rising),
        total(pieces[1], turned),
        total(join(qkv_own, qkv_far), rising),
        total(pieces[2], turned),
        [thin_sum[:, t] for t in range(8)],
        thin_sum[:, 8 : 8 + ups].reshape(-1),
    )


def local(
    size,
    inputs,
    segment_ids,
    cotangent,
    first_gain,
    first_bias,
    w_qkv,
    query_bias,
    value_bias,
    w_proj,
    proj_bias,
    second_gain,
    second_bias,
    w_up,
    up_bias,
    w_down,
    down_bias,
):
    local_shape = inputs.shape
    width = local_shape[-1]
    band = lax.axis_index("band")
    band_at = band.astype(jnp.int32).reshape(1)
    tokens = inputs.reshape(-1, width)
    seg_own = segment_ids
    queries, k_own, v_own, normed, k_far, v_far, seg_far = project_qkv(
        tokens, seg_own, w_qkv, first_gain, first_bias, query_bias, value_bias
    )
    keys = (seg_own, seg_far, k_own, k_far, v_own, v_far)
    attended, query_lanes = attend_forward(band_at, queries, *keys)
    output, residual_grad, attended_grad, mlp_sums, up_sums, *pieces = mlp(
        size,
        tokens,
        attended,
        cotangent.reshape(-1, width),
        w_proj,
        w_up,
        w_down,
        proj_bias,
        second_gain,
        second_bias,
        up_bias,
        down_bias,
    )
    if size == 16:
        turns = [[(i, i ^ bits) for i in range(size)] for bits in (1, 2, 3, 8, 12)]
        sent = (*pieces[1:4], *pieces[6:8])
        pieces = [pieces[0], *pieces[4:6]] + [lax.ppermute(a, "dp", turn) for a, turn in zip(sent, turns)]
    query_grad, dk_own, dk_far, dv_own, dv_far, output = attend_backward(
        band_at, output, query_lanes, attended_grad, attended, *keys
    )
    if size == 16:
        input_grad, down_sum, wide_sum, vec, up_vec = finish(
            query_grad, dk_own, dk_far, dv_own, dv_far, normed, tokens, residual_grad, w_qkv, pieces, first_gain, mlp_sums, up_sums
        )
        first, second = 3 * width // 2, 3 * width // 2 + w_up.shape[1] // 2
        qkv_sum, up_sum, proj_sum = wide_sum[:, :first], wide_sum[:, first:second], wide_sum[:, second:]
        vectors, up_vector = [vec[t] for t in range(8)], up_vec.reshape(-1)
    else:
        input_grad, down_sum, up_sum, qkv_sum, proj_sum, vectors, up_vector = finish_any(
            size, band_at, query_grad, dk_own, dk_far, dv_own, dv_far, normed, tokens, residual_grad, w_qkv, pieces, first_gain, mlp_sums, up_sums
        )
    return (
        output.reshape(local_shape),
        input_grad.reshape(local_shape),
        vectors[0],
        vectors[1],
        qkv_sum,
        vectors[2],
        vectors[3],
        proj_sum,
        vectors[7],
        vectors[5],
        vectors[6],
        up_sum,
        up_vector,
        down_sum,
        vectors[4],
    )


def solution(mesh):
    size = mesh.shape["dp"]
    placed = (P("dp", "band", None), P("dp", "band"), P("dp", "band", None)) + (P(),) * 13
    split, thin = P("dp", "band"), P("dp")
    wide = P("dp", "band", None)
    return jax.shard_map(
        functools.partial(local, size),
        mesh=mesh,
        in_specs=placed,
        out_specs=(wide, wide, thin, thin, split, thin, thin, split, thin, thin, thin, split, thin, split, thin),
        check_vma=False,
    )
```

```python
import functools

import jax
import jax.numpy as jnp
from jax import lax
from jax.experimental import pallas as pl
from jax.experimental.pallas import tpu as pltpu
from jax.sharding import PartitionSpec as P

EPS = 1e-05
HEADS = 12
HEAD_DIM = 64
NEG_LARGE = -1e30
PAIRS = HEADS // 2
CHUNK = 256
EDGE = 64
MIB = 1 << 20
f32, bf16 = jnp.float32, jnp.bfloat16
NN = (((1,), (0,)), ((), ()))
NT = (((1,), (1,)), ((), ()))


def mm(a, b, dims=NN):
    return lax.dot_general(a, b, dims, preferred_element_type=f32)


def low_lanes(rows):
    return lax.broadcasted_iota(jnp.int32, (rows, 128), 1) < HEAD_DIM


def side_lanes(rows):
    return lax.broadcasted_iota(jnp.int32, (rows, 128), 1) & (HEAD_DIM - 1)


def split3(x):
    high = x.astype(bf16).astype(f32)
    middle = (x - high).astype(bf16).astype(f32)
    return high, middle, x - high - middle


def place(side, parts, base):
    for t, part in enumerate(parts):
        base = jnp.where(side == 16 + t, part, base)
    return base


def as_column(row):
    return jnp.broadcast_to(row, (8, row.shape[1])).T[:, 0:1]


def key_window(seg_own, seg_far, block, BQ, BK):
    own, far = seg_own[...].astype(f32), seg_far[...].astype(f32)

    def below(limit):
        return jnp.sum((own < limit).astype(f32) + (far < limit).astype(f32)).astype(jnp.int32)

    mine = seg_own[:, pl.ds(pl.multiple_of(block * BQ, BQ), BQ)].astype(f32)
    row = lax.broadcasted_iota(jnp.int32, mine.shape, 1)
    lo = (below(jnp.min(mine)) // 128) * 128
    blocks = (below(jnp.max(mine) + 1.0) - lo + BK - 1) // BK
    start = jnp.minimum(lo, 2 * own.shape[1] - blocks * BK)
    early_end = below(jnp.min(jnp.where(row >= EDGE, mine, 99.0)))
    late_start = below(jnp.max(jnp.where(row < BQ - EDGE, mine, -1.0)) + 1.0)
    early = jnp.clip((early_end - start) // BK, 0, blocks)
    late = jnp.clip((start + blocks * BK - late_start) // BK, 0, blocks - early)
    return start, blocks, early, late


def over_blocks(count, early, late, rows, body, paired=False):
    for first, end, part in (
        (0, early, slice(0, EDGE)),
        (early, count - late, slice(0, rows)),
        (count - late, count, slice(rows - EDGE, rows)),
    ):

        def step(j, c, part=part):
            body(j, part)
            return c

        if paired and part == slice(0, rows):

            def two(j, c, first=first, part=part):
                body(first + 2 * j, part)
                body(first + 2 * j + 1, part)
                return c

            pairs = (end - first) // 2
            lax.fori_loop(0, pairs, two, 0)
            first = first + 2 * pairs
        lax.fori_loop(first, end, step, 0)


def fill_pairs(src, dst, rows, low, extra):
    for p in range(PAIRS):
        pair = src[:, p * 128 : (p + 1) * 128]
        dst[2 * p, rows, :] = jnp.where(low, pair, extra)
        dst[2 * p + 1, rows, :] = jnp.where(low, extra, pair)


def fill_keys(band, i, k_own, k_far, v_own, v_far, seg_own, seg_far, kaug, vaug, value_extra):
    local = kaug.shape[1] // 2
    low, side = low_lanes(CHUNK), side_lanes(CHUNK)
    here = pl.ds(pl.multiple_of(i * CHUNK, CHUNK), CHUNK)
    for k, v, seg, first in ((k_own, v_own, seg_own, band), (k_far, v_far, seg_far, 1 - band)):
        rows = pl.ds(pl.multiple_of(first * local + i * CHUNK, CHUNK), CHUNK)
        extra = jnp.where(side < 16, jnp.where(side == as_column(seg[:, here]), 0.0, NEG_LARGE), jnp.where(side < 19, -1.0, 0.0))
        fill_pairs(k, kaug, rows, low, extra.astype(bf16))
        fill_pairs(v, vaug, rows, low, value_extra)


def attend_fwd_kernel(fills, BQ, BK, band_ref, q_ref, k_own, k_far, v_own, v_far,
                      seg_own, seg_far, o_ref, qaug_ref, kaug, vaug, qm, s_all, mx, acc):
    i = pl.program_id(0)

    @pl.when(i < fills)
    def _():
        fill_keys(band_ref[0], i, k_own, k_far, v_own, v_far, seg_own, seg_far, kaug, vaug, jnp.ones((CHUNK, 128), bf16))

    @pl.when(i >= fills)
    def _():
        low, side = low_lanes(BQ), side_lanes(BQ)
        block = i - fills
        ids = as_column(seg_own[:, pl.ds(pl.multiple_of(block * BQ, BQ), BQ)])
        own = (side == ids).astype(f32).astype(bf16)
        for p in range(PAIRS):
            pair = q_ref[:, p * 128 : (p + 1) * 128]
            qm[2 * p] = jnp.where(low, pair, own)
            qm[2 * p + 1] = jnp.where(low, own, pair)
        mx[...] = jnp.full(mx.shape, -3e38, f32)
        acc[...] = jnp.zeros(acc.shape, f32)
        start, count, early, late = key_window(seg_own, seg_far, block, BQ, BK)

        def first(j, part):
            at = pl.multiple_of(start + j * BK, 128)
            out = pl.ds(pl.multiple_of(j * BK, BK), BK)
            for h in range(HEADS):
                s = mm(qm[h, part, :], kaug[h, pl.ds(at, BK), :], NT)
                s_all[h, part, out] = s
                m = mx[h, part, :]
                for t in range(BK // 128):
                    m = jnp.maximum(m, s[:, t * 128 : (t + 1) * 128])
                mx[h, part, :] = m

        over_blocks(count, early, late, BQ, first, True)
        for h in range(HEADS):
            mx[h] = jnp.broadcast_to(jnp.max(mx[h], axis=1, keepdims=True), (BQ, 128))

        def second(j, part):
            at = pl.multiple_of(start + j * BK, 128)
            src = pl.ds(pl.multiple_of(j * BK, BK), BK)
            for h in range(HEADS):
                p = jnp.exp(s_all[h, part, src] - jnp.concatenate([mx[h, part, :]] * (BK // 128), axis=1)).astype(bf16)
                acc[h, part, :] += mm(p, vaug[h, pl.ds(at, BK), :])

        over_blocks(count, early, late, BQ, second)
        ids = (side == ids).astype(f32)
        for p in range(PAIRS):
            even, odd = acc[2 * p], acc[2 * p + 1]
            total = jnp.where(low, pltpu.roll(even, HEAD_DIM, 1), pltpu.roll(odd, HEAD_DIM, 1))
            o_ref[:, p * 128 : (p + 1) * 128] = (jnp.where(low, even, odd) / total).astype(bf16)
            pair = q_ref[:, p * 128 : (p + 1) * 128]
            extra = [place(side, split3(mx[2 * p + e] + jnp.log(sums)), ids).astype(bf16) for e, sums in enumerate((even, odd))]
            qaug_ref[2 * p] = jnp.where(low, pair, extra[0])
            qaug_ref[2 * p + 1] = jnp.where(low, extra[1], pair)


def attend_forward(band, q, seg_own, seg_far, k_own, k_far, v_own, v_far, BQ=256, BK=256):
    rows, width = q.shape
    fills, steps = rows // CHUNK, rows // BQ
    mine = lambda i, *_: (jnp.clip(i - fills, 0, steps - 1), 0)
    fill = lambda i, *_: (jnp.minimum(i, fills - 1), 0)
    wide = pl.BlockSpec((CHUNK, width), fill)
    thin = pl.BlockSpec((1, rows), lambda i, *_: (0, 0))
    return pl.pallas_call(
        functools.partial(attend_fwd_kernel, fills, BQ, BK),
        out_shape=(jax.ShapeDtypeStruct((rows, width), bf16), jax.ShapeDtypeStruct((HEADS, rows, 128), bf16)),
        grid_spec=pltpu.PrefetchScalarGridSpec(
            num_scalar_prefetch=1,
            grid=(fills + steps,),
            in_specs=[pl.BlockSpec((BQ, width), mine), wide, wide, wide, wide, thin, thin],
            out_specs=[pl.BlockSpec((BQ, width), mine), pl.BlockSpec((HEADS, BQ, 128), lambda i, *_: (0, jnp.clip(i - fills, 0, steps - 1), 0))],
            scratch_shapes=[
                pltpu.VMEM((HEADS, 2 * rows, 128), bf16),
                pltpu.VMEM((HEADS, 2 * rows, 128), bf16),
                pltpu.VMEM((HEADS, BQ, 128), bf16),
                pltpu.VMEM((HEADS, BQ, 2 * rows), f32),
                pltpu.VMEM((HEADS, BQ, 128), f32),
                pltpu.VMEM((HEADS, BQ, 128), f32),
            ],
        ),
        compiler_params=pltpu.CompilerParams(vmem_limit_bytes=56 * MIB),
        cost_estimate=pl.CostEstimate(flops=30 * 10**9, bytes_accessed=10 * 10**6, transcendentals=0),
        name="attend_forward",
    )(band, q, k_own, k_far, v_own, v_far, seg_own, seg_far)


def attend_bwd_kernel(fills, steps, BQ, BK, band_ref, qm, do_ref, o_ref,
                      k_own, k_far, v_own, v_far, seg_own, seg_far, carried, dq_ref, dkt_own, dkt_far, dvt_own, dvt_far, carried_out,
                      kaug, vaug, dom, lqt, ldot, eqt, edot, dq_acc, dk_acc, dv_acc):
    i = pl.program_id(0)
    band = band_ref[0]
    local = kaug.shape[1] // 2

    @pl.when(i < fills)
    def _():
        side = side_lanes(CHUNK)
        extra = jnp.where((side >= 16) & (side < 19), -1.0, 0.0).astype(bf16)
        fill_keys(band, i, k_own, k_far, v_own, v_far, seg_own, seg_far, kaug, vaug, extra)
        for part in range(2):
            cols = pl.ds(pl.multiple_of(part * local + i * CHUNK, CHUNK), CHUNK)
            for p in range(PAIRS):
                dk_acc[p, :, cols] = jnp.zeros((128, CHUNK), f32)
                dv_acc[p, :, cols] = jnp.zeros((128, CHUNK), f32)

    @pl.when((i >= fills) & (i < fills + steps))
    def _():
        low, side = low_lanes(BQ), side_lanes(BQ)
        block = i - fills
        carried_out[...] = carried[...]
        lane = lax.broadcasted_iota(jnp.int32, (256, 256), 0) & 127
        column = lax.broadcasted_iota(jnp.int32, (256, 256), 1)
        adder = ((lane < HEAD_DIM) == (column < 128)).astype(f32).astype(bf16)
        for p in range(PAIRS):
            cols = slice(p * 128, (p + 1) * 128)
            q_pair, do_pair = jnp.where(low, qm[2 * p], qm[2 * p + 1]), do_ref[:, cols]
            prod = do_pair.astype(f32) * o_ref[:, cols].astype(f32)
            high = prod.astype(bf16)
            rest = (prod - high.astype(f32)).astype(bf16)
            delta = mm(jnp.concatenate([high, rest], axis=1), adder)
            for e in range(2):
                extra = place(side, split3(delta[:, e * 128 : (e + 1) * 128]), jnp.zeros((BQ, 128), f32)).astype(bf16)
                dom[2 * p + e] = jnp.where(low, do_pair, extra) if e == 0 else jnp.where(low, extra, do_pair)
            for pair, dst, edges in ((q_pair, lqt, eqt), (do_pair, ldot, edot)):
                flipped = pair.T
                upper = lax.broadcasted_iota(jnp.int32, flipped.shape, 0) < HEAD_DIM
                zero = jnp.zeros_like(flipped)
                even, odd = jnp.where(upper, flipped, zero), jnp.where(upper, zero, flipped)
                dst[p, :, 0:BQ] = even
                dst[p, :, BQ : 2 * BQ] = odd
                edges[0, p] = jnp.concatenate([even[:, 0:EDGE], odd[:, 0:EDGE]], axis=1)
                edges[1, p] = jnp.concatenate([even[:, BQ - EDGE :], odd[:, BQ - EDGE :]], axis=1)
        lefts = {-1: (lqt, ldot), 0: (eqt.at[0], edot.at[0]), BQ - EDGE: (eqt.at[1], edot.at[1])}
        dq_acc[...] = jnp.zeros(dq_acc.shape, f32)
        start, count, early, late = key_window(seg_own, seg_far, block, BQ, BK)

        def step(j, part):
            window = pl.ds(pl.multiple_of(start + j * BK, 128), BK)
            left_q, left_do = lefts[part.start if part.stop - part.start < BQ else -1]

            def scores(h):
                return mm(qm[h, part, :], kaug[h, window, :], NT), mm(dom[h, part, :], vaug[h, window, :], NT)

            ahead = scores(0)
            kept = []
            for h in range(HEADS):
                p = h // 2
                s, dp = ahead
                if h + 1 < HEADS:
                    ahead = scores(h + 1)
                prob = jnp.exp(s)
                ds = (prob * dp).astype(bf16)
                kept.append((prob.astype(bf16), ds))
                dq_acc[h, part, :] += mm(ds, kaug[h, window, :])
                if h % 2:
                    dv_acc[p, :, window] += mm(left_do[p], jnp.concatenate([kept[0][0], kept[1][0]], axis=0))
                    dk_acc[p, :, window] += mm(left_q[p], jnp.concatenate([kept[0][1], kept[1][1]], axis=0))
                    kept = []

        over_blocks(count, early, late, BQ, step)
        for p in range(PAIRS):
            pair = jnp.where(low, dq_acc[2 * p], dq_acc[2 * p + 1]) * HEAD_DIM**-0.5
            dq_ref[:, p * 128 : (p + 1) * 128] = pair.astype(bf16)

    @pl.when(i >= fills + steps)
    def _():
        j = i - fills - steps
        for p in range(PAIRS):
            rows = slice(p * 128, (p + 1) * 128)
            for first, dk_out, dv_out in ((band, dkt_own, dvt_own), (1 - band, dkt_far, dvt_far)):
                cols = pl.ds(pl.multiple_of(first * local + j * CHUNK, CHUNK), CHUNK)
                dk_out[rows, :] = dk_acc[p, :, cols].astype(bf16)
                dv_out[rows, :] = dv_acc[p, :, cols].astype(bf16)


def attend_backward(band, carried, qaug, do, o, seg_own, seg_far, k_own, k_far, v_own, v_far, BQ=256, BK=256):
    rows, width = do.shape
    fills, steps = rows // CHUNK, rows // BQ
    mine = lambda i, *_: (jnp.clip(i - fills, 0, steps - 1), 0)
    fill = lambda i, *_: (jnp.minimum(i, fills - 1), 0)
    drain = lambda i, *_: (0, jnp.clip(i - fills - steps, 0, fills - 1))
    wide = pl.BlockSpec((CHUNK, width), fill)
    thin = pl.BlockSpec((1, rows), lambda i, *_: (0, 0))
    block = pl.BlockSpec((BQ, width), mine)
    flat = jax.ShapeDtypeStruct((width, rows), bf16)
    return pl.pallas_call(
        functools.partial(attend_bwd_kernel, fills, steps, BQ, BK),
        out_shape=(jax.ShapeDtypeStruct((rows, width), bf16), flat, flat, flat, flat, jax.ShapeDtypeStruct(carried.shape, carried.dtype)),
        grid_spec=pltpu.PrefetchScalarGridSpec(
            num_scalar_prefetch=1,
            grid=(fills + steps + fills,),
            in_specs=[pl.BlockSpec((HEADS, BQ, 128), lambda i, *_: (0, jnp.clip(i - fills, 0, steps - 1), 0)), block, block, wide, wide, wide, wide, thin, thin, block],
            out_specs=[block] + [pl.BlockSpec((width, CHUNK), drain)] * 4 + [block],
            scratch_shapes=[
                pltpu.VMEM((HEADS, 2 * rows, 128), bf16),
                pltpu.VMEM((HEADS, 2 * rows, 128), bf16),
                pltpu.VMEM((HEADS, BQ, 128), bf16),
                pltpu.VMEM((PAIRS, 128, 2 * BQ), bf16),
                pltpu.VMEM((PAIRS, 128, 2 * BQ), bf16),
                pltpu.VMEM((2, PAIRS, 128, 2 * EDGE), bf16),
                pltpu.VMEM((2, PAIRS, 128, 2 * EDGE), bf16),
                pltpu.VMEM((HEADS, BQ, 128), f32),
                pltpu.VMEM((PAIRS, 128, 2 * rows), f32),
                pltpu.VMEM((PAIRS, 128, 2 * rows), f32),
            ],
        ),
        compiler_params=pltpu.CompilerParams(vmem_limit_bytes=56 * MIB),
        cost_estimate=pl.CostEstimate(flops=45 * 10**9, bytes_accessed=20 * 10**6, transcendentals=0),
        name="attend_backward",
    )(band, qaug, do, o, k_own, k_far, v_own, v_far, seg_own, seg_far, carried)


MESH = pl.DeviceIdType.MESH
TN = (((0,), (0,)), ((), ()))
SLICE = 768


def gelu_and_slope(u):
    below = 0.5 + 0.5 * lax.erf(u * 0.5**0.5)
    return u * below, below + u * jnp.exp(u * u * -0.5) * (0.5 / 3.141592653589793) ** 0.5


def normalize(rows):
    centred = rows - jnp.mean(rows, axis=-1, keepdims=True)
    scale = lax.rsqrt(jnp.mean(centred * centred, axis=-1, keepdims=True) + EPS)
    return centred * scale, scale


def add_sums(ref, row, values, first):
    sums = jnp.sum(values, axis=0, keepdims=True)
    at = slice(row, row + 1)
    ref[at, :] = jnp.where(first, sums, ref[at, :] + sums)


def as_row(ref):
    return ref[...].reshape(1, -1)


def add_low(dst, a, b):
    dst[...] = (a[...].astype(f32) + b[...].astype(f32)).astype(bf16)


def mlp_kernel(sorted_out, blocks, rows, slices, tok_ref, att_ref, cot_ref, wproj, wup, wdown, pbias, gain, shift, ubias, dbias,
               out_ref, rgrad_ref, agrad_ref, sums_ref, usums_ref, *rest):
    outs, scratch = rest[: 8 if sorted_out else 3], rest[8 if sorted_out else 3 :]
    hid, ugr, n2s, bgs, ags, ats, d_own, d_far, d_in, u_in, p_own, p_far, p_in, send_sem, recv_sem, *held = scratch
    stores = []
    if sorted_out:
        store_sem = held.pop()
        stores = [pltpu.make_async_copy(held[q], outs[q], store_sem.at[q]) for q in range(4)]
        outs = (*held, *outs[4:])
    i = pl.program_id(0)
    me, band = lax.axis_index("dp"), lax.axis_index("band")
    other = (me, 1 - band)
    width = tok_ref.shape[1]
    half, per_half = width // 2, slices // 2

    def push(t, src, dst):
        return pltpu.make_async_remote_copy(
            src_ref=src, dst_ref=dst, send_sem=send_sem.at[t], recv_sem=recv_sem.at[t], device_id=other, device_id_type=MESH
        )

    def d_copy(j):
        at = pl.ds(pl.multiple_of(j * SLICE, SLICE), SLICE)
        return push(j, d_far.at[at, :], d_in.at[at, :])

    def u_copy(c):
        return push(slices + c, hid.at[0:width, pl.ds(pl.multiple_of(c * SLICE, SLICE), SLICE)], u_in.at[c])

    def p_copy():
        return push(slices + per_half, p_far, p_in)

    @pl.when(i == 0)
    def _():
        barrier = pltpu.get_barrier_semaphore()
        pl.semaphore_signal(barrier, inc=1, device_id=other, device_id_type=MESH)

    @pl.when(i == blocks)
    def _():
        pl.semaphore_wait(pltpu.get_barrier_semaphore(), 1)

    @pl.when(i < blocks)
    def _():
        here = pl.ds(pl.multiple_of(i * rows, rows), rows)
        first = i == 0
        att = att_ref[...]
        ats[here, :] = att
        residual = tok_ref[...] + mm(att, wproj[...]) + as_row(pbias)
        xhat, scale = normalize(residual)
        n2 = (xhat * as_row(gain) + as_row(shift)).astype(bf16)
        n2s[here, :] = n2
        cot = cot_ref[...]
        bg = cot.astype(bf16)
        bgs[here, :] = bg
        add_sums(sums_ref, 0, bg.astype(f32), first)
        for c in range(slices):
            cols = slice(c * SLICE, (c + 1) * SLICE)
            hidden, slope = gelu_and_slope(mm(n2, wup[:, cols]) + ubias[cols].reshape(1, -1))
            hid[here, cols] = hidden.astype(bf16)
            grad = (mm(bg, wdown[cols, :], NT) * slope).astype(bf16)
            ugr[here, cols] = grad
            sums = jnp.sum(grad.astype(f32), axis=0, keepdims=True)
            usums_ref[0:1, cols] = jnp.where(first, sums, usums_ref[0:1, cols] + sums)
        out_ref[...] = residual + mm(hid[here, :], wdown[...]) + as_row(dbias)
        e = mm(ugr[here, :], wup[...], NT)
        add_sums(sums_ref, 1, e * xhat, first)
        add_sums(sums_ref, 2, e, first)
        f = e * as_row(gain)
        rgrad = cot + scale * (f - jnp.mean(f, axis=-1, keepdims=True) - xhat * jnp.mean(f * xhat, axis=-1, keepdims=True))
        rgrad_ref[...] = rgrad
        ag = rgrad.astype(bf16)
        ags[here, :] = ag
        add_sums(sums_ref, 3, ag.astype(f32), first)
        agrad_ref[...] = mm(ag, wproj[...], NT).astype(bf16)

    def columns(grad, own, far, at):
        left, right = grad[:, :half].astype(bf16), grad[:, half:].astype(bf16)
        own[at, :] = jnp.where(band == 0, left, right)
        far[at, :] = jnp.where(band == 0, right, left)

    @pl.when((i >= blocks) & (i < blocks + slices))
    def _():
        j = i - blocks
        at = pl.ds(pl.multiple_of(j * SLICE, SLICE), SLICE)
        columns(mm(hid[:, at], bgs[...], TN), d_own, d_far, at)
        d_copy(j).start()

    def up_slice(which):
        at = pl.ds(pl.multiple_of(which * SLICE, SLICE), SLICE)
        return mm(n2s[...], ugr[:, at], TN).astype(bf16)

    x, y = me & 1, (me >> 1) & 1

    z = me >> 2
    shard = width // 16

    corners = [(y ^ (q >> 1)) * 2 + (x ^ (q & 1)) for q in range(4)]

    def down_arrived(j):
        d_copy(j).wait_recv()
        if not sorted_out:
            at = pl.ds(pl.multiple_of(j * SLICE, SLICE), SLICE)
            add_low(outs[0].at[at, :], d_own.at[at, :], d_in.at[at, :])
            return
        for q in range(4):
            at = pl.ds(pl.multiple_of(j * SLICE + corners[q] * 4 * shard, shard), 2 * shard)
            add_low(outs[q].at[j, 0 : 2 * shard], d_own.at[at, :], d_in.at[at, :])

    def down_along_z(d):
        if sorted_out:
            for t in range(4):
                at = pl.ds(pl.multiple_of((z ^ d) * SLICE + t * 4 * shard + 2 * shard, shard), 2 * shard)
                add_low(outs[4 + d].at[t // 2, t % 2, 0 : 2 * shard], d_own.at[at, :], d_in.at[at, :])

    def up_arrived(c):
        u_copy(c).wait_recv()
        own = hid.at[0:width, (per_half + c) * SLICE : (per_half + c + 1) * SLICE]
        if not sorted_out:
            add_low(outs[1].at[:, c * SLICE : (c + 1) * SLICE], own, u_in.at[c])
            return

        def fold(dst, s, part):
            at = pl.ds(pl.multiple_of(s * shard, shard), shard)
            cols = slice(part * half, (part + 1) * half)
            add_low(dst.at[(2 + part) * shard : (3 + part) * shard], own.at[at, cols], u_in.at[c, at, cols])

        def near(zz, carry):
            for q in range(4):
                for part in range(2):
                    fold(outs[q].at[zz], zz * 4 + corners[q], part)
            return carry

        def along(s, carry):
            for d in range(4):
                for part in range(2):
                    fold(outs[4 + d].at[s >> 1, s & 1], (z ^ d) * 4 + s, part)
            return carry

        lax.fori_loop(0, 4, near if c == 0 else along, 0, unroll=2)

    def proj_arrived():
        p_copy().wait_recv()
        if not sorted_out:
            add_low(outs[2], p_own, p_in)
            return

        def one(zz, carry):
            for q in range(4):
                at = pl.ds(pl.multiple_of((zz * 4 + corners[q]) * shard, shard), shard)
                add_low(outs[q].at[zz, 4 * shard : 5 * shard], p_own.at[at, :], p_in.at[at, :])
            return carry

        lax.fori_loop(0, 4, one, 0, unroll=2)

    middle = blocks + slices
    @pl.when(i == middle)
    def _():
        columns(mm(ats[...], ags[...], TN), p_own, p_far, slice(None))
        p_copy().start()

    for c in range(per_half):
        at = slice(c * SLICE, (c + 1) * SLICE)

        @pl.when(i == middle + 1 + c)
        def _(c=c, at=at):
            hid[0:width, at] = up_slice((1 - band) * per_half + c)
            u_copy(c).start()
            for j in range(2 * c, 2 * c + 2):
                down_arrived(j)

        @pl.when(i == middle + 1 + per_half + c)
        def _(c=c):
            hid[0:width, (per_half + c) * SLICE : (per_half + c + 1) * SLICE] = up_slice(band * per_half + c)
            for d in range(2 * c, 2 * c + 2):
                down_along_z(d)
            if c == 0:
                proj_arrived()
            else:
                up_arrived(c - 1)

    @pl.when(i == middle + slices)
    def _():
        for store in stores:
            store.start()
        up_arrived(per_half - 1)
        for j in range(slices):
            d_copy(j).wait_send()
        for c in range(per_half):
            u_copy(c).wait_send()
        p_copy().wait_send()
        for store in stores:
            store.wait()


def mlp(size, tokens, attended, cotangent, w_proj, w_up, w_down, proj_bias, gain, shift, up_bias, down_bias, rows=256):
    count, width = tokens.shape
    ff = w_up.shape[1]
    blocks, slices = count // rows, ff // SLICE
    half, per_half = width // 2, slices // 2
    sorted_out = size == 16
    one = pl.Buffered(1)
    mine = lambda i: (jnp.minimum(i, blocks - 1), 0)
    block = pl.BlockSpec((rows, width), mine)

    def full(a):
        return pl.BlockSpec(a.shape, lambda i: (0,) * len(a.shape), pipeline_mode=one)

    vectors = (proj_bias, gain, shift, up_bias, down_bias)
    shape = jax.ShapeDtypeStruct
    if sorted_out:
        sixteenth = width // 16
        pieces = [shape((4, 5 * sixteenth, half), bf16)] * 4
        pieces += [shape((2, 2, 4 * sixteenth, half), bf16)] * 4
    else:
        pieces = [shape((ff, half), bf16), shape((width, ff // 2), bf16), shape((width, half), bf16)]
    kept = [shape((8, width), f32), shape((8, ff), f32)] + pieces
    low = lambda *s: pltpu.VMEM(s, bf16)
    direct = pieces[:4] if sorted_out else []
    held = [low(*a.shape) for a in direct] + [pltpu.SemaphoreType.DMA((4,))] * sorted_out
    copies = slices + per_half + 1
    return pl.pallas_call(
        functools.partial(mlp_kernel, sorted_out, blocks, rows, slices),
        out_shape=[shape((count, width), f32), shape((count, width), f32), shape((count, width), bf16)] + kept,
        grid=(blocks + 2 * slices + 1,),
        in_specs=[block, block, block] + [full(a) for a in (w_proj, w_up, w_down, *vectors)],
        out_specs=[block, block, block] + [pl.BlockSpec(memory_space=pl.ANY) if a in direct else full(a) for a in kept],
        scratch_shapes=[
            low(count, ff),
            low(count, ff),
            *([low(count, width)] * 4),
            *([low(ff, half)] * 3),
            low(per_half, width, SLICE),
            *([low(width, half)] * 3),
            pltpu.SemaphoreType.DMA((copies,)),
            pltpu.SemaphoreType.DMA((copies,)),
            *held,
        ],
        compiler_params=pltpu.CompilerParams(vmem_limit_bytes=62 * MIB, collective_id=1, has_side_effects=True),
        cost_estimate=pl.CostEstimate(flops=40 * 10**9, bytes_accessed=40 * 10**6, transcendentals=0),
        name="mlp",
    )(tokens, attended, cotangent, w_proj, w_up, w_down, *vectors)


def qkv_kernel(steps, tok_ref, seg_ref, w_ref, gain, shift, qbias, vbias, q_ref, k_ref, v_ref, n_ref, k_far, v_far, seg_far,
               n_all, k_all, v_all, send_sem, recv_sem):
    i = pl.program_id(0)
    last = pl.num_programs(0) - 1
    other = (lax.axis_index("dp"), 1 - lax.axis_index("band"))
    rows, width = tok_ref.shape

    def push(t, src, dst):
        return pltpu.make_async_remote_copy(
            src_ref=src, dst_ref=dst, send_sem=send_sem.at[t], recv_sem=recv_sem.at[t], device_id=other, device_id_type=MESH
        )

    def copies(j):
        at = pl.ds(pl.multiple_of(j * rows, rows), rows)
        return push(2 * j, k_all.at[at, :], k_far.at[at, :]), push(2 * j + 1, v_all.at[at, :], v_far.at[at, :])

    segs = push(send_sem.shape[0] - 1, seg_ref, seg_far)

    @pl.when(i == 0)
    def _():
        barrier = pltpu.get_barrier_semaphore()
        pl.semaphore_signal(barrier, inc=1, device_id=other, device_id_type=MESH)

    @pl.when(i == 1)
    def _():
        pl.semaphore_wait(pltpu.get_barrier_semaphore(), 1)
        segs.start()
        for copy in copies(0):
            copy.start()

    @pl.when(i < steps)
    def _():
        here = pl.ds(pl.multiple_of(i * rows, rows), rows)
        xhat, _ = normalize(tok_ref[...])
        n1 = (xhat * as_row(gain) + as_row(shift)).astype(bf16)
        n_ref[...] = n1
        n_all[here, :] = n1
        k = mm(n1, w_ref[:, width : 2 * width]).astype(bf16)
        k_ref[...] = k
        k_all[here, :] = k
        v = (mm(n1, w_ref[:, 2 * width :]) + as_row(vbias)).astype(bf16)
        v_ref[...] = v
        v_all[here, :] = v

    @pl.when((i >= 1) & (i < steps))
    def _():
        for copy in copies(i):
            copy.start()

    @pl.when(i >= steps)
    def _():
        here = pl.ds(pl.multiple_of((i - steps) * rows, rows), rows)
        q = (mm(n_all[here, :], w_ref[:, :width]) + as_row(qbias)).astype(bf16)
        q_ref[...] = q * jnp.asarray(HEAD_DIM**-0.5, bf16)

    @pl.when(i == last)
    def _():
        segs.wait()
        for j in range(k_all.shape[0] // rows):
            for copy in copies(j):
                copy.wait()


def project_qkv(tokens, seg, w_qkv, gain, shift, query_bias, value_bias, rows=256):
    count, width = tokens.shape
    one = pl.Buffered(1)
    steps = count // rows
    block = pl.BlockSpec((rows, width), lambda i: (jnp.minimum(i, steps - 1), 0))
    late = pl.BlockSpec((rows, width), lambda i: (jnp.maximum(i - steps, 0), 0))
    vectors = (gain, shift, query_bias, value_bias)
    hbm = pl.BlockSpec(memory_space=pl.ANY)
    low = jax.ShapeDtypeStruct((count, width), bf16)
    return pl.pallas_call(
        functools.partial(qkv_kernel, steps),
        out_shape=(low,) * 6 + (jax.ShapeDtypeStruct(seg.shape, seg.dtype),),
        grid=(2 * steps,),
        in_specs=[block, hbm] + [pl.BlockSpec(a.shape, lambda i, n=a.ndim: (0,) * n, pipeline_mode=one) for a in (w_qkv, *vectors)],
        out_specs=[late] + [block] * 3 + [hbm] * 3,
        scratch_shapes=[
            pltpu.VMEM((count, width), bf16),
            pltpu.VMEM((count, width), bf16),
            pltpu.VMEM((count, width), bf16),
            pltpu.SemaphoreType.DMA((2 * steps + 1,)),
            pltpu.SemaphoreType.DMA((2 * steps + 1,)),
        ],
        compiler_params=pltpu.CompilerParams(vmem_limit_bytes=60 * MIB, collective_id=2, has_side_effects=True),
        cost_estimate=pl.CostEstimate(flops=4 * 10**9, bytes_accessed=13 * 10**6, transcendentals=0),
        name="project_qkv",
    )(tokens, seg, w_qkv, *vectors)


def qkv_grad_kernel(blocks, rows, band_ref, dq_ref, dk_own, dk_far, dv_own, dv_far, n_ref, packed_ref, own_ref, far_ref, sums_ref, packed):
    i = pl.program_id(0)
    band = band_ref[0]
    width = dq_ref.shape[1]
    half = own_ref.shape[1]

    @pl.when(i < blocks)
    def _():
        here = pl.ds(pl.multiple_of(i * rows, rows), rows)
        first = i == 0
        dq = dq_ref[...]
        packed_ref[:, :width] = dq
        packed[here, :width] = dq
        add_sums(sums_ref, 0, dq.astype(f32), first)
        for t, (own, far) in enumerate(((dk_own, dk_far), (dv_own, dv_far))):
            for p in range(width // 128):
                at = slice(p * 128, (p + 1) * 128)
                to = slice((t + 1) * width + p * 128, (t + 1) * width + (p + 1) * 128)
                turned = (own[at, :].astype(f32) + far[at, :].astype(f32)).astype(bf16).T
                packed_ref[:, to] = turned
                packed[here, to] = turned
        add_sums(sums_ref, 1, packed_ref[:, 2 * width :].astype(f32), first)

    def columns(which):
        at = pl.ds(pl.multiple_of(which * half, 128), half)
        return mm(n_ref[...], packed[:, at], TN).astype(bf16)

    @pl.when(i == blocks)
    def _():
        far_ref[...] = columns(1 - band)

    @pl.when(i == blocks + 1)
    def _():
        own_ref[...] = columns(band)


def qkv_grads(band, dq, dk_own, dk_far, dv_own, dv_far, normed, rows=256):
    count, width = dq.shape
    blocks = count // rows
    half = 3 * width // 2
    one = pl.Buffered(1)
    mine = lambda i, *_: (jnp.minimum(i, blocks - 1), 0)
    flip = lambda i, *_: (0, jnp.minimum(i, blocks - 1))
    whole = lambda i, *_: (0, 0)
    shape = jax.ShapeDtypeStruct
    return pl.pallas_call(
        functools.partial(qkv_grad_kernel, blocks, rows),
        out_shape=(shape((count, 3 * width), bf16), shape((width, half), bf16), shape((width, half), bf16), shape((8, width), f32)),
        grid_spec=pltpu.PrefetchScalarGridSpec(
            num_scalar_prefetch=1,
            grid=(blocks + 2,),
            in_specs=[pl.BlockSpec((rows, width), mine)]
            + [pl.BlockSpec((width, rows), flip)] * 4
            + [pl.BlockSpec((count, width), whole, pipeline_mode=one)],
            out_specs=[
                pl.BlockSpec((rows, 3 * width), mine),
                pl.BlockSpec((width, half), whole, pipeline_mode=one),
                pl.BlockSpec((width, half), whole, pipeline_mode=one),
                pl.BlockSpec((8, width), whole, pipeline_mode=one),
            ],
            scratch_shapes=[pltpu.VMEM((count, 3 * width), bf16)],
        ),
        compiler_params=pltpu.CompilerParams(vmem_limit_bytes=40 * MIB),
        cost_estimate=pl.CostEstimate(flops=8 * 10**9, bytes_accessed=18 * 10**6, transcendentals=0),
        name="qkv_grads",
    )(band, dq, dk_own, dk_far, dv_own, dv_far, normed)


def input_grad_kernel(packed_ref, tok_ref, rgrad_ref, w_ref, gain, out_ref, sums_ref):
    first = pl.program_id(0) == 0
    e = mm(packed_ref[...], w_ref[...], NT)
    xhat, scale = normalize(tok_ref[...])
    add_sums(sums_ref, 0, e * xhat, first)
    add_sums(sums_ref, 1, e, first)
    f = e * gain[...]
    back = scale * (f - jnp.mean(f, axis=-1, keepdims=True) - xhat * jnp.mean(f * xhat, axis=-1, keepdims=True))
    out_ref[...] = rgrad_ref[...] + back


def input_grads(packed, tokens, rgrad, w_qkv, gain, rows=256):
    count, width = tokens.shape
    one = pl.Buffered(1)
    block = pl.BlockSpec((rows, width), lambda i: (i, 0))
    return pl.pallas_call(
        input_grad_kernel,
        out_shape=(jax.ShapeDtypeStruct((count, width), f32), jax.ShapeDtypeStruct((8, width), f32)),
        grid=(count // rows,),
        in_specs=[
            pl.BlockSpec((rows, packed.shape[1]), lambda i: (i, 0)),
            block,
            block,
            pl.BlockSpec(w_qkv.shape, lambda i: (0, 0), pipeline_mode=one),
            pl.BlockSpec((1, width), lambda i: (0, 0), pipeline_mode=one),
        ],
        out_specs=[block, pl.BlockSpec((8, width), lambda i: (0, 0), pipeline_mode=one)],
        compiler_params=pltpu.CompilerParams(vmem_limit_bytes=32 * MIB),
        cost_estimate=pl.CostEstimate(flops=6 * 10**9, bytes_accessed=18 * 10**6, transcendentals=0),
        name="input_grads",
    )(packed, tokens, rgrad, w_qkv, gain.reshape(1, -1))


def finish_kernel(
    dq_hbm, dko_hbm, dkf_hbm, dvo_hbm, dvf_hbm, n_hbm, tok_hbm, rgrad_hbm, w_hbm, pk_hbm, ck_hbm, c1_hbm, px_hbm, py_hbm, pd_hbm, c2_hbm, c3_hbm, gain, msums, usums,
    out_hbm, down_out, wide_out, vec_out, usum_out,
    packed, dko, dko_in, dvo, dvo_in, n1, tok, out, wq, pk, p_one, ck, cols, far_in, tail,
    c_one, c_two, p_thr, c_thr, ta_one, tb_one, ta_two, tb_two, ta_thr, tb_thr, vec, vec_band, vec_x, vec_y, vec_z,
    load_sem, store_sem, swap_send, swap_recv, send, recv, vsend, vrecv,
):
    me = lax.axis_index("dp")
    band = lax.axis_index("band")
    x, y, z = me & 1, (me >> 1) & 1, me >> 2
    rows, width = tok.shape
    half = far_in.shape[-1]
    peer_band = (me, 1 - band)
    peer_x = (me ^ 1, band)
    peer_y = (me ^ 2, band)
    peers_z = [(((z + d) & 3) * 4 + (me & 3), band) for d in (1, 2, 3)]

    def load(t, src, dst):
        return pltpu.make_async_copy(src, dst, load_sem.at[t])

    loads = {
        "queries": (load(6, dq_hbm, packed.at[:, 0:width]), load(7, n_hbm, n1)),
        "keys": (load(4, dko_hbm, dko), load(5, dvo_hbm, dvo)),
        "early": (load(0, pk_hbm, pk), load(1, px_hbm, p_one.at[0]), load(2, py_hbm, p_one.at[1]), load(3, pd_hbm, p_one.at[2])),
        "along": (load(8, ck_hbm, ck), load(13, c2_hbm, c_one.at[1]), load(14, c3_hbm, c_one.at[2])),
        "rows": (load(10, w_hbm, wq), load(11, tok_hbm, tok), load(12, rgrad_hbm, out)),
    }

    def fetch(name):
        for copy in loads[name]:
            copy.start()

    def ready(name):
        for copy in loads[name]:
            copy.wait()

    for name in ("queries", "keys", "early"):
        fetch(name)

    barrier = pltpu.get_barrier_semaphore()
    for peer in (peer_band, peer_x, peer_y, *peers_z):
        pl.semaphore_signal(barrier, inc=1, device_id=peer, device_id_type=MESH)
    pl.semaphore_wait(barrier, 6)

    pending = []

    def push(src, dst, peer, s, r):
        copy = pltpu.make_async_remote_copy(src_ref=src, dst_ref=dst, send_sem=s, recv_sem=r, device_id=peer, device_id_type=MESH)
        copy.start()
        pending.append(copy)
        return copy

    swap_k = push(dkf_hbm, dko_in, peer_band, swap_send.at[0], swap_recv.at[0])
    swap_v = push(dvf_hbm, dvo_in, peer_band, swap_send.at[1], swap_recv.at[1])
    c_near = push(c1_hbm, c_one.at[0], (me ^ 4, band), send.at[2, 2], recv.at[2, 2])

    def put(dst, src):
        dst[...] = src[...]

    def each_shard(body):
        def step(s, c):
            body(s >> 2, (s >> 1) & 1, s & 1)
            return c

        lax.fori_loop(0, 16, step, 0, unroll=4)

    def second_stage(t, kept, one, two, mine, peer):
        def total(s, c):
            add_low(one.at[s >> 1, s & 1], one.at[s >> 1, s & 1], kept(s >> 1, s & 1))
            return c

        lax.fori_loop(0, 8, total, 0, unroll=True)
        return push(one.at[:, 1 - mine], two, peer, send.at[t, 0], recv.at[t, 0])

    def third_stage(t, one, two, three, mine, copy):
        copy.wait_recv()

        def total(zz, c):
            add_low(two.at[zz], two.at[zz], one.at[zz, mine])
            return c

        lax.fori_loop(0, 4, total, 0, unroll=True)
        return [push(two.at[(z + d) & 3], three.at[d - 1], peers_z[d - 1], send.at[t, d], recv.at[t, d]) for d in (1, 2, 3)]

    def last(two, three, copies):
        for copy in copies:
            copy.wait_recv()
        total = two[z].astype(f32)
        for d in range(3):
            total = total + three[d].astype(f32)
        return total

    def columns(t):
        cols[:, :, :, :, t * width : (t + 1) * width] = (
            mm(n1[...], packed[:, t * width : (t + 1) * width], TN).astype(bf16).reshape(cols.shape[:-1] + (width,))
        )

    def turn(t, own, other):
        def step(i, c):
            here = pl.ds(pl.multiple_of(i * 256, 256), 256)
            for p in range(width // 128):
                at = slice(p * 128, (p + 1) * 128)
                turned = (own[at, here].astype(f32) + other[at, here].astype(f32)).astype(bf16).T
                packed[here, t * width + p * 128 : t * width + (p + 1) * 128] = turned
            return c

        lax.fori_loop(0, rows // 256, step, 0, unroll=2)

    def swap(t, start, size, to):
        return pltpu.make_async_remote_copy(
            src_ref=cols.at[:, :, :, :, pl.ds(pl.multiple_of(start, 128), size)],
            dst_ref=far_in.at[:, :, :, :, pl.ds(pl.multiple_of(to, 128), size)],
            send_sem=swap_send.at[t],
            recv_sem=swap_recv.at[t],
            device_id=peer_band,
            device_id_type=MESH,
        )

    third = width // 2
    swap_near = swap(2, (3 - band) * third, third, band * width)
    swap_wide = swap(3, (1 - band) * 2 * width, width, (1 - band) * third)
    ready("queries")
    columns(0)
    fetch("along")
    fetch("rows")

    @pl.when(band == 1)
    def _():
        swap_wide.start()

    ready("early")

    def plane(zz, c):
        total = pk[zz].astype(f32)
        for t in range(3):
            total = total + p_one[t, zz].astype(f32)
        pk[zz] = total.astype(bf16)
        return c

    lax.fori_loop(0, 4, plane, 0, unroll=True)
    p_copies = [push(pk.at[(z + d) & 3], p_thr.at[d - 1], peers_z[d - 1], send.at[0, d], recv.at[0, d]) for d in (1, 2, 3)]
    ready("keys")
    swap_k.wait_recv()
    turn(1, dko, dko_in)
    columns(1)
    swap_near.start()
    swap_v.wait_recv()
    turn(2, dvo, dvo_in)
    columns(2)

    @pl.when(band == 0)
    def _():
        swap_wide.start()

    swap_near.wait()
    swap_wide.wait()
    mine = pl.ds(pl.multiple_of(band * half, 128), half)
    each_shard(lambda i, j, k: add_low(tail.at[i, j, k], cols.at[i, j, k, :, mine], far_in.at[i, j, k]))
    cut = ta_one.shape[-1]
    ta_first = push(tail.at[:, :, 1 - x, :, 0:cut], ta_one, peer_x, send.at[3, 4], recv.at[3, 4])
    tb_first = push(tail.at[:, 1 - y, :, :, cut:half], tb_one, peer_y, send.at[4, 4], recv.at[4, 4])

    ready("rows")
    vec[...] = jnp.zeros(vec.shape, f32)

    def rows_back(i, c):
        here = pl.ds(pl.multiple_of(i * 256, 256), 256)
        e = mm(packed[here, :], wq[...], NT)
        xhat, scale = normalize(tok[here, :])
        vec[0:1, :] = vec[0:1, :] + jnp.sum(e * xhat, axis=0, keepdims=True)
        vec[1:2, :] = vec[1:2, :] + jnp.sum(e, axis=0, keepdims=True)
        vec[2:3, :] = vec[2:3, :] + jnp.sum(packed[here, 0:width].astype(f32), axis=0, keepdims=True)
        vec[3:4, :] = vec[3:4, :] + jnp.sum(packed[here, 2 * width : 3 * width].astype(f32), axis=0, keepdims=True)
        f = e * as_row(gain)
        back = scale * (f - jnp.mean(f, axis=-1, keepdims=True) - xhat * jnp.mean(f * xhat, axis=-1, keepdims=True))
        out[here, :] = out[here, :] + back
        return c

    lax.fori_loop(0, rows // 256, rows_back, 0)
    store = pltpu.make_async_copy(out, out_hbm, store_sem)
    store.start()
    vec[4:8, :] = msums[0:4, :]
    for t in range(usums.shape[1] // width):
        vec[8 + t : 9 + t, :] = usums[0:1, t * width : (t + 1) * width]
    v_band = push(vec, vec_band, peer_band, vsend.at[0], vrecv.at[0])
    v_band.wait()
    vec_band[...] = vec[...] + vec_band[...]
    v_z = [push(vec_band, vec_z.at[d], peers_z[d], vsend.at[3 + d], vrecv.at[3 + d]) for d in range(3)]
    ta_first.wait_recv()
    ta_copy = second_stage(3, lambda i, j: tail.at[i, j, x, :, 0:cut], ta_one, ta_two, y, peer_y)
    tb_first.wait_recv()
    tb_copy = second_stage(4, lambda i, j: tail.at[i, y, j, :, cut:half], tb_one, tb_two, x, peer_x)
    for copy in v_z:
        copy.wait()
    vec_z[0] = vec_band[...] + vec_z[0] + vec_z[1] + vec_z[2]
    v_x = push(vec_z.at[0], vec_x, peer_x, vsend.at[1], vrecv.at[1])
    c_near.wait_recv()
    ready("along")

    def along(s, c):
        i, j = s >> 1, s & 1
        total = ck[i, j].astype(f32)
        for d in range(3):
            total = total + c_one[d, i, j].astype(f32)
        ck[i, j] = total.astype(bf16)
        return c

    lax.fori_loop(0, 4, along, 0, unroll=True)
    c_copy = push(ck.at[:, 1 - x], c_two, peer_x, send.at[2, 0], recv.at[2, 0])

    ta_copies = third_stage(3, ta_one, ta_two, ta_thr, y, ta_copy)
    tb_copies = third_stage(4, tb_one, tb_two, tb_thr, x, tb_copy)
    v_x.wait()
    vec_x[...] = vec_z[0] + vec_x[...]
    v_y = push(vec_x, vec_y, peer_y, vsend.at[2], vrecv.at[2])
    c_copy.wait_recv()
    add_low(c_two.at[0], c_two.at[0], ck.at[0, x])
    add_low(c_two.at[1], c_two.at[1], ck.at[1, x])
    c_last = push(c_two.at[1 - y], c_thr, peer_y, send.at[2, 1], recv.at[2, 1])
    v_y.wait()
    vec[...] = vec_x[...] + vec_y[...]
    shard = vec_out.shape[1]
    vec_out[...] = pltpu.roll(vec[0:8, :], width - me * shard, 1)[:, 0:shard]
    wide = usum_out.shape[1]
    per_row = width // wide
    row = vec[pl.ds(8 + me // per_row, 1), :]
    usum_out[...] = pltpu.roll(jnp.broadcast_to(row, (8, width)), width - (me % per_row) * wide, 1)[0:1, 0:wide]
    shard = width // 16
    p_sum = last(pk, p_thr, p_copies)
    c_last.wait_recv()
    c_sum = c_two[y].astype(f32) + c_thr[...].astype(f32)
    down_out[0 : 2 * shard, :] = p_sum[0 : 2 * shard]
    down_out[2 * shard : 4 * shard, :] = c_sum[0 : 2 * shard]
    ups = [part[t * shard : (t + 1) * shard] for part in (p_sum, c_sum) for t in (2, 3)]
    for t, part in enumerate(ups):
        wide_out[:, half + t * third : half + (t + 1) * third] = part
    wide_out[:, half + 4 * third :] = p_sum[4 * shard : 5 * shard]
    wide_out[:, 0:cut] = last(ta_two, ta_thr, ta_copies)
    wide_out[:, cut:half] = last(tb_two, tb_thr, tb_copies)
    done = {id(c) for c in (v_band, v_x, v_y, *v_z)}
    for copy in pending:
        if id(copy) not in done:
            copy.wait_send()
    store.wait()


def finish(dq, dk_own, dk_far, dv_own, dv_far, normed, tokens, rgrad, w_qkv, pieces, gain, msums, usums):
    rows, width = tokens.shape
    ff = usums.shape[1]
    half = 3 * width // 2
    shards = (4, 2, 2)
    third, shard = width // 2, width // 16
    q_shape = shards + (shard, half)
    p_piece, c_piece = (5 * shard, third), (4 * shard, third)
    cut = half // 256 * 128 + 128
    ta_piece, tb_piece = (shard, cut), (shard, half - cut)
    hbm, vmem = pl.BlockSpec(memory_space=pl.ANY), pl.BlockSpec(memory_space=pltpu.VMEM)
    shape = jax.ShapeDtypeStruct
    low = lambda *s: pltpu.VMEM(s, bf16)
    dma = pltpu.SemaphoreType.DMA
    return pl.pallas_call(
        finish_kernel,
        out_shape=(
            shape((rows, width), f32),
            shape((ff // 16, width // 2), f32),
            shape((width // 16, half + ff // 2 + width // 2), f32),
            shape((8, width // 16), f32),
            shape((1, ff // 16), f32),
        ),
        in_specs=[hbm] * 17 + [vmem] * 3,
        out_specs=[hbm] + [vmem] * 4,
        scratch_shapes=[
            low(rows, 3 * width),
            *([low(width, rows)] * 4),
            low(rows, width),
            pltpu.VMEM((rows, width), f32),
            pltpu.VMEM((rows, width), f32),
            low(width, 3 * width),
            low(4, *p_piece),
            low(3, 4, *p_piece),
            low(2, 2, *c_piece),
            low(*shards, shard, 3 * width),
            low(*q_shape),
            low(*q_shape),
            low(3, 2, 2, *c_piece),
            low(2, *c_piece),
            low(3, *p_piece),
            low(*c_piece),
            low(4, 2, *ta_piece),
            low(4, 2, *tb_piece),
            low(4, *ta_piece),
            low(4, *tb_piece),
            low(3, *ta_piece),
            low(3, *tb_piece),
            pltpu.VMEM((16, width), f32),
            pltpu.VMEM((16, width), f32),
            pltpu.VMEM((16, width), f32),
            pltpu.VMEM((16, width), f32),
            pltpu.VMEM((3, 16, width), f32),
            dma((16,)),
            dma,
            dma((4,)),
            dma((4,)),
            dma((5, 5)),
            dma((5, 5)),
            dma((6,)),
            dma((6,)),
        ],
        compiler_params=pltpu.CompilerParams(vmem_limit_bytes=52 * MIB, collective_id=0, has_side_effects=True),
        cost_estimate=pl.CostEstimate(flops=20 * 10**9, bytes_accessed=40 * 10**6, transcendentals=0),
        name="finish",
    )(dq, dk_own, dk_far, dv_own, dv_far, normed, tokens, rgrad, w_qkv, *pieces,
      gain, msums, usums)


def swap_band(x):
    return lax.ppermute(x, "band", [(0, 1), (1, 0)])


def pick(x, which, axis):
    return lax.dynamic_index_in_dim(x, which, axis, keepdims=False)


def halve(x, axis, bit, size):
    mine = (lax.axis_index("dp") >> bit) & 1
    arrived = lax.ppermute(pick(x, 1 - mine, axis), "dp", [(i, i ^ (1 << bit)) for i in range(size)])
    return pick(x, mine, axis).astype(f32) + arrived.astype(f32)


class Reduction:
    def __init__(self, x, order, size):
        rows, columns = x.shape
        levels = size.bit_length() - 1
        self.size = size
        self.x = x.reshape((2,) * levels + (rows // size, columns))
        self.left = list(range(levels - 1, -1, -1))
        self.order = list(order)

    def step(self):
        if self.order:
            bit = self.order.pop(0)
            x = halve(self.x, self.left.index(bit), bit, self.size)
            self.left.remove(bit)
            self.x = x.astype(bf16) if self.left else x

    def finish(self):
        while self.order:
            self.step()
        return self.x


def finish_any(size, band_at, query_grad, dk_own, dk_far, dv_own, dv_far, normed, tokens, residual_grad, w_qkv, pieces, gain, msums, usums):
    width = tokens.shape[1]
    rising = list(range(size.bit_length() - 1))
    turned = [1, 0] + rising[2:]
    packed, qkv_own, qkv_far, qkv_sums = qkv_grads(
        band_at, query_grad, dk_own, swap_band(dk_far), dv_own, swap_band(dv_far), normed
    )
    input_grad, first_sums = input_grads(packed, tokens, residual_grad, w_qkv, gain)

    def total(x, order):
        return Reduction(x, order, size).finish()

    def join(own, far):
        return (own.astype(f32) + swap_band(far).astype(f32)).astype(bf16)

    tall = jnp.concatenate([first_sums[:2], qkv_sums[:2], msums[:4]], axis=0)
    thin = jnp.concatenate([tall.T, usums[0].reshape(width, -1)], axis=1)
    thin = jnp.pad(thin, ((0, 0), (0, 128 - thin.shape[1]))).astype(bf16)
    thin_sum = total(join(thin, thin), turned)
    ups = usums.shape[1] // width
    return (
        input_grad,
        total(pieces[0], rising),
        total(pieces[1], turned),
        total(join(qkv_own, qkv_far), rising),
        total(pieces[2], turned),
        [thin_sum[:, t] for t in range(8)],
        thin_sum[:, 8 : 8 + ups].reshape(-1),
    )


def local(
    size,
    inputs,
    segment_ids,
    cotangent,
    first_gain,
    first_bias,
    w_qkv,
    query_bias,
    value_bias,
    w_proj,
    proj_bias,
    second_gain,
    second_bias,
    w_up,
    up_bias,
    w_down,
    down_bias,
):
    local_shape = inputs.shape
    width = local_shape[-1]
    band = lax.axis_index("band")
    band_at = band.astype(jnp.int32).reshape(1)
    tokens = inputs.reshape(-1, width)
    seg_own = segment_ids
    queries, k_own, v_own, normed, k_far, v_far, seg_far = project_qkv(
        tokens, seg_own, w_qkv, first_gain, first_bias, query_bias, value_bias
    )
    keys = (seg_own, seg_far, k_own, k_far, v_own, v_far)
    attended, query_lanes = attend_forward(band_at, queries, *keys)
    output, residual_grad, attended_grad, mlp_sums, up_sums, *pieces = mlp(
        size,
        tokens,
        attended,
        cotangent.reshape(-1, width),
        w_proj,
        w_up,
        w_down,
        proj_bias,
        second_gain,
        second_bias,
        up_bias,
        down_bias,
    )
    if size == 16:
        turns = [[(i, i ^ bits) for i in range(size)] for bits in (1, 2, 3, 8, 12)]
        sent = (*pieces[1:4], *pieces[6:8])
        pieces = [pieces[0], *pieces[4:6]] + [lax.ppermute(a, "dp", turn) for a, turn in zip(sent, turns)]
    query_grad, dk_own, dk_far, dv_own, dv_far, output = attend_backward(
        band_at, output, query_lanes, attended_grad, attended, *keys
    )
    if size == 16:
        input_grad, down_sum, wide_sum, vec, up_vec = finish(
            query_grad, dk_own, dk_far, dv_own, dv_far, normed, tokens, residual_grad, w_qkv, pieces, first_gain, mlp_sums, up_sums
        )
        first, second = 3 * width // 2, 3 * width // 2 + w_up.shape[1] // 2
        qkv_sum, up_sum, proj_sum = wide_sum[:, :first], wide_sum[:, first:second], wide_sum[:, second:]
        vectors, up_vector = [vec[t] for t in range(8)], up_vec.reshape(-1)
    else:
        input_grad, down_sum, up_sum, qkv_sum, proj_sum, vectors, up_vector = finish_any(
            size, band_at, query_grad, dk_own, dk_far, dv_own, dv_far, normed, tokens, residual_grad, w_qkv, pieces, first_gain, mlp_sums, up_sums
        )
    return (
        output.reshape(local_shape),
        input_grad.reshape(local_shape),
        vectors[0],
        vectors[1],
        qkv_sum,
        vectors[2],
        vectors[3],
        proj_sum,
        vectors[7],
        vectors[5],
        vectors[6],
        up_sum,
        up_vector,
        down_sum,
        vectors[4],
    )


def solution(mesh):
    size = mesh.shape["dp"]
    placed = (P("dp", "band", None), P("dp", "band"), P("dp", "band", None)) + (P(),) * 13
    split, thin = P("dp", "band"), P("dp")
    wide = P("dp", "band", None)
    return jax.shard_map(
        functools.partial(local, size),
        mesh=mesh,
        in_specs=placed,
        out_specs=(wide, wide, thin, thin, split, thin, thin, split, thin, thin, thin, split, thin, split, thin),
        check_vma=False,
    )
```
